32 devices in a mesh: dp: 8 (over z, y), tensor: 4 (over x, core).
Axes of the slice: x: 2, y: 2, z: 4, core: 2. Of those that a mesh axis runs over, the one named last changes fastest.
Arguments:
- tokens: bfloat16 [16384, 768], P(('dp', 'tensor')), may hold values from -6 to 6
- cotangent: bfloat16 [16384, 768], P(('dp', 'tensor')), may hold values from -6 to 6
- qkv_weight: float32 [3, 768, 768], P(None, 'dp', 'tensor'), may hold values from -0.21875 to 0.21875
- qv_bias: float32 [2, 768], P(None, 'tensor'), may hold values from -1.8 to 1.8
- out_weight: float32 [768, 768], P('tensor', 'dp'), may hold values from -1 to 1
- out_bias: float32 [768], replicated, may hold values from -1.8 to 1.8
- first_gain: float32 [768], replicated, may hold values from 0.5 to 1.5
- first_shift: float32 [768], replicated, may hold values from -1.2 to 1.2
- up_weight: float32 [768, 3072], P('dp', 'tensor'), may hold values from -0.21875 to 0.21875
- up_bias: float32 [3072], P('tensor'), may hold values from -1.8 to 1.8
- down_weight: float32 [3072, 768], P('tensor', 'dp'), may hold values from -0.109375 to 0.109375
- down_bias: float32 [768], replicated, may hold values from -1.8 to 1.8
- second_gain: float32 [768], replicated, may hold values from 0.5 to 1.5
- second_shift: float32 [768], replicated, may hold values from -1.2 to 1.2
- act_ranges: float32 [4], replicated, may hold values from 0.5 to 3.5, as said below
- long_lengths: int32 [8], P('dp'), may hold values from 128 to 512, as said below
- short_lengths: int32 [96], P('dp'), may hold values from 32 to 128, as said below
Outputs:
- layer_out: bfloat16 [16384, 768], P(('dp', 'tensor'))
- tokens_grad: bfloat16 [16384, 768], P(('dp', 'tensor'))
- qkv_grad: float32 [3, 768, 768], P(None, 'dp', 'tensor')
- qv_bias_grad: float32 [2, 768], P(None, 'tensor')
- out_grad: float32 [768, 768], P('tensor', 'dp')
- out_bias_grad: float32 [768], replicated
- first_gain_grad: float32 [768], replicated
- first_shift_grad: float32 [768], replicated
- up_grad: float32 [768, 3072], P('dp', 'tensor')
- up_bias_grad: float32 [3072], P('tensor')
- down_grad: float32 [3072, 768], P('tensor', 'dp')
- down_bias_grad: float32 [768], replicated
- second_gain_grad: float32 [768], replicated
- second_shift_grad: float32 [768], replicated
- new_ranges: float32 [4], replicated
The draws below stay inside these ranges and needn't reach their ends.
Inputs may be any that keep to these rules, and one draw needn't show every extreme that they name: Each long sequence uses its first long_lengths slots; at least a quarter of 512, and some sequence uses all 512. Each short sequence uses its first short_lengths slots; at least a quarter of 128, and some sequence uses all 128. `act_ranges`: entry 1 lies in 0.5 to 0.8, the others in 2.5 to 3.5.
All inputs are finite; a program needn't handle non-finite values.
Results may differ from the reference program's by a relative error of at most 0.018.
The reference program's roundings to bfloat16 on the way count: a program that leaves them out, or rounds other values in their place, can miss the bound.
Values may be sent and summed in bfloat16 or wider, within the bound.
No kernel may reach another device: no remote copies, remote signals or barrier semaphores. Data moves between devices by JAX's collectives and lax.ppermute only.
A program may use at most 128 MiB of HBM per device.

```python
import jax
import jax.numpy as jnp
from jax import lax

D = 768
HEADS = 12
HEAD_DIM = 64
FF = 3072
LONG_LEN = 512
SHORT_LEN = 128
LONG_DEV = 1
SHORT_DEV = 12
TOKENS = 16384
LONG_COUNT = 8
SHORT_COUNT = 96
N_DP = 8


def draw_act_ranges(key, part):
    low_ends = jnp.array([2.5, 0.5, 2.5, 2.5], jnp.float32)
    high_ends = jnp.array([3.5, 0.8, 3.5, 3.5], jnp.float32)
    fraction = jax.random.uniform(key, (4,), jnp.float32)
    return low_ends * jnp.exp(fraction * jnp.log(high_ends / low_ends))


def draw_lengths(key, how_many, longest):
    shortest = longest // 4
    drawn_lengths = jax.random.randint(jax.random.fold_in(key, 1), (how_many,), shortest, longest + 1)
    shuffled = jax.random.permutation(jax.random.fold_in(key, 2), how_many)
    return drawn_lengths.at[shuffled[0]].set(longest).at[shuffled[1]].set(shortest)


def draw_long_lengths(key, part):
    return draw_lengths(key, LONG_COUNT, LONG_LEN)


def draw_short_lengths(key, part):
    return draw_lengths(key, SHORT_COUNT, SHORT_LEN)


def with_spikes(values, rng, source, target, parts, factor):
    def block_of(dim):
        return (jnp.arange(values.shape[dim]) // (values.shape[dim] // parts)).reshape((-1,) + (1,) * (values.ndim - 1 - dim))

    near = jax.random.permutation(rng, parts)[block_of(target)]
    far = (block_of(target) + parts // 2) % parts
    return jnp.where((block_of(source) == near) | (block_of(source) == far), factor * values, values)


def steps_of(rng, shape, cuts, low, top_value):
    factor_of, own = 1.0, jax.random.fold_in(rng, 6)
    for dim, shards_of in cuts:
        steps = jnp.exp(jax.random.uniform(jax.random.fold_in(own, dim), (shards_of,), jnp.float32, low / len(cuts), top_value / len(cuts)))
        factor_of = factor_of * jnp.repeat(steps, shape[dim] // shards_of).reshape([-1 if axis == dim else 1 for axis in range(len(shape))])
    return factor_of


def centred(rng, dims, width, most, split=(), held_as=jnp.bfloat16):
    level = steps_of(rng, dims, split, -0.22, 0.18) if split else 1.0
    drawn = jax.random.normal(rng, dims, jnp.float32) * width * level
    return jnp.minimum(jnp.maximum(drawn, -most), most).astype(held_as)


def bell_draw_with(key, extent, spread, reach, cuts, heavy, held_as=jnp.bfloat16):
    drawn = spread * jax.random.normal(key, extent, jnp.float32)
    if cuts:
        drawn = drawn * steps_of(key, extent, cuts, -0.22, 0.18)
    return jnp.clip(with_spikes(drawn, jax.random.fold_in(key, 3), *heavy), -reach, reach).astype(held_as)


def setup_inputs(seed: int = 0) -> dict:
    key_list = jax.random.split(jax.random.key(seed), 18)
    return {
        "tokens": centred(key_list[0], (TOKENS, D), 1.0, 6.0, ((0, 32),)),
        "cotangent": bell_draw_with(key_list[1], (TOKENS, D), 1.0, 6.0, ((0, 32),), (0, 1, 32, 2.75)),
        "qkv_weight": centred(key_list[2], (3, D, D), D ** -0.5, 0.21875, ((1, 8), (2, 4)), jnp.float32),
        "qv_bias": centred(key_list[3], (2, D), 0.3, 1.8, ((1, 4),), jnp.float32),
        "out_weight": centred(key_list[4], (D, D), (HEAD_DIM // 2) ** -0.5, 1.0, ((0, 4), (1, 8)), jnp.float32),
        "out_bias": centred(key_list[5], (D,), 0.3, 1.8, (), jnp.float32),
        "first_gain": jnp.clip(1.0 + 0.1 * jax.random.normal(key_list[6], (D,), jnp.float32), 0.5, 1.5),
        "first_shift": centred(key_list[7], (D,), 0.2, 1.2, (), jnp.float32),
        "up_weight": centred(key_list[8], (D, FF), D ** -0.5, 0.21875, ((0, 8), (1, 4)), jnp.float32),
        "up_bias": centred(key_list[9], (FF,), 0.3, 1.8, ((0, 4),), jnp.float32),
        "down_weight": centred(key_list[10], (FF, D), FF ** -0.5, 0.109375, ((0, 4), (1, 8)), jnp.float32),
        "down_bias": centred(key_list[11], (D,), 0.3, 1.8, (), jnp.float32),
        "second_gain": jnp.clip(1.0 + 0.1 * jax.random.normal(key_list[12], (D,), jnp.float32), 0.5, 1.5),
        "second_shift": centred(key_list[13], (D,), 0.2, 1.2, (), jnp.float32),
        "act_ranges": draw_act_ranges(jax.random.fold_in(key_list[17], 71), 0),
        "long_lengths": draw_long_lengths(jax.random.fold_in(key_list[17], 71), 0),
        "short_lengths": draw_short_lengths(jax.random.fold_in(key_list[17], 71), 0),
    }


HIGHEST = lax.Precision.HIGHEST
ema_decay = 0.9
epsilon = 1e-06

@jax.custom_vjp
def low(v):
    return lax.optimization_barrier(v.astype(jnp.bfloat16)).astype(jnp.float32)

@jax.custom_vjp
def low_back(v):
    return v

def low_keep(v):
    return (low(v), None)

def low_pass(kept, grad):
    return (grad,)

def back_keep(v):
    return (v, None)

def back_low(kept, grad):
    return (low(grad),)
low.defvjp(low_keep, low_pass)
low_back.defvjp(back_keep, back_low)

def matmul(left, right):
    return jnp.dot(left, right, precision=HIGHEST, preferred_element_type=jnp.float32)

def saturate(values, limit):
    return limit * jnp.tanh(values / limit)

def block_masks(long_part, short_part):
    per_block = LONG_LEN // SHORT_LEN
    position = jnp.arange(LONG_LEN, dtype=jnp.int32)
    long_segment = jnp.zeros((long_part.shape[0], LONG_LEN), jnp.int32)
    long_valid = position[None, :] < long_part[:, None]
    short_rows = short_part.reshape(-1, per_block)
    short_segment = jnp.broadcast_to(position // SHORT_LEN, (short_rows.shape[0], LONG_LEN))
    short_limit = jnp.repeat(short_rows, SHORT_LEN, axis=1)
    short_valid = (position % SHORT_LEN)[None, :] < short_limit
    return (jnp.concatenate([long_segment, short_segment], 0), jnp.concatenate([long_valid, short_valid], 0))

def layer_norm(summed, gain, shift):
    average = lax.optimization_barrier(jnp.mean(summed, axis=-1, keepdims=True))
    centered = summed - average
    return centered * lax.rsqrt(lax.optimization_barrier(jnp.mean(centered * centered, axis=-1, keepdims=True)) + epsilon) * gain + shift

def attend(pieces):
    queries, key_rows, values, segment, key_valid = pieces
    scores = jnp.einsum('qhd,khd->hqk', queries, key_rows, precision=HIGHEST) * HEAD_DIM ** (-0.5)
    scores = low_back(scores)
    allowed = (segment[:, None] == segment[None, :]) & key_valid[None, :]
    masked = jnp.where(allowed[None, :, :], scores, -1000000000.0)
    shares = jax.nn.softmax(masked, axis=-1)
    return jnp.einsum('hqk,khd->qhd', low(shares), values, precision=HIGHEST)

def layer_group(inputs, params, act_ranges, segment, key_valid):
    qkv_low, qv_bias, out_low, out_bias, first_gain, first_shift, up_low, up_bias, down_low, down_bias, second_gain, second_shift = params
    row_total = inputs.shape[0]
    in_clip = low(jnp.clip(inputs, -act_ranges[0], act_ranges[0]))
    queries = low_back(low(matmul(in_clip, qkv_low[0]) + qv_bias[0]))
    key_rows = low_back(low(matmul(in_clip, qkv_low[1])))
    values = low_back(low(matmul(in_clip, qkv_low[2]) + qv_bias[1]))
    blocked = (row_total // LONG_LEN, LONG_LEN, HEADS, HEAD_DIM)
    context = lax.map(jax.checkpoint(attend), (queries.reshape(blocked), key_rows.reshape(blocked), values.reshape(blocked), segment, key_valid))
    context = context.reshape(row_total, D)
    ctx_clip = low(saturate(low_back(context), act_ranges[1]))
    first_sum = inputs + low_back(matmul(ctx_clip, out_low)) + out_bias
    middle = layer_norm(first_sum, first_gain, first_shift)
    mid_clip = low(saturate(middle, act_ranges[2]))
    hidden = jax.nn.gelu(low_back(matmul(mid_clip, up_low) + up_bias), approximate=False)
    act_clip = low(saturate(hidden, act_ranges[3]))
    second_sum = middle + low_back(matmul(act_clip, down_low)) + down_bias
    result = layer_norm(second_sum, second_gain, second_shift)
    maxima = jnp.stack([jnp.max(jnp.abs(inputs)), jnp.max(jnp.abs(context)), jnp.max(jnp.abs(middle)), jnp.max(jnp.abs(hidden))])
    return (result, maxima)

def reference(tokens, cotangent, qkv_weight, qv_bias, out_weight, out_bias, first_gain, first_shift, up_weight, up_bias, down_weight, down_bias, second_gain, second_shift, act_ranges, long_lengths, short_lengths):
    segment, key_valid = jax.vmap(block_masks)(long_lengths.reshape(N_DP, LONG_DEV), short_lengths.reshape(N_DP, SHORT_DEV))

    def forward(inputs, qkv_arg, qv_arg, out_arg, out_bias_arg, gain_one, shift_one, up_arg, up_bias_arg, down_arg, down_bias_arg, gain_two, shift_two):
        lowered = (low(qkv_arg), qv_arg, low(out_arg), out_bias_arg, gain_one, shift_one, low(up_arg), up_bias_arg, low(down_arg), down_bias_arg, gain_two, shift_two)

        def group_step(carried, group_data):
            group_rows, group_segment, group_valid = group_data
            result, maxima = layer_group(group_rows, lowered, act_ranges, group_segment, group_valid)
            return (carried, (result, maxima))
        carried, (results, maxima) = lax.scan(jax.checkpoint(group_step), jnp.zeros((), jnp.float32), (inputs.reshape(N_DP, -1, D), segment, key_valid))
        return (results.reshape(-1, D), lax.optimization_barrier(jnp.max(maxima, axis=0)))
    primals = (tokens.astype(jnp.float32), qkv_weight, qv_bias, out_weight, out_bias, first_gain, first_shift, up_weight, up_bias, down_weight, down_bias, second_gain, second_shift)
    result, pullback, maxima = jax.vjp(forward, *primals, has_aux=True)
    gradients = pullback(cotangent.astype(jnp.float32))
    new_ranges = ema_decay * act_ranges + (1.0 - ema_decay) * maxima
    return (result.astype(jnp.bfloat16), gradients[0].astype(jnp.bfloat16), gradients[1], gradients[2], gradients[3], gradients[4], gradients[5], gradients[6], gradients[7], gradients[8], gradients[9], gradients[10], gradients[11], gradients[12], new_ranges)
```

```python
import itertools

import jax
import jax.numpy as jnp
from jax import lax
from jax.sharding import PartitionSpec as P

HEAD_DIM = 64
LONG_LEN = 512
SHORT_LEN = 128
ALL = ("dp", "tensor")

ema_decay = 0.9
epsilon = 1e-06
root_half = 0.7071067811865476
density_scale = 0.3989422804014327
NEG = -1000000000.0

f32 = jnp.float32
bf16 = jnp.bfloat16


def mm(left, right):
    return jnp.dot(left, right, preferred_element_type=f32)


def mm_tn(left, right):
    return lax.dot_general(left, right, (((0,), (0,)), ((), ())), preferred_element_type=f32)


def mm_nt(left, right):
    return lax.dot_general(left, right, (((1,), (1,)), ((), ())), preferred_element_type=f32)


def _lin(z, y, x, c):
    return (z * 2 + y) * 4 + x * 2 + c


def _perm(fn):
    out = []
    for z, y, x, c in itertools.product(range(4), range(2), range(2), range(2)):
        out.append((_lin(z, y, x, c), _lin(*fn(z, y, x, c))))
    return out


PC = _perm(lambda z, y, x, c: (z, y, x, 1 - c))
PX = _perm(lambda z, y, x, c: (z, y, 1 - x, c))
PY = _perm(lambda z, y, x, c: (z, 1 - y, x, c))
PZ = [_perm(lambda z, y, x, c, k=k: ((z + k) % 4, y, x, c)) for k in range(4)]
PZX = [_perm(lambda z, y, x, c, k=k: (z ^ k, y, x, c)) for k in range(4)]


def send(value, perm):
    return lax.ppermute(value, ALL, perm)


class Grid:
    blocks = 4

    def __init__(self):
        dp = lax.axis_index("dp")
        lane = lax.axis_index("tensor")
        self.z, self.y = dp // 2, dp % 2
        self.x, self.c = lane // 2, lane % 2

    def absolute(self, near, far_y):
        both = jnp.stack([near, far_y], 1)
        by_z = jnp.flip(both, 0)
        twice = jnp.concatenate([by_z, by_z], 0)
        placed = lax.dynamic_slice_in_dim(twice, (3 - self.z) % 4, 4, 0)
        placed = jnp.where(self.y == 0, placed, jnp.flip(placed, 1))
        return placed.reshape(-1, near.shape[-1])

    def gather(self, shard):
        own = shard[None]
        far = jnp.stack([send(shard, PZ[k]) for k in (1, 2, 3)])
        line = jnp.concatenate([own, far], 0)
        over_x = jnp.concatenate([send(own, PX), send(far, PX)], 0)
        over_y = jnp.concatenate([send(own, PY), send(far, PY)], 0)
        diag = jnp.concatenate([send(over_y[:2], PX), send(over_x[2:], PY)], 0)
        mine = jnp.stack([self.absolute(line, over_y), self.absolute(over_x, diag)])
        theirs = send(mine, PC)
        return jnp.concatenate([mine, theirs], 0)

    def relative(self, grads):
        n, rows, cols = grads.shape
        split = grads.reshape(n, 4, 2, rows // 8, cols)
        split = jnp.where(self.y == 0, split, jnp.flip(split, 2))
        twice = jnp.concatenate([split, split], 1)
        return lax.dynamic_slice_in_dim(twice, self.z, 4, 1).swapaxes(1, 2)

    def scatter_sum(self, grads):
        got = send(grads[2:].astype(bf16), PC)
        both = self.relative((grads[:2] + got.astype(f32)).astype(bf16))
        from_x = send(both[1, 1, :2], PX)
        from_y = send(both[1, 1, 2:], PY)
        y_out = jnp.concatenate([both[0, 1, :2] + from_x, both[0, 1, 2:]], 0)
        x_out = jnp.concatenate([both[1, 0, :2], both[1, 0, 2:] + from_y], 0)
        in_x = send(x_out, PX)
        in_y = send(y_out, PY)
        line = both[0, 0].astype(f32) + in_x.astype(f32) + in_y.astype(f32)
        low = line.astype(bf16)
        parts = [send(low[k], PZ[k]) for k in (1, 2, 3)]
        return line[0] + parts[0].astype(f32) + parts[1].astype(f32) + parts[2].astype(f32)

    def gather_lane(self, vec):
        over_x = send(vec, PX)
        pair = jnp.stack([vec, over_x])
        return jnp.concatenate([pair, send(pair, PC)], 0)

    def order_lane(self, rel):
        grid = rel.reshape((2, 2) + rel.shape[1:])
        grid = jnp.where(self.x == 0, grid, jnp.flip(grid, 1))
        grid = jnp.where(self.c == 0, grid, jnp.flip(grid, 0))
        return grid.swapaxes(0, 1).reshape(rel.shape)

    def sum_max(self, sums, tops):
        for perm in (PC, PX, PY, PZX[1], PZX[2]):
            sums = sums + send(sums, perm)
            tops = jnp.maximum(tops, send(tops, perm))
        return sums, tops


class Plain:
    def __init__(self):
        self.blocks = lax.axis_size("tensor")

    def gather(self, shard):
        rows = lax.all_gather(shard, "dp", axis=0, tiled=True)
        return lax.all_gather(rows, "tensor", axis=0)

    def scatter_sum(self, grads):
        own = lax.psum_scatter(grads, "tensor", scatter_dimension=0, tiled=False)
        return lax.psum_scatter(own, "dp", scatter_dimension=0, tiled=True)

    def gather_lane(self, vec):
        return lax.all_gather(vec, "tensor", axis=0)

    def order_lane(self, rel):
        return rel

    def sum_max(self, sums, tops):
        return lax.psum(sums, ALL), lax.pmax(tops, ALL)


def saturate(values, limit):
    return limit * jnp.tanh(values / limit)


def saturate_slope(values, limit):
    bent = jnp.tanh(values / limit)
    return 1.0 - bent * bent


def gelu_slope(values):
    return (
        0.5 * (1.0 + lax.erf(values * root_half))
        + values * jnp.exp(-0.5 * values * values) * density_scale
    )


def block_masks(long_part, short_part):
    per_block = LONG_LEN // SHORT_LEN
    position = jnp.arange(LONG_LEN, dtype=jnp.int32)
    long_segment = jnp.zeros((long_part.shape[0], LONG_LEN), jnp.int32)
    long_valid = position[None, :] < long_part[:, None]
    short_rows = short_part.reshape(-1, per_block)
    short_segment = jnp.broadcast_to(position // SHORT_LEN, (short_rows.shape[0], LONG_LEN))
    short_limit = jnp.repeat(short_rows, SHORT_LEN, axis=1)
    short_valid = (position % SHORT_LEN)[None, :] < short_limit
    return (
        jnp.concatenate([long_segment, short_segment], 0),
        jnp.concatenate([long_valid, short_valid], 0),
    )


def norm_forward(summed):
    centered = summed - jnp.mean(summed, axis=-1, keepdims=True)
    inv_scale = lax.rsqrt(jnp.mean(centered * centered, axis=-1, keepdims=True) + epsilon)
    return centered * inv_scale, inv_scale


def norm_backward(incoming, normed, inv_scale, gain):
    scaled = incoming * gain
    row_mean = jnp.mean(scaled, axis=-1, keepdims=True)
    row_cross = jnp.mean(scaled * normed, axis=-1, keepdims=True)
    grad_in = inv_scale * (scaled - row_mean - normed * row_cross)
    return grad_in, jnp.sum(incoming * normed, axis=0), jnp.sum(incoming, axis=0)


def make_body(special):
    def body(
        tokens,
        cotangent,
        qkv_weight,
        qv_bias,
        out_weight,
        out_bias,
        first_gain,
        first_shift,
        up_weight,
        up_bias,
        down_weight,
        down_bias,
        second_gain,
        second_shift,
        act_ranges,
        long_lengths,
        short_lengths,
    ):
        net = Grid() if special else Plain()
        lane = lax.axis_index("tensor")
        rows = tokens.shape[0]
        assert rows == LONG_LEN
        cols = qkv_weight.shape[2]
        heads = cols // HEAD_DIM
        blocks = net.blocks

        shard_a = jnp.concatenate(
            [qkv_weight[0], qkv_weight[1], qkv_weight[2], out_weight.T], 1
        ).astype(bf16)
        biases = net.gather_lane(jnp.concatenate([qv_bias[0], qv_bias[1], up_bias]))
        full_a = net.gather(shard_a)
        full_u = net.gather(up_weight.astype(bf16))
        full_d = net.gather(down_weight.T.astype(bf16))

        inputs = tokens.astype(f32)
        in_clip = jnp.clip(inputs, -act_ranges[0], act_ranges[0]).astype(bf16)

        def part(j):
            return full_a[:, :, j * cols : (j + 1) * cols]

        def project(j):
            return jnp.einsum("td,ade->tae", in_clip, part(j), preferred_element_type=f32)

        shape = (rows, blocks * heads, HEAD_DIM)
        queries = (project(0) + biases[:, :cols]).astype(bf16).reshape(shape)
        key_rows = project(1).astype(bf16).reshape(shape)
        values = (project(2) + biases[:, cols : 2 * cols]).astype(bf16).reshape(shape)
        segments, valids = block_masks(long_lengths, short_lengths)
        segment = lax.dynamic_index_in_dim(segments, lane, 0, False)
        key_valid = lax.dynamic_index_in_dim(valids, lane, 0, False)
        allowed = (segment[:, None] == segment[None, :]) & key_valid[None, :]
        score_scale = HEAD_DIM ** (-0.5)
        scores = (
            jnp.einsum("qhd,khd->hqk", queries, key_rows, preferred_element_type=f32) * score_scale
        )
        scores = jnp.where(allowed[None], scores, NEG)
        expanded = jnp.exp(scores - jnp.max(scores, axis=-1, keepdims=True))
        shares = expanded / jnp.sum(expanded, axis=-1, keepdims=True)
        low_shares = shares.astype(bf16)
        context = jnp.einsum("hqk,khd->qhd", low_shares, values, preferred_element_type=f32)
        context = context.reshape(rows, blocks, cols)
        ctx_clip = saturate(context, act_ranges[1]).astype(bf16)
        attn_out = jnp.einsum("tae,ade->td", ctx_clip, part(3), preferred_element_type=f32)
        first_normed, first_inv = norm_forward(inputs + attn_out + out_bias)
        middle = first_normed * first_gain + first_shift
        mid_clip = saturate(middle, act_ranges[2]).astype(bf16)
        up_out = jnp.einsum("td,ade->tae", mid_clip, full_u, preferred_element_type=f32)
        up_out = up_out + biases[:, 2 * cols :]
        hidden = jax.nn.gelu(up_out, approximate=False)
        act_clip = saturate(hidden, act_ranges[3]).astype(bf16)
        ffn_out = jnp.einsum("tae,ade->td", act_clip, full_d, preferred_element_type=f32)
        second_normed, second_inv = norm_forward(middle + ffn_out + down_bias)
        layer_out = (second_normed * second_gain + second_shift).astype(bf16)
        tops = jnp.stack([jnp.max(jnp.abs(v)) for v in (inputs, context, middle, hidden)])

        grad_second, second_gain_part, second_shift_part = norm_backward(
            cotangent.astype(f32), second_normed, second_inv, second_gain
        )
        ffn_grad = grad_second.astype(bf16)
        down_grad = jnp.einsum("td,tae->ade", ffn_grad, act_clip, preferred_element_type=f32)
        down_grad = net.scatter_sum(down_grad).T
        grad_act = jnp.einsum("td,ade->tae", ffn_grad, full_d, preferred_element_type=f32)
        grad_act = grad_act * saturate_slope(hidden, act_ranges[3])
        grad_up = (grad_act * gelu_slope(up_out)).astype(bf16)
        up_grad = jnp.einsum("td,tae->ade", mid_clip, grad_up, preferred_element_type=f32)
        up_grad = net.scatter_sum(up_grad)
        mid_sum = jnp.einsum("tae,ade->td", grad_up, full_u, preferred_element_type=f32)
        grad_middle = grad_second + mid_sum * saturate_slope(middle, act_ranges[2])
        grad_first, first_gain_part, first_shift_part = norm_backward(
            grad_middle, first_normed, first_inv, first_gain
        )
        attn_grad = grad_first.astype(bf16)
        out_grad = jnp.einsum("td,tae->ade", attn_grad, ctx_clip, preferred_element_type=f32)
        grad_ctx = jnp.einsum("td,ade->tae", attn_grad, part(3), preferred_element_type=f32)
        grad_ctx = (grad_ctx * saturate_slope(context, act_ranges[1])).astype(bf16).reshape(shape)
        grad_shares = jnp.einsum("qhd,khd->hqk", grad_ctx, values, preferred_element_type=f32)
        row_inner = jnp.sum(shares * grad_shares, axis=-1, keepdims=True)
        grad_scores = (shares * (grad_shares - row_inner)).astype(bf16)
        grad_values = jnp.einsum("hqk,qhd->khd", low_shares, grad_ctx, preferred_element_type=f32)
        grad_queries = jnp.einsum("hqk,khd->qhd", grad_scores, key_rows, preferred_element_type=f32)
        grad_keys = jnp.einsum("hqk,qhd->khd", grad_scores, queries, preferred_element_type=f32)
        flat = (rows, blocks, cols)
        grad_queries = (grad_queries * score_scale).astype(bf16).reshape(flat)
        grad_keys = (grad_keys * score_scale).astype(bf16).reshape(flat)
        grad_values = grad_values.astype(bf16).reshape(flat)
        stacked = jnp.concatenate([grad_queries, grad_keys, grad_values], -1)
        qkv_grad = jnp.einsum("td,tae->ade", in_clip, stacked, preferred_element_type=f32)
        a_grad = net.scatter_sum(jnp.concatenate([qkv_grad, out_grad], -1))
        qkv_grad = jnp.stack([a_grad[:, j * cols : (j + 1) * cols] for j in range(3)])
        out_grad = a_grad[:, 3 * cols :].T
        input_sum = jnp.einsum(
            "tae,ade->td", stacked, full_a[:, :, : 3 * cols], preferred_element_type=f32
        )
        tokens_grad = grad_first + jnp.where(jnp.abs(inputs) <= act_ranges[0], input_sum, 0.0)

        laned = jnp.concatenate(
            [
                jnp.sum(grad_queries.astype(f32), axis=0),
                jnp.sum(grad_values.astype(f32), axis=0),
                jnp.sum(grad_up.astype(f32), axis=0),
            ],
            -1,
        )
        shared = jnp.stack(
            [
                jnp.sum(grad_first, axis=0),
                first_gain_part,
                first_shift_part,
                jnp.sum(grad_second, axis=0),
                second_gain_part,
                second_shift_part,
            ]
        )
        wide = laned.shape[1]
        sums = jnp.concatenate([net.order_lane(laned).reshape(-1), shared.reshape(-1)])
        sums, tops = net.sum_max(sums, tops)
        own = lax.dynamic_slice_in_dim(sums, lane * wide, wide)
        shared = sums[blocks * wide :].reshape(shared.shape)
        qv_bias_grad = own[: 2 * cols].reshape(2, cols)
        new_ranges = ema_decay * act_ranges + (1.0 - ema_decay) * tops
        return (
            layer_out,
            tokens_grad.astype(bf16),
            qkv_grad,
            qv_bias_grad,
            out_grad,
            shared[0],
            shared[1],
            shared[2],
            up_grad,
            own[2 * cols :],
            down_grad,
            shared[3],
            shared[4],
            shared[5],
            new_ranges,
        )

    return body


def solution(mesh):
    in_specs = (
        P(ALL, None),
        P(ALL, None),
        P(None, "dp", "tensor"),
        P(None, "tensor"),
        P("tensor", "dp"),
        P(),
        P(),
        P(),
        P("dp", "tensor"),
        P("tensor"),
        P("tensor", "dp"),
        P(),
        P(),
        P(),
        P(),
        P("dp"),
        P("dp"),
    )
    out_specs = (
        P(ALL, None),
        P(ALL, None),
        P(None, "dp", "tensor"),
        P(None, "tensor"),
        P("tensor", "dp"),
        P(),
        P(),
        P(),
        P("dp", "tensor"),
        P("tensor"),
        P("tensor", "dp"),
        P(),
        P(),
        P(),
        P(),
    )
    special = mesh.shape["dp"] == 8 and mesh.shape["tensor"] == 4
    return jax.shard_map(
        make_body(special), mesh=mesh, in_specs=in_specs, out_specs=out_specs, check_vma=False
    )
```

```python
import functools
import itertools

import jax
import jax.numpy as jnp
from jax import lax
from jax.experimental import pallas as pl
from jax.experimental.pallas import tpu as pltpu
from jax.sharding import PartitionSpec as P

HEAD_DIM = 64
LONG_LEN = 512
SHORT_LEN = 128
ALL = ("dp", "tensor")

ema_decay = 0.9
epsilon = 1e-06
root_half = 0.7071067811865476
density_scale = 0.3989422804014327
score_scale = HEAD_DIM ** (-0.5)
NEG = -1000000000.0

f32 = jnp.float32
bf16 = jnp.bfloat16


def mm(left, right):
    return jnp.dot(left, right, preferred_element_type=f32)


def mm_tn(left, right):
    return lax.dot_general(left, right, (((0,), (0,)), ((), ())), preferred_element_type=f32)


def mm_nt(left, right):
    return lax.dot_general(left, right, (((1,), (1,)), ((), ())), preferred_element_type=f32)


def _lin(z, y, x, c):
    return (z * 2 + y) * 4 + x * 2 + c


def _perm(fn):
    out = []
    for z, y, x, c in itertools.product(range(4), range(2), range(2), range(2)):
        out.append((_lin(z, y, x, c), _lin(*fn(z, y, x, c))))
    return out


PC = _perm(lambda z, y, x, c: (z, y, x, 1 - c))
PX = _perm(lambda z, y, x, c: (z, y, 1 - x, c))
PY = _perm(lambda z, y, x, c: (z, 1 - y, x, c))
PZ1 = _perm(lambda z, y, x, c: (z ^ 1, y, x, c))
PZ2 = _perm(lambda z, y, x, c: (z ^ 2, y, x, c))


def send(value, perm):
    return lax.ppermute(value, ALL, perm)


class Pieces:
    def __init__(self, bufs, plan):
        self.bufs, self.plan = list(bufs), plan


class Grid:
    parts = 8

    def gather(self, shard):
        own = shard[None]
        pair = jnp.concatenate([own, send(own, PZ1)], 0)
        line = jnp.concatenate([pair, send(pair, PZ2)], 0)
        over_x = send(line, PX)
        over_y = send(line, PY)
        diag_x = send(over_y[:2], PX)
        diag_y = send(over_x[2:], PY)
        near = [line, over_x, over_y, diag_x, diag_y]
        far = [send(b, PC) for b in near]
        rows = shard.shape[0]
        plan = []
        for base, lane in ((0, 0), (5, 2)):
            for k in range(4):
                plan.append((base, k, lane, rows, 2 * k))
                plan.append((base + 1, k, lane + 1, rows, 2 * k))
                plan.append((base + 2, k, lane, rows, 2 * k + 1))
                plan.append((base + 3 + k // 2, k % 2, lane + 1, rows, 2 * k + 1))
        return Pieces(near + far, plan)

    @staticmethod
    def slot(block, dp):
        place = block ^ dp
        return (place & 1) * 4 + (place >> 1)

    def scatter_sum(self, near, far):
        got = send(far, PC)
        shape = (2, 2, 4) + near.shape[2:]
        near, got = near.reshape(shape), got.reshape(shape)

        def both(i, j, ks=slice(None)):
            return near[i, j, ks].astype(f32) + got[i, j, ks].astype(f32)

        lo, hi = slice(0, 2), slice(2, 4)
        from_x = send(both(1, 1, lo).astype(bf16), PX).astype(f32)
        from_y = send(both(1, 1, hi).astype(bf16), PY).astype(f32)
        x_out = jnp.concatenate([both(1, 0, lo), both(1, 0, hi) + from_y], 0).astype(bf16)
        y_out = jnp.concatenate([both(0, 1, lo) + from_x, both(0, 1, hi)], 0).astype(bf16)
        in_x, in_y = send(x_out, PX).astype(f32), send(y_out, PY).astype(f32)
        far_z = (both(0, 0, hi) + in_x[2:] + in_y[2:]).astype(bf16)
        from_z = send(far_z, PZ2).astype(f32)
        near_z = both(0, 0, lo) + in_x[:2] + in_y[:2] + from_z
        return near_z[0] + send(near_z[1].astype(bf16), PZ1).astype(f32)

    def gather_lane(self, vec):
        pair = jnp.stack([vec, send(vec, PX)])
        return jnp.concatenate([pair, send(pair, PC)], 0)

    def order_lane(self, rel):
        lane = lax.axis_index("tensor")
        grid = rel.reshape((2, 2) + rel.shape[1:])
        grid = jnp.where(lane // 2 == 0, grid, jnp.flip(grid, 1))
        grid = jnp.where(lane % 2 == 0, grid, jnp.flip(grid, 0))
        return grid.swapaxes(0, 1).reshape(rel.shape)

    def sum_max(self, both, is_top):
        for perm in (PC, PX, PY, PZ1, PZ2):
            other = send(both, perm)
            both = jnp.where(is_top, jnp.maximum(both, other), both + other)
        return both


class Plain:
    parts = 1

    def gather(self, shard):
        rows = lax.all_gather(shard, "dp", axis=0, tiled=True)
        full = lax.all_gather(rows, "tensor", axis=0)
        return Pieces([full], [(0, k, k, full.shape[1], 0) for k in range(full.shape[0])])

    @staticmethod
    def slot(block, dp):
        return block

    def scatter_sum(self, near, far):
        grads = jnp.concatenate([near, far], 0)
        grads = grads.reshape((grads.shape[0], -1, grads.shape[-1])).astype(f32)
        own = lax.psum_scatter(grads, "tensor", scatter_dimension=0, tiled=False)
        return lax.psum_scatter(own, "dp", scatter_dimension=0, tiled=True)

    def gather_lane(self, vec):
        return lax.all_gather(vec, "tensor", axis=0)

    def order_lane(self, rel):
        return rel

    def sum_max(self, both, is_top):
        return jnp.where(is_top, lax.pmax(both, ALL), lax.psum(both, ALL))


VM = pl.BlockSpec(memory_space=pltpu.VMEM)
SM = pl.BlockSpec(memory_space=pltpu.SMEM)
HB = pl.BlockSpec(memory_space=pl.ANY)


def like(shape, dtype=f32):
    return jax.ShapeDtypeStruct(shape, dtype)


def call(kernel, name, ins, specs, outs, scratch=(), flops=0, moved=0):
    return pl.pallas_call(
        kernel,
        name=name,
        out_shape=outs,
        in_specs=specs,
        out_specs=[VM] * len(outs),
        scratch_shapes=list(scratch),
        compiler_params=pltpu.CompilerParams(vmem_limit_bytes=60 * 2**20),
        cost_estimate=pl.CostEstimate(flops=flops, bytes_accessed=moved, transcendentals=0),
    )(*ins)


def start_loads(plan, refs, dst, sems, dp, cols=None):
    copies = []
    for n, (buf, sub, lane, rows, place) in enumerate(plan):
        at = pl.multiple_of((dp ^ place) * rows, rows) if rows < dst.shape[1] else 0
        src = refs[buf].at[sub] if cols is None else refs[buf].at[sub, :, pl.ds(*cols)]
        copy = pltpu.make_async_copy(src, dst.at[lane, pl.ds(at, rows)], sems.at[n])
        copy.start()
        copies.append(copy)
    return copies


def wait_all(copies):
    for copy in copies:
        copy.wait()


def row_stats(summed):
    centered = summed - jnp.mean(summed, axis=-1, keepdims=True)
    inv = lax.rsqrt(jnp.mean(centered * centered, axis=-1, keepdims=True) + epsilon)
    return centered * inv, inv


def norm_backward(scaled, normed, inv):
    row_mean = jnp.mean(scaled, axis=-1, keepdims=True)
    row_cross = jnp.mean(scaled * normed, axis=-1, keepdims=True)
    return inv * (scaled - row_mean - normed * row_cross)


def col_sum(values):
    return jnp.sum(values, axis=0, keepdims=True)


def top_of(values):
    return jnp.full((1, 128), jnp.max(jnp.abs(values)), f32)


def attn_forward(plan, nb, dims, dp_ref, lim, tokens, qkv_bias, q_seg, k_seg, vecs, *rest):
    blocks, cols, width = dims
    bufs, rest = rest[:nb], rest[nb:]
    qkv_out, lse_out, in_t, ctx_low, ctx_slope, normed_out, inv_out, middle_out, mid_slope, mid_low, mid_t, top_out = rest[:12]
    weight, in_low, mask, ctx_t, acc, top_ctx, sems = rest[12:]
    heads = cols // HEAD_DIM
    low_q = 3 * cols + HEAD_DIM
    loads = start_loads(plan, bufs, weight, sems, dp_ref[0])
    inputs = tokens[...].astype(f32)
    in_low[...] = jnp.clip(inputs, -lim[0], lim[0]).astype(bf16)
    in_t[...] = in_low[...].T
    top_out[0:1, :] = top_of(inputs)
    mask[...] = jnp.where(k_seg[...] == q_seg[...], 0.0, NEG)
    acc[...] = jnp.zeros_like(acc)
    ctx_t[0:HEAD_DIM, :] = jnp.zeros((HEAD_DIM, ctx_t.shape[1]), f32)
    top_ctx[...] = jnp.zeros_like(top_ctx)
    wait_all(loads)

    def step(lane, carry):
        qkv = (mm(in_low[...], weight[lane, :, :low_q]) + qkv_bias[lane]).astype(bf16)
        qkv_out[lane] = qkv
        for h in range(heads):
            at = h * HEAD_DIM
            q = qkv[:, at : at + HEAD_DIM]
            k = qkv[:, cols + at : cols + at + HEAD_DIM]
            v = qkv[:, 2 * cols + at : 2 * cols + at + HEAD_DIM]
            scores = mm_nt(k, q) * score_scale + mask[...]
            peak = jnp.max(scores, axis=0, keepdims=True)
            grown = jnp.exp(scores - peak)
            total = jnp.sum(grown, axis=0, keepdims=True)
            lse_out[lane, h : h + 1, :] = peak + jnp.log(total)
            shares = (grown * (1.0 / total)).astype(bf16)
            ctx_t[HEAD_DIM + at : 2 * HEAD_DIM + at, :] = mm_tn(v, shares)
        context = ctx_t[...].T
        bent = jnp.tanh(context * lim[5])
        low = (lim[1] * bent).astype(bf16)
        ctx_low[lane] = low
        ctx_slope[lane] = 1.0 - bent * bent
        top_ctx[...] = jnp.maximum(top_ctx[...], jnp.max(jnp.abs(context).reshape(-1, 8, context.shape[1]), axis=0))
        acc[...] += mm_nt(low, weight[lane, :, low_q - 2 * HEAD_DIM :])
        return carry

    lax.fori_loop(0, blocks, step, 0)
    top_out[1:2, :] = top_of(top_ctx[...])
    normed, inv = row_stats(tokens[...].astype(f32) + acc[...] + vecs[0:1, :])
    normed_out[...] = normed
    inv_out[...] = inv
    middle = normed * vecs[1:2, :] + vecs[2:3, :]
    middle_out[...] = middle
    bent = jnp.tanh(middle * lim[6])
    low = (lim[2] * bent).astype(bf16)
    mid_low[...] = low
    mid_slope[...] = 1.0 - bent * bent
    mid_t[...] = low.T
    top_out[2:3, :] = top_of(middle)


def up_forward(plan, nb, dims, dp_ref, lim, mid_low, up_bias, *rest):
    blocks, cols, width = dims
    bufs, rest = rest[:nb], rest[nb:]
    act_out, slope_out, top_out, weight, top_hid, sems = rest
    loads = start_loads(plan, bufs, weight, sems, dp_ref[0])
    top_hid[...] = jnp.zeros_like(top_hid)
    wait_all(loads)

    def step(lane, carry):
        up = mm(mid_low[...], weight[lane]) + up_bias[lane]
        half = 0.5 * (1.0 + lax.erf(up * root_half))
        hidden = up * half
        top_hid[...] = jnp.maximum(top_hid[...], jnp.max(jnp.abs(hidden).reshape(-1, 8, hidden.shape[1]), axis=0))
        bent = jnp.tanh(hidden * lim[7])
        act_out[lane] = (lim[3] * bent).astype(bf16)
        slope_out[lane] = (1.0 - bent * bent) * (half + up * jnp.exp(-0.5 * up * up) * density_scale)
        return carry

    lax.fori_loop(0, blocks, step, 0)
    top_out[...] = jnp.broadcast_to(top_of(top_hid[...]), top_out.shape)


def down_forward(plan, nb, dims, dp_ref, act, middle, cotangent, vecs, *rest):
    blocks, cols, width = dims
    bufs, rest = rest[:nb], rest[nb:]
    layer_out, grad_out, ffn_low, ffn_t, sums, weight, acc, sems = rest
    loads = start_loads(plan, bufs, weight, sems, dp_ref[0])
    acc[...] = middle[...] + vecs[3:4, :]
    wait_all(loads)

    def step(lane, carry):
        acc[...] += mm_nt(act[lane], weight[lane])
        return carry

    lax.fori_loop(0, blocks, step, 0)
    normed, inv = row_stats(acc[...])
    layer_out[...] = (normed * vecs[4:5, :] + vecs[5:6, :]).astype(bf16)
    incoming = cotangent[...].astype(f32)
    grad = norm_backward(incoming * vecs[4:5, :], normed, inv)
    grad_out[...] = grad
    low = grad.astype(bf16)
    ffn_low[...] = low
    ffn_t[...] = low.T
    sums[...] = jnp.zeros_like(sums)
    sums[0:1, :] = col_sum(grad)
    sums[1:2, :] = col_sum(incoming * normed)
    sums[2:3, :] = col_sum(incoming)


def weight_grad(first, slot, parts, dp_ref, left_t, right, out):
    rows = left_t.shape[0] // parts

    def step(i, carry):
        grad = mm(left_t[...], right[first + i]).astype(bf16)
        for block in range(parts):
            out[i, slot(block, dp_ref[0])] = grad[block * rows : (block + 1) * rows]
        return carry

    lax.fori_loop(0, out.shape[0], step, 0)


def act_backward(plan, nb, dims, dp_ref, ffn_low, slope, *rest):
    blocks, cols, width = dims
    bufs, rest = rest[:nb], rest[nb:]
    grad_up, sums, weight, sems = rest
    wait_all(start_loads(plan, bufs, weight, sems, dp_ref[0]))

    def step(lane, carry):
        low = (mm(ffn_low[...], weight[lane]) * slope[lane]).astype(bf16)
        grad_up[lane] = low
        sums[lane] = col_sum(low.astype(f32))
        return carry

    lax.fori_loop(0, blocks, step, 0)


def mid_backward(plans, nbs, dims, dp_ref, grad_up, grad_second, mid_slope, normed, inv, vecs, ctx_slope, *rest):
    blocks, cols, width = dims
    up_bufs, rest = rest[: nbs[0]], rest[nbs[0] :]
    a_bufs, rest = rest[: nbs[1]], rest[nbs[1] :]
    grad_out, attn_t, grad_ctx, sums, weight, out_weight, acc, attn_low, up_sems, a_sems = rest
    at = 3 * cols - HEAD_DIM
    up_loads = start_loads(plans[0], up_bufs, weight, up_sems, dp_ref[0])
    a_loads = start_loads(plans[1], a_bufs, out_weight, a_sems, dp_ref[0], (at, cols + HEAD_DIM))
    acc[...] = jnp.zeros_like(acc)
    wait_all(up_loads)

    def step(lane, carry):
        acc[...] += mm_nt(grad_up[lane], weight[lane])
        return carry

    lax.fori_loop(0, blocks, step, 0)
    incoming = grad_second[...] + acc[...] * mid_slope[...]
    grad = norm_backward(incoming * vecs[1:2, :], normed[...], inv[...])
    grad_out[...] = grad
    attn_low[...] = grad.astype(bf16)
    attn_t[...] = attn_low[...].T
    sums[...] = jnp.zeros_like(sums)
    sums[0:1, :] = col_sum(grad)
    sums[1:2, :] = col_sum(incoming * normed[...])
    sums[2:3, :] = col_sum(incoming)
    wait_all(a_loads)

    def spread(lane, carry):
        grad_ctx[lane] = (mm(attn_low[...], out_weight[lane]) * ctx_slope[lane]).astype(bf16)
        return carry

    lax.fori_loop(0, blocks, spread, 0)


def attn_backward(dims, qkv, lse, grad_ctx, q_seg, k_seg, out, sums, mask):
    blocks, cols, width = dims
    heads = cols // HEAD_DIM
    mask[...] = jnp.where(k_seg[...] == q_seg[...], 0.0, NEG)

    def step(lane, carry):
        for h in range(heads):
            at = h * HEAD_DIM
            q = qkv[lane, :, at : at + HEAD_DIM]
            k = qkv[lane, :, cols + at : cols + at + HEAD_DIM]
            v = qkv[lane, :, 2 * cols + at : 2 * cols + at + HEAD_DIM]
            grad = grad_ctx[lane, :, HEAD_DIM + at : 2 * HEAD_DIM + at]
            shares = jnp.exp(mm_nt(k, q) * score_scale + mask[...] - lse[lane, h : h + 1, :])
            grad_shares = mm_nt(v, grad)
            inner = jnp.sum(shares * grad_shares, axis=0, keepdims=True)
            grad_scores = (shares * (grad_shares - inner)).astype(bf16)
            grad_v = mm(shares.astype(bf16), grad)
            grad_k = mm(grad_scores, q) * score_scale
            grad_q = (mm_tn(k, grad_scores) * score_scale).T
            out[lane, :, at : at + HEAD_DIM] = grad_q.astype(bf16)
            out[lane, :, cols + at : cols + at + HEAD_DIM] = grad_k.astype(bf16)
            out[lane, :, 2 * cols + at : 2 * cols + at + HEAD_DIM] = grad_v.astype(bf16)
        out[lane, :, 3 * cols :] = jnp.zeros((out.shape[1], HEAD_DIM), bf16)
        sums[lane] = col_sum(out[lane].astype(f32))
        return carry

    lax.fori_loop(0, blocks, step, 0)


def in_weight_grad(first, slot, parts, dims, dp_ref, in_t, attn_t, grad_qkv, ctx_low, out):
    blocks, cols, width = dims
    rows = in_t.shape[0] // parts
    at = 3 * cols - HEAD_DIM
    end = 3 * cols + HEAD_DIM

    def step(i, carry):
        left = mm(in_t[...], grad_qkv[first + i])
        right = mm(attn_t[...], ctx_low[first + i])
        mixed = (left[:, at:] + right[:, : end - at]).astype(bf16)
        for block in range(parts):
            rs = slice(block * rows, (block + 1) * rows)
            place = slot(block, dp_ref[0])
            out[i, place, :, :at] = left[rs, :at].astype(bf16)
            out[i, place, :, at:end] = mixed[rs]
            out[i, place, :, end:] = right[rs, end - at :].astype(bf16)
        return carry

    lax.fori_loop(0, out.shape[0], step, 0)


def token_backward(plan, nb, dims, dp_ref, lim, grad_qkv, grad_first, tokens, *rest):
    blocks, cols, width = dims
    bufs, rest = rest[:nb], rest[nb:]
    out, weight, acc, sems = rest
    loads = start_loads(plan, bufs, weight, sems, dp_ref[0], (0, 3 * cols + HEAD_DIM))
    acc[...] = jnp.zeros_like(acc)
    wait_all(loads)

    def step(lane, carry):
        acc[...] += mm_nt(grad_qkv[lane], weight[lane])
        return carry

    lax.fori_loop(0, blocks, step, 0)
    inputs = tokens[...].astype(f32)
    out[...] = (grad_first[...] + jnp.where(jnp.abs(inputs) <= lim[0], acc[...], 0.0)).astype(bf16)


def block_masks(long_part, short_part):
    per_block = LONG_LEN // SHORT_LEN
    position = jnp.arange(LONG_LEN, dtype=jnp.int32)
    long_segment = jnp.zeros((long_part.shape[0], LONG_LEN), jnp.int32)
    long_valid = position[None, :] < long_part[:, None]
    short_rows = short_part.reshape(-1, per_block)
    short_segment = jnp.broadcast_to(position // SHORT_LEN, (short_rows.shape[0], LONG_LEN))
    short_limit = jnp.repeat(short_rows, SHORT_LEN, axis=1)
    short_valid = (position % SHORT_LEN)[None, :] < short_limit
    return (
        jnp.concatenate([long_segment, short_segment], 0),
        jnp.concatenate([long_valid, short_valid], 0),
    )


def make_body(special):
    def body(
        tokens,
        cotangent,
        qkv_weight,
        qv_bias,
        out_weight,
        out_bias,
        first_gain,
        first_shift,
        up_weight,
        up_bias,
        down_weight,
        down_bias,
        second_gain,
        second_shift,
        act_ranges,
        long_lengths,
        short_lengths,
    ):
        net = Grid() if special else Plain()
        lane = lax.axis_index("tensor")
        dp = jnp.full((1,), lax.axis_index("dp"), jnp.int32)
        rows, width = tokens.shape
        assert rows == LONG_LEN
        cols = qkv_weight.shape[2]
        blocks = lax.axis_size("tensor")
        dims = (blocks, cols, width)
        wide = 3 * cols + HEAD_DIM
        out_cols = cols + HEAD_DIM

        shard_a = jnp.concatenate(
            [qkv_weight[0], qkv_weight[1], qkv_weight[2], out_weight.T], 1
        ).astype(bf16)
        biases = net.gather_lane(jnp.concatenate([qv_bias[0], qv_bias[1], up_bias]))
        full_a = net.gather(shard_a)
        full_u = net.gather(up_weight.astype(bf16))
        full_d = net.gather(down_weight.T.astype(bf16))

        def sems(pieces):
            return pltpu.SemaphoreType.DMA((len(pieces.plan),))

        def vmem(*shape, dtype=f32):
            return pltpu.VMEM(shape, dtype)

        qkv_bias = jnp.concatenate(
            [
                biases[:, :cols],
                jnp.zeros((blocks, cols), f32),
                biases[:, cols : 2 * cols],
                jnp.zeros((blocks, HEAD_DIM), f32),
            ],
            1,
        )[:, None]
        up_biases = biases[:, None, 2 * cols :]
        limits = jnp.concatenate([act_ranges, 1.0 / act_ranges])
        vecs = jnp.stack(
            [out_bias, first_gain, first_shift, down_bias, second_gain, second_shift, out_bias, out_bias]
        )
        segments, valids = block_masks(long_lengths, short_lengths)
        q_seg = lax.dynamic_slice_in_dim(segments, lane, 1, 0)
        k_seg = lax.dynamic_slice_in_dim(jnp.where(valids, segments, -1), lane, 1, 0).reshape(rows, 1)

        n_a, n_u, n_d = len(full_a.bufs), len(full_u.bufs), len(full_d.bufs)
        unit = 2 * rows * width * width * blocks
        moved = 2 * width * width * blocks
        qkv, lse, in_t, ctx_low, ctx_slope, normed, inv, middle, mid_slope, mid_low, mid_t, tops = call(
            functools.partial(attn_forward, full_a.plan, n_a, dims),
            "attn_forward",
            [dp, limits, tokens, qkv_bias, q_seg, k_seg, vecs] + full_a.bufs,
            [SM, SM] + [VM] * 5 + [HB] * n_a,
            [
                like((blocks, rows, wide), bf16),
                like((blocks, 8, rows)),
                like((width, rows), bf16),
                like((blocks, rows, out_cols), bf16),
                like((blocks, rows, out_cols)),
                like((rows, width)),
                like((rows, 1)),
                like((rows, width)),
                like((rows, width)),
                like((rows, width), bf16),
                like((width, rows), bf16),
                like((8, 128)),
            ],
            [
                vmem(blocks, width, 4 * cols, dtype=bf16),
                vmem(rows, width, dtype=bf16),
                vmem(rows, rows),
                vmem(out_cols, rows),
                vmem(rows, width),
                vmem(8, out_cols),
                sems(full_a),
            ],
            4 * unit,
            3 * moved,
        )
        up_cols = up_weight.shape[1]
        act, slope, top_hid = call(
            functools.partial(up_forward, full_u.plan, n_u, dims),
            "up_forward",
            [dp, limits, mid_low, up_biases] + full_u.bufs,
            [SM, SM, VM, VM] + [HB] * n_u,
            [like((blocks, rows, up_cols), bf16), like((blocks, rows, up_cols)), like((8, 128))],
            [vmem(blocks, width, up_cols, dtype=bf16), vmem(8, up_cols), sems(full_u)],
            2 * unit,
            3 * moved,
        )
        layer_out, grad_second, ffn_low, ffn_t, sums_b = call(
            functools.partial(down_forward, full_d.plan, n_d, dims),
            "down_forward",
            [dp, act, middle, cotangent, vecs] + full_d.bufs,
            [SM] + [VM] * 4 + [HB] * n_d,
            [
                like((rows, width), bf16),
                like((rows, width)),
                like((rows, width), bf16),
                like((width, rows), bf16),
                like((8, width)),
            ],
            [vmem(blocks, width, up_cols, dtype=bf16), vmem(rows, width), sems(full_d)],
            unit,
            2 * moved,
        )

        half = blocks // 2
        grad_shape = like((half, net.parts, width // net.parts, up_cols), bf16)

        def grad_of(name, left_t, right):
            def side(first, tag):
                return call(
                    functools.partial(weight_grad, first, net.slot, net.parts),
                    name + tag,
                    [dp, left_t, right],
                    [SM, VM, VM],
                    [grad_shape],
                    (),
                    unit // 2,
                    moved,
                )[0]

            far = side(half, "_far")
            return side(0, "_near"), far

        down_near, down_far = grad_of("down_grad", ffn_t, act)
        down_grad = net.scatter_sum(down_near, down_far).T
        grad_up, up_sums = call(
            functools.partial(act_backward, full_d.plan, n_d, dims),
            "act_backward",
            [dp, ffn_low, slope] + full_d.bufs,
            [SM, VM, VM] + [HB] * n_d,
            [like((blocks, rows, up_cols), bf16), like((blocks, 1, up_cols))],
            [vmem(blocks, width, up_cols, dtype=bf16), sems(full_d)],
            unit,
            3 * moved,
        )
        up_near, up_far = grad_of("up_grad", mid_t, grad_up)
        up_grad = net.scatter_sum(up_near, up_far)
        grad_first, attn_t, grad_ctx, sums_a = call(
            functools.partial(mid_backward, (full_u.plan, full_a.plan), (n_u, n_a), dims),
            "mid_backward",
            [dp, grad_up, grad_second, mid_slope, normed, inv, vecs, ctx_slope] + full_u.bufs + full_a.bufs,
            [SM] + [VM] * 7 + [HB] * (n_u + n_a),
            [
                like((rows, width)),
                like((width, rows), bf16),
                like((blocks, rows, out_cols), bf16),
                like((8, width)),
            ],
            [
                vmem(blocks, width, up_cols, dtype=bf16),
                vmem(blocks, width, out_cols, dtype=bf16),
                vmem(rows, width),
                vmem(rows, width, dtype=bf16),
                sems(full_u),
                sems(full_a),
            ],
            unit + unit // 3,
            3 * moved,
        )
        grad_qkv, qkv_sums = call(
            functools.partial(attn_backward, dims),
            "attn_backward",
            [qkv, lse, grad_ctx, q_seg, k_seg],
            [VM] * 5,
            [like((blocks, rows, wide), bf16), like((blocks, 1, wide))],
            [vmem(rows, rows)],
            4 * unit,
            2 * moved,
        )

        def in_side(first, tag):
            return call(
                functools.partial(in_weight_grad, first, net.slot, net.parts, dims),
                "in_grad" + tag,
                [dp, in_t, attn_t, grad_qkv, ctx_low],
                [SM] + [VM] * 4,
                [grad_shape],
                (),
                unit // 2,
                moved,
            )[0]

        a_far = in_side(half, "_far")
        a_near = in_side(0, "_near")
        a_grad = net.scatter_sum(a_near, a_far)
        qkv_grad = jnp.stack([a_grad[:, j * cols : (j + 1) * cols] for j in range(3)])
        out_grad = a_grad[:, 3 * cols :].T
        tokens_grad = call(
            functools.partial(token_backward, full_a.plan, n_a, dims),
            "token_backward",
            [dp, limits, grad_qkv, grad_first, tokens] + full_a.bufs,
            [SM, SM, VM, VM, VM] + [HB] * n_a,
            [like((rows, width), bf16)],
            [vmem(blocks, width, wide, dtype=bf16), vmem(rows, width), sems(full_a)],
            unit,
            2 * moved,
        )[0]

        laned = jnp.concatenate(
            [qkv_sums[:, 0, :cols], qkv_sums[:, 0, 2 * cols : 3 * cols], up_sums[:, 0]], -1
        )
        per_lane = laned.shape[1]
        top_row = jnp.concatenate([tops[:3], top_hid[:1]], 0)
        packed = jnp.concatenate(
            [net.order_lane(laned).reshape(-1, 128), sums_a[:3].reshape(-1, 128), sums_b[:3].reshape(-1, 128), top_row], 0
        )
        is_top = (jnp.arange(packed.shape[0]) >= packed.shape[0] - 4)[:, None]
        packed = net.sum_max(packed, is_top)
        own = lax.dynamic_slice_in_dim(packed, lane * (per_lane // 128), per_lane // 128).reshape(-1)
        shared = packed[blocks * per_lane // 128 : -4].reshape(6, width)
        qv_bias_grad = own[: 2 * cols].reshape(2, cols)
        new_ranges = ema_decay * act_ranges + (1.0 - ema_decay) * packed[-4:, 0]
        return (
            layer_out,
            tokens_grad,
            qkv_grad,
            qv_bias_grad,
            out_grad,
            shared[0],
            shared[1],
            shared[2],
            up_grad,
            own[2 * cols :],
            down_grad,
            shared[3],
            shared[4],
            shared[5],
            new_ranges,
        )

    return body


def solution(mesh):
    in_specs = (
        P(ALL, None),
        P(ALL, None),
        P(None, "dp", "tensor"),
        P(None, "tensor"),
        P("tensor", "dp"),
        P(),
        P(),
        P(),
        P("dp", "tensor"),
        P("tensor"),
        P("tensor", "dp"),
        P(),
        P(),
        P(),
        P(),
        P("dp"),
        P("dp"),
    )
    out_specs = (
        P(ALL, None),
        P(ALL, None),
        P(None, "dp", "tensor"),
        P(None, "tensor"),
        P("tensor", "dp"),
        P(),
        P(),
        P(),
        P("dp", "tensor"),
        P("tensor"),
        P("tensor", "dp"),
        P(),
        P(),
        P(),
        P(),
    )
    special = mesh.shape["dp"] == 8 and mesh.shape["tensor"] == 4
    return jax.shard_map(
        make_body(special), mesh=mesh, in_specs=in_specs, out_specs=out_specs, check_vma=False
    )
```

```python
import functools
import itertools

import jax
import jax.numpy as jnp
from jax import lax
from jax.experimental import pallas as pl
from jax.experimental.pallas import tpu as pltpu
from jax.sharding import PartitionSpec as P

HEAD_DIM = 64
LONG_LEN = 512
SHORT_LEN = 128
ALL = ("dp", "tensor")

ema_decay = 0.9
epsilon = 1e-06
root_half = 0.7071067811865476
density_scale = 0.3989422804014327
score_scale = HEAD_DIM ** (-0.5)
NEG = -1000000000.0

f32 = jnp.float32
bf16 = jnp.bfloat16


def mm(left, right):
    return jnp.dot(left, right, preferred_element_type=f32)


def mm_tn(left, right):
    return lax.dot_general(left, right, (((0,), (0,)), ((), ())), preferred_element_type=f32)


def mm_nt(left, right):
    return lax.dot_general(left, right, (((1,), (1,)), ((), ())), preferred_element_type=f32)


def _lin(z, y, x, c):
    return (z * 2 + y) * 4 + x * 2 + c


def _perm(fn):
    out = []
    for z, y, x, c in itertools.product(range(4), range(2), range(2), range(2)):
        out.append((_lin(z, y, x, c), _lin(*fn(z, y, x, c))))
    return out


PC = _perm(lambda z, y, x, c: (z, y, x, 1 - c))
PX = _perm(lambda z, y, x, c: (z, y, 1 - x, c))
PY = _perm(lambda z, y, x, c: (z, 1 - y, x, c))
PZ1 = _perm(lambda z, y, x, c: (z ^ 1, y, x, c))
PZ2 = _perm(lambda z, y, x, c: (z ^ 2, y, x, c))


def tie(*trees):
    leaves, spec = jax.tree.flatten(trees)
    return jax.tree.unflatten(spec, lax.optimization_barrier(leaves))


class Job:
    def __init__(self, stages):
        self.stages, self.value, self.out, self.flight, self.over = stages, None, [], [], False
        self.take(None)

    def take(self, got):
        if not self.over:
            try:
                self.out = self.stages.send(got)
            except StopIteration as stop:
                self.value, self.out, self.over = stop.value, [], True


def step(ins, run=None, start=(), finish=()):
    ins, sends = tie(ins, [[value for value, _ in job.out] for job in start])
    for job, values in zip(start, sends):
        job.flight = [lax.ppermute(v, ALL, perm) for v, (_, perm) in zip(values, job.out)]
    outs = run(*ins) if run else ins
    outs, got = tie(outs, [job.flight for job in finish])
    for job, values in zip(finish, got):
        job.flight = []
        job.take(values)
    return outs


class Pieces:
    def __init__(self, plan):
        self.bufs, self.plan = {}, plan

    def part(self, lanes):
        names = sorted({p[0] for p in self.plan if p[2] in lanes})
        plan = [[(names.index(b), s, r, at) for b, s, lane, r, at in self.plan if lane == want] for want in lanes]
        return [self.bufs[n] for n in names], plan


Z_ORDER = (0, 2, 1, 3)


class Grid:
    parts = 8

    @staticmethod
    def gather(shard, pieces):
        own = shard[None]
        rows = shard.shape[0]
        for base, lane in ((0, 0), (5, 1)):
            for i, k in enumerate(Z_ORDER):
                pieces.plan.append((base, i, lane, rows, 2 * k))
                pieces.plan.append((base + 1, i, lane, rows, 2 * k + 1))
                pieces.plan.append((base + 2, i, lane + 2, rows, 2 * k))
                pieces.plan.append((base + 3 + i // 2, i % 2, lane + 2, rows, 2 * k + 1))
        (far_z,) = yield [(own, PZ2)]
        pair = jnp.concatenate([own, far_z], 0)
        (near_z,) = yield [(pair, PZ1)]
        line = jnp.concatenate([pair, near_z], 0)
        over_x, over_y, line_far = yield [(line, PX), (line, PY), (line, PC)]
        pieces.bufs.update({0: line, 1: over_y, 2: over_x, 5: line_far})
        diag_x, diag_y, over_y_far, over_x_far = yield [
            (over_y[:2], PX),
            (over_x[2:], PY),
            (over_y, PC),
            (over_x, PC),
        ]
        pieces.bufs.update({3: diag_x, 4: diag_y, 6: over_y_far, 7: over_x_far})
        diag_x_far, diag_y_far = yield [(diag_x, PC), (diag_y, PC)]
        pieces.bufs.update({8: diag_x_far, 9: diag_y_far})

    @staticmethod
    def slot(block, dp):
        place = block ^ dp
        return (place & 1) * 4 + (place & 2) + (place >> 2)

    @staticmethod
    def scatter_sum(far, near, late):
        if isinstance(far, list):
            far1, near1 = far[0], near[0]
            (got1,) = yield [(far1, PC)]
            out_x, out_y = add_first(near1, got1)
            from_x, from_y = yield [(out_x, PX), (out_y, PY)]
            (got0,) = yield [(late["far"], PC)]
            near0 = late["near"]
            out_x, out_y = add_second(near1, got1, near0, got0, from_x, from_y)
        else:
            (got,) = yield [(far, PC)]
            out_x, out_y = add_first(near, got)
            from_x, from_y = yield [(out_x, PX), (out_y, PY)]
            near0, got0 = near, got
            out_x, out_y = add_second(near, got, near, got, from_x, from_y)
        in_x, in_y = yield [(out_x, PX), (out_y, PY)]
        return near0, got0, in_x, in_y

    @staticmethod
    def scatter_line(*parts):
        out_z, kept = add_third(*parts)
        (from_z,) = yield [(out_z, PZ1)]
        out_z, kept = add_fourth(kept, from_z)
        (last,) = yield [(out_z, PZ2)]
        return [kept[n] + last[n].astype(f32) for n in range(len(parts))]

    @staticmethod
    def gather_lane(vec):
        (other,) = yield [(vec, PX)]
        pair = jnp.stack([vec, other])
        (more,) = yield [(pair, PC)]
        return jnp.stack([pair, more], 1).reshape((4,) + vec.shape)

    @staticmethod
    def sum_max(both, is_top):
        for perm in (PZ2, PZ1, PX, PY, PC):
            (other,) = yield [(both, perm)]
            both = jnp.where(is_top, jnp.maximum(both, other), both + other)
        return both

    @staticmethod
    def me():
        return lax.axis_index("dp"), lax.axis_index("tensor")


class Plain:
    parts = 1

    @staticmethod
    def gather(shard, pieces):
        rows = lax.all_gather(shard, "dp", axis=0, tiled=True)
        full = lax.all_gather(rows, "tensor", axis=0)
        pieces.plan.extend((0, k, k, full.shape[1], 0) for k in range(full.shape[0]))
        pieces.bufs[0] = full
        return
        yield

    @staticmethod
    def slot(block, dp):
        return block

    @staticmethod
    def scatter_sum(far, near, late):
        if isinstance(far, list):
            while not late:
                yield []
            parts = [late["near"], late["far"], near[0], far[0]]
        else:
            parts = [near[0], far[0], near[1], far[1]]
        grads = jnp.stack(parts).astype(f32)
        return grads.reshape((4, -1, grads.shape[-1]))
        yield

    @staticmethod
    def scatter_line(*parts):
        own = [lax.psum_scatter(p, "tensor", scatter_dimension=0, tiled=False) for p in parts]
        return [lax.psum_scatter(o, "dp", scatter_dimension=0, tiled=True) for o in own]
        yield

    @staticmethod
    def gather_lane(vec):
        return lax.all_gather(vec, "tensor", axis=0)
        yield

    @staticmethod
    def sum_max(both, is_top):
        return jnp.where(is_top, lax.pmax(both, ALL), lax.psum(both, ALL))
        yield

    @staticmethod
    def me():
        return 0, 0


VM = pl.BlockSpec(memory_space=pltpu.VMEM)
SM = pl.BlockSpec(memory_space=pltpu.SMEM)
HB = pl.BlockSpec(memory_space=pl.ANY)
VMEM_MIB = 14


def like(shape, dtype=f32):
    return jax.ShapeDtypeStruct(shape, dtype)


def call(kernel, name, specs, outs, scratch=(), flops=0, moved=0):
    return pl.pallas_call(
        kernel,
        name=name,
        out_shape=outs,
        in_specs=specs,
        out_specs=[VM] * len(outs),
        scratch_shapes=list(scratch),
        compiler_params=pltpu.CompilerParams(vmem_limit_bytes=VMEM_MIB * 2**20),
        cost_estimate=pl.CostEstimate(flops=flops, bytes_accessed=moved, transcendentals=0),
    )


def glue(kernel, outs, *ins):
    return call(kernel, kernel.__name__, [VM] * len(ins), outs)(*ins)


def add_first(near, got):
    part = like((2,) + near.shape[-2:], bf16)
    near, got = near.reshape((-1, 8) + near.shape[-2:]), got.reshape((-1, 8) + got.shape[-2:])

    def first_sums(near, got, out_x, out_y):
        top = near.shape[0] - 1
        for k in range(2):
            out_x[k] = (near[top, 4 + k].astype(f32) + got[top, 4 + k].astype(f32)).astype(bf16)
            out_y[k] = (near[top, 6 + k].astype(f32) + got[top, 6 + k].astype(f32)).astype(bf16)

    return glue(first_sums, [part, part], near, got)


def add_second(near1, got1, near0, got0, from_x, from_y):
    rows = near1.shape[-2:]
    joint = near1 is near0
    ins = [near1, got1] if joint else [near1, got1, near0, got0]
    ins = [value.reshape((-1, 8) + rows) for value in ins]

    def second_sums(*refs):
        *sums, from_x, from_y, out_x, out_y = refs
        near1, got1, near0, got0 = sums * 2 if joint else sums
        top = near1.shape[0] - 1
        for k in range(4):
            over_x = near1[top, k].astype(f32) + got1[top, k].astype(f32)
            over_y = near0[0, 4 + k].astype(f32) + got0[0, 4 + k].astype(f32)
            if k < 2:
                over_y = over_y + from_x[k].astype(f32)
            else:
                over_x = over_x + from_y[k - 2].astype(f32)
            out_x[k] = over_x.astype(bf16)
            out_y[k] = over_y.astype(bf16)

    part = like((4,) + rows, bf16)
    return glue(second_sums, [part, part], *ins, from_x, from_y)


def add_third(*parts):
    rows = parts[0][0].shape[-2:]
    ins = []
    for near, got, in_x, in_y in parts:
        ins += [near.reshape((-1, 8) + rows), got.reshape((-1, 8) + rows), in_x, in_y]

    def third_sums(*refs):
        out, kept = refs[-2:]
        for n in range(len(parts)):
            near, got, in_x, in_y = refs[4 * n : 4 * n + 4]
            for k in range(4):
                total = near[0, k].astype(f32) + got[0, k].astype(f32) + in_x[k].astype(f32) + in_y[k].astype(f32)
                if k < 2:
                    kept[n, k] = total
                else:
                    out[n, k - 2] = total.astype(bf16)

    shape = (len(parts), 2) + rows
    return glue(third_sums, [like(shape, bf16), like(shape)], *ins)


def add_fourth(kept, from_z):
    def fourth_sums(kept, from_z, out, mine):
        for n in range(kept.shape[0]):
            mine[n] = kept[n, 0] + from_z[n, 0].astype(f32)
            out[n] = (kept[n, 1] + from_z[n, 1].astype(f32)).astype(bf16)

    shape = kept.shape[:1] + kept.shape[2:]
    return glue(fourth_sums, [like(shape, bf16), like(shape)], kept, from_z)


class Loads:
    def __init__(self, plan, refs, dst, sems, dp, cols=None):
        self.plan, self.dst, self.sems, self.dp = plan, dst, sems, dp
        for lane, pieces in enumerate(plan):
            for n, (buf, sub, rows, place) in enumerate(pieces):
                src = refs[buf].at[sub] if cols is None else refs[buf].at[sub, :, pl.ds(*cols)]
                pltpu.make_async_copy(src, self.spot(lane, rows, place), sems.at[lane, n]).start()

    def spot(self, lane, rows, place):
        at = pl.multiple_of((self.dp ^ place) * rows, rows) if rows < self.dst.shape[1] else 0
        return self.dst.at[lane, pl.ds(at, rows)]

    def wait(self, lane):
        for n, (_, _, rows, place) in enumerate(self.plan[0]):
            spot = self.spot(lane, rows, place)
            pltpu.make_async_copy(spot, spot, self.sems.at[lane, n]).wait()


def row(vec):
    return vec[...].reshape(1, -1)


def row_stats(summed):
    centered = summed - jnp.mean(summed, axis=-1, keepdims=True)
    inv = lax.rsqrt(jnp.mean(centered * centered, axis=-1, keepdims=True) + epsilon)
    return centered * inv, inv


def norm_backward(scaled, normed, inv):
    row_mean = jnp.mean(scaled, axis=-1, keepdims=True)
    row_cross = jnp.mean(scaled * normed, axis=-1, keepdims=True)
    return inv * (scaled - row_mean - normed * row_cross)


def col_sum(values):
    return jnp.sum(values, axis=0, keepdims=True)


def top_of(values):
    return jnp.full((1, 128), jnp.max(jnp.abs(values)), f32)


def fill_mask(mask, longs, shorts):
    per_block = LONG_LEN // SHORT_LEN
    block = lax.axis_index("tensor")
    n_long = longs.shape[0]
    is_long = block < n_long
    whole = longs[jnp.minimum(block, n_long - 1)]
    first = jnp.maximum(block - n_long, 0) * per_block
    shift = jnp.where(is_long, LONG_LEN.bit_length() - 1, SHORT_LEN.bit_length() - 1)
    size = jnp.where(is_long, LONG_LEN, SHORT_LEN)
    k_pos = lax.broadcasted_iota(jnp.int32, (LONG_LEN, 1), 0)
    q_pos = lax.broadcasted_iota(jnp.int32, (1, LONG_LEN), 1)
    k_seg = lax.shift_right_logical(k_pos, jnp.full_like(k_pos, shift))
    q_seg = lax.shift_right_logical(q_pos, jnp.full_like(q_pos, shift))
    limit = jnp.zeros_like(k_pos)
    for j in range(per_block):
        limit = jnp.where(k_seg == j, jnp.where(is_long, whole, shorts[first + j]), limit)
    k_seg = jnp.where(k_pos - k_seg * size < limit, k_seg, -1)
    mask[...] = jnp.where(k_seg == q_seg, 0.0, NEG)


def attn_forward(net, plan, nb, dims, lim, longs, shorts, tokens, bias, *rest):
    blocks, cols, width = dims
    bufs, rest = rest[:nb], rest[nb:]
    qkv_out, lse_out, in_t, ctx_low, ctx_slope, top_out, weight, in_low, mask, ctx_t, top_ctx, sems = rest
    heads = cols // HEAD_DIM
    low_q = 3 * cols + HEAD_DIM
    loads = Loads(plan, bufs, weight, sems, net.me()[0])
    inputs = tokens[...].astype(f32)
    in_low[...] = jnp.clip(inputs, -lim[0], lim[0]).astype(bf16)
    in_t[...] = in_low[...].T
    top_out[0:1, :] = top_of(inputs)
    fill_mask(mask, longs, shorts)
    ctx_t[0:HEAD_DIM, :] = jnp.zeros((HEAD_DIM, ctx_t.shape[1]), f32)
    top_ctx[...] = jnp.zeros_like(top_ctx)
    inv_limit = 1.0 / jnp.full((1, 1), lim[1], f32)

    def each(lane, carry):
        loads.wait(lane)
        qkv = (mm(in_low[...], weight[lane, :, :low_q]) + bias[lane, :, :low_q]).astype(bf16)
        qkv_out[lane] = qkv
        for h in range(heads):
            at = h * HEAD_DIM
            q = qkv[:, at : at + HEAD_DIM]
            k = qkv[:, cols + at : cols + at + HEAD_DIM]
            v = qkv[:, 2 * cols + at : 2 * cols + at + HEAD_DIM]
            scores = mm_nt(k, q) * score_scale + mask[...]
            peak = jnp.max(scores, axis=0, keepdims=True)
            grown = jnp.exp(scores - peak)
            total = jnp.sum(grown, axis=0, keepdims=True)
            lse_out[lane, h : h + 1, :] = peak + jnp.log(total)
            shares = (grown * (1.0 / total)).astype(bf16)
            ctx_t[HEAD_DIM + at : 2 * HEAD_DIM + at, :] = mm_tn(v, shares)
        context = ctx_t[...].T
        bent = jnp.tanh(context * inv_limit)
        ctx_low[lane] = (lim[1] * bent).astype(bf16)
        ctx_slope[lane] = 1.0 - bent * bent
        top_ctx[...] = jnp.maximum(top_ctx[...], jnp.max(jnp.abs(context).reshape(-1, 8, context.shape[1]), axis=0))
        return carry

    lax.fori_loop(0, blocks, each, 0)
    top_out[1:2, :] = top_of(top_ctx[...])


def attn_finish(dims, lim, ctx_low, tokens, out_bias, gain, shift, weight, *outs):
    blocks, cols, width = dims
    normed_out, inv_out, middle_out, mid_slope, mid_low, mid_t, top_out, acc = outs
    at = 3 * cols - HEAD_DIM
    acc[...] = tokens[...].astype(f32) + row(out_bias)

    def each(lane, carry):
        acc[...] += mm_nt(ctx_low[lane], weight[lane, :, at:])
        return carry

    lax.fori_loop(0, blocks, each, 0)
    normed, inv = row_stats(acc[...])
    normed_out[...] = normed
    inv_out[...] = inv
    middle = normed * row(gain) + row(shift)
    middle_out[...] = middle
    bent = jnp.tanh(middle * (1.0 / jnp.full((1, 1), lim[2], f32)))
    low = (lim[2] * bent).astype(bf16)
    mid_low[...] = low
    mid_slope[...] = 1.0 - bent * bent
    mid_t[...] = low.T
    top_out[...] = jnp.broadcast_to(top_of(middle), top_out.shape)


def up_forward(net, plan, nb, first, low_q, lim, mid_low, bias, *rest):
    bufs, rest = rest[:nb], rest[nb:]
    act_out, slope_out, top_out, weight, top_hid, sems = rest
    loads = Loads(plan, bufs, weight, sems, net.me()[0])
    top_hid[...] = jnp.zeros_like(top_hid)
    inv_limit = 1.0 / jnp.full((1, 1), lim[3], f32)

    def each(lane, carry):
        loads.wait(lane)
        up = mm(mid_low[...], weight[lane]) + bias[first + lane, :, low_q:]
        half = 0.5 * (1.0 + lax.erf(up * root_half))
        hidden = up * half
        top_hid[...] = jnp.maximum(top_hid[...], jnp.max(jnp.abs(hidden).reshape(-1, 8, hidden.shape[1]), axis=0))
        bent = jnp.tanh(hidden * inv_limit)
        act_out[lane] = (lim[3] * bent).astype(bf16)
        slope_out[lane] = (1.0 - bent * bent) * (half + up * jnp.exp(-0.5 * up * up) * density_scale)
        return carry

    lax.fori_loop(0, weight.shape[0], each, 0)
    top_out[...] = jnp.broadcast_to(top_of(top_hid[...]), top_out.shape)


def down_both(net, plan, nb, act0, act1, slope0, slope1, middle, cotangent, down_bias, gain, shift, *rest):
    bufs, rest = rest[:nb], rest[nb:]
    layer_out, grad_out, ffn_t, sums, grad_up, up_sums, weight, acc, ffn_low, sems = rest
    loads = Loads(plan, bufs, weight, sems, net.me()[0])
    acc[...] = middle[...] + row(down_bias)
    half = act0.shape[0]
    for act, first in ((act0, 0), (act1, half)):

        def each(i, carry):
            loads.wait(first + i)
            acc[...] += mm_nt(act[i], weight[first + i])
            return carry

        lax.fori_loop(0, half, each, 0)
    normed, inv = row_stats(acc[...])
    layer_out[...] = (normed * row(gain) + row(shift)).astype(bf16)
    incoming = cotangent[...].astype(f32)
    grad = norm_backward(incoming * row(gain), normed, inv)
    grad_out[...] = grad
    ffn_low[...] = grad.astype(bf16)
    ffn_t[...] = ffn_low[...].T
    sums[...] = jnp.zeros_like(sums)
    sums[0:1, :] = col_sum(grad)
    sums[1:2, :] = col_sum(incoming * normed)
    sums[2:3, :] = col_sum(incoming)
    lane_me = net.me()[1]
    for slope, first in ((slope0, 0), (slope1, half)):

        def back(i, carry):
            low = (mm(ffn_low[...], weight[first + i]) * slope[i]).astype(bf16)
            grad_up[first + i] = low
            up_sums[(first + i) ^ lane_me] = col_sum(low.astype(f32))
            return carry

        lax.fori_loop(0, half, back, 0)


def weight_grad(net, left_t, *rest):
    *rights, far, near = rest
    rows = left_t.shape[0] // net.parts
    dp = net.me()[0]
    half = far.shape[0]
    for x in range(half):
        for out, lane in ((far, 2 * x + 1), (near, 2 * x)):
            right = rights[lane // rights[0].shape[0]]
            grad = mm(left_t[...], right[lane % right.shape[0]]).astype(bf16)
            for block in range(net.parts):
                out[x, net.slot(block, dp)] = grad[block * rows : (block + 1) * rows]


def mid_backward(dims, grad_up, grad_second, mid_slope, normed, inv, gain, ctx_slope, weight0, weight1, out_weight, *outs):
    blocks, cols, width = dims
    grad_out, attn_t, grad_ctx, sums, acc, attn_low = outs
    at = 3 * cols - HEAD_DIM
    acc[...] = jnp.zeros_like(acc)
    half = weight0.shape[0]
    for weight, first in ((weight0, 0), (weight1, half)):

        def each(i, carry):
            acc[...] += mm_nt(grad_up[first + i], weight[i])
            return carry

        lax.fori_loop(0, half, each, 0)
    incoming = grad_second[...] + acc[...] * mid_slope[...]
    grad = norm_backward(incoming * row(gain), normed[...], inv[...])
    grad_out[...] = grad
    attn_low[...] = grad.astype(bf16)
    attn_t[...] = attn_low[...].T
    sums[...] = jnp.zeros_like(sums)
    sums[0:1, :] = col_sum(grad)
    sums[1:2, :] = col_sum(incoming * normed[...])
    sums[2:3, :] = col_sum(incoming)

    def spread(lane, carry):
        grad_ctx[lane] = (mm(attn_low[...], out_weight[lane, :, at:]) * ctx_slope[lane]).astype(bf16)
        return carry

    lax.fori_loop(0, blocks, spread, 0)


def attn_backward(net, first, dims, longs, shorts, qkv, lse, grad_ctx, *rest):
    blocks, cols, width = dims
    extra, (out, sums, mask) = (), rest[-3:]
    if len(rest) > 3:
        *extra, out, packed, sums, mask = rest
    heads = cols // HEAD_DIM
    fill_mask(mask, longs, shorts)
    sums[...] = jnp.zeros_like(sums)
    lane_me = net.me()[1]

    def each(i, carry):
        lane = first + i
        for h in range(heads):
            at = h * HEAD_DIM
            q = qkv[lane, :, at : at + HEAD_DIM]
            k = qkv[lane, :, cols + at : cols + at + HEAD_DIM]
            v = qkv[lane, :, 2 * cols + at : 2 * cols + at + HEAD_DIM]
            grad = grad_ctx[lane, :, HEAD_DIM + at : 2 * HEAD_DIM + at]
            shares = jnp.exp(mm_nt(k, q) * score_scale + mask[...] - lse[lane, h : h + 1, :])
            grad_shares = mm_nt(v, grad)
            inner = jnp.sum(shares * grad_shares, axis=0, keepdims=True)
            grad_scores = (shares * (grad_shares - inner)).astype(bf16)
            grad_v = mm(shares.astype(bf16), grad)
            grad_k = mm(grad_scores, q) * score_scale
            grad_q = (mm_tn(k, grad_scores) * score_scale).T
            out[i, :, at : at + HEAD_DIM] = grad_q.astype(bf16)
            out[i, :, cols + at : cols + at + HEAD_DIM] = grad_k.astype(bf16)
            out[i, :, 2 * cols + at : 2 * cols + at + HEAD_DIM] = grad_v.astype(bf16)
        out[i, :, 3 * cols :] = jnp.zeros((out.shape[1], HEAD_DIM), bf16)
        sums[lane ^ lane_me] = col_sum(out[i].astype(f32))
        return carry

    lax.fori_loop(0, out.shape[0], each, 0)
    if extra:
        more, up_sums, sums_a, sums_b, tops_a, tops_m, top0, top1 = extra
        packed[...] = jnp.zeros_like(packed)
        for j in range(blocks):
            packed[j : j + 1, :] = up_sums[j]
            packed[blocks + j : blocks + j + 1, : sums.shape[2]] = sums[j] + more[j]
        packed[2 * blocks : 2 * blocks + 3, :] = sums_a[0:3, :]
        packed[2 * blocks + 3 : 2 * blocks + 6, :] = sums_b[0:3, :]
        tops = (tops_a[0:1, :], tops_a[1:2, :], tops_m[0:1, :], jnp.maximum(top0[0:1, :], top1[0:1, :]))
        for j, top in enumerate(tops):
            packed[2 * blocks + 6 : 2 * blocks + 7, 128 * j : 128 * j + 128] = top


def in_weight_grad(net, first, dims, in_t, attn_t, grad_qkv, ctx_low, far, near):
    blocks, cols, width = dims
    rows = in_t.shape[0] // net.parts
    at = 3 * cols - HEAD_DIM
    end = 3 * cols + HEAD_DIM
    dp = net.me()[0]
    for i, out in ((1, far), (0, near)):
        left = mm(in_t[...], grad_qkv[i])
        right = mm(attn_t[...], ctx_low[first + i])
        mixed = (left[:, at:] + right[:, : end - at]).astype(bf16)
        for block in range(net.parts):
            rs = slice(block * rows, (block + 1) * rows)
            place = net.slot(block, dp)
            out[place, :, :at] = left[rs, :at].astype(bf16)
            out[place, :, at:end] = mixed[rs]
            out[place, :, end:] = right[rs, end - at :].astype(bf16)


def token_backward(dims, lim, grad_qkv0, grad_qkv1, grad_first, tokens, weight, out, acc):
    blocks, cols, width = dims
    wide = 3 * cols + HEAD_DIM
    acc[...] = jnp.zeros_like(acc)
    half = grad_qkv0.shape[0]
    for grad, first in ((grad_qkv0, 0), (grad_qkv1, half)):

        def each(i, carry):
            acc[...] += mm_nt(grad[i], weight[first + i, :, :wide])
            return carry

        lax.fori_loop(0, half, each, 0)
    inputs = tokens[...].astype(f32)
    out[...] = (grad_first[...] + jnp.where(jnp.abs(inputs) <= lim[0], acc[...], 0.0)).astype(bf16)


def make_body(net):
    def body(
        tokens,
        cotangent,
        qkv_weight,
        qv_bias,
        out_weight,
        out_bias,
        first_gain,
        first_shift,
        up_weight,
        up_bias,
        down_weight,
        down_bias,
        second_gain,
        second_shift,
        act_ranges,
        long_lengths,
        short_lengths,
    ):
        lane = lax.axis_index("tensor")
        rows, width = tokens.shape
        assert rows == LONG_LEN
        cols = qkv_weight.shape[2]
        up_cols = up_weight.shape[1]
        blocks = lax.axis_size("tensor")
        half = blocks // 2
        dims = (blocks, cols, width)
        wide = 3 * cols + HEAD_DIM
        out_cols = cols + HEAD_DIM
        every = tuple(range(blocks))

        pieces_a, pieces_u, pieces_d = Pieces([]), Pieces([]), Pieces([])
        shard_a = jnp.concatenate(
            [qkv_weight[0], qkv_weight[1], qkv_weight[2], out_weight.T], 1
        ).astype(bf16)
        job_a = Job(net.gather(shard_a, pieces_a))
        bias_row = jnp.concatenate(
            [qv_bias[0], jnp.zeros((cols,), f32), qv_bias[1], jnp.zeros((HEAD_DIM,), f32), up_bias]
        )
        job_b = Job(net.gather_lane(bias_row[None]))
        job_u = Job(net.gather(up_weight.astype(bf16), pieces_u))
        job_d = Job(net.gather(down_weight.T.astype(bf16), pieces_d))

        def vmem(*shape, dtype=f32):
            return pltpu.VMEM(shape, dtype)

        def sems(plan):
            return pltpu.SemaphoreType.DMA((len(plan), len(plan[0])))

        unit = 2 * rows * width * width * blocks
        moved = 2 * width * width * blocks

        step((), None, [job_a, job_b], [job_a, job_b])
        step((), None, [job_a, job_b], [job_a, job_b])
        step((), None, [job_a, job_u], [job_a, job_u])
        step((), None, [job_a, job_u, job_d], [job_a])
        step((), None, [job_a], [job_a, job_u, job_d])
        biases = job_b.value

        bufs, plan = pieces_a.part(every)
        qkv, lse, in_t, ctx_low, ctx_slope, tops_a, weight_a = step(
            (act_ranges, long_lengths, short_lengths, tokens, biases, *bufs),
            call(
                functools.partial(attn_forward, net, plan, len(bufs), dims),
                "attn_forward",
                [SM] * 3 + [VM] * 2 + [HB] * len(bufs),
                [
                    like((blocks, rows, wide), bf16),
                    like((blocks, 8, rows)),
                    like((width, rows), bf16),
                    like((blocks, rows, out_cols), bf16),
                    like((blocks, rows, out_cols)),
                    like((8, 128)),
                    like((blocks, width, 4 * cols), bf16),
                ],
                [vmem(rows, width, dtype=bf16), vmem(rows, rows), vmem(out_cols, rows), vmem(8, out_cols), sems(plan)],
                4 * unit,
                3 * moved,
            ),
            [job_u, job_d],
            [job_u, job_d],
        )
        normed, inv, middle, mid_slope, mid_low, mid_t, tops_m = step(
            (act_ranges, ctx_low, tokens, out_bias, first_gain, first_shift, weight_a),
            call(
                functools.partial(attn_finish, dims),
                "attn_finish",
                [SM] + [VM] * 6,
                [
                    like((rows, width)),
                    like((rows, 1)),
                    like((rows, width)),
                    like((rows, width)),
                    like((rows, width), bf16),
                    like((width, rows), bf16),
                    like((8, 128)),
                ],
                [vmem(rows, width)],
                2 * unit,
                2 * moved,
            ),
            [job_u, job_d],
            [job_u],
        )

        def up_part(lanes, start, finish):
            bufs, plan = pieces_u.part(lanes)
            return step(
                (act_ranges, mid_low, biases, *bufs),
                call(
                    functools.partial(up_forward, net, plan, len(bufs), lanes[0], wide),
                    f"up_forward_{lanes[0]}",
                    [SM] + [VM] * 2 + [HB] * len(bufs),
                    [
                        like((half, rows, up_cols), bf16),
                        like((half, rows, up_cols)),
                        like((8, 128)),
                        like((half, width, up_cols), bf16),
                    ],
                    [vmem(8, up_cols), sems(plan)],
                    2 * unit,
                    2 * moved,
                ),
                start,
                finish,
            )

        act0, slope0, top0, weight_u0 = up_part(every[:half], [job_u], [job_u, job_d])
        act1, slope1, top1, weight_u1 = up_part(every[half:], [job_d], [job_d])
        step((), None, [job_d], [job_d])
        bufs_d, plan_d = pieces_d.part(every)
        layer_out, grad_second, ffn_t, sums_b, grad_up, up_sums = step(
            (act0, act1, slope0, slope1, middle, cotangent, down_bias, second_gain, second_shift, *bufs_d),
            call(
                functools.partial(down_both, net, plan_d, len(bufs_d)),
                "down_both",
                [VM] * 9 + [HB] * len(bufs_d),
                [
                    like((rows, width), bf16),
                    like((rows, width)),
                    like((width, rows), bf16),
                    like((8, width)),
                    like((blocks, rows, up_cols), bf16),
                    like((blocks, 1, up_cols)),
                ],
                [
                    vmem(blocks, width, up_cols, dtype=bf16),
                    vmem(rows, width),
                    vmem(rows, width, dtype=bf16),
                    sems(plan_d),
                ],
                2 * unit,
                4 * moved,
            ),
        )

        grad_shape = like((net.parts, width // net.parts, up_cols), bf16)
        both_shape = like((half,) + grad_shape.shape, bf16)

        def grad_of(name, left_t, rights, start=(), finish=()):
            return step(
                (left_t, *rights),
                call(
                    functools.partial(weight_grad, net),
                    name,
                    [VM] * (1 + len(rights)),
                    [both_shape, both_shape],
                    (),
                    unit,
                    moved,
                ),
                start,
                finish,
            )

        late_a = {}
        sum_d = Job(net.scatter_sum(*grad_of("down_grad", ffn_t, (act0, act1)), None))
        sum_u = Job(net.scatter_sum(*grad_of("up_grad", mid_t, (grad_up,), [sum_d], [sum_d]), None))
        grad_first, attn_t, grad_ctx, sums_a = step(
            (grad_up, grad_second, mid_slope, normed, inv, first_gain, ctx_slope, weight_u0, weight_u1, weight_a),
            call(
                functools.partial(mid_backward, dims),
                "mid_backward",
                [VM] * 10,
                [
                    like((rows, width)),
                    like((width, rows), bf16),
                    like((blocks, rows, out_cols), bf16),
                    like((8, width)),
                ],
                [vmem(rows, width), vmem(rows, width, dtype=bf16)],
                unit + unit // 3,
                3 * moved,
            ),
            [sum_d, sum_u],
            [sum_d, sum_u],
        )

        def back_part(first, extra=(), start=(), finish=()):
            return step(
                (long_lengths, short_lengths, qkv, lse, grad_ctx, *extra),
                call(
                    functools.partial(attn_backward, net, first, dims),
                    f"attn_backward_{first}",
                    [SM] * 2 + [VM] * (3 + len(extra)),
                    [like((half, rows, wide), bf16), like((16, width)) if extra else like((blocks, 1, wide))],
                    ([vmem(blocks, 1, wide)] if extra else []) + [vmem(rows, rows)],
                    4 * unit,
                    2 * moved,
                ),
                start,
                finish,
            )

        def in_part(grad_qkv, first, start=(), finish=()):
            return step(
                (in_t, attn_t, grad_qkv, ctx_low),
                call(
                    functools.partial(in_weight_grad, net, first, dims),
                    f"in_grad_{first}",
                    [VM] * 4,
                    [grad_shape, grad_shape],
                    (),
                    unit // 2,
                    moved,
                ),
                start,
                finish,
            )

        grad_qkv1, q_sums1 = back_part(half, (), [sum_u, sum_d], [])
        far, near = in_part(grad_qkv1, half)
        sum_a = Job(net.scatter_sum([far], [near], late_a))
        extra = (q_sums1, up_sums, sums_a, sums_b, tops_a, tops_m, top0, top1)
        grad_qkv0, packed = back_part(0, extra, [sum_a], [sum_u, sum_d, sum_a])
        is_top = (jnp.arange(packed.shape[0]) == 2 * blocks + 6)[:, None]
        sum_s = Job(net.sum_max(packed, is_top))
        far, near = in_part(grad_qkv0, 0, [sum_a, sum_u, sum_s], [])
        late_a.update(far=far, near=near)
        step((), None, [], [sum_a, sum_s])
        tokens_grad = step(
            (act_ranges, grad_qkv0, grad_qkv1, grad_first, tokens, weight_a),
            call(
                functools.partial(token_backward, dims),
                "token_backward",
                [SM] + [VM] * 5,
                [like((rows, width), bf16)],
                [vmem(rows, width)],
                unit,
                2 * moved,
            ),
            [sum_a, sum_s],
            [sum_a, sum_s],
        )[0]
        step((), None, [sum_a, sum_s], [sum_u, sum_s])
        line_du = Job(net.scatter_line(sum_d.value, sum_u.value))
        step((), None, [line_du, sum_s], [sum_a, sum_s])
        line_a = Job(net.scatter_line(sum_a.value))
        step((), None, [line_a, sum_s], [line_du, line_a, sum_s])
        step((), None, [line_a, line_du], [line_du, line_a])

        down_grad, up_grad = line_du.value
        down_grad = down_grad.T
        (a_grad,), packed = line_a.value, sum_s.value
        qkv_grad = jnp.stack([a_grad[:, j * cols : (j + 1) * cols] for j in range(3)])
        out_grad = a_grad[:, 3 * cols :].T
        own = lax.dynamic_slice_in_dim(packed, blocks + lane, 1)
        shared = packed[2 * blocks : 2 * blocks + 6]
        qv_bias_grad = jnp.concatenate([own[:, :cols], own[:, 2 * cols : 3 * cols]], 0)
        up_bias_grad = lax.dynamic_slice_in_dim(packed, lane, 1)[0]
        new_ranges = ema_decay * act_ranges + (1.0 - ema_decay) * packed[2 * blocks + 6, 0:512:128]
        return (
            layer_out,
            tokens_grad,
            qkv_grad,
            qv_bias_grad,
            out_grad,
            shared[0],
            shared[1],
            shared[2],
            up_grad,
            up_bias_grad,
            down_grad,
            shared[3],
            shared[4],
            shared[5],
            new_ranges,
        )

    return body


def solution(mesh):
    in_specs = (
        P(ALL, None),
        P(ALL, None),
        P(None, "dp", "tensor"),
        P(None, "tensor"),
        P("tensor", "dp"),
        P(),
        P(),
        P(),
        P("dp", "tensor"),
        P("tensor"),
        P("tensor", "dp"),
        P(),
        P(),
        P(),
        P(),
        P("dp"),
        P("dp"),
    )
    out_specs = (
        P(ALL, None),
        P(ALL, None),
        P(None, "dp", "tensor"),
        P(None, "tensor"),
        P("tensor", "dp"),
        P(),
        P(),
        P(),
        P("dp", "tensor"),
        P("tensor"),
        P("tensor", "dp"),
        P(),
        P(),
        P(),
        P(),
    )
    net = Grid() if mesh.shape["dp"] == 8 and mesh.shape["tensor"] == 4 else Plain()
    return jax.shard_map(make_body(net), mesh=mesh, in_specs=in_specs, out_specs=out_specs, check_vma=False)
```

```python
import functools
import itertools

import jax
import jax.numpy as jnp
from jax import lax
from jax.experimental import pallas as pl
from jax.experimental.pallas import tpu as pltpu
from jax.sharding import PartitionSpec as P

HEAD_DIM = 64
LONG_LEN = 512
SHORT_LEN = 128
ALL = ("dp", "tensor")

ema_decay = 0.9
epsilon = 1e-06
root_half = 0.7071067811865476
density_scale = 0.3989422804014327
score_scale = HEAD_DIM ** (-0.5)
NEG = -1000000000.0

f32 = jnp.float32
bf16 = jnp.bfloat16


def mm(left, right):
    return jnp.dot(left, right, preferred_element_type=f32)


def mm_tn(left, right):
    return lax.dot_general(left, right, (((0,), (0,)), ((), ())), preferred_element_type=f32)


def mm_nt(left, right):
    return lax.dot_general(left, right, (((1,), (1,)), ((), ())), preferred_element_type=f32)


def _lin(z, y, x, c):
    return (z * 2 + y) * 4 + x * 2 + c


def _perm(fn):
    out = []
    for z, y, x, c in itertools.product(range(4), range(2), range(2), range(2)):
        out.append((_lin(z, y, x, c), _lin(*fn(z, y, x, c))))
    return out


PC = _perm(lambda z, y, x, c: (z, y, x, 1 - c))
PX = _perm(lambda z, y, x, c: (z, y, 1 - x, c))
PY = _perm(lambda z, y, x, c: (z, 1 - y, x, c))
PZ1 = _perm(lambda z, y, x, c: (z ^ 1, y, x, c))
PZ2 = _perm(lambda z, y, x, c: (z ^ 2, y, x, c))


def tie(*trees):
    leaves, spec = jax.tree.flatten(trees)
    return jax.tree.unflatten(spec, lax.optimization_barrier(leaves))


class Job:
    def __init__(self, stages):
        self.stages, self.value, self.out, self.flight, self.over = stages, None, [], [], False
        self.take(None)

    def take(self, got):
        if not self.over:
            try:
                self.out = self.stages.send(got)
            except StopIteration as stop:
                self.value, self.out, self.over = stop.value, [], True


def step(ins, run=None, start=(), finish=()):
    ins, sends = tie(ins, [[value for value, _ in job.out] for job in start])
    for job, values in zip(start, sends):
        job.flight = [lax.ppermute(v, ALL, perm) for v, (_, perm) in zip(values, job.out)]
    outs = run(*ins) if run else ins
    outs, got = tie(outs, [job.flight for job in finish])
    for job, values in zip(finish, got):
        job.flight = []
        job.take(values)
    return outs


class Pieces:
    def __init__(self, plan):
        self.bufs, self.plan = {}, plan

    def part(self, lanes):
        plan = [p for p in self.plan if p[1] in lanes]
        names = sorted({p[0] for p in plan})
        return [self.bufs[n] for n in names], [(names.index(b), lane, lanes[0], k, y) for b, lane, k, y in plan]


class Grid:
    parts = 8

    @staticmethod
    def gather(shard, pieces, line_later=False):
        own = shard[None]
        for base, lane in ((0, 0), (5, 1)):
            pieces.plan.append((base, lane, 0, 0))
            pieces.plan.append((base + 1, lane, 0, 1))
            pieces.plan.append((base + 2, lane + 2, 0, 0))
            pieces.plan.append((base + 3, lane + 2, 0, 1))
            pieces.plan.append((base + 4, lane + 2, 2, 1))
        (far_z,) = yield [(own, PZ2)]
        pair = jnp.concatenate([own, far_z], 0)
        (near_z,) = yield [(pair, PZ1)]
        line = jnp.concatenate([pair, near_z], 0)
        to_core = [(line, PC)]
        now, later = ([], to_core) if line_later else (to_core, [])
        over_x, over_y, *rest = yield [(line, PX), (line, PY)] + now
        diag_x, diag_y, over_y_far, *more = yield [(over_y[:2], PX), (over_x[2:], PY), (over_y, PC)] + later
        (line_far,) = rest + more
        pieces.bufs.update({0: line, 1: over_y, 2: over_x, 3: diag_x, 4: diag_y, 5: line_far, 6: over_y_far})
        over_x_far, diag_x_far, diag_y_far = yield [(over_x, PC), (diag_x, PC), (diag_y, PC)]
        pieces.bufs.update({7: over_x_far, 8: diag_x_far, 9: diag_y_far})

    @staticmethod
    def slot(block, dp):
        place = block ^ dp
        return (place & 1) * 4 + (place & 2) + (place >> 2)

    @staticmethod
    def scatter_sum(far, near):
        (got,) = yield [(far, PC)]
        out_x, out_y = add_first(near, got)
        from_x, from_y = yield [(out_x, PX), (out_y, PY)]
        out_x, out_y = add_second(near, got, from_x, from_y)
        in_x, in_y = yield [(out_x, PX), (out_y, PY)]
        return near, got, in_x, in_y

    @staticmethod
    def scatter_line(*parts):
        out_z, kept = add_third(*parts)
        (from_z,) = yield [(out_z, PZ1)]
        out_z, kept = add_fourth(kept, from_z)
        (last,) = yield [(out_z, PZ2)]
        return [kept[n] + last[n].astype(f32) for n in range(len(parts))]

    @staticmethod
    def gather_lane(vec):
        (other,) = yield [(vec, PX)]
        pair = jnp.stack([vec, other])
        (more,) = yield [(pair, PC)]
        return jnp.stack([pair, more], 1).reshape((4,) + vec.shape)

    @staticmethod
    def sum_max(both, is_top):
        for perm in (PZ2, PZ1, PC, PX, PY):
            (other,) = yield [(both, perm)]
            both = jnp.where(is_top, jnp.maximum(both, other), both + other)
        return both

    @staticmethod
    def me():
        return lax.axis_index("dp"), lax.axis_index("tensor")


class Plain:
    parts = 1

    @staticmethod
    def gather(shard, pieces, line_later=False):
        rows = lax.all_gather(shard, "dp", axis=0, tiled=True)
        full = lax.all_gather(rows, "tensor", axis=0)
        for k in range(full.shape[0]):
            pieces.plan.append((k, k, None, None))
            pieces.bufs[k] = full[k][None]
        return
        yield

    @staticmethod
    def slot(block, dp):
        return block

    @staticmethod
    def scatter_sum(far, near):
        grads = jnp.stack([near[0], far[0], near[1], far[1]]).astype(f32)
        return grads.reshape((4, -1, grads.shape[-1]))
        yield

    @staticmethod
    def scatter_line(*parts):
        own = [lax.psum_scatter(p, "tensor", scatter_dimension=0, tiled=False) for p in parts]
        return [lax.psum_scatter(o, "dp", scatter_dimension=0, tiled=True) for o in own]
        yield

    @staticmethod
    def gather_lane(vec):
        return lax.all_gather(vec, "tensor", axis=0)
        yield

    @staticmethod
    def sum_max(both, is_top):
        return jnp.where(is_top, lax.pmax(both, ALL), lax.psum(both, ALL))
        yield

    @staticmethod
    def me():
        return 0, 0


VM = pl.BlockSpec(memory_space=pltpu.VMEM)
SM = pl.BlockSpec(memory_space=pltpu.SMEM)
VMEM_MIB = 14


def like(shape, dtype=f32):
    return jax.ShapeDtypeStruct(shape, dtype)


def call(kernel, name, specs, outs, scratch=(), flops=0, moved=0):
    return pl.pallas_call(
        kernel,
        name=name,
        out_shape=outs,
        in_specs=specs,
        out_specs=[VM] * len(outs),
        scratch_shapes=list(scratch),
        compiler_params=pltpu.CompilerParams(vmem_limit_bytes=VMEM_MIB * 2**20),
        cost_estimate=pl.CostEstimate(flops=flops, bytes_accessed=moved, transcendentals=0),
    )


def glue(kernel, outs, *ins):
    return call(kernel, kernel.__name__, [VM] * len(ins), outs)(*ins)


def add_first(near, got):
    def first_sums(near, got, out_x, out_y):
        for k in range(2):
            out_x[k] = (near[1, 4 + k].astype(f32) + got[1, 4 + k].astype(f32)).astype(bf16)
            out_y[k] = (near[1, 6 + k].astype(f32) + got[1, 6 + k].astype(f32)).astype(bf16)

    part = like((2,) + near.shape[2:], bf16)
    return glue(first_sums, [part, part], near, got)


def add_second(near, got, from_x, from_y):
    def second_sums(near, got, from_x, from_y, out_x, out_y):
        for k in range(4):
            over_x = near[1, k].astype(f32) + got[1, k].astype(f32)
            over_y = near[0, 4 + k].astype(f32) + got[0, 4 + k].astype(f32)
            if k < 2:
                over_y = over_y + from_x[k].astype(f32)
            else:
                over_x = over_x + from_y[k - 2].astype(f32)
            out_x[k] = over_x.astype(bf16)
            out_y[k] = over_y.astype(bf16)

    part = like((4,) + near.shape[2:], bf16)
    return glue(second_sums, [part, part], near, got, from_x, from_y)


def add_third(*parts):
    rows = parts[0][0].shape[-2:]
    ins = []
    for near, got, in_x, in_y in parts:
        ins += [near.reshape((-1, 8) + rows), got.reshape((-1, 8) + rows), in_x, in_y]

    def third_sums(*refs):
        out, kept = refs[-2:]
        for n in range(len(parts)):
            near, got, in_x, in_y = refs[4 * n : 4 * n + 4]
            for k in range(4):
                total = near[0, k].astype(f32) + got[0, k].astype(f32) + in_x[k].astype(f32) + in_y[k].astype(f32)
                if k < 2:
                    kept[n, k] = total
                else:
                    out[n, k - 2] = total.astype(bf16)

    shape = (len(parts), 2) + rows
    return glue(third_sums, [like(shape, bf16), like(shape)], *ins)


def add_fourth(kept, from_z):
    def fourth_sums(kept, from_z, out, mine):
        for n in range(kept.shape[0]):
            mine[n] = kept[n, 0] + from_z[n, 0].astype(f32)
            out[n] = (kept[n, 1] + from_z[n, 1].astype(f32)).astype(bf16)

    shape = kept.shape[:1] + kept.shape[2:]
    return glue(fourth_sums, [like(shape, bf16), like(shape)], kept, from_z)


def assemble(plan, bufs, dst, dp):
    for buf, lane, first, k, y in plan:
        src, to = bufs[buf], lane - first
        if k is None:
            dst[to] = src[0]
            continue
        rows = src.shape[1]

        def move(i, carry):
            z = k + i
            place = 4 * (z & 1) + 2 * (z >> 1) + y
            dst[to, pl.ds(pl.multiple_of((dp ^ place) * rows, rows), rows)] = src[i]
            return carry

        lax.fori_loop(0, src.shape[0], move, 0)


def row(vec):
    return vec[...].reshape(1, -1)


def row_stats(summed):
    centered = summed - jnp.mean(summed, axis=-1, keepdims=True)
    inv = lax.rsqrt(jnp.mean(centered * centered, axis=-1, keepdims=True) + epsilon)
    return centered * inv, inv


def norm_backward(scaled, normed, inv):
    row_mean = jnp.mean(scaled, axis=-1, keepdims=True)
    row_cross = jnp.mean(scaled * normed, axis=-1, keepdims=True)
    return inv * (scaled - row_mean - normed * row_cross)


def col_sum(values):
    return jnp.sum(values, axis=0, keepdims=True)


def top_of(values):
    return jnp.full((1, 128), jnp.max(jnp.abs(values)), f32)


def fill_mask(mask, longs, shorts):
    per_block = LONG_LEN // SHORT_LEN
    block = lax.axis_index("tensor")
    n_long = longs.shape[0]
    is_long = block < n_long
    whole = longs[jnp.minimum(block, n_long - 1)]
    first = jnp.maximum(block - n_long, 0) * per_block
    shift = jnp.where(is_long, LONG_LEN.bit_length() - 1, SHORT_LEN.bit_length() - 1)
    size = jnp.where(is_long, LONG_LEN, SHORT_LEN)
    k_pos = lax.broadcasted_iota(jnp.int32, (LONG_LEN, 1), 0)
    q_pos = lax.broadcasted_iota(jnp.int32, (1, LONG_LEN), 1)
    k_seg = lax.shift_right_logical(k_pos, jnp.full_like(k_pos, shift))
    q_seg = lax.shift_right_logical(q_pos, jnp.full_like(q_pos, shift))
    limit = jnp.zeros_like(k_pos)
    for j in range(per_block):
        limit = jnp.where(k_seg == j, jnp.where(is_long, whole, shorts[first + j]), limit)
    k_seg = jnp.where(k_pos - k_seg * size < limit, k_seg, -1)
    mask[...] = jnp.where(k_seg == q_seg, 0.0, NEG)


def attn_forward(net, plan, nb, dims, lim, longs, shorts, tokens, bias, *rest):
    blocks, cols, width = dims
    bufs, rest = rest[:nb], rest[nb:]
    qkv_out, lse_out, in_t, ctx_low, ctx_slope, top_out, weight, in_low, mask, ctx_t, top_ctx = rest
    heads = cols // HEAD_DIM
    low_q = 3 * cols + HEAD_DIM
    assemble(plan, bufs, weight, net.me()[0])
    inputs = tokens[...].astype(f32)
    in_low[...] = jnp.clip(inputs, -lim[0], lim[0]).astype(bf16)
    in_t[...] = in_low[...].T
    top_out[0:1, :] = top_of(inputs)
    fill_mask(mask, longs, shorts)
    ctx_t[0:HEAD_DIM, :] = jnp.zeros((HEAD_DIM, ctx_t.shape[1]), f32)
    top_ctx[...] = jnp.zeros_like(top_ctx)
    inv_limit = 1.0 / jnp.full((1, 1), lim[1], f32)

    def each(lane, carry):
        qkv = (mm(in_low[...], weight[lane, :, :low_q]) + bias[lane, :, :low_q]).astype(bf16)
        qkv_out[lane] = qkv
        for h in range(heads):
            at = h * HEAD_DIM
            q = qkv[:, at : at + HEAD_DIM]
            k = qkv[:, cols + at : cols + at + HEAD_DIM]
            v = qkv[:, 2 * cols + at : 2 * cols + at + HEAD_DIM]
            scores = mm_nt(k, q) * score_scale + mask[...]
            peak = jnp.max(scores, axis=0, keepdims=True)
            grown = jnp.exp(scores - peak)
            total = jnp.sum(grown, axis=0, keepdims=True)
            lse_out[lane, h : h + 1, :] = peak + jnp.log(total)
            shares = (grown * (1.0 / total)).astype(bf16)
            ctx_t[HEAD_DIM + at : 2 * HEAD_DIM + at, :] = mm_tn(v, shares)
        context = ctx_t[...].T
        bent = jnp.tanh(context * inv_limit)
        ctx_low[lane] = (lim[1] * bent).astype(bf16)
        ctx_slope[lane] = 1.0 - bent * bent
        top_ctx[...] = jnp.maximum(top_ctx[...], jnp.max(jnp.abs(context).reshape(-1, 8, context.shape[1]), axis=0))
        return carry

    lax.fori_loop(0, blocks, each, 0)
    top_out[1:2, :] = top_of(top_ctx[...])


def attn_finish(dims, lim, ctx_low, tokens, out_bias, gain, shift, weight, *outs):
    blocks, cols, width = dims
    normed_out, inv_out, middle_out, mid_slope, mid_low, mid_t, top_out, acc = outs
    at = 3 * cols - HEAD_DIM
    acc[...] = tokens[...].astype(f32) + row(out_bias)

    def each(lane, carry):
        acc[...] += mm_nt(ctx_low[lane], weight[lane, :, at:])
        return carry

    lax.fori_loop(0, blocks, each, 0)
    normed, inv = row_stats(acc[...])
    normed_out[...] = normed
    inv_out[...] = inv
    middle = normed * row(gain) + row(shift)
    middle_out[...] = middle
    bent = jnp.tanh(middle * (1.0 / jnp.full((1, 1), lim[2], f32)))
    low = (lim[2] * bent).astype(bf16)
    mid_low[...] = low
    mid_slope[...] = 1.0 - bent * bent
    mid_t[...] = low.T
    top_out[...] = jnp.broadcast_to(top_of(middle), top_out.shape)


def up_forward(net, plan, nb, first, low_q, lim, mid_low, bias, *rest):
    bufs, rest = rest[:nb], rest[nb:]
    act_out, slope_out, top_out, weight, top_hid = rest
    assemble(plan, bufs, weight, net.me()[0])
    top_hid[...] = jnp.zeros_like(top_hid)
    inv_limit = 1.0 / jnp.full((1, 1), lim[3], f32)

    def each(lane, carry):
        up = mm(mid_low[...], weight[lane]) + bias[first + lane, :, low_q:]
        half = 0.5 * (1.0 + lax.erf(up * root_half))
        hidden = up * half
        top_hid[...] = jnp.maximum(top_hid[...], jnp.max(jnp.abs(hidden).reshape(-1, 8, hidden.shape[1]), axis=0))
        bent = jnp.tanh(hidden * inv_limit)
        act_out[lane] = (lim[3] * bent).astype(bf16)
        slope_out[lane] = (1.0 - bent * bent) * (half + up * jnp.exp(-0.5 * up * up) * density_scale)
        return carry

    lax.fori_loop(0, weight.shape[0], each, 0)
    top_out[...] = jnp.broadcast_to(top_of(top_hid[...]), top_out.shape)


def down_both(net, plan, nb, act0, act1, slope0, slope1, middle, cotangent, down_bias, gain, shift, *rest):
    bufs, rest = rest[:nb], rest[nb:]
    layer_out, grad_out, ffn_t, sums, grad_up, up_sums, weight, acc, ffn_low = rest
    assemble(plan, bufs, weight, net.me()[0])
    acc[...] = middle[...] + row(down_bias)
    half = act0.shape[0]
    for act, first in ((act0, 0), (act1, half)):

        def each(i, carry):
            acc[...] += mm_nt(act[i], weight[first + i])
            return carry

        lax.fori_loop(0, half, each, 0)
    normed, inv = row_stats(acc[...])
    layer_out[...] = (normed * row(gain) + row(shift)).astype(bf16)
    incoming = cotangent[...].astype(f32)
    grad = norm_backward(incoming * row(gain), normed, inv)
    grad_out[...] = grad
    ffn_low[...] = grad.astype(bf16)
    ffn_t[...] = ffn_low[...].T
    sums[...] = jnp.zeros_like(sums)
    sums[0:1, :] = col_sum(grad)
    sums[1:2, :] = col_sum(incoming * normed)
    sums[2:3, :] = col_sum(incoming)
    lane_me = net.me()[1]
    for slope, first in ((slope0, 0), (slope1, half)):

        def back(i, carry):
            low = (mm(ffn_low[...], weight[first + i]) * slope[i]).astype(bf16)
            grad_up[first + i] = low
            up_sums[(first + i) ^ lane_me] = col_sum(low.astype(f32))
            return carry

        lax.fori_loop(0, half, back, 0)


def weight_grad(net, left_t, *rest):
    *rights, far, near = rest
    rows = left_t.shape[0] // net.parts
    dp = net.me()[0]
    half = far.shape[0]
    for x in range(half):
        for out, lane in ((far, 2 * x + 1), (near, 2 * x)):
            right = rights[lane // rights[0].shape[0]]
            grad = mm(left_t[...], right[lane % right.shape[0]]).astype(bf16)
            for block in range(net.parts):
                out[x, net.slot(block, dp)] = grad[block * rows : (block + 1) * rows]


def mid_backward(dims, grad_up, grad_second, mid_slope, normed, inv, gain, ctx_slope, weight0, weight1, out_weight, *outs):
    blocks, cols, width = dims
    grad_out, attn_t, grad_ctx, sums, acc, attn_low = outs
    at = 3 * cols - HEAD_DIM
    acc[...] = jnp.zeros_like(acc)
    half = weight0.shape[0]
    for weight, first in ((weight0, 0), (weight1, half)):

        def each(i, carry):
            acc[...] += mm_nt(grad_up[first + i], weight[i])
            return carry

        lax.fori_loop(0, half, each, 0)
    incoming = grad_second[...] + acc[...] * mid_slope[...]
    grad = norm_backward(incoming * row(gain), normed[...], inv[...])
    grad_out[...] = grad
    attn_low[...] = grad.astype(bf16)
    attn_t[...] = attn_low[...].T
    sums[...] = jnp.zeros_like(sums)
    sums[0:1, :] = col_sum(grad)
    sums[1:2, :] = col_sum(incoming * normed[...])
    sums[2:3, :] = col_sum(incoming)

    def spread(lane, carry):
        grad_ctx[lane] = (mm(attn_low[...], out_weight[lane, :, at:]) * ctx_slope[lane]).astype(bf16)
        return carry

    lax.fori_loop(0, blocks, spread, 0)


def attn_backward(net, dims, longs, shorts, qkv, lse, grad_ctx, in_t, attn_t, ctx_low, *rest):
    blocks, cols, width = dims
    up_sums, sums_a, sums_b, tops_a, tops_m, top0, top1, out, far, near, packed, sums, mask = rest
    heads = cols // HEAD_DIM
    rows = in_t.shape[0] // net.parts
    start = 3 * cols - HEAD_DIM
    end = 3 * cols + HEAD_DIM
    fill_mask(mask, longs, shorts)
    dp, lane_me = net.me()

    def each(lane, carry):
        for h in range(heads):
            at = h * HEAD_DIM
            q = qkv[lane, :, at : at + HEAD_DIM]
            k = qkv[lane, :, cols + at : cols + at + HEAD_DIM]
            v = qkv[lane, :, 2 * cols + at : 2 * cols + at + HEAD_DIM]
            grad = grad_ctx[lane, :, HEAD_DIM + at : 2 * HEAD_DIM + at]
            shares = jnp.exp(mm_nt(k, q) * score_scale + mask[...] - lse[lane, h : h + 1, :])
            grad_shares = mm_nt(v, grad)
            inner = jnp.sum(shares * grad_shares, axis=0, keepdims=True)
            grad_scores = (shares * (grad_shares - inner)).astype(bf16)
            grad_v = mm(shares.astype(bf16), grad)
            grad_k = mm(grad_scores, q) * score_scale
            grad_q = (mm_tn(k, grad_scores) * score_scale).T
            out[lane, :, at : at + HEAD_DIM] = grad_q.astype(bf16)
            out[lane, :, cols + at : cols + at + HEAD_DIM] = grad_k.astype(bf16)
            out[lane, :, 2 * cols + at : 2 * cols + at + HEAD_DIM] = grad_v.astype(bf16)
        out[lane, :, 3 * cols :] = jnp.zeros((out.shape[1], HEAD_DIM), bf16)
        sums[lane ^ lane_me] = col_sum(out[lane].astype(f32))
        return carry

    lax.fori_loop(0, blocks, each, 0)

    def weights(x, carry):
        for core, to in ((1, far), (0, near)):
            left = mm(in_t[...], out[2 * x + core])
            right = mm(attn_t[...], ctx_low[2 * x + core])
            mixed = (left[:, start:] + right[:, : end - start]).astype(bf16)
            for block in range(net.parts):
                rs = slice(block * rows, (block + 1) * rows)
                place = net.slot(block, dp)
                to[x, place, :, :start] = left[rs, :start].astype(bf16)
                to[x, place, :, start:end] = mixed[rs]
                to[x, place, :, end:] = right[rs, end - start :].astype(bf16)
        return carry

    lax.fori_loop(0, far.shape[0], weights, 0)
    packed[...] = jnp.zeros_like(packed)
    for j in range(blocks):
        packed[j : j + 1, :] = up_sums[j]
        packed[blocks + j : blocks + j + 1, : sums.shape[2]] = sums[j]
    packed[2 * blocks : 2 * blocks + 3, :] = sums_a[0:3, :]
    packed[2 * blocks + 3 : 2 * blocks + 6, :] = sums_b[0:3, :]
    tops = (tops_a[0:1, :], tops_a[1:2, :], tops_m[0:1, :], jnp.maximum(top0[0:1, :], top1[0:1, :]))
    for j, top in enumerate(tops):
        packed[2 * blocks + 6 : 2 * blocks + 7, 128 * j : 128 * j + 128] = top


def token_backward(dims, lim, grad_qkv, grad_first, tokens, weight, out, acc):
    blocks, cols, width = dims
    acc[...] = jnp.zeros_like(acc)

    def each(lane, carry):
        acc[...] += mm_nt(grad_qkv[lane], weight[lane, :, : 3 * cols + HEAD_DIM])
        return carry

    lax.fori_loop(0, blocks, each, 0)
    inputs = tokens[...].astype(f32)
    out[...] = (grad_first[...] + jnp.where(jnp.abs(inputs) <= lim[0], acc[...], 0.0)).astype(bf16)


def make_body(net):
    def body(
        tokens,
        cotangent,
        qkv_weight,
        qv_bias,
        out_weight,
        out_bias,
        first_gain,
        first_shift,
        up_weight,
        up_bias,
        down_weight,
        down_bias,
        second_gain,
        second_shift,
        act_ranges,
        long_lengths,
        short_lengths,
    ):
        lane = lax.axis_index("tensor")
        rows, width = tokens.shape
        assert rows == LONG_LEN
        cols = qkv_weight.shape[2]
        up_cols = up_weight.shape[1]
        blocks = lax.axis_size("tensor")
        half = blocks // 2
        dims = (blocks, cols, width)
        wide = 3 * cols + HEAD_DIM
        out_cols = cols + HEAD_DIM
        every = tuple(range(blocks))

        pieces_a, pieces_u, pieces_d = Pieces([]), Pieces([]), Pieces([])
        shard_a = jnp.concatenate(
            [qkv_weight[0], qkv_weight[1], qkv_weight[2], out_weight.T], 1
        ).astype(bf16)
        job_a = Job(net.gather(shard_a, pieces_a))
        bias_row = jnp.concatenate(
            [qv_bias[0], jnp.zeros((cols,), f32), qv_bias[1], jnp.zeros((HEAD_DIM,), f32), up_bias]
        )
        job_b = Job(net.gather_lane(bias_row[None]))
        job_u = Job(net.gather(up_weight.astype(bf16), pieces_u))
        job_d = Job(net.gather(down_weight.T.astype(bf16), pieces_d, True))

        def vmem(*shape, dtype=f32):
            return pltpu.VMEM(shape, dtype)

        unit = 2 * rows * width * width * blocks
        moved = 2 * width * width * blocks

        step((), None, [job_a, job_b], [job_a, job_b])
        step((), None, [job_a, job_u, job_b], [job_a, job_u, job_b])
        step((), None, [job_a, job_u], [job_a, job_u])
        step((), None, [job_a, job_d], [job_a, job_d])
        step((), None, [job_u, job_a], [job_a])
        biases = job_b.value

        bufs, plan = pieces_a.part(every)
        qkv, lse, in_t, ctx_low, ctx_slope, tops_a, weight_a = step(
            (act_ranges, long_lengths, short_lengths, tokens, biases, *bufs),
            call(
                functools.partial(attn_forward, net, plan, len(bufs), dims),
                "attn_forward",
                [SM] * 3 + [VM] * 2 + [VM] * len(bufs),
                [
                    like((blocks, rows, wide), bf16),
                    like((blocks, 8, rows)),
                    like((width, rows), bf16),
                    like((blocks, rows, out_cols), bf16),
                    like((blocks, rows, out_cols)),
                    like((8, 128)),
                    like((blocks, width, 4 * cols), bf16),
                ],
                [vmem(rows, width, dtype=bf16), vmem(rows, rows), vmem(out_cols, rows), vmem(8, out_cols)],
                4 * unit,
                3 * moved,
            ),
            [job_d],
            [job_u, job_d],
        )
        normed, inv, middle, mid_slope, mid_low, mid_t, tops_m = step(
            (act_ranges, ctx_low, tokens, out_bias, first_gain, first_shift, weight_a),
            call(
                functools.partial(attn_finish, dims),
                "attn_finish",
                [SM] + [VM] * 6,
                [
                    like((rows, width)),
                    like((rows, 1)),
                    like((rows, width)),
                    like((rows, width)),
                    like((rows, width), bf16),
                    like((width, rows), bf16),
                    like((8, 128)),
                ],
                [vmem(rows, width)],
                2 * unit,
                2 * moved,
            ),
            [job_u, job_d],
            [job_u],
        )

        def up_part(lanes, start, finish):
            bufs, plan = pieces_u.part(lanes)
            return step(
                (act_ranges, mid_low, biases, *bufs),
                call(
                    functools.partial(up_forward, net, plan, len(bufs), lanes[0], wide),
                    f"up_forward_{lanes[0]}",
                    [SM] + [VM] * 2 + [VM] * len(bufs),
                    [
                        like((half, rows, up_cols), bf16),
                        like((half, rows, up_cols)),
                        like((8, 128)),
                        like((half, width, up_cols), bf16),
                    ],
                    [vmem(8, up_cols)],
                    2 * unit,
                    2 * moved,
                ),
                start,
                finish,
            )

        act0, slope0, top0, weight_u0 = up_part(every[:half], [job_u], [job_u])
        act1, slope1, top1, weight_u1 = up_part(every[half:], [], [job_d])
        step((), None, [job_d], [job_d])
        step((), None, [job_d], [job_d])
        bufs_d, plan_d = pieces_d.part(every)
        layer_out, grad_second, ffn_t, sums_b, grad_up, up_sums = step(
            (act0, act1, slope0, slope1, middle, cotangent, down_bias, second_gain, second_shift, *bufs_d),
            call(
                functools.partial(down_both, net, plan_d, len(bufs_d)),
                "down_both",
                [VM] * 9 + [VM] * len(bufs_d),
                [
                    like((rows, width), bf16),
                    like((rows, width)),
                    like((width, rows), bf16),
                    like((8, width)),
                    like((blocks, rows, up_cols), bf16),
                    like((blocks, 1, up_cols)),
                ],
                [
                    vmem(blocks, width, up_cols, dtype=bf16),
                    vmem(rows, width),
                    vmem(rows, width, dtype=bf16),
                ],
                2 * unit,
                4 * moved,
            ),
        )

        grad_shape = like((net.parts, width // net.parts, up_cols), bf16)
        both_shape = like((half,) + grad_shape.shape, bf16)

        def grad_of(name, left_t, rights, start=(), finish=()):
            return step(
                (left_t, *rights),
                call(
                    functools.partial(weight_grad, net),
                    name,
                    [VM] * (1 + len(rights)),
                    [both_shape, both_shape],
                    (),
                    unit,
                    moved,
                ),
                start,
                finish,
            )

        sum_d = Job(net.scatter_sum(*grad_of("down_grad", ffn_t, (act0, act1))))
        sum_u = Job(net.scatter_sum(*grad_of("up_grad", mid_t, (grad_up,), [sum_d], [sum_d])))
        grad_first, attn_t, grad_ctx, sums_a = step(
            (grad_up, grad_second, mid_slope, normed, inv, first_gain, ctx_slope, weight_u0, weight_u1, weight_a),
            call(
                functools.partial(mid_backward, dims),
                "mid_backward",
                [VM] * 10,
                [
                    like((rows, width)),
                    like((width, rows), bf16),
                    like((blocks, rows, out_cols), bf16),
                    like((8, width)),
                ],
                [vmem(rows, width), vmem(rows, width, dtype=bf16)],
                unit + unit // 3,
                3 * moved,
            ),
            [sum_d, sum_u],
            [sum_d, sum_u],
        )

        grad_qkv, far, near, packed = step(
            (long_lengths, short_lengths, qkv, lse, grad_ctx, in_t, attn_t, ctx_low)
            + (up_sums, sums_a, sums_b, tops_a, tops_m, top0, top1),
            call(
                functools.partial(attn_backward, net, dims),
                "attn_backward",
                [SM] * 2 + [VM] * 13,
                [like((blocks, rows, wide), bf16), both_shape, both_shape, like((16, width))],
                [vmem(blocks, 1, wide), vmem(rows, rows)],
                4 * unit,
                2 * moved,
            ),
            [sum_u, sum_d],
            [sum_u, sum_d],
        )
        sum_a = Job(net.scatter_sum(far, near))
        is_top = (jnp.arange(packed.shape[0]) == 2 * blocks + 6)[:, None]
        sum_s = Job(net.sum_max(packed, is_top))
        line_d = Job(net.scatter_line(sum_d.value))
        tokens_grad = step(
            (act_ranges, grad_qkv, grad_first, tokens, weight_a),
            call(
                functools.partial(token_backward, dims),
                "token_backward",
                [SM] + [VM] * 4,
                [like((rows, width), bf16)],
                [vmem(rows, width)],
                unit,
                2 * moved,
            ),
            [sum_a, sum_u, line_d, sum_s],
            [sum_a, line_d, sum_s],
        )[0]
        step((), None, [sum_a, sum_s], [sum_a, sum_u, sum_s])
        line_u = Job(net.scatter_line(sum_u.value))
        step((), None, [sum_a, line_d, line_u, sum_s], [line_d, line_u, sum_s])
        step((), None, [line_u, sum_s], [sum_a, sum_s])
        line_a = Job(net.scatter_line(sum_a.value))
        step((), None, [line_a, sum_s], [line_u, line_a, sum_s])
        step((), None, [line_a], [line_a])

        (down_grad,), (up_grad,) = line_d.value, line_u.value
        down_grad = down_grad.T
        (a_grad,), packed = line_a.value, sum_s.value
        qkv_grad = jnp.stack([a_grad[:, j * cols : (j + 1) * cols] for j in range(3)])
        out_grad = a_grad[:, 3 * cols :].T
        own = lax.dynamic_slice_in_dim(packed, blocks + lane, 1)
        shared = packed[2 * blocks : 2 * blocks + 6]
        qv_bias_grad = jnp.concatenate([own[:, :cols], own[:, 2 * cols : 3 * cols]], 0)
        up_bias_grad = lax.dynamic_slice_in_dim(packed, lane, 1)[0]
        new_ranges = ema_decay * act_ranges + (1.0 - ema_decay) * packed[2 * blocks + 6, 0:512:128]
        return (
            layer_out,
            tokens_grad,
            qkv_grad,
            qv_bias_grad,
            out_grad,
            shared[0],
            shared[1],
            shared[2],
            up_grad,
            up_bias_grad,
            down_grad,
            shared[3],
            shared[4],
            shared[5],
            new_ranges,
        )

    return body


def solution(mesh):
    in_specs = (
        P(ALL, None),
        P(ALL, None),
        P(None, "dp", "tensor"),
        P(None, "tensor"),
        P("tensor", "dp"),
        P(),
        P(),
        P(),
        P("dp", "tensor"),
        P("tensor"),
        P("tensor", "dp"),
        P(),
        P(),
        P(),
        P(),
        P("dp"),
        P("dp"),
    )
    out_specs = (
        P(ALL, None),
        P(ALL, None),
        P(None, "dp", "tensor"),
        P(None, "tensor"),
        P("tensor", "dp"),
        P(),
        P(),
        P(),
        P("dp", "tensor"),
        P("tensor"),
        P("tensor", "dp"),
        P(),
        P(),
        P(),
        P(),
    )
    net = Grid() if mesh.shape["dp"] == 8 and mesh.shape["tensor"] == 4 else Plain()
    return jax.shard_map(make_body(net), mesh=mesh, in_specs=in_specs, out_specs=out_specs, check_vma=False)
```

```python
import functools
import itertools

import jax
import jax.numpy as jnp
from jax import lax
from jax.experimental import pallas as pl
from jax.experimental.pallas import tpu as pltpu
from jax.sharding import PartitionSpec as P

HEAD_DIM = 64
LONG_LEN = 512
SHORT_LEN = 128
ALL = ("dp", "tensor")

ema_decay = 0.9
epsilon = 1e-06
root_half = 0.7071067811865476
density_scale = 0.3989422804014327
score_scale = HEAD_DIM ** (-0.5)
NEG = -1000000000.0

f32 = jnp.float32
bf16 = jnp.bfloat16


def mm(left, right):
    return jnp.dot(left, right, preferred_element_type=f32)


def mm_tn(left, right):
    return lax.dot_general(left, right, (((0,), (0,)), ((), ())), preferred_element_type=f32)


def mm_nt(left, right):
    return lax.dot_general(left, right, (((1,), (1,)), ((), ())), preferred_element_type=f32)


def _lin(z, y, x, c):
    return (z * 2 + y) * 4 + x * 2 + c


def _perm(fn):
    out = []
    for z, y, x, c in itertools.product(range(4), range(2), range(2), range(2)):
        out.append((_lin(z, y, x, c), _lin(*fn(z, y, x, c))))
    return out


PC = _perm(lambda z, y, x, c: (z, y, x, 1 - c))
PX = _perm(lambda z, y, x, c: (z, y, 1 - x, c))
PY = _perm(lambda z, y, x, c: (z, 1 - y, x, c))
PZ1 = _perm(lambda z, y, x, c: (z ^ 1, y, x, c))
PZ2 = _perm(lambda z, y, x, c: (z ^ 2, y, x, c))


def tie(*trees):
    leaves, spec = jax.tree.flatten(trees)
    return jax.tree.unflatten(spec, lax.optimization_barrier(leaves))


class Job:
    def __init__(self, stages):
        self.stages, self.value, self.out, self.flight, self.over = stages, None, [], [], False
        self.take(None)

    def take(self, got):
        if not self.over:
            try:
                self.out = self.stages.send(got)
            except StopIteration as stop:
                self.value, self.out, self.over = stop.value, [], True


def step(ins, run=None, start=(), finish=()):
    ins, sends = tie(ins, [[value for value, _ in job.out] for job in start])
    for job, values in zip(start, sends):
        job.flight = [lax.ppermute(v, ALL, perm) for v, (_, perm) in zip(values, job.out)]
    outs = run(*ins) if run else ins
    outs, got = tie(outs, [job.flight for job in finish])
    for job, values in zip(finish, got):
        job.flight = []
        job.take(values)
    return outs


class Pieces:
    def __init__(self, plan):
        self.bufs, self.plan = {}, plan

    def part(self, lanes):
        plan = [p for p in self.plan if p[1] in lanes]
        names = sorted({p[0] for p in plan})
        return [self.bufs[n] for n in names], [(names.index(b), lane, lanes[0], k, y) for b, lane, k, y in plan]


class Grid:
    parts = 8

    @staticmethod
    def gather(shard, pieces, line_later=False):
        own = shard[None]
        for base, lane in ((0, 0), (5, 1)):
            pieces.plan.append((base, lane, 0, 0))
            pieces.plan.append((base + 1, lane, 0, 1))
            pieces.plan.append((base + 2, lane + 2, 0, 0))
            pieces.plan.append((base + 3, lane + 2, 0, 1))
            pieces.plan.append((base + 4, lane + 2, 2, 1))
        (far_z,) = yield [(own, PZ2)]
        pair = jnp.concatenate([own, far_z], 0)
        (near_z,) = yield [(pair, PZ1)]
        line = jnp.concatenate([pair, near_z], 0)
        to_core = [(line, PC)]
        now, later = ([], to_core) if line_later else (to_core, [])
        over_x, over_y, *rest = yield [(line, PX), (line, PY)] + now
        diag_x, diag_y, over_y_far, *more = yield [(over_y[:2], PX), (over_x[2:], PY), (over_y, PC)] + later
        (line_far,) = rest + more
        pieces.bufs.update({0: line, 1: over_y, 2: over_x, 3: diag_x, 4: diag_y, 5: line_far, 6: over_y_far})
        over_x_far, diag_x_far, diag_y_far = yield [(over_x, PC), (diag_x, PC), (diag_y, PC)]
        pieces.bufs.update({7: over_x_far, 8: diag_x_far, 9: diag_y_far})

    @staticmethod
    def slot(block, dp):
        place = block ^ dp
        return (place & 1) * 4 + (place & 2) + (place >> 2)

    @staticmethod
    def scatter_sum(far, near):
        (got,) = yield [(far, PC)]
        out_x, out_y = add_first(near, got)
        from_x, from_y = yield [(out_x, PX), (out_y, PY)]
        out_x, out_y = add_second(near, got, from_x, from_y)
        in_x, in_y = yield [(out_x, PX), (out_y, PY)]
        return near, got, in_x, in_y

    @staticmethod
    def scatter_line(near, got, in_x, in_y):
        out_z, kept = add_third(near, got, in_x, in_y)
        (from_z,) = yield [(out_z, PZ1)]
        out_z, kept = add_fourth(kept, from_z)
        (last,) = yield [(out_z, PZ2)]
        return kept + last.astype(f32)

    @staticmethod
    def scatter_z_first(far, near):
        (got,) = yield [(far, PC)]
        (from_z,) = yield [(add_near_z(near, got), PZ1)]
        out_x, out_y = add_corner(near, got, from_z)
        from_x, from_y = yield [(out_x, PX), (out_y, PY)]
        out_x, out_y = add_sides(near, got, from_z, from_x, from_y)
        in_x, in_y = yield [(out_x, PX), (out_y, PY)]
        out_z, kept = add_own(near, got, from_z, in_x, in_y)
        (last,) = yield [(out_z, PZ2)]
        return kept + last.astype(f32)

    @staticmethod
    def gather_lane(vec):
        (other,) = yield [(vec, PX)]
        pair = jnp.stack([vec, other])
        (more,) = yield [(pair, PC)]
        return jnp.stack([pair, more], 1).reshape((4,) + vec.shape)

    @staticmethod
    def sum_max(both, is_top):
        for perm in (PZ2, PZ1, PC, PX, PY):
            (other,) = yield [(both, perm)]
            both = jnp.where(is_top, jnp.maximum(both, other), both + other)
        return both

    @staticmethod
    def me():
        return lax.axis_index("dp"), lax.axis_index("tensor")


class Plain:
    parts = 1

    @staticmethod
    def gather(shard, pieces, line_later=False):
        rows = lax.all_gather(shard, "dp", axis=0, tiled=True)
        full = lax.all_gather(rows, "tensor", axis=0)
        for k in range(full.shape[0]):
            pieces.plan.append((k, k, None, None))
            pieces.bufs[k] = full[k][None]
        return
        yield

    @staticmethod
    def slot(block, dp):
        return block

    @staticmethod
    def scatter_sum(far, near):
        grads = jnp.stack([near[0], far[0], near[1], far[1]]).astype(f32)
        return (grads.reshape((4, -1, grads.shape[-1])),)
        yield

    @staticmethod
    def scatter_line(grads):
        own = lax.psum_scatter(grads, "tensor", scatter_dimension=0, tiled=False)
        return lax.psum_scatter(own, "dp", scatter_dimension=0, tiled=True)
        yield

    @staticmethod
    def scatter_z_first(far, near):
        grads = yield from Plain.scatter_sum(far, near)
        return (yield from Plain.scatter_line(*grads))

    @staticmethod
    def gather_lane(vec):
        return lax.all_gather(vec, "tensor", axis=0)
        yield

    @staticmethod
    def sum_max(both, is_top):
        return jnp.where(is_top, lax.pmax(both, ALL), lax.psum(both, ALL))
        yield

    @staticmethod
    def me():
        return 0, 0


VM = pl.BlockSpec(memory_space=pltpu.VMEM)
SM = pl.BlockSpec(memory_space=pltpu.SMEM)
VMEM_MIB = 14


def like(shape, dtype=f32):
    return jax.ShapeDtypeStruct(shape, dtype)


def call(kernel, name, specs, outs, scratch=(), flops=0, moved=0):
    return pl.pallas_call(
        kernel,
        name=name,
        out_shape=outs,
        in_specs=specs,
        out_specs=[VM] * len(outs),
        scratch_shapes=list(scratch),
        compiler_params=pltpu.CompilerParams(vmem_limit_bytes=VMEM_MIB * 2**20),
        cost_estimate=pl.CostEstimate(flops=flops, bytes_accessed=moved, transcendentals=0),
    )


def glue(kernel, outs, *ins):
    return call(kernel, kernel.__name__, [VM] * len(ins), outs)(*ins)


def add_first(near, got):
    def first_sums(near, got, out_x, out_y):
        for k in range(2):
            out_x[k] = (near[1, 4 + k].astype(f32) + got[1, 4 + k].astype(f32)).astype(bf16)
            out_y[k] = (near[1, 6 + k].astype(f32) + got[1, 6 + k].astype(f32)).astype(bf16)

    part = like((2,) + near.shape[2:], bf16)
    return glue(first_sums, [part, part], near, got)


def add_second(near, got, from_x, from_y):
    def second_sums(near, got, from_x, from_y, out_x, out_y):
        for k in range(4):
            over_x = near[1, k].astype(f32) + got[1, k].astype(f32)
            over_y = near[0, 4 + k].astype(f32) + got[0, 4 + k].astype(f32)
            if k < 2:
                over_y = over_y + from_x[k].astype(f32)
            else:
                over_x = over_x + from_y[k - 2].astype(f32)
            out_x[k] = over_x.astype(bf16)
            out_y[k] = over_y.astype(bf16)

    part = like((4,) + near.shape[2:], bf16)
    return glue(second_sums, [part, part], near, got, from_x, from_y)


def add_third(near, got, in_x, in_y):
    def third_sums(near, got, in_x, in_y, out, kept):
        for k in range(4):
            total = near[0, k].astype(f32) + got[0, k].astype(f32) + in_x[k].astype(f32) + in_y[k].astype(f32)
            if k < 2:
                kept[k] = total
            else:
                out[k - 2] = total.astype(bf16)

    shape = (2,) + near.shape[2:]
    return glue(third_sums, [like(shape, bf16), like(shape)], near, got, in_x, in_y)


def add_fourth(kept, from_z):
    def fourth_sums(kept, from_z, out, mine):
        mine[...] = kept[0] + from_z[0].astype(f32)
        out[...] = (kept[1] + from_z[1].astype(f32)).astype(bf16)

    shape = kept.shape[1:]
    return glue(fourth_sums, [like(shape, bf16), like(shape)], kept, from_z)


def add_near_z(near, got):
    def near_z_sums(near, got, out):
        for y in range(2):
            for k in range(2):
                out[:, 2 * y + k] = (near[:, 4 * y + 2 + k].astype(f32) + got[:, 4 * y + 2 + k].astype(f32)).astype(bf16)

    return glue(near_z_sums, [like((2, 4) + near.shape[2:], bf16)], near, got)[0]


def three(near, got, from_z, x, y, k):
    return near[x, 4 * y + k].astype(f32) + got[x, 4 * y + k].astype(f32) + from_z[x, 2 * y + k].astype(f32)


def add_corner(near, got, from_z):
    def corner_sums(near, got, from_z, out_x, out_y):
        out_x[...] = three(near, got, from_z, 1, 1, 0).astype(bf16)
        out_y[...] = three(near, got, from_z, 1, 1, 1).astype(bf16)

    part = like(near.shape[2:], bf16)
    return glue(corner_sums, [part, part], near, got, from_z)


def add_sides(near, got, from_z, from_x, from_y):
    def side_sums(near, got, from_z, from_x, from_y, out_x, out_y):
        out_x[0] = three(near, got, from_z, 1, 0, 0).astype(bf16)
        out_x[1] = (three(near, got, from_z, 1, 0, 1) + from_y[...].astype(f32)).astype(bf16)
        out_y[0] = (three(near, got, from_z, 0, 1, 0) + from_x[...].astype(f32)).astype(bf16)
        out_y[1] = three(near, got, from_z, 0, 1, 1).astype(bf16)

    part = like((2,) + near.shape[2:], bf16)
    return glue(side_sums, [part, part], near, got, from_z, from_x, from_y)


def add_own(near, got, from_z, in_x, in_y):
    def own_sums(near, got, from_z, in_x, in_y, out, kept):
        kept[...] = three(near, got, from_z, 0, 0, 0) + in_x[0].astype(f32) + in_y[0].astype(f32)
        out[...] = (three(near, got, from_z, 0, 0, 1) + in_x[1].astype(f32) + in_y[1].astype(f32)).astype(bf16)

    shape = near.shape[2:]
    return glue(own_sums, [like(shape, bf16), like(shape)], near, got, from_z, in_x, in_y)


def attn_shard(qkv_weight, out_weight):
    _, rows, cols = qkv_weight.shape

    def attn_weights(qkv, out_weight, out):
        for j in range(3):
            out[:, j * cols : (j + 1) * cols] = qkv[j].astype(bf16)
        out[:, 3 * cols :] = out_weight[...].T.astype(bf16)

    return glue(attn_weights, [like((rows, 4 * cols), bf16)], qkv_weight, out_weight)[0]


def assemble(plan, bufs, dst, dp):
    for buf, lane, first, k, y in plan:
        src, to = bufs[buf], lane - first
        if k is None:
            dst[to] = src[0]
            continue
        rows = src.shape[1]

        def move(i, carry):
            z = k + i
            place = 4 * (z & 1) + 2 * (z >> 1) + y
            dst[to, pl.ds(pl.multiple_of((dp ^ place) * rows, rows), rows)] = src[i]
            return carry

        lax.fori_loop(0, src.shape[0], move, 0)


def row(vec):
    return vec[...].reshape(1, -1)


def row_stats(summed):
    centered = summed - jnp.mean(summed, axis=-1, keepdims=True)
    inv = lax.rsqrt(jnp.mean(centered * centered, axis=-1, keepdims=True) + epsilon)
    return centered * inv, inv


def norm_backward(scaled, normed, inv):
    row_mean = jnp.mean(scaled, axis=-1, keepdims=True)
    row_cross = jnp.mean(scaled * normed, axis=-1, keepdims=True)
    return inv * (scaled - row_mean - normed * row_cross)


def col_sum(values):
    return jnp.sum(values, axis=0, keepdims=True)


def top_of(values):
    return jnp.full((1, 128), jnp.max(jnp.abs(values)), f32)


def fill_mask(mask, longs, shorts):
    per_block = LONG_LEN // SHORT_LEN
    block = lax.axis_index("tensor")
    n_long = longs.shape[0]
    is_long = block < n_long
    whole = longs[jnp.minimum(block, n_long - 1)]
    first = jnp.maximum(block - n_long, 0) * per_block
    shift = jnp.where(is_long, LONG_LEN.bit_length() - 1, SHORT_LEN.bit_length() - 1)
    size = jnp.where(is_long, LONG_LEN, SHORT_LEN)
    k_pos = lax.broadcasted_iota(jnp.int32, (LONG_LEN, 1), 0)
    q_pos = lax.broadcasted_iota(jnp.int32, (1, LONG_LEN), 1)
    k_seg = lax.shift_right_logical(k_pos, jnp.full_like(k_pos, shift))
    q_seg = lax.shift_right_logical(q_pos, jnp.full_like(q_pos, shift))
    limit = jnp.zeros_like(k_pos)
    for j in range(per_block):
        limit = jnp.where(k_seg == j, jnp.where(is_long, whole, shorts[first + j]), limit)
    k_seg = jnp.where(k_pos - k_seg * size < limit, k_seg, -1)
    mask[...] = jnp.where(k_seg == q_seg, 0.0, NEG)


def attn_forward(net, plan, nb, dims, lim, longs, shorts, tokens, bias, *rest):
    blocks, cols, width = dims
    bufs, rest = rest[:nb], rest[nb:]
    qkv_out, lse_out, in_t, ctx_low, ctx_slope, top_out, weight, in_low, mask, ctx_t, top_ctx = rest
    heads = cols // HEAD_DIM
    low_q = 3 * cols + HEAD_DIM
    assemble(plan, bufs, weight, net.me()[0])
    inputs = tokens[...].astype(f32)
    in_low[...] = jnp.clip(inputs, -lim[0], lim[0]).astype(bf16)
    in_t[...] = in_low[...].T
    top_out[0:1, :] = top_of(inputs)
    fill_mask(mask, longs, shorts)
    ctx_t[0:HEAD_DIM, :] = jnp.zeros((HEAD_DIM, ctx_t.shape[1]), f32)
    top_ctx[...] = jnp.zeros_like(top_ctx)
    inv_limit = 1.0 / jnp.full((1, 1), lim[1], f32)

    def each(lane, carry):
        qkv = (mm(in_low[...], weight[lane, :, :low_q]) + bias[lane, :, :low_q]).astype(bf16)
        qkv_out[lane] = qkv
        for h in range(heads):
            at = h * HEAD_DIM
            q = qkv[:, at : at + HEAD_DIM]
            k = qkv[:, cols + at : cols + at + HEAD_DIM]
            v = qkv[:, 2 * cols + at : 2 * cols + at + HEAD_DIM]
            scores = mm_nt(k, q) * score_scale + mask[...]
            peak = jnp.max(scores, axis=0, keepdims=True)
            grown = jnp.exp(scores - peak)
            total = jnp.sum(grown, axis=0, keepdims=True)
            lse_out[lane, h : h + 1, :] = peak + jnp.log(total)
            shares = (grown * (1.0 / total)).astype(bf16)
            ctx_t[HEAD_DIM + at : 2 * HEAD_DIM + at, :] = mm_tn(v, shares)
        context = ctx_t[...].T
        bent = jnp.tanh(context * inv_limit)
        ctx_low[lane] = (lim[1] * bent).astype(bf16)
        ctx_slope[lane] = 1.0 - bent * bent
        top_ctx[...] = jnp.maximum(top_ctx[...], jnp.max(jnp.abs(context).reshape(-1, 8, context.shape[1]), axis=0))
        return carry

    lax.fori_loop(0, blocks, each, 0)
    top_out[1:2, :] = top_of(top_ctx[...])


def attn_finish(dims, lim, ctx_low, tokens, out_bias, gain, shift, weight, *outs):
    blocks, cols, width = dims
    normed_out, inv_out, middle_out, mid_slope, mid_low, mid_t, top_out, acc = outs
    at = 3 * cols - HEAD_DIM
    acc[...] = tokens[...].astype(f32) + row(out_bias)

    def each(lane, carry):
        acc[...] += mm_nt(ctx_low[lane], weight[lane, :, at:])
        return carry

    lax.fori_loop(0, blocks, each, 0)
    normed, inv = row_stats(acc[...])
    normed_out[...] = normed
    inv_out[...] = inv
    middle = normed * row(gain) + row(shift)
    middle_out[...] = middle
    bent = jnp.tanh(middle * (1.0 / jnp.full((1, 1), lim[2], f32)))
    low = (lim[2] * bent).astype(bf16)
    mid_low[...] = low
    mid_slope[...] = 1.0 - bent * bent
    mid_t[...] = low.T
    top_out[...] = jnp.broadcast_to(top_of(middle), top_out.shape)


def up_forward(net, plan, nb, first, low_q, lim, mid_low, bias, *rest):
    bufs, rest = rest[:nb], rest[nb:]
    act_out, slope_out, top_out, weight, top_hid = rest
    assemble(plan, bufs, weight, net.me()[0])
    top_hid[...] = jnp.zeros_like(top_hid)
    inv_limit = 1.0 / jnp.full((1, 1), lim[3], f32)

    def each(lane, carry):
        up = mm(mid_low[...], weight[lane]) + bias[first + lane, :, low_q:]
        half = 0.5 * (1.0 + lax.erf(up * root_half))
        hidden = up * half
        top_hid[...] = jnp.maximum(top_hid[...], jnp.max(jnp.abs(hidden).reshape(-1, 8, hidden.shape[1]), axis=0))
        bent = jnp.tanh(hidden * inv_limit)
        act_out[lane] = (lim[3] * bent).astype(bf16)
        slope_out[lane] = (1.0 - bent * bent) * (half + up * jnp.exp(-0.5 * up * up) * density_scale)
        return carry

    lax.fori_loop(0, weight.shape[0], each, 0)
    top_out[...] = jnp.broadcast_to(top_of(top_hid[...]), top_out.shape)


def down_both(net, plan, nb, act0, act1, slope0, slope1, middle, cotangent, down_bias, gain, shift, *rest):
    bufs, rest = rest[:nb], rest[nb:]
    layer_out, grad_out, ffn_t, sums, grad_up, up_sums, weight, acc, ffn_low = rest
    assemble(plan, bufs, weight, net.me()[0])
    acc[...] = middle[...] + row(down_bias)
    half = act0.shape[0]
    for act, first in ((act0, 0), (act1, half)):

        def each(i, carry):
            acc[...] += mm_nt(act[i], weight[first + i])
            return carry

        lax.fori_loop(0, half, each, 0)
    normed, inv = row_stats(acc[...])
    layer_out[...] = (normed * row(gain) + row(shift)).astype(bf16)
    incoming = cotangent[...].astype(f32)
    grad = norm_backward(incoming * row(gain), normed, inv)
    grad_out[...] = grad
    ffn_low[...] = grad.astype(bf16)
    ffn_t[...] = ffn_low[...].T
    sums[...] = jnp.zeros_like(sums)
    sums[0:1, :] = col_sum(grad)
    sums[1:2, :] = col_sum(incoming * normed)
    sums[2:3, :] = col_sum(incoming)
    lane_me = net.me()[1]
    for slope, first in ((slope0, 0), (slope1, half)):

        def back(i, carry):
            low = (mm(ffn_low[...], weight[first + i]) * slope[i]).astype(bf16)
            grad_up[first + i] = low
            up_sums[(first + i) ^ lane_me] = col_sum(low.astype(f32))
            return carry

        lax.fori_loop(0, half, back, 0)


def weight_grad(net, left_t, *rest):
    *rights, far, near = rest
    rows = left_t.shape[0] // net.parts
    dp = net.me()[0]
    half = far.shape[0]
    for x in range(half):
        for out, lane in ((far, 2 * x + 1), (near, 2 * x)):
            right = rights[lane // rights[0].shape[0]]
            grad = mm(left_t[...], right[lane % right.shape[0]]).astype(bf16)
            for block in range(net.parts):
                out[x, net.slot(block, dp)] = grad[block * rows : (block + 1) * rows]


def mid_backward(dims, grad_up, grad_second, mid_slope, normed, inv, gain, ctx_slope, weight0, weight1, out_weight, *outs):
    blocks, cols, width = dims
    grad_out, attn_t, grad_ctx, sums, acc, attn_low = outs
    at = 3 * cols - HEAD_DIM
    acc[...] = jnp.zeros_like(acc)
    half = weight0.shape[0]
    for weight, first in ((weight0, 0), (weight1, half)):

        def each(i, carry):
            acc[...] += mm_nt(grad_up[first + i], weight[i])
            return carry

        lax.fori_loop(0, half, each, 0)
    incoming = grad_second[...] + acc[...] * mid_slope[...]
    grad = norm_backward(incoming * row(gain), normed[...], inv[...])
    grad_out[...] = grad
    attn_low[...] = grad.astype(bf16)
    attn_t[...] = attn_low[...].T
    sums[...] = jnp.zeros_like(sums)
    sums[0:1, :] = col_sum(grad)
    sums[1:2, :] = col_sum(incoming * normed[...])
    sums[2:3, :] = col_sum(incoming)

    def spread(lane, carry):
        grad_ctx[lane] = (mm(attn_low[...], out_weight[lane, :, at:]) * ctx_slope[lane]).astype(bf16)
        return carry

    lax.fori_loop(0, blocks, spread, 0)


def attn_backward(net, dims, longs, shorts, qkv, lse, grad_ctx, in_t, attn_t, ctx_low, *rest):
    blocks, cols, width = dims
    up_sums, sums_a, sums_b, tops_a, tops_m, top0, top1, out, far, near, packed, sums, mask = rest
    heads = cols // HEAD_DIM
    rows = in_t.shape[0] // net.parts
    start = 3 * cols - HEAD_DIM
    end = 3 * cols + HEAD_DIM
    fill_mask(mask, longs, shorts)
    dp, lane_me = net.me()

    def each(lane, carry):
        for h in range(heads):
            at = h * HEAD_DIM
            q = qkv[lane, :, at : at + HEAD_DIM]
            k = qkv[lane, :, cols + at : cols + at + HEAD_DIM]
            v = qkv[lane, :, 2 * cols + at : 2 * cols + at + HEAD_DIM]
            grad = grad_ctx[lane, :, HEAD_DIM + at : 2 * HEAD_DIM + at]
            shares = jnp.exp(mm_nt(k, q) * score_scale + mask[...] - lse[lane, h : h + 1, :])
            grad_shares = mm_nt(v, grad)
            inner = jnp.sum(shares * grad_shares, axis=0, keepdims=True)
            grad_scores = (shares * (grad_shares - inner)).astype(bf16)
            grad_v = mm(shares.astype(bf16), grad)
            grad_k = mm(grad_scores, q) * score_scale
            grad_q = (mm_tn(k, grad_scores) * score_scale).T
            out[lane, :, at : at + HEAD_DIM] = grad_q.astype(bf16)
            out[lane, :, cols + at : cols + at + HEAD_DIM] = grad_k.astype(bf16)
            out[lane, :, 2 * cols + at : 2 * cols + at + HEAD_DIM] = grad_v.astype(bf16)
        out[lane, :, 3 * cols :] = jnp.zeros((out.shape[1], HEAD_DIM), bf16)
        sums[lane ^ lane_me] = col_sum(out[lane].astype(f32))
        return carry

    lax.fori_loop(0, blocks, each, 0)

    def weights(x, carry):
        for core, to in ((1, far), (0, near)):
            left = mm(in_t[...], out[2 * x + core])
            right = mm(attn_t[...], ctx_low[2 * x + core])
            mixed = (left[:, start:] + right[:, : end - start]).astype(bf16)
            for block in range(net.parts):
                rs = slice(block * rows, (block + 1) * rows)
                place = net.slot(block, dp)
                to[x, place, :, :start] = left[rs, :start].astype(bf16)
                to[x, place, :, start:end] = mixed[rs]
                to[x, place, :, end:] = right[rs, end - start :].astype(bf16)
        return carry

    lax.fori_loop(0, far.shape[0], weights, 0)
    packed[...] = jnp.zeros_like(packed)
    for j in range(blocks):
        packed[j : j + 1, :] = up_sums[j]
        packed[blocks + j : blocks + j + 1, : sums.shape[2]] = sums[j]
    packed[2 * blocks : 2 * blocks + 3, :] = sums_a[0:3, :]
    packed[2 * blocks + 3 : 2 * blocks + 6, :] = sums_b[0:3, :]
    tops = (tops_a[0:1, :], tops_a[1:2, :], tops_m[0:1, :], jnp.maximum(top0[0:1, :], top1[0:1, :]))
    for j, top in enumerate(tops):
        packed[2 * blocks + 6 : 2 * blocks + 7, 128 * j : 128 * j + 128] = top


def token_backward(dims, lim, grad_qkv, grad_first, tokens, weight, out, acc):
    blocks, cols, width = dims
    acc[...] = jnp.zeros_like(acc)

    def each(lane, carry):
        acc[...] += mm_nt(grad_qkv[lane], weight[lane, :, : 3 * cols + HEAD_DIM])
        return carry

    lax.fori_loop(0, blocks, each, 0)
    inputs = tokens[...].astype(f32)
    out[...] = (grad_first[...] + jnp.where(jnp.abs(inputs) <= lim[0], acc[...], 0.0)).astype(bf16)


def make_body(net):
    def body(
        tokens,
        cotangent,
        qkv_weight,
        qv_bias,
        out_weight,
        out_bias,
        first_gain,
        first_shift,
        up_weight,
        up_bias,
        down_weight,
        down_bias,
        second_gain,
        second_shift,
        act_ranges,
        long_lengths,
        short_lengths,
    ):
        lane = lax.axis_index("tensor")
        rows, width = tokens.shape
        assert rows == LONG_LEN
        cols = qkv_weight.shape[2]
        up_cols = up_weight.shape[1]
        blocks = lax.axis_size("tensor")
        half = blocks // 2
        dims = (blocks, cols, width)
        wide = 3 * cols + HEAD_DIM
        out_cols = cols + HEAD_DIM
        every = tuple(range(blocks))

        pieces_a, pieces_u, pieces_d = Pieces([]), Pieces([]), Pieces([])
        shard_a = attn_shard(qkv_weight, out_weight)
        job_a = Job(net.gather(shard_a, pieces_a))
        bias_row = jnp.concatenate(
            [qv_bias[0], jnp.zeros((cols,), f32), qv_bias[1], jnp.zeros((HEAD_DIM,), f32), up_bias]
        )
        job_b = Job(net.gather_lane(bias_row[None]))
        job_u = Job(net.gather(up_weight.astype(bf16), pieces_u))
        job_d = Job(net.gather(down_weight.T.astype(bf16), pieces_d, True))

        def vmem(*shape, dtype=f32):
            return pltpu.VMEM(shape, dtype)

        unit = 2 * rows * width * width * blocks
        moved = 2 * width * width * blocks

        step((), None, [job_a, job_b], [job_a, job_b])
        step((), None, [job_a, job_b], [job_a, job_b])
        step((), None, [job_a, job_u, job_d], [job_a, job_u, job_d])
        step((), None, [job_a, job_u], [job_a, job_u])
        step((), None, [job_u, job_a], [job_a])
        biases = job_b.value

        bufs, plan = pieces_a.part(every)
        qkv, lse, in_t, ctx_low, ctx_slope, tops_a, weight_a = step(
            (act_ranges, long_lengths, short_lengths, tokens, biases, *bufs),
            call(
                functools.partial(attn_forward, net, plan, len(bufs), dims),
                "attn_forward",
                [SM] * 3 + [VM] * 2 + [VM] * len(bufs),
                [
                    like((blocks, rows, wide), bf16),
                    like((blocks, 8, rows)),
                    like((width, rows), bf16),
                    like((blocks, rows, out_cols), bf16),
                    like((blocks, rows, out_cols)),
                    like((8, 128)),
                    like((blocks, width, 4 * cols), bf16),
                ],
                [vmem(rows, width, dtype=bf16), vmem(rows, rows), vmem(out_cols, rows), vmem(8, out_cols)],
                4 * unit,
                3 * moved,
            ),
            [],
            [job_u],
        )
        normed, inv, middle, mid_slope, mid_low, mid_t, tops_m = step(
            (act_ranges, ctx_low, tokens, out_bias, first_gain, first_shift, weight_a),
            call(
                functools.partial(attn_finish, dims),
                "attn_finish",
                [SM] + [VM] * 6,
                [
                    like((rows, width)),
                    like((rows, 1)),
                    like((rows, width)),
                    like((rows, width)),
                    like((rows, width), bf16),
                    like((width, rows), bf16),
                    like((8, 128)),
                ],
                [vmem(rows, width)],
                2 * unit,
                2 * moved,
            ),
            [job_u, job_d],
            [job_u, job_d],
        )

        def up_part(lanes, start, finish):
            bufs, plan = pieces_u.part(lanes)
            return step(
                (act_ranges, mid_low, biases, *bufs),
                call(
                    functools.partial(up_forward, net, plan, len(bufs), lanes[0], wide),
                    f"up_forward_{lanes[0]}",
                    [SM] + [VM] * 2 + [VM] * len(bufs),
                    [
                        like((half, rows, up_cols), bf16),
                        like((half, rows, up_cols)),
                        like((8, 128)),
                        like((half, width, up_cols), bf16),
                    ],
                    [vmem(8, up_cols)],
                    2 * unit,
                    2 * moved,
                ),
                start,
                finish,
            )

        act0, slope0, top0, weight_u0 = up_part(every[:half], [job_u, job_d], [job_u])
        act1, slope1, top1, weight_u1 = up_part(every[half:], [], [job_d])
        step((), None, [job_d], [job_d])
        step((), None, [job_d], [job_d])
        bufs_d, plan_d = pieces_d.part(every)
        layer_out, grad_second, ffn_t, sums_b, grad_up, up_sums = step(
            (act0, act1, slope0, slope1, middle, cotangent, down_bias, second_gain, second_shift, *bufs_d),
            call(
                functools.partial(down_both, net, plan_d, len(bufs_d)),
                "down_both",
                [VM] * 9 + [VM] * len(bufs_d),
                [
                    like((rows, width), bf16),
                    like((rows, width)),
                    like((width, rows), bf16),
                    like((8, width)),
                    like((blocks, rows, up_cols), bf16),
                    like((blocks, 1, up_cols)),
                ],
                [
                    vmem(blocks, width, up_cols, dtype=bf16),
                    vmem(rows, width),
                    vmem(rows, width, dtype=bf16),
                ],
                2 * unit,
                4 * moved,
            ),
        )

        grad_shape = like((net.parts, width // net.parts, up_cols), bf16)
        both_shape = like((half,) + grad_shape.shape, bf16)

        def grad_of(name, left_t, rights, start=(), finish=()):
            return step(
                (left_t, *rights),
                call(
                    functools.partial(weight_grad, net),
                    name,
                    [VM] * (1 + len(rights)),
                    [both_shape, both_shape],
                    (),
                    unit,
                    moved,
                ),
                start,
                finish,
            )

        sum_d = Job(net.scatter_z_first(*grad_of("down_grad", ffn_t, (act0, act1))))
        sum_u = Job(net.scatter_sum(*grad_of("up_grad", mid_t, (grad_up,), [sum_d], [sum_d])))
        step((), None, [sum_u, sum_d], [sum_u])
        grad_first, attn_t, grad_ctx, sums_a = step(
            (grad_up, grad_second, mid_slope, normed, inv, first_gain, ctx_slope, weight_u0, weight_u1, weight_a),
            call(
                functools.partial(mid_backward, dims),
                "mid_backward",
                [VM] * 10,
                [
                    like((rows, width)),
                    like((width, rows), bf16),
                    like((blocks, rows, out_cols), bf16),
                    like((8, width)),
                ],
                [vmem(rows, width), vmem(rows, width, dtype=bf16)],
                unit + unit // 3,
                3 * moved,
            ),
            [sum_u],
            [sum_u],
        )

        grad_qkv, far, near, packed = step(
            (long_lengths, short_lengths, qkv, lse, grad_ctx, in_t, attn_t, ctx_low)
            + (up_sums, sums_a, sums_b, tops_a, tops_m, top0, top1),
            call(
                functools.partial(attn_backward, net, dims),
                "attn_backward",
                [SM] * 2 + [VM] * 13,
                [like((blocks, rows, wide), bf16), both_shape, both_shape, like((16, width))],
                [vmem(blocks, 1, wide), vmem(rows, rows)],
                4 * unit,
                2 * moved,
            ),
            [sum_u],
            [sum_u, sum_d],
        )
        sum_a = Job(net.scatter_sum(far, near))
        is_top = (jnp.arange(packed.shape[0]) == 2 * blocks + 6)[:, None]
        sum_s = Job(net.sum_max(packed, is_top))
        line_u = Job(net.scatter_line(*sum_u.value))
        tokens_grad = step(
            (act_ranges, grad_qkv, grad_first, tokens, weight_a),
            call(
                functools.partial(token_backward, dims),
                "token_backward",
                [SM] + [VM] * 4,
                [like((rows, width), bf16)],
                [vmem(rows, width)],
                unit,
                2 * moved,
            ),
            [sum_a, sum_d, line_u],
            [sum_a, sum_d],
        )[0]
        step((), None, [sum_a, sum_d], [sum_a, sum_d, line_u])
        step((), None, [sum_a, line_u, sum_d, sum_s], [line_u, sum_d, sum_s])
        step((), None, [sum_s], [sum_a, sum_s])
        line_a = Job(net.scatter_line(*sum_a.value))
        step((), None, [line_a, sum_s], [sum_s])
        step((), None, [sum_s], [line_a, sum_s])
        step((), None, [line_a, sum_s], [line_a, sum_s])

        down_grad, up_grad, a_grad, packed = sum_d.value, line_u.value, line_a.value, sum_s.value
        down_grad = down_grad.T
        qkv_grad = jnp.stack([a_grad[:, j * cols : (j + 1) * cols] for j in range(3)])
        out_grad = a_grad[:, 3 * cols :].T
        own = lax.dynamic_slice_in_dim(packed, blocks + lane, 1)
        shared = packed[2 * blocks : 2 * blocks + 6]
        qv_bias_grad = jnp.concatenate([own[:, :cols], own[:, 2 * cols : 3 * cols]], 0)
        up_bias_grad = lax.dynamic_slice_in_dim(packed, lane, 1)[0]
        new_ranges = ema_decay * act_ranges + (1.0 - ema_decay) * packed[2 * blocks + 6, 0:512:128]
        return (
            layer_out,
            tokens_grad,
            qkv_grad,
            qv_bias_grad,
            out_grad,
            shared[0],
            shared[1],
            shared[2],
            up_grad,
            up_bias_grad,
            down_grad,
            shared[3],
            shared[4],
            shared[5],
            new_ranges,
        )

    return body


def solution(mesh):
    in_specs = (
        P(ALL, None),
        P(ALL, None),
        P(None, "dp", "tensor"),
        P(None, "tensor"),
        P("tensor", "dp"),
        P(),
        P(),
        P(),
        P("dp", "tensor"),
        P("tensor"),
        P("tensor", "dp"),
        P(),
        P(),
        P(),
        P(),
        P("dp"),
        P("dp"),
    )
    out_specs = (
        P(ALL, None),
        P(ALL, None),
        P(None, "dp", "tensor"),
        P(None, "tensor"),
        P("tensor", "dp"),
        P(),
        P(),
        P(),
        P("dp", "tensor"),
        P("tensor"),
        P("tensor", "dp"),
        P(),
        P(),
        P(),
        P(),
    )
    net = Grid() if mesh.shape["dp"] == 8 and mesh.shape["tensor"] == 4 else Plain()
    return jax.shard_map(make_body(net), mesh=mesh, in_specs=in_specs, out_specs=out_specs, check_vma=False)
```

```python
import functools
import itertools

import jax
import jax.numpy as jnp
from jax import lax
from jax.experimental import pallas as pl
from jax.experimental.pallas import tpu as pltpu
from jax.sharding import PartitionSpec as P

HEAD_DIM = 64
LONG_LEN = 512
SHORT_LEN = 128
ALL = ("dp", "tensor")

ema_decay = 0.9
epsilon = 1e-06
root_half = 0.7071067811865476
density_scale = 0.3989422804014327
score_scale = HEAD_DIM ** (-0.5)
NEG = -1000000000.0

f32 = jnp.float32
bf16 = jnp.bfloat16


def mm(left, right):
    return jnp.dot(left, right, preferred_element_type=f32)


def mm_tn(left, right):
    return lax.dot_general(left, right, (((0,), (0,)), ((), ())), preferred_element_type=f32)


def mm_nt(left, right):
    return lax.dot_general(left, right, (((1,), (1,)), ((), ())), preferred_element_type=f32)


def _lin(z, y, x, c):
    return (z * 2 + y) * 4 + x * 2 + c


def _perm(fn):
    out = []
    for z, y, x, c in itertools.product(range(4), range(2), range(2), range(2)):
        out.append((_lin(z, y, x, c), _lin(*fn(z, y, x, c))))
    return out


PC = _perm(lambda z, y, x, c: (z, y, x, 1 - c))
PX = _perm(lambda z, y, x, c: (z, y, 1 - x, c))
PY = _perm(lambda z, y, x, c: (z, 1 - y, x, c))
PZ1 = _perm(lambda z, y, x, c: (z ^ 1, y, x, c))
PZ2 = _perm(lambda z, y, x, c: (z ^ 2, y, x, c))


def tie(*trees):
    leaves, spec = jax.tree.flatten(trees)
    return jax.tree.unflatten(spec, lax.optimization_barrier(leaves))


class Job:
    def __init__(self, stages):
        self.stages, self.value, self.out, self.flight, self.over = stages, None, [], [], False
        self.take(None)

    def take(self, got):
        if not self.over:
            try:
                self.out = self.stages.send(got)
            except StopIteration as stop:
                self.value, self.out, self.over = stop.value, [], True


def step(ins, run=None, start=(), finish=()):
    ins, sends = tie(ins, [[value for value, _ in job.out] for job in start])
    for job, values in zip(start, sends):
        job.flight = [lax.ppermute(v, ALL, perm) for v, (_, perm) in zip(values, job.out)]
    outs = run(*ins) if run else ins
    outs, got = tie(outs, [job.flight for job in finish])
    for job, values in zip(finish, got):
        job.flight = []
        job.take(values)
    return outs


class Pieces:
    def __init__(self, plan):
        self.bufs, self.plan = {}, plan

    def part(self, lanes):
        plan = [p for p in self.plan if p[1] in lanes]
        names = sorted({p[0] for p in plan})
        return [self.bufs[n] for n in names], [(names.index(b), lane, lanes[0], k, y) for b, lane, k, y in plan]


class Grid:
    parts = 8

    @staticmethod
    def gather(shard, pieces, line_later=False):
        own = shard[None]
        for base, lane in ((0, 0), (5, 1)):
            pieces.plan.append((base, lane, 0, 0))
            pieces.plan.append((base + 1, lane, 0, 1))
            pieces.plan.append((base + 2, lane + 2, 0, 0))
            pieces.plan.append((base + 3, lane + 2, 0, 1))
            pieces.plan.append((base + 4, lane + 2, 2, 1))
        (far_z,) = yield [(own, PZ2)]
        pair = jnp.concatenate([own, far_z], 0)
        (near_z,) = yield [(pair, PZ1)]
        line = jnp.concatenate([pair, near_z], 0)
        to_core = [(line, PC)]
        now, later = ([], to_core) if line_later else (to_core, [])
        over_x, over_y, *rest = yield [(line, PX), (line, PY)] + now
        diag_x, diag_y, over_y_far, *more = yield [(over_y[:2], PX), (over_x[2:], PY), (over_y, PC)] + later
        (line_far,) = rest + more
        pieces.bufs.update({0: line, 1: over_y, 2: over_x, 3: diag_x, 4: diag_y, 5: line_far, 6: over_y_far})
        over_x_far, diag_x_far, diag_y_far = yield [(over_x, PC), (diag_x, PC), (diag_y, PC)]
        pieces.bufs.update({7: over_x_far, 8: diag_x_far, 9: diag_y_far})

    @staticmethod
    def slot(block, dp):
        place = block ^ dp
        return (place & 1) * 4 + (place & 2) + (place >> 2)

    @staticmethod
    def scatter_sum(far, near):
        (got,) = yield [(far, PC)]
        out_x, out_y = add_first(near, got)
        from_x, from_y = yield [(out_x, PX), (out_y, PY)]
        out_x, out_y = add_second(near, got, from_x, from_y)
        in_x, in_y = yield [(out_x, PX), (out_y, PY)]
        return near, got, in_x, in_y

    @staticmethod
    def scatter_line(near, got, in_x, in_y):
        out_z, kept = add_third(near, got, in_x, in_y)
        (from_z,) = yield [(out_z, PZ1)]
        out_z, kept = add_fourth(kept, from_z)
        (last,) = yield [(out_z, PZ2)]
        return kept + last.astype(f32)

    @staticmethod
    def scatter_z_first(far, near):
        (got,) = yield [(far, PC)]
        out_1, out_0 = add_near_z(near, got)
        (from_1,) = yield [(out_1, PZ1)]
        out_x, out_y = add_corner(near, got, from_1)
        from_x, from_y, from_0 = yield [(out_x, PX), (out_y, PY), (out_0, PZ1)]
        out_x, out_y = add_sides(near, got, from_1, from_0, from_x, from_y)
        in_x, in_y = yield [(out_x, PX), (out_y, PY)]
        out_z, kept = add_own(near, got, from_0, in_x, in_y)
        (last,) = yield [(out_z, PZ2)]
        return kept + last.astype(f32)

    @staticmethod
    def gather_lane(vec):
        (other,) = yield [(vec, PX)]
        pair = jnp.stack([vec, other])
        (more,) = yield [(pair, PC)]
        return jnp.stack([pair, more], 1).reshape((4,) + vec.shape)

    @staticmethod
    def sum_max(both, is_top):
        for perm in (PZ2, PZ1, PC, PX, PY):
            (other,) = yield [(both, perm)]
            both = jnp.where(is_top, jnp.maximum(both, other), both + other)
        return both

    @staticmethod
    def me():
        return lax.axis_index("dp"), lax.axis_index("tensor")


class Plain:
    parts = 1

    @staticmethod
    def gather(shard, pieces, line_later=False):
        rows = lax.all_gather(shard, "dp", axis=0, tiled=True)
        full = lax.all_gather(rows, "tensor", axis=0)
        for k in range(full.shape[0]):
            pieces.plan.append((k, k, None, None))
            pieces.bufs[k] = full[k][None]
        return
        yield

    @staticmethod
    def slot(block, dp):
        return block

    @staticmethod
    def scatter_sum(far, near):
        grads = jnp.stack([near[0], far[0], near[1], far[1]]).astype(f32)
        return (grads.reshape((4, -1, grads.shape[-1])),)
        yield

    @staticmethod
    def scatter_line(grads):
        own = lax.psum_scatter(grads, "tensor", scatter_dimension=0, tiled=False)
        return lax.psum_scatter(own, "dp", scatter_dimension=0, tiled=True)
        yield

    @staticmethod
    def scatter_z_first(far, near):
        grads = yield from Plain.scatter_sum(far, near)
        return (yield from Plain.scatter_line(*grads))

    @staticmethod
    def gather_lane(vec):
        return lax.all_gather(vec, "tensor", axis=0)
        yield

    @staticmethod
    def sum_max(both, is_top):
        return jnp.where(is_top, lax.pmax(both, ALL), lax.psum(both, ALL))
        yield

    @staticmethod
    def me():
        return 0, 0


VM = pl.BlockSpec(memory_space=pltpu.VMEM)
SM = pl.BlockSpec(memory_space=pltpu.SMEM)
VMEM_MIB = 14


def like(shape, dtype=f32):
    return jax.ShapeDtypeStruct(shape, dtype)


def call(kernel, name, specs, outs, scratch=(), flops=0, moved=0):
    return pl.pallas_call(
        kernel,
        name=name,
        out_shape=outs,
        in_specs=specs,
        out_specs=[VM] * len(outs),
        scratch_shapes=list(scratch),
        compiler_params=pltpu.CompilerParams(vmem_limit_bytes=VMEM_MIB * 2**20),
        cost_estimate=pl.CostEstimate(flops=flops, bytes_accessed=moved, transcendentals=0),
    )


def glue(kernel, outs, *ins):
    return call(kernel, kernel.__name__, [VM] * len(ins), outs)(*ins)


def add_first(near, got):
    def first_sums(near, got, out_x, out_y):
        for k in range(2):
            out_x[k] = (near[1, 4 + k].astype(f32) + got[1, 4 + k].astype(f32)).astype(bf16)
            out_y[k] = (near[1, 6 + k].astype(f32) + got[1, 6 + k].astype(f32)).astype(bf16)

    part = like((2,) + near.shape[2:], bf16)
    return glue(first_sums, [part, part], near, got)


def add_second(near, got, from_x, from_y):
    def second_sums(near, got, from_x, from_y, out_x, out_y):
        for k in range(4):
            over_x = near[1, k].astype(f32) + got[1, k].astype(f32)
            over_y = near[0, 4 + k].astype(f32) + got[0, 4 + k].astype(f32)
            if k < 2:
                over_y = over_y + from_x[k].astype(f32)
            else:
                over_x = over_x + from_y[k - 2].astype(f32)
            out_x[k] = over_x.astype(bf16)
            out_y[k] = over_y.astype(bf16)

    part = like((4,) + near.shape[2:], bf16)
    return glue(second_sums, [part, part], near, got, from_x, from_y)


def add_third(near, got, in_x, in_y):
    def third_sums(near, got, in_x, in_y, out, kept):
        for k in range(4):
            total = near[0, k].astype(f32) + got[0, k].astype(f32) + in_x[k].astype(f32) + in_y[k].astype(f32)
            if k < 2:
                kept[k] = total
            else:
                out[k - 2] = total.astype(bf16)

    shape = (2,) + near.shape[2:]
    return glue(third_sums, [like(shape, bf16), like(shape)], near, got, in_x, in_y)


def add_fourth(kept, from_z):
    def fourth_sums(kept, from_z, out, mine):
        mine[...] = kept[0] + from_z[0].astype(f32)
        out[...] = (kept[1] + from_z[1].astype(f32)).astype(bf16)

    shape = kept.shape[1:]
    return glue(fourth_sums, [like(shape, bf16), like(shape)], kept, from_z)


def add_near_z(near, got):
    def near_z_sums(near, got, out_1, out_0):
        for x, out in ((1, out_1), (0, out_0)):
            for y in range(2):
                for k in range(2):
                    at = 4 * y + 2 + k
                    out[2 * y + k] = (near[x, at].astype(f32) + got[x, at].astype(f32)).astype(bf16)

    part = like((4,) + near.shape[2:], bf16)
    return glue(near_z_sums, [part, part], near, got)


def three(near, got, from_z, x, y, k):
    return near[x, 4 * y + k].astype(f32) + got[x, 4 * y + k].astype(f32) + from_z[2 * y + k].astype(f32)


def add_corner(near, got, from_1):
    def corner_sums(near, got, from_1, out_x, out_y):
        out_x[...] = three(near, got, from_1, 1, 1, 0).astype(bf16)
        out_y[...] = three(near, got, from_1, 1, 1, 1).astype(bf16)

    part = like(near.shape[2:], bf16)
    return glue(corner_sums, [part, part], near, got, from_1)


def add_sides(near, got, from_1, from_0, from_x, from_y):
    def side_sums(near, got, from_1, from_0, from_x, from_y, out_x, out_y):
        out_x[0] = three(near, got, from_1, 1, 0, 0).astype(bf16)
        out_x[1] = (three(near, got, from_1, 1, 0, 1) + from_y[...].astype(f32)).astype(bf16)
        out_y[0] = (three(near, got, from_0, 0, 1, 0) + from_x[...].astype(f32)).astype(bf16)
        out_y[1] = three(near, got, from_0, 0, 1, 1).astype(bf16)

    part = like((2,) + near.shape[2:], bf16)
    return glue(side_sums, [part, part], near, got, from_1, from_0, from_x, from_y)


def add_own(near, got, from_0, in_x, in_y):
    def own_sums(near, got, from_0, in_x, in_y, out, kept):
        kept[...] = three(near, got, from_0, 0, 0, 0) + in_x[0].astype(f32) + in_y[0].astype(f32)
        out[...] = (three(near, got, from_0, 0, 0, 1) + in_x[1].astype(f32) + in_y[1].astype(f32)).astype(bf16)

    shape = near.shape[2:]
    return glue(own_sums, [like(shape, bf16), like(shape)], near, got, from_0, in_x, in_y)


def attn_shard(qkv_weight, out_weight):
    _, rows, cols = qkv_weight.shape

    def attn_weights(qkv, out_weight, out):
        for j in range(3):
            out[:, j * cols : (j + 1) * cols] = qkv[j].astype(bf16)
        out[:, 3 * cols :] = out_weight[...].T.astype(bf16)

    return glue(attn_weights, [like((rows, 4 * cols), bf16)], qkv_weight, out_weight)[0]


def assemble(plan, bufs, dst, dp):
    for buf, lane, first, k, y in plan:
        src, to = bufs[buf], lane - first
        if k is None:
            dst[to] = src[0]
            continue
        rows = src.shape[1]

        def move(i, carry):
            z = k + i
            place = 4 * (z & 1) + 2 * (z >> 1) + y
            dst[to, pl.ds(pl.multiple_of((dp ^ place) * rows, rows), rows)] = src[i]
            return carry

        lax.fori_loop(0, src.shape[0], move, 0)


def row(vec):
    return vec[...].reshape(1, -1)


def row_stats(summed):
    centered = summed - jnp.mean(summed, axis=-1, keepdims=True)
    inv = lax.rsqrt(jnp.mean(centered * centered, axis=-1, keepdims=True) + epsilon)
    return centered * inv, inv


def norm_backward(scaled, normed, inv):
    row_mean = jnp.mean(scaled, axis=-1, keepdims=True)
    row_cross = jnp.mean(scaled * normed, axis=-1, keepdims=True)
    return inv * (scaled - row_mean - normed * row_cross)


def col_sum(values):
    return jnp.sum(values, axis=0, keepdims=True)


def top_of(values):
    return jnp.full((1, 128), jnp.max(jnp.abs(values)), f32)


def fill_mask(mask, longs, shorts):
    per_block = LONG_LEN // SHORT_LEN
    block = lax.axis_index("tensor")
    n_long = longs.shape[0]
    is_long = block < n_long
    whole = longs[jnp.minimum(block, n_long - 1)]
    first = jnp.maximum(block - n_long, 0) * per_block
    shift = jnp.where(is_long, LONG_LEN.bit_length() - 1, SHORT_LEN.bit_length() - 1)
    size = jnp.where(is_long, LONG_LEN, SHORT_LEN)
    k_pos = lax.broadcasted_iota(jnp.int32, (LONG_LEN, 1), 0)
    q_pos = lax.broadcasted_iota(jnp.int32, (1, LONG_LEN), 1)
    k_seg = lax.shift_right_logical(k_pos, jnp.full_like(k_pos, shift))
    q_seg = lax.shift_right_logical(q_pos, jnp.full_like(q_pos, shift))
    limit = jnp.zeros_like(k_pos)
    for j in range(per_block):
        limit = jnp.where(k_seg == j, jnp.where(is_long, whole, shorts[first + j]), limit)
    k_seg = jnp.where(k_pos - k_seg * size < limit, k_seg, -1)
    mask[...] = jnp.where(k_seg == q_seg, 0.0, NEG)


def attn_forward(net, plan, nb, dims, lim, longs, shorts, tokens, bias, *rest):
    blocks, cols, width = dims
    bufs, rest = rest[:nb], rest[nb:]
    qkv_out, lse_out, in_t, ctx_low, ctx_slope, top_out, weight, in_low, mask, ctx_t, top_ctx = rest
    heads = cols // HEAD_DIM
    low_q = 3 * cols + HEAD_DIM
    assemble(plan, bufs, weight, net.me()[0])
    inputs = tokens[...].astype(f32)
    in_low[...] = jnp.clip(inputs, -lim[0], lim[0]).astype(bf16)
    in_t[...] = in_low[...].T
    top_out[0:1, :] = top_of(inputs)
    fill_mask(mask, longs, shorts)
    ctx_t[0:HEAD_DIM, :] = jnp.zeros((HEAD_DIM, ctx_t.shape[1]), f32)
    top_ctx[...] = jnp.zeros_like(top_ctx)
    inv_limit = 1.0 / jnp.full((1, 1), lim[1], f32)

    def each(lane, carry):
        qkv = (mm(in_low[...], weight[lane, :, :low_q]) + bias[lane, :, :low_q]).astype(bf16)
        qkv_out[lane] = qkv
        for h in range(heads):
            at = h * HEAD_DIM
            q = qkv[:, at : at + HEAD_DIM]
            k = qkv[:, cols + at : cols + at + HEAD_DIM]
            v = qkv[:, 2 * cols + at : 2 * cols + at + HEAD_DIM]
            scores = mm_nt(k, q) * score_scale + mask[...]
            peak = jnp.max(scores, axis=0, keepdims=True)
            grown = jnp.exp(scores - peak)
            total = jnp.sum(grown, axis=0, keepdims=True)
            lse_out[lane, h : h + 1, :] = peak + jnp.log(total)
            shares = (grown * (1.0 / total)).astype(bf16)
            ctx_t[HEAD_DIM + at : 2 * HEAD_DIM + at, :] = mm_tn(v, shares)
        context = ctx_t[...].T
        bent = jnp.tanh(context * inv_limit)
        ctx_low[lane] = (lim[1] * bent).astype(bf16)
        ctx_slope[lane] = 1.0 - bent * bent
        top_ctx[...] = jnp.maximum(top_ctx[...], jnp.max(jnp.abs(context).reshape(-1, 8, context.shape[1]), axis=0))
        return carry

    lax.fori_loop(0, blocks, each, 0)
    top_out[1:2, :] = top_of(top_ctx[...])


def attn_finish(dims, lim, ctx_low, tokens, out_bias, gain, shift, weight, *outs):
    blocks, cols, width = dims
    normed_out, inv_out, middle_out, mid_slope, mid_low, mid_t, top_out, acc = outs
    at = 3 * cols - HEAD_DIM
    acc[...] = tokens[...].astype(f32) + row(out_bias)

    def each(lane, carry):
        acc[...] += mm_nt(ctx_low[lane], weight[lane, :, at:])
        return carry

    lax.fori_loop(0, blocks, each, 0)
    normed, inv = row_stats(acc[...])
    normed_out[...] = normed
    inv_out[...] = inv
    middle = normed * row(gain) + row(shift)
    middle_out[...] = middle
    bent = jnp.tanh(middle * (1.0 / jnp.full((1, 1), lim[2], f32)))
    low = (lim[2] * bent).astype(bf16)
    mid_low[...] = low
    mid_slope[...] = 1.0 - bent * bent
    mid_t[...] = low.T
    top_out[...] = jnp.broadcast_to(top_of(middle), top_out.shape)


def up_forward(net, plan, nb, first, low_q, lim, mid_low, bias, *rest):
    bufs, rest = rest[:nb], rest[nb:]
    act_out, slope_out, top_out, weight, top_hid = rest
    assemble(plan, bufs, weight, net.me()[0])
    top_hid[...] = jnp.zeros_like(top_hid)
    inv_limit = 1.0 / jnp.full((1, 1), lim[3], f32)

    def each(lane, carry):
        up = mm(mid_low[...], weight[lane]) + bias[first + lane, :, low_q:]
        half = 0.5 * (1.0 + lax.erf(up * root_half))
        hidden = up * half
        top_hid[...] = jnp.maximum(top_hid[...], jnp.max(jnp.abs(hidden).reshape(-1, 8, hidden.shape[1]), axis=0))
        bent = jnp.tanh(hidden * inv_limit)
        act_out[lane] = (lim[3] * bent).astype(bf16)
        slope_out[lane] = (1.0 - bent * bent) * (half + up * jnp.exp(-0.5 * up * up) * density_scale)
        return carry

    lax.fori_loop(0, weight.shape[0], each, 0)
    top_out[...] = jnp.broadcast_to(top_of(top_hid[...]), top_out.shape)


def down_both(net, plan, nb, act0, act1, slope0, slope1, middle, cotangent, down_bias, gain, shift, *rest):
    bufs, rest = rest[:nb], rest[nb:]
    layer_out, grad_out, ffn_t, sums, grad_up, up_sums, weight, acc, ffn_low = rest
    assemble(plan, bufs, weight, net.me()[0])
    acc[...] = middle[...] + row(down_bias)
    half = act0.shape[0]
    for act, first in ((act0, 0), (act1, half)):

        def each(i, carry):
            acc[...] += mm_nt(act[i], weight[first + i])
            return carry

        lax.fori_loop(0, half, each, 0)
    normed, inv = row_stats(acc[...])
    layer_out[...] = (normed * row(gain) + row(shift)).astype(bf16)
    incoming = cotangent[...].astype(f32)
    grad = norm_backward(incoming * row(gain), normed, inv)
    grad_out[...] = grad
    ffn_low[...] = grad.astype(bf16)
    ffn_t[...] = ffn_low[...].T
    sums[...] = jnp.zeros_like(sums)
    sums[0:1, :] = col_sum(grad)
    sums[1:2, :] = col_sum(incoming * normed)
    sums[2:3, :] = col_sum(incoming)
    lane_me = net.me()[1]
    for slope, first in ((slope0, 0), (slope1, half)):

        def back(i, carry):
            low = (mm(ffn_low[...], weight[first + i]) * slope[i]).astype(bf16)
            grad_up[first + i] = low
            up_sums[(first + i) ^ lane_me] = col_sum(low.astype(f32))
            return carry

        lax.fori_loop(0, half, back, 0)


def weight_grad(net, left_t, *rest):
    *rights, far, near = rest
    rows = left_t.shape[0] // net.parts
    dp = net.me()[0]
    half = far.shape[0]
    for x in range(half):
        for out, lane in ((far, 2 * x + 1), (near, 2 * x)):
            right = rights[lane // rights[0].shape[0]]
            grad = mm(left_t[...], right[lane % right.shape[0]]).astype(bf16)
            for block in range(net.parts):
                out[x, net.slot(block, dp)] = grad[block * rows : (block + 1) * rows]


def mid_backward(dims, grad_up, grad_second, mid_slope, normed, inv, gain, ctx_slope, weight0, weight1, out_weight, *outs):
    blocks, cols, width = dims
    grad_out, attn_t, grad_ctx, sums, acc, attn_low = outs
    at = 3 * cols - HEAD_DIM
    acc[...] = jnp.zeros_like(acc)
    half = weight0.shape[0]
    for weight, first in ((weight0, 0), (weight1, half)):

        def each(i, carry):
            acc[...] += mm_nt(grad_up[first + i], weight[i])
            return carry

        lax.fori_loop(0, half, each, 0)
    incoming = grad_second[...] + acc[...] * mid_slope[...]
    grad = norm_backward(incoming * row(gain), normed[...], inv[...])
    grad_out[...] = grad
    attn_low[...] = grad.astype(bf16)
    attn_t[...] = attn_low[...].T
    sums[...] = jnp.zeros_like(sums)
    sums[0:1, :] = col_sum(grad)
    sums[1:2, :] = col_sum(incoming * normed[...])
    sums[2:3, :] = col_sum(incoming)

    def spread(lane, carry):
        grad_ctx[lane] = (mm(attn_low[...], out_weight[lane, :, at:]) * ctx_slope[lane]).astype(bf16)
        return carry

    lax.fori_loop(0, blocks, spread, 0)


def attn_backward(net, dims, longs, shorts, qkv, lse, grad_ctx, in_t, attn_t, ctx_low, *rest):
    blocks, cols, width = dims
    up_sums, sums_a, sums_b, tops_a, tops_m, top0, top1, out, far, near, packed, sums, mask = rest
    heads = cols // HEAD_DIM
    rows = in_t.shape[0] // net.parts
    start = 3 * cols - HEAD_DIM
    end = 3 * cols + HEAD_DIM
    fill_mask(mask, longs, shorts)
    dp, lane_me = net.me()

    def each(lane, carry):
        for h in range(heads):
            at = h * HEAD_DIM
            q = qkv[lane, :, at : at + HEAD_DIM]
            k = qkv[lane, :, cols + at : cols + at + HEAD_DIM]
            v = qkv[lane, :, 2 * cols + at : 2 * cols + at + HEAD_DIM]
            grad = grad_ctx[lane, :, HEAD_DIM + at : 2 * HEAD_DIM + at]
            shares = jnp.exp(mm_nt(k, q) * score_scale + mask[...] - lse[lane, h : h + 1, :])
            grad_shares = mm_nt(v, grad)
            inner = jnp.sum(shares * grad_shares, axis=0, keepdims=True)
            grad_scores = (shares * (grad_shares - inner)).astype(bf16)
            grad_v = mm(shares.astype(bf16), grad)
            grad_k = mm(grad_scores, q) * score_scale
            grad_q = (mm_tn(k, grad_scores) * score_scale).T
            out[lane, :, at : at + HEAD_DIM] = grad_q.astype(bf16)
            out[lane, :, cols + at : cols + at + HEAD_DIM] = grad_k.astype(bf16)
            out[lane, :, 2 * cols + at : 2 * cols + at + HEAD_DIM] = grad_v.astype(bf16)
        out[lane, :, 3 * cols :] = jnp.zeros((out.shape[1], HEAD_DIM), bf16)
        sums[lane ^ lane_me] = col_sum(out[lane].astype(f32))
        return carry

    lax.fori_loop(0, blocks, each, 0)

    def weights(x, carry):
        for core, to in ((1, far), (0, near)):
            left = mm(in_t[...], out[2 * x + core])
            right = mm(attn_t[...], ctx_low[2 * x + core])
            mixed = (left[:, start:] + right[:, : end - start]).astype(bf16)
            for block in range(net.parts):
                rs = slice(block * rows, (block + 1) * rows)
                place = net.slot(block, dp)
                to[x, place, :, :start] = left[rs, :start].astype(bf16)
                to[x, place, :, start:end] = mixed[rs]
                to[x, place, :, end:] = right[rs, end - start :].astype(bf16)
        return carry

    lax.fori_loop(0, far.shape[0], weights, 0)
    packed[...] = jnp.zeros_like(packed)
    for j in range(blocks):
        packed[j : j + 1, :] = up_sums[j]
        packed[blocks + j : blocks + j + 1, : sums.shape[2]] = sums[j]
    packed[2 * blocks : 2 * blocks + 3, :] = sums_a[0:3, :]
    packed[2 * blocks + 3 : 2 * blocks + 6, :] = sums_b[0:3, :]
    tops = (tops_a[0:1, :], tops_a[1:2, :], tops_m[0:1, :], jnp.maximum(top0[0:1, :], top1[0:1, :]))
    for j, top in enumerate(tops):
        packed[2 * blocks + 6 : 2 * blocks + 7, 128 * j : 128 * j + 128] = top


def token_backward(dims, lim, grad_qkv, grad_first, tokens, weight, out, acc):
    blocks, cols, width = dims
    acc[...] = jnp.zeros_like(acc)

    def each(lane, carry):
        acc[...] += mm_nt(grad_qkv[lane], weight[lane, :, : 3 * cols + HEAD_DIM])
        return carry

    lax.fori_loop(0, blocks, each, 0)
    inputs = tokens[...].astype(f32)
    out[...] = (grad_first[...] + jnp.where(jnp.abs(inputs) <= lim[0], acc[...], 0.0)).astype(bf16)


def make_body(net):
    def body(
        tokens,
        cotangent,
        qkv_weight,
        qv_bias,
        out_weight,
        out_bias,
        first_gain,
        first_shift,
        up_weight,
        up_bias,
        down_weight,
        down_bias,
        second_gain,
        second_shift,
        act_ranges,
        long_lengths,
        short_lengths,
    ):
        lane = lax.axis_index("tensor")
        rows, width = tokens.shape
        assert rows == LONG_LEN
        cols = qkv_weight.shape[2]
        up_cols = up_weight.shape[1]
        blocks = lax.axis_size("tensor")
        half = blocks // 2
        dims = (blocks, cols, width)
        wide = 3 * cols + HEAD_DIM
        out_cols = cols + HEAD_DIM
        every = tuple(range(blocks))

        pieces_a, pieces_u, pieces_d = Pieces([]), Pieces([]), Pieces([])
        shard_a = attn_shard(qkv_weight, out_weight)
        job_a = Job(net.gather(shard_a, pieces_a))
        bias_row = jnp.concatenate(
            [qv_bias[0], jnp.zeros((cols,), f32), qv_bias[1], jnp.zeros((HEAD_DIM,), f32), up_bias]
        )
        job_b = Job(net.gather_lane(bias_row[None]))
        job_u = Job(net.gather(up_weight.astype(bf16), pieces_u))
        job_d = Job(net.gather(down_weight.T.astype(bf16), pieces_d, True))

        def vmem(*shape, dtype=f32):
            return pltpu.VMEM(shape, dtype)

        unit = 2 * rows * width * width * blocks
        moved = 2 * width * width * blocks

        step((), None, [job_a], [job_a])
        step((), None, [job_a, job_b], [job_a, job_b])
        step((), None, [job_a, job_u, job_b], [job_a, job_u, job_b])
        step((), None, [job_a, job_u, job_d], [job_a, job_u, job_d])
        step((), None, [job_u, job_a], [job_a])
        biases = job_b.value

        bufs, plan = pieces_a.part(every)
        qkv, lse, in_t, ctx_low, ctx_slope, tops_a, weight_a = step(
            (act_ranges, long_lengths, short_lengths, tokens, biases, *bufs),
            call(
                functools.partial(attn_forward, net, plan, len(bufs), dims),
                "attn_forward",
                [SM] * 3 + [VM] * 2 + [VM] * len(bufs),
                [
                    like((blocks, rows, wide), bf16),
                    like((blocks, 8, rows)),
                    like((width, rows), bf16),
                    like((blocks, rows, out_cols), bf16),
                    like((blocks, rows, out_cols)),
                    like((8, 128)),
                    like((blocks, width, 4 * cols), bf16),
                ],
                [vmem(rows, width, dtype=bf16), vmem(rows, rows), vmem(out_cols, rows), vmem(8, out_cols)],
                4 * unit,
                3 * moved,
            ),
            [],
            [job_u],
        )
        normed, inv, middle, mid_slope, mid_low, mid_t, tops_m = step(
            (act_ranges, ctx_low, tokens, out_bias, first_gain, first_shift, weight_a),
            call(
                functools.partial(attn_finish, dims),
                "attn_finish",
                [SM] + [VM] * 6,
                [
                    like((rows, width)),
                    like((rows, 1)),
                    like((rows, width)),
                    like((rows, width)),
                    like((rows, width), bf16),
                    like((width, rows), bf16),
                    like((8, 128)),
                ],
                [vmem(rows, width)],
                2 * unit,
                2 * moved,
            ),
            [job_u, job_d],
            [job_u, job_d],
        )

        def up_part(lanes, start, finish):
            bufs, plan = pieces_u.part(lanes)
            return step(
                (act_ranges, mid_low, biases, *bufs),
                call(
                    functools.partial(up_forward, net, plan, len(bufs), lanes[0], wide),
                    f"up_forward_{lanes[0]}",
                    [SM] + [VM] * 2 + [VM] * len(bufs),
                    [
                        like((half, rows, up_cols), bf16),
                        like((half, rows, up_cols)),
                        like((8, 128)),
                        like((half, width, up_cols), bf16),
                    ],
                    [vmem(8, up_cols)],
                    2 * unit,
                    2 * moved,
                ),
                start,
                finish,
            )

        act0, slope0, top0, weight_u0 = up_part(every[:half], [job_u, job_d], [job_u])
        act1, slope1, top1, weight_u1 = up_part(every[half:], [], [job_d])
        step((), None, [job_d], [job_d])
        step((), None, [job_d], [job_d])
        bufs_d, plan_d = pieces_d.part(every)
        layer_out, grad_second, ffn_t, sums_b, grad_up, up_sums = step(
            (act0, act1, slope0, slope1, middle, cotangent, down_bias, second_gain, second_shift, *bufs_d),
            call(
                functools.partial(down_both, net, plan_d, len(bufs_d)),
                "down_both",
                [VM] * 9 + [VM] * len(bufs_d),
                [
                    like((rows, width), bf16),
                    like((rows, width)),
                    like((width, rows), bf16),
                    like((8, width)),
                    like((blocks, rows, up_cols), bf16),
                    like((blocks, 1, up_cols)),
                ],
                [
                    vmem(blocks, width, up_cols, dtype=bf16),
                    vmem(rows, width),
                    vmem(rows, width, dtype=bf16),
                ],
                2 * unit,
                4 * moved,
            ),
        )

        grad_shape = like((net.parts, width // net.parts, up_cols), bf16)
        both_shape = like((half,) + grad_shape.shape, bf16)

        def grad_of(name, left_t, rights, start=(), finish=()):
            return step(
                (left_t, *rights),
                call(
                    functools.partial(weight_grad, net),
                    name,
                    [VM] * (1 + len(rights)),
                    [both_shape, both_shape],
                    (),
                    unit,
                    moved,
                ),
                start,
                finish,
            )

        sum_u = Job(net.scatter_sum(*grad_of("up_grad", mid_t, (grad_up,))))
        sum_d = Job(net.scatter_z_first(*grad_of("down_grad", ffn_t, (act0, act1), [sum_u], [sum_u])))
        grad_first, attn_t, grad_ctx, sums_a = step(
            (grad_up, grad_second, mid_slope, normed, inv, first_gain, ctx_slope, weight_u0, weight_u1, weight_a),
            call(
                functools.partial(mid_backward, dims),
                "mid_backward",
                [VM] * 10,
                [
                    like((rows, width)),
                    like((width, rows), bf16),
                    like((blocks, rows, out_cols), bf16),
                    like((8, width)),
                ],
                [vmem(rows, width), vmem(rows, width, dtype=bf16)],
                unit + unit // 3,
                3 * moved,
            ),
            [sum_d, sum_u],
            [sum_d, sum_u],
        )

        grad_qkv, far, near, packed = step(
            (long_lengths, short_lengths, qkv, lse, grad_ctx, in_t, attn_t, ctx_low)
            + (up_sums, sums_a, sums_b, tops_a, tops_m, top0, top1),
            call(
                functools.partial(attn_backward, net, dims),
                "attn_backward",
                [SM] * 2 + [VM] * 13,
                [like((blocks, rows, wide), bf16), both_shape, both_shape, like((16, width))],
                [vmem(blocks, 1, wide), vmem(rows, rows)],
                4 * unit,
                2 * moved,
            ),
            [sum_u, sum_d],
            [sum_u, sum_d],
        )
        sum_a = Job(net.scatter_sum(far, near))
        is_top = (jnp.arange(packed.shape[0]) == 2 * blocks + 6)[:, None]
        sum_s = Job(net.sum_max(packed, is_top))
        line_u = Job(net.scatter_line(*sum_u.value))
        step((), None, [sum_a, sum_d, sum_s], [sum_a, sum_s])
        tokens_grad = step(
            (act_ranges, grad_qkv, grad_first, tokens, weight_a),
            call(
                functools.partial(token_backward, dims),
                "token_backward",
                [SM] + [VM] * 4,
                [like((rows, width), bf16)],
                [vmem(rows, width)],
                unit,
                2 * moved,
            ),
            [sum_a],
            [sum_a, sum_d],
        )[0]
        step((), None, [sum_a, line_u, sum_s], [line_u, sum_s])
        step((), None, [line_u, sum_s], [sum_a, sum_s])
        line_a = Job(net.scatter_line(*sum_a.value))
        step((), None, [line_a, sum_d, sum_s], [line_a, sum_d, sum_s])
        step((), None, [line_a, sum_d, sum_s], [line_a, sum_d, line_u, sum_s])

        down_grad, up_grad, a_grad, packed = sum_d.value, line_u.value, line_a.value, sum_s.value
        down_grad = down_grad.T
        qkv_grad = jnp.stack([a_grad[:, j * cols : (j + 1) * cols] for j in range(3)])
        out_grad = a_grad[:, 3 * cols :].T
        own = lax.dynamic_slice_in_dim(packed, blocks + lane, 1)
        shared = packed[2 * blocks : 2 * blocks + 6]
        qv_bias_grad = jnp.concatenate([own[:, :cols], own[:, 2 * cols : 3 * cols]], 0)
        up_bias_grad = lax.dynamic_slice_in_dim(packed, lane, 1)[0]
        new_ranges = ema_decay * act_ranges + (1.0 - ema_decay) * packed[2 * blocks + 6, 0:512:128]
        return (
            layer_out,
            tokens_grad,
            qkv_grad,
            qv_bias_grad,
            out_grad,
            shared[0],
            shared[1],
            shared[2],
            up_grad,
            up_bias_grad,
            down_grad,
            shared[3],
            shared[4],
            shared[5],
            new_ranges,
        )

    return body


def solution(mesh):
    in_specs = (
        P(ALL, None),
        P(ALL, None),
        P(None, "dp", "tensor"),
        P(None, "tensor"),
        P("tensor", "dp"),
        P(),
        P(),
        P(),
        P("dp", "tensor"),
        P("tensor"),
        P("tensor", "dp"),
        P(),
        P(),
        P(),
        P(),
        P("dp"),
        P("dp"),
    )
    out_specs = (
        P(ALL, None),
        P(ALL, None),
        P(None, "dp", "tensor"),
        P(None, "tensor"),
        P("tensor", "dp"),
        P(),
        P(),
        P(),
        P("dp", "tensor"),
        P("tensor"),
        P("tensor", "dp"),
        P(),
        P(),
        P(),
        P(),
    )
    net = Grid() if mesh.shape["dp"] == 8 and mesh.shape["tensor"] == 4 else Plain()
    return jax.shard_map(make_body(net), mesh=mesh, in_specs=in_specs, out_specs=out_specs, check_vma=False)
```

```python
import functools
import itertools

import jax
import jax.numpy as jnp
from jax import lax
from jax.experimental import pallas as pl
from jax.experimental.pallas import tpu as pltpu
from jax.sharding import PartitionSpec as P

HEAD_DIM = 64
LONG_LEN = 512
SHORT_LEN = 128
ALL = ("dp", "tensor")

ema_decay = 0.9
epsilon = 1e-06
root_half = 0.7071067811865476
density_scale = 0.3989422804014327
score_scale = HEAD_DIM ** (-0.5)
NEG = -1000000000.0

f32 = jnp.float32
bf16 = jnp.bfloat16


def mm(left, right):
    return jnp.dot(left, right, preferred_element_type=f32)


def mm_tn(left, right):
    return lax.dot_general(left, right, (((0,), (0,)), ((), ())), preferred_element_type=f32)


def mm_nt(left, right):
    return lax.dot_general(left, right, (((1,), (1,)), ((), ())), preferred_element_type=f32)


def _lin(z, y, x, c):
    return (z * 2 + y) * 4 + x * 2 + c


def _perm(fn):
    out = []
    for z, y, x, c in itertools.product(range(4), range(2), range(2), range(2)):
        out.append((_lin(z, y, x, c), _lin(*fn(z, y, x, c))))
    return out


PC = _perm(lambda z, y, x, c: (z, y, x, 1 - c))
PX = _perm(lambda z, y, x, c: (z, y, 1 - x, c))
PY = _perm(lambda z, y, x, c: (z, 1 - y, x, c))
PZ1 = _perm(lambda z, y, x, c: (z ^ 1, y, x, c))
PZ2 = _perm(lambda z, y, x, c: (z ^ 2, y, x, c))


def tie(*trees):
    leaves, spec = jax.tree.flatten(trees)
    return jax.tree.unflatten(spec, lax.optimization_barrier(leaves))


class Job:
    def __init__(self, stages):
        self.stages, self.value, self.out, self.flight, self.over = stages, None, [], [], False
        self.take(None)

    def take(self, got):
        if not self.over:
            try:
                self.out = self.stages.send(got)
            except StopIteration as stop:
                self.value, self.out, self.over = stop.value, [], True


def step(ins, run=None, start=(), finish=()):
    ins, sends = tie(ins, [[value for value, _ in job.out] for job in start])
    for job, values in zip(start, sends):
        job.flight = [lax.ppermute(v, ALL, perm) for v, (_, perm) in zip(values, job.out)]
    outs = run(*ins) if run else ins
    outs, got = tie(outs, [job.flight for job in finish])
    for job, values in zip(finish, got):
        job.flight = []
        job.take(values)
    return outs


class Pieces:
    def __init__(self, plan):
        self.bufs, self.plan = {}, plan

    def part(self, lanes):
        plan = [p for p in self.plan if p[1] in lanes]
        names = sorted({p[0] for p in plan})
        return [self.bufs[n] for n in names], [(names.index(b), lane - lanes[0], at, col) for b, lane, at, col in plan]


class Grid:
    parts = 8

    @staticmethod
    def gather(shard, pieces):
        own = shard[None]
        for base, lane in ((0, 0), (5, 1)):
            pieces.plan.append((base, lane, (0, 4, 2, 6), 0))
            pieces.plan.append((base + 1, lane, (1, 5, 3, 7), 0))
            pieces.plan.append((base + 2, lane + 2, (0, 4, 2, 6), 0))
            pieces.plan.append((base + 3, lane + 2, (1, 5), 0))
            pieces.plan.append((base + 4, lane + 2, (3, 7), 0))
        (far_z,) = yield [(own, PZ2)]
        pair = jnp.concatenate([own, far_z], 0)
        (near_z,) = yield [(pair, PZ1)]
        line = jnp.concatenate([pair, near_z], 0)
        over_x, over_y, line_far = yield [(line, PX), (line, PY), (line, PC)]
        pieces.bufs.update({0: line, 1: over_y, 2: over_x, 5: line_far})
        diag_x, diag_y, over_y_far, over_x_far = yield [
            (over_y[:2], PX),
            (over_x[2:], PY),
            (over_y, PC),
            (over_x, PC),
        ]
        pieces.bufs.update({3: diag_x, 4: diag_y, 6: over_y_far, 7: over_x_far})
        diag_x_far, diag_y_far = yield [(diag_x, PC), (diag_y, PC)]
        pieces.bufs.update({8: diag_x_far, 9: diag_y_far})

    @staticmethod
    def gather_plane_first(shard, pieces, first_col):
        own = shard[None]
        over_x, over_y = yield [(own, PX), (own, PY)]
        (diag,) = yield [(over_y, PX)]
        plane = jnp.concatenate([own, over_y, over_x, diag], 0)
        (far_z,) = yield [(plane, PZ2)]
        half = jnp.concatenate([plane, far_z], 0)
        (near_z,) = yield [(half, PZ1)]
        half_far, near_z_far = yield [(half, PC), (near_z, PC)]
        for n, (buf, core) in enumerate(((half, 0), (near_z, 0), (half_far, 1), (near_z_far, 1))):
            near = 2 * (n % 2)
            name = 20 + n
            pieces.bufs[name] = buf
            for x in range(2):
                places = tuple(4 * far + near + y for far in range(2) for y in range(2))
                pieces.plan.append((name, 2 * x + core, (x, places), first_col))

    @staticmethod
    def slot(block, dp):
        place = block ^ dp
        return (place & 1) * 4 + (place & 2) + (place >> 2)

    @staticmethod
    def scatter_sum(far, near):
        (got,) = yield [(far, PC)]
        out_x, out_y = add_first(near, got)
        from_x, from_y = yield [(out_x, PX), (out_y, PY)]
        out_x, out_y = add_second(near, got, from_x, from_y)
        in_x, in_y = yield [(out_x, PX), (out_y, PY)]
        return near, got, in_x, in_y

    @staticmethod
    def scatter_line(near, got, in_x, in_y):
        out_z, kept = add_third(near, got, in_x, in_y)
        (from_z,) = yield [(out_z, PZ1)]
        out_z, kept = add_fourth(kept, from_z)
        (last,) = yield [(out_z, PZ2)]
        return kept, last

    @staticmethod
    def scatter_z_first(far, near):
        (got,) = yield [(far, PC)]
        out_1, out_0 = add_near_z(near, got)
        (from_1,) = yield [(out_1, PZ1)]
        out_x, out_y = add_corner(near, got, from_1)
        from_x, from_y, from_0 = yield [(out_x, PX), (out_y, PY), (out_0, PZ1)]
        out_x, out_y = add_sides(near, got, from_1, from_0, from_x, from_y)
        in_x, in_y = yield [(out_x, PX), (out_y, PY)]
        out_z, kept = add_own(near, got, from_0, in_x, in_y)
        (last,) = yield [(out_z, PZ2)]
        return kept, last

    @staticmethod
    def gather_lane(vec):
        (other,) = yield [(vec, PX)]
        pair = jnp.stack([vec, other])
        (more,) = yield [(pair, PC)]
        return jnp.stack([pair, more], 1).reshape((4,) + vec.shape)

    @staticmethod
    def sum_max(both, is_top):
        for perm in (PC, PX, PY, PZ1, PZ2):
            (other,) = yield [(both, perm)]
            both = jnp.where(is_top, jnp.maximum(both, other), both + other)
        return both

    @staticmethod
    def me():
        return lax.axis_index("dp"), lax.axis_index("tensor")


class Plain:
    parts = 1

    @staticmethod
    def gather(shard, pieces, first_col=0):
        rows = lax.all_gather(shard, "dp", axis=0, tiled=True)
        full = lax.all_gather(rows, "tensor", axis=0)
        for k in range(full.shape[0]):
            pieces.plan.append((first_col + k, k, None, first_col))
            pieces.bufs[first_col + k] = full[k][None]
        return
        yield

    gather_plane_first = gather

    @staticmethod
    def slot(block, dp):
        return block

    @staticmethod
    def scatter_sum(far, near):
        grads = jnp.stack([near[0], far[0], near[1], far[1]]).astype(f32)
        return (grads.reshape((4, -1, grads.shape[-1])),)
        yield

    @staticmethod
    def scatter_line(grads):
        own = lax.psum_scatter(grads, "tensor", scatter_dimension=0, tiled=False)
        own = lax.psum_scatter(own, "dp", scatter_dimension=0, tiled=True)
        return own, jnp.zeros_like(own)
        yield

    @staticmethod
    def scatter_z_first(far, near):
        grads = yield from Plain.scatter_sum(far, near)
        return (yield from Plain.scatter_line(*grads))

    @staticmethod
    def gather_lane(vec):
        return lax.all_gather(vec, "tensor", axis=0)
        yield

    @staticmethod
    def sum_max(both, is_top):
        return jnp.where(is_top, lax.pmax(both, ALL), lax.psum(both, ALL))
        yield

    @staticmethod
    def me():
        return 0, 0


VM = pl.BlockSpec(memory_space=pltpu.VMEM)
SM = pl.BlockSpec(memory_space=pltpu.SMEM)
VMEM_MIB = 14


def like(shape, dtype=f32):
    return jax.ShapeDtypeStruct(shape, dtype)


def call(kernel, name, specs, outs, scratch=(), flops=0, moved=0):
    return pl.pallas_call(
        kernel,
        name=name,
        out_shape=outs,
        in_specs=specs,
        out_specs=[VM] * len(outs),
        scratch_shapes=list(scratch),
        compiler_params=pltpu.CompilerParams(vmem_limit_bytes=VMEM_MIB * 2**20),
        cost_estimate=pl.CostEstimate(flops=flops, bytes_accessed=moved, transcendentals=0),
    )


def glue(kernel, outs, *ins):
    return call(kernel, kernel.__name__, [VM] * len(ins), outs)(*ins)


def add_first(near, got):
    def first_sums(near, got, out_x, out_y):
        for k in range(2):
            out_x[k] = (near[1, 4 + k].astype(f32) + got[1, 4 + k].astype(f32)).astype(bf16)
            out_y[k] = (near[1, 6 + k].astype(f32) + got[1, 6 + k].astype(f32)).astype(bf16)

    part = like((2,) + near.shape[2:], bf16)
    return glue(first_sums, [part, part], near, got)


def add_second(near, got, from_x, from_y):
    def second_sums(near, got, from_x, from_y, out_x, out_y):
        for k in range(4):
            over_x = near[1, k].astype(f32) + got[1, k].astype(f32)
            over_y = near[0, 4 + k].astype(f32) + got[0, 4 + k].astype(f32)
            if k < 2:
                over_y = over_y + from_x[k].astype(f32)
            else:
                over_x = over_x + from_y[k - 2].astype(f32)
            out_x[k] = over_x.astype(bf16)
            out_y[k] = over_y.astype(bf16)

    part = like((4,) + near.shape[2:], bf16)
    return glue(second_sums, [part, part], near, got, from_x, from_y)


def add_third(near, got, in_x, in_y):
    def third_sums(near, got, in_x, in_y, out, kept):
        for k in range(4):
            total = near[0, k].astype(f32) + got[0, k].astype(f32) + in_x[k].astype(f32) + in_y[k].astype(f32)
            if k < 2:
                kept[k] = total
            else:
                out[k - 2] = total.astype(bf16)

    shape = (2,) + near.shape[2:]
    return glue(third_sums, [like(shape, bf16), like(shape)], near, got, in_x, in_y)


def add_fourth(kept, from_z):
    def fourth_sums(kept, from_z, out, mine):
        mine[...] = kept[0] + from_z[0].astype(f32)
        out[...] = (kept[1] + from_z[1].astype(f32)).astype(bf16)

    shape = kept.shape[1:]
    return glue(fourth_sums, [like(shape, bf16), like(shape)], kept, from_z)


def add_near_z(near, got):
    def near_z_sums(near, got, out_1, out_0):
        for x, out in ((1, out_1), (0, out_0)):
            for y in range(2):
                for k in range(2):
                    at = 4 * y + 2 + k
                    out[2 * y + k] = (near[x, at].astype(f32) + got[x, at].astype(f32)).astype(bf16)

    part = like((4,) + near.shape[2:], bf16)
    return glue(near_z_sums, [part, part], near, got)


def three(near, got, from_z, x, y, k):
    return near[x, 4 * y + k].astype(f32) + got[x, 4 * y + k].astype(f32) + from_z[2 * y + k].astype(f32)


def add_corner(near, got, from_1):
    def corner_sums(near, got, from_1, out_x, out_y):
        out_x[...] = three(near, got, from_1, 1, 1, 0).astype(bf16)
        out_y[...] = three(near, got, from_1, 1, 1, 1).astype(bf16)

    part = like(near.shape[2:], bf16)
    return glue(corner_sums, [part, part], near, got, from_1)


def add_sides(near, got, from_1, from_0, from_x, from_y):
    def side_sums(near, got, from_1, from_0, from_x, from_y, out_x, out_y):
        out_x[0] = three(near, got, from_1, 1, 0, 0).astype(bf16)
        out_x[1] = (three(near, got, from_1, 1, 0, 1) + from_y[...].astype(f32)).astype(bf16)
        out_y[0] = (three(near, got, from_0, 0, 1, 0) + from_x[...].astype(f32)).astype(bf16)
        out_y[1] = three(near, got, from_0, 0, 1, 1).astype(bf16)

    part = like((2,) + near.shape[2:], bf16)
    return glue(side_sums, [part, part], near, got, from_1, from_0, from_x, from_y)


def add_own(near, got, from_0, in_x, in_y):
    def own_sums(near, got, from_0, in_x, in_y, out, kept):
        kept[...] = three(near, got, from_0, 0, 0, 0) + in_x[0].astype(f32) + in_y[0].astype(f32)
        out[...] = (three(near, got, from_0, 0, 0, 1) + in_x[1].astype(f32) + in_y[1].astype(f32)).astype(bf16)

    shape = near.shape[2:]
    return glue(own_sums, [like(shape, bf16), like(shape)], near, got, from_0, in_x, in_y)


def attn_grads(kept, last):
    rows, width = kept.shape
    cols = width // 4

    def attn_sums(kept, last, qkv, out):
        total = kept[...] + last[...].astype(f32)
        for j in range(3):
            qkv[j] = total[:, j * cols : (j + 1) * cols]
        out[...] = total[:, 3 * cols :].T

    return glue(attn_sums, [like((3, rows, cols)), like((cols, rows))], kept, last)


def attn_shard(qkv_weight, out_weight):
    _, rows, cols = qkv_weight.shape

    def attn_weights(qkv, out_weight, out):
        for j in range(3):
            out[:, j * cols : (j + 1) * cols] = qkv[j].astype(bf16)
        out[:, 3 * cols :] = out_weight[...].T.astype(bf16)

    return glue(attn_weights, [like((rows, 4 * cols), bf16)], qkv_weight, out_weight)[0]


def assemble(plan, bufs, dst, dp):
    for buf, lane, places, col in plan:
        src = bufs[buf]
        _, rows, width = src.shape
        cols = pl.ds(col, width)
        if places is None:
            dst[lane, :, cols] = src[0]
            continue
        index = list(range(len(places)))
        if isinstance(places[1], tuple):
            x, places = places
            index = [4 * (n // 2) + 2 * x + n % 2 for n in range(len(places))]
        for n, place in zip(index, places):
            dst[lane, pl.ds(pl.multiple_of((dp ^ place) * rows, rows), rows), cols] = src[n]


def row(vec):
    return vec[...].reshape(1, -1)


def row_stats(summed):
    centered = summed - jnp.mean(summed, axis=-1, keepdims=True)
    inv = lax.rsqrt(jnp.mean(centered * centered, axis=-1, keepdims=True) + epsilon)
    return centered * inv, inv


def norm_backward(scaled, normed, inv):
    row_mean = jnp.mean(scaled, axis=-1, keepdims=True)
    row_cross = jnp.mean(scaled * normed, axis=-1, keepdims=True)
    return inv * (scaled - row_mean - normed * row_cross)


def col_sum(values):
    return jnp.sum(values, axis=0, keepdims=True)


def top_of(values):
    return jnp.full((1, 128), jnp.max(jnp.abs(values)), f32)


def fill_mask(mask, longs, shorts):
    per_block = LONG_LEN // SHORT_LEN
    block = lax.axis_index("tensor")
    n_long = longs.shape[0]
    is_long = block < n_long
    whole = longs[jnp.minimum(block, n_long - 1)]
    first = jnp.maximum(block - n_long, 0) * per_block
    shift = jnp.where(is_long, LONG_LEN.bit_length() - 1, SHORT_LEN.bit_length() - 1)
    size = jnp.where(is_long, LONG_LEN, SHORT_LEN)
    k_pos = lax.broadcasted_iota(jnp.int32, (LONG_LEN, 1), 0)
    q_pos = lax.broadcasted_iota(jnp.int32, (1, LONG_LEN), 1)
    k_seg = lax.shift_right_logical(k_pos, jnp.full_like(k_pos, shift))
    q_seg = lax.shift_right_logical(q_pos, jnp.full_like(q_pos, shift))
    limit = jnp.zeros_like(k_pos)
    for j in range(per_block):
        limit = jnp.where(k_seg == j, jnp.where(is_long, whole, shorts[first + j]), limit)
    k_seg = jnp.where(k_pos - k_seg * size < limit, k_seg, -1)
    mask[...] = jnp.where(k_seg == q_seg, 0.0, NEG)


def attn_forward(net, plan, nb, dims, lim, longs, shorts, tokens, bias, *rest):
    blocks, cols, width = dims
    bufs, rest = rest[:nb], rest[nb:]
    qkv_out, lse_out, in_t, ctx_low, ctx_slope, top_out, weight, in_low, mask, ctx_t, top_ctx = rest
    heads = cols // HEAD_DIM
    low_q = 3 * cols + HEAD_DIM
    assemble(plan, bufs, weight, net.me()[0])
    inputs = tokens[...].astype(f32)
    in_low[...] = jnp.clip(inputs, -lim[0], lim[0]).astype(bf16)
    in_t[...] = in_low[...].T
    top_out[0:1, :] = top_of(inputs)
    fill_mask(mask, longs, shorts)
    ctx_t[0:HEAD_DIM, :] = jnp.zeros((HEAD_DIM, ctx_t.shape[1]), f32)
    top_ctx[...] = jnp.zeros_like(top_ctx)
    inv_limit = 1.0 / jnp.full((1, 1), lim[1], f32)

    def each(lane, carry):
        qkv = (mm(in_low[...], weight[lane, :, :low_q]) + bias[lane, :, :low_q]).astype(bf16)
        qkv_out[lane] = qkv
        for h in range(heads):
            at = h * HEAD_DIM
            q = qkv[:, at : at + HEAD_DIM]
            k = qkv[:, cols + at : cols + at + HEAD_DIM]
            v = qkv[:, 2 * cols + at : 2 * cols + at + HEAD_DIM]
            scores = mm_nt(k, q) * score_scale + mask[...]
            peak = jnp.max(scores, axis=0, keepdims=True)
            grown = jnp.exp(scores - peak)
            total = jnp.sum(grown, axis=0, keepdims=True)
            lse_out[lane, h : h + 1, :] = peak + jnp.log(total)
            shares = (grown * (1.0 / total)).astype(bf16)
            ctx_t[HEAD_DIM + at : 2 * HEAD_DIM + at, :] = mm_tn(v, shares)
        context = ctx_t[...].T
        bent = jnp.tanh(context * inv_limit)
        ctx_low[lane] = (lim[1] * bent).astype(bf16)
        ctx_slope[lane] = 1.0 - bent * bent
        top_ctx[...] = jnp.maximum(top_ctx[...], jnp.max(jnp.abs(context).reshape(-1, 8, context.shape[1]), axis=0))
        return carry

    lax.fori_loop(0, blocks, each, 0)
    top_out[1:2, :] = top_of(top_ctx[...])


def attn_finish(dims, lim, ctx_low, tokens, out_bias, gain, shift, weight, *outs):
    blocks, cols, width = dims
    normed_out, inv_out, middle_out, mid_slope, mid_low, mid_t, top_out, acc = outs
    at = 3 * cols - HEAD_DIM
    acc[...] = tokens[...].astype(f32) + row(out_bias)

    def each(lane, carry):
        acc[...] += mm_nt(ctx_low[lane], weight[lane, :, at:])
        return carry

    lax.fori_loop(0, blocks, each, 0)
    normed, inv = row_stats(acc[...])
    normed_out[...] = normed
    inv_out[...] = inv
    middle = normed * row(gain) + row(shift)
    middle_out[...] = middle
    bent = jnp.tanh(middle * (1.0 / jnp.full((1, 1), lim[2], f32)))
    low = (lim[2] * bent).astype(bf16)
    mid_low[...] = low
    mid_slope[...] = 1.0 - bent * bent
    mid_t[...] = low.T
    top_out[...] = jnp.broadcast_to(top_of(middle), top_out.shape)


def up_forward(net, plan, nb, first, low_q, lim, mid_low, bias, *rest):
    bufs, rest = rest[:nb], rest[nb:]
    act_out, slope_out, top_out, weight, top_hid = rest
    assemble(plan, bufs, weight, net.me()[0])
    top_hid[...] = jnp.zeros_like(top_hid)
    inv_limit = 1.0 / jnp.full((1, 1), lim[3], f32)

    def each(lane, carry):
        up = mm(mid_low[...], weight[lane]) + bias[first + lane, :, low_q:]
        half = 0.5 * (1.0 + lax.erf(up * root_half))
        hidden = up * half
        top_hid[...] = jnp.maximum(top_hid[...], jnp.max(jnp.abs(hidden).reshape(-1, 8, hidden.shape[1]), axis=0))
        bent = jnp.tanh(hidden * inv_limit)
        act_out[lane] = (lim[3] * bent).astype(bf16)
        slope_out[lane] = (1.0 - bent * bent) * (half + up * jnp.exp(-0.5 * up * up) * density_scale)
        return carry

    lax.fori_loop(0, weight.shape[0], each, 0)
    top_out[...] = jnp.broadcast_to(top_of(top_hid[...]), top_out.shape)


def down_both(net, plan, nb, act0, act1, slope0, slope1, middle, cotangent, down_bias, gain, shift, *rest):
    bufs, rest = rest[:nb], rest[nb:]
    layer_out, grad_out, ffn_t, sums, grad_up, up_sums, weight, acc, ffn_low = rest
    assemble(plan, bufs, weight, net.me()[0])
    acc[...] = middle[...] + row(down_bias)
    half = act0.shape[0]
    for act, first in ((act0, 0), (act1, half)):

        def each(i, carry):
            acc[...] += mm_nt(act[i], weight[first + i])
            return carry

        lax.fori_loop(0, half, each, 0)
    normed, inv = row_stats(acc[...])
    layer_out[...] = (normed * row(gain) + row(shift)).astype(bf16)
    incoming = cotangent[...].astype(f32)
    grad = norm_backward(incoming * row(gain), normed, inv)
    grad_out[...] = grad
    ffn_low[...] = grad.astype(bf16)
    ffn_t[...] = ffn_low[...].T
    sums[...] = jnp.zeros_like(sums)
    sums[0:1, :] = col_sum(grad)
    sums[1:2, :] = col_sum(incoming * normed)
    sums[2:3, :] = col_sum(incoming)
    lane_me = net.me()[1]
    for slope, first in ((slope0, 0), (slope1, half)):

        def back(i, carry):
            low = (mm(ffn_low[...], weight[first + i]) * slope[i]).astype(bf16)
            grad_up[first + i] = low
            up_sums[(first + i) ^ lane_me] = col_sum(low.astype(f32))
            return carry

        lax.fori_loop(0, half, back, 0)


def weight_grad(net, left_t, *rest):
    *rights, far, near = rest
    rows = left_t.shape[0] // net.parts
    dp = net.me()[0]
    half = far.shape[0]
    for x in range(half):
        for out, lane in ((far, 2 * x + 1), (near, 2 * x)):
            right = rights[lane // rights[0].shape[0]]
            grad = mm(left_t[...], right[lane % right.shape[0]]).astype(bf16)
            for block in range(net.parts):
                out[x, net.slot(block, dp)] = grad[block * rows : (block + 1) * rows]


def mid_backward(dims, grad_up, grad_second, mid_slope, normed, inv, gain, ctx_slope, weight0, weight1, out_weight, *outs):
    blocks, cols, width = dims
    grad_out, attn_t, grad_ctx, sums, acc, attn_low = outs
    at = 3 * cols - HEAD_DIM
    acc[...] = jnp.zeros_like(acc)
    half = weight0.shape[0]
    for weight, first in ((weight0, 0), (weight1, half)):

        def each(i, carry):
            acc[...] += mm_nt(grad_up[first + i], weight[i])
            return carry

        lax.fori_loop(0, half, each, 0)
    incoming = grad_second[...] + acc[...] * mid_slope[...]
    grad = norm_backward(incoming * row(gain), normed[...], inv[...])
    grad_out[...] = grad
    attn_low[...] = grad.astype(bf16)
    attn_t[...] = attn_low[...].T
    sums[...] = jnp.zeros_like(sums)
    sums[0:1, :] = col_sum(grad)
    sums[1:2, :] = col_sum(incoming * normed[...])
    sums[2:3, :] = col_sum(incoming)

    def spread(lane, carry):
        grad_ctx[lane] = (mm(attn_low[...], out_weight[lane, :, at:]) * ctx_slope[lane]).astype(bf16)
        return carry

    lax.fori_loop(0, blocks, spread, 0)


def attn_backward(net, dims, longs, shorts, qkv, lse, grad_ctx, in_t, attn_t, ctx_low, *rest):
    blocks, cols, width = dims
    up_sums, sums_a, sums_b, tops_a, tops_m, top0, top1, out, far, near, packed, sums, mask = rest
    heads = cols // HEAD_DIM
    rows = in_t.shape[0] // net.parts
    start = 3 * cols - HEAD_DIM
    end = 3 * cols + HEAD_DIM
    fill_mask(mask, longs, shorts)
    dp, lane_me = net.me()

    def each(lane, carry):
        for h in range(heads):
            at = h * HEAD_DIM
            q = qkv[lane, :, at : at + HEAD_DIM]
            k = qkv[lane, :, cols + at : cols + at + HEAD_DIM]
            v = qkv[lane, :, 2 * cols + at : 2 * cols + at + HEAD_DIM]
            grad = grad_ctx[lane, :, HEAD_DIM + at : 2 * HEAD_DIM + at]
            shares = jnp.exp(mm_nt(k, q) * score_scale + mask[...] - lse[lane, h : h + 1, :])
            grad_shares = mm_nt(v, grad)
            inner = jnp.sum(shares * grad_shares, axis=0, keepdims=True)
            grad_scores = (shares * (grad_shares - inner)).astype(bf16)
            grad_v = mm(shares.astype(bf16), grad)
            grad_k = mm(grad_scores, q) * score_scale
            grad_q = (mm_tn(k, grad_scores) * score_scale).T
            out[lane, :, at : at + HEAD_DIM] = grad_q.astype(bf16)
            out[lane, :, cols + at : cols + at + HEAD_DIM] = grad_k.astype(bf16)
            out[lane, :, 2 * cols + at : 2 * cols + at + HEAD_DIM] = grad_v.astype(bf16)
        out[lane, :, 3 * cols :] = jnp.zeros((out.shape[1], HEAD_DIM), bf16)
        sums[lane ^ lane_me] = col_sum(out[lane].astype(f32))
        return carry

    lax.fori_loop(0, blocks, each, 0)

    def weights(x, carry):
        for core, to in ((1, far), (0, near)):
            left = mm(in_t[...], out[2 * x + core])
            right = mm(attn_t[...], ctx_low[2 * x + core])
            mixed = (left[:, start:] + right[:, : end - start]).astype(bf16)
            for block in range(net.parts):
                rs = slice(block * rows, (block + 1) * rows)
                place = net.slot(block, dp)
                to[x, place, :, :start] = left[rs, :start].astype(bf16)
                to[x, place, :, start:end] = mixed[rs]
                to[x, place, :, end:] = right[rs, end - start :].astype(bf16)
        return carry

    lax.fori_loop(0, far.shape[0], weights, 0)
    packed[...] = jnp.zeros_like(packed)
    for j in range(blocks):
        packed[j : j + 1, :] = up_sums[j]
        packed[blocks + j : blocks + j + 1, : sums.shape[2]] = sums[j]
    packed[2 * blocks : 2 * blocks + 3, :] = sums_a[0:3, :]
    packed[2 * blocks + 3 : 2 * blocks + 6, :] = sums_b[0:3, :]
    tops = (tops_a[0:1, :], tops_a[1:2, :], tops_m[0:1, :], jnp.maximum(top0[0:1, :], top1[0:1, :]))
    for j, top in enumerate(tops):
        packed[2 * blocks + 6 : 2 * blocks + 7, 128 * j : 128 * j + 128] = top


def token_backward(dims, lim, grad_qkv, grad_first, tokens, weight, out, acc):
    blocks, cols, width = dims
    acc[...] = jnp.zeros_like(acc)

    def each(lane, carry):
        acc[...] += mm_nt(grad_qkv[lane], weight[lane, :, : 3 * cols + HEAD_DIM])
        return carry

    lax.fori_loop(0, blocks, each, 0)
    inputs = tokens[...].astype(f32)
    out[...] = (grad_first[...] + jnp.where(jnp.abs(inputs) <= lim[0], acc[...], 0.0)).astype(bf16)


def make_body(net):
    def body(
        tokens,
        cotangent,
        qkv_weight,
        qv_bias,
        out_weight,
        out_bias,
        first_gain,
        first_shift,
        up_weight,
        up_bias,
        down_weight,
        down_bias,
        second_gain,
        second_shift,
        act_ranges,
        long_lengths,
        short_lengths,
    ):
        lane = lax.axis_index("tensor")
        rows, width = tokens.shape
        assert rows == LONG_LEN
        cols = qkv_weight.shape[2]
        up_cols = up_weight.shape[1]
        blocks = lax.axis_size("tensor")
        half = blocks // 2
        dims = (blocks, cols, width)
        wide = 3 * cols + HEAD_DIM
        out_cols = cols + HEAD_DIM
        every = tuple(range(blocks))

        pieces_a, pieces_u, pieces_d = Pieces([]), Pieces([]), Pieces([])
        shard_a = attn_shard(qkv_weight, out_weight)
        job_a = Job(net.gather(shard_a, pieces_a))
        bias_row = jnp.concatenate(
            [qv_bias[0], jnp.zeros((cols,), f32), qv_bias[1], jnp.zeros((HEAD_DIM,), f32), up_bias]
        )
        job_b = Job(net.gather_lane(bias_row[None]))
        job_u = Job(net.gather(up_weight.astype(bf16), pieces_u))
        shard_d = down_weight.T.astype(bf16)
        col = up_cols // 2
        job_d = Job(net.gather(shard_d[:, :col], pieces_d))
        job_p = Job(net.gather_plane_first(shard_d[:, col:], pieces_d, col))

        def vmem(*shape, dtype=f32):
            return pltpu.VMEM(shape, dtype)

        unit = 2 * rows * width * width * blocks
        moved = 2 * width * width * blocks

        step((), None, [job_a, job_p, job_b], [job_a, job_p, job_b])
        step((), None, [job_a, job_p, job_b], [job_a, job_p, job_b])
        step((), None, [job_a, job_u, job_d], [job_a, job_u, job_d])
        step((), None, [job_a, job_u], [job_a, job_u])
        step((), None, [job_a, job_u], [job_a])
        biases = job_b.value

        bufs, plan = pieces_a.part(every)
        qkv, lse, in_t, ctx_low, ctx_slope, tops_a, weight_a = step(
            (act_ranges, long_lengths, short_lengths, tokens, biases, *bufs),
            call(
                functools.partial(attn_forward, net, plan, len(bufs), dims),
                "attn_forward",
                [SM] * 3 + [VM] * 2 + [VM] * len(bufs),
                [
                    like((blocks, rows, wide), bf16),
                    like((blocks, 8, rows)),
                    like((width, rows), bf16),
                    like((blocks, rows, out_cols), bf16),
                    like((blocks, rows, out_cols)),
                    like((8, 128)),
                    like((blocks, width, 4 * cols), bf16),
                ],
                [vmem(rows, width, dtype=bf16), vmem(rows, rows), vmem(out_cols, rows), vmem(8, out_cols)],
                4 * unit,
                3 * moved,
            ),
            [job_d, job_p],
            [job_u, job_d, job_p],
        )
        normed, inv, middle, mid_slope, mid_low, mid_t, tops_m = step(
            (act_ranges, ctx_low, tokens, out_bias, first_gain, first_shift, weight_a),
            call(
                functools.partial(attn_finish, dims),
                "attn_finish",
                [SM] + [VM] * 6,
                [
                    like((rows, width)),
                    like((rows, 1)),
                    like((rows, width)),
                    like((rows, width)),
                    like((rows, width), bf16),
                    like((width, rows), bf16),
                    like((8, 128)),
                ],
                [vmem(rows, width)],
                2 * unit,
                2 * moved,
            ),
            [job_u, job_p],
            [job_u],
        )

        def up_part(lanes, start, finish):
            bufs, plan = pieces_u.part(lanes)
            return step(
                (act_ranges, mid_low, biases, *bufs),
                call(
                    functools.partial(up_forward, net, plan, len(bufs), lanes[0], wide),
                    f"up_forward_{lanes[0]}",
                    [SM] + [VM] * 2 + [VM] * len(bufs),
                    [
                        like((half, rows, up_cols), bf16),
                        like((half, rows, up_cols)),
                        like((8, 128)),
                        like((half, width, up_cols), bf16),
                    ],
                    [vmem(8, up_cols)],
                    2 * unit,
                    2 * moved,
                ),
                start,
                finish,
            )

        act0, slope0, top0, weight_u0 = up_part(every[:half], [job_u, job_d], [job_u])
        act1, slope1, top1, weight_u1 = up_part(every[half:], [], [job_d, job_p])
        step((), None, [job_d], [job_d])
        step((), None, [job_d, job_p], [job_d, job_p])
        bufs_d, plan_d = pieces_d.part(every)
        layer_out, grad_second, ffn_t, sums_b, grad_up, up_sums = step(
            (act0, act1, slope0, slope1, middle, cotangent, down_bias, second_gain, second_shift, *bufs_d),
            call(
                functools.partial(down_both, net, plan_d, len(bufs_d)),
                "down_both",
                [VM] * 9 + [VM] * len(bufs_d),
                [
                    like((rows, width), bf16),
                    like((rows, width)),
                    like((width, rows), bf16),
                    like((8, width)),
                    like((blocks, rows, up_cols), bf16),
                    like((blocks, 1, up_cols)),
                ],
                [
                    vmem(blocks, width, up_cols, dtype=bf16),
                    vmem(rows, width),
                    vmem(rows, width, dtype=bf16),
                ],
                2 * unit,
                4 * moved,
            ),
        )

        grad_shape = like((net.parts, width // net.parts, up_cols), bf16)
        both_shape = like((half,) + grad_shape.shape, bf16)

        def grad_of(name, left_t, rights, start=(), finish=()):
            return step(
                (left_t, *rights),
                call(
                    functools.partial(weight_grad, net),
                    name,
                    [VM] * (1 + len(rights)),
                    [both_shape, both_shape],
                    (),
                    unit,
                    moved,
                ),
                start,
                finish,
            )

        sum_u = Job(net.scatter_sum(*grad_of("up_grad", mid_t, (grad_up,))))
        sum_d = Job(net.scatter_z_first(*grad_of("down_grad", ffn_t, (act0, act1), [sum_u], [sum_u])))
        grad_first, attn_t, grad_ctx, sums_a = step(
            (grad_up, grad_second, mid_slope, normed, inv, first_gain, ctx_slope, weight_u0, weight_u1, weight_a),
            call(
                functools.partial(mid_backward, dims),
                "mid_backward",
                [VM] * 10,
                [
                    like((rows, width)),
                    like((width, rows), bf16),
                    like((blocks, rows, out_cols), bf16),
                    like((8, width)),
                ],
                [vmem(rows, width), vmem(rows, width, dtype=bf16)],
                unit + unit // 3,
                3 * moved,
            ),
            [sum_d, sum_u],
            [sum_d, sum_u],
        )

        grad_qkv, far, near, packed = step(
            (long_lengths, short_lengths, qkv, lse, grad_ctx, in_t, attn_t, ctx_low)
            + (up_sums, sums_a, sums_b, tops_a, tops_m, top0, top1),
            call(
                functools.partial(attn_backward, net, dims),
                "attn_backward",
                [SM] * 2 + [VM] * 13,
                [like((blocks, rows, wide), bf16), both_shape, both_shape, like((16, width))],
                [vmem(blocks, 1, wide), vmem(rows, rows)],
                4 * unit,
                2 * moved,
            ),
            [sum_u, sum_d],
            [sum_u, sum_d],
        )
        sum_a = Job(net.scatter_sum(far, near))
        is_top = (jnp.arange(packed.shape[0]) == 2 * blocks + 6)[:, None]
        sum_s = Job(net.sum_max(packed, is_top))
        line_u = Job(net.scatter_line(*sum_u.value))
        step((), None, [sum_a, sum_d, sum_s], [sum_a, sum_s])
        tokens_grad = step(
            (act_ranges, grad_qkv, grad_first, tokens, weight_a),
            call(
                functools.partial(token_backward, dims),
                "token_backward",
                [SM] + [VM] * 4,
                [like((rows, width), bf16)],
                [vmem(rows, width)],
                unit,
                2 * moved,
            ),
            [sum_a, line_u, sum_s],
            [sum_a, sum_d, sum_s],
        )[0]
        step((), None, [sum_a, sum_s], [line_u])
        step((), None, [line_u], [sum_a, sum_s])
        line_a = Job(net.scatter_line(*sum_a.value))
        step((), None, [line_a, sum_d, sum_s], [line_a, sum_d, line_u, sum_s])
        step((), None, [line_a, sum_d, sum_s], [line_a, sum_d, sum_s])

        packed = sum_s.value
        down_grad, up_grad = (kept + last.astype(f32) for kept, last in (sum_d.value, line_u.value))
        down_grad = down_grad.T
        qkv_grad, out_grad = attn_grads(*line_a.value)
        own = lax.dynamic_slice_in_dim(packed, blocks + lane, 1)
        shared = packed[2 * blocks : 2 * blocks + 6]
        qv_bias_grad = jnp.concatenate([own[:, :cols], own[:, 2 * cols : 3 * cols]], 0)
        up_bias_grad = lax.dynamic_slice_in_dim(packed, lane, 1)[0]
        new_ranges = ema_decay * act_ranges + (1.0 - ema_decay) * packed[2 * blocks + 6, 0:512:128]
        return (
            layer_out,
            tokens_grad,
            qkv_grad,
            qv_bias_grad,
            out_grad,
            shared[0],
            shared[1],
            shared[2],
            up_grad,
            up_bias_grad,
            down_grad,
            shared[3],
            shared[4],
            shared[5],
            new_ranges,
        )

    return body


def solution(mesh):
    in_specs = (
        P(ALL, None),
        P(ALL, None),
        P(None, "dp", "tensor"),
        P(None, "tensor"),
        P("tensor", "dp"),
        P(),
        P(),
        P(),
        P("dp", "tensor"),
        P("tensor"),
        P("tensor", "dp"),
        P(),
        P(),
        P(),
        P(),
        P("dp"),
        P("dp"),
    )
    out_specs = (
        P(ALL, None),
        P(ALL, None),
        P(None, "dp", "tensor"),
        P(None, "tensor"),
        P("tensor", "dp"),
        P(),
        P(),
        P(),
        P("dp", "tensor"),
        P("tensor"),
        P("tensor", "dp"),
        P(),
        P(),
        P(),
        P(),
    )
    net = Grid() if mesh.shape["dp"] == 8 and mesh.shape["tensor"] == 4 else Plain()
    return jax.shard_map(make_body(net), mesh=mesh, in_specs=in_specs, out_specs=out_specs, check_vma=False)
```

```python
import functools
import itertools

import jax
import jax.numpy as jnp
from jax import lax
from jax.experimental import pallas as pl
from jax.experimental.pallas import tpu as pltpu
from jax.sharding import PartitionSpec as P

HEAD_DIM = 64
LONG_LEN = 512
SHORT_LEN = 128
ALL = ("dp", "tensor")

ema_decay = 0.9
epsilon = 1e-06
root_half = 0.7071067811865476
density_scale = 0.3989422804014327
score_scale = HEAD_DIM ** (-0.5)
NEG = -1000000000.0

f32 = jnp.float32
bf16 = jnp.bfloat16


def mm(left, right):
    return jnp.dot(left, right, preferred_element_type=f32)


def mm_tn(left, right):
    return lax.dot_general(left, right, (((0,), (0,)), ((), ())), preferred_element_type=f32)


def mm_nt(left, right):
    return lax.dot_general(left, right, (((1,), (1,)), ((), ())), preferred_element_type=f32)


def _lin(z, y, x, c):
    return (z * 2 + y) * 4 + x * 2 + c


def _perm(fn):
    out = []
    for z, y, x, c in itertools.product(range(4), range(2), range(2), range(2)):
        out.append((_lin(z, y, x, c), _lin(*fn(z, y, x, c))))
    return out


PC = _perm(lambda z, y, x, c: (z, y, x, 1 - c))
PX = _perm(lambda z, y, x, c: (z, y, 1 - x, c))
PY = _perm(lambda z, y, x, c: (z, 1 - y, x, c))
PZ1 = _perm(lambda z, y, x, c: (z ^ 1, y, x, c))
PZ2 = _perm(lambda z, y, x, c: (z ^ 2, y, x, c))


def tie(*trees):
    leaves, spec = jax.tree.flatten(trees)
    return jax.tree.unflatten(spec, lax.optimization_barrier(leaves))


class Job:
    def __init__(self, stages):
        self.stages, self.value, self.out, self.flight, self.over = stages, None, [], [], False
        self.take(None)

    def take(self, got):
        if not self.over:
            try:
                self.out = self.stages.send(got)
            except StopIteration as stop:
                self.value, self.out, self.over = stop.value, [], True


def step(ins, run=None, start=(), finish=()):
    ins, sends = tie(ins, [[value for value, _ in job.out] for job in start])
    for job, values in zip(start, sends):
        job.flight = [lax.ppermute(v, ALL, perm) for v, (_, perm) in zip(values, job.out)]
    outs = run(*ins) if run else ins
    outs, got = tie(outs, [job.flight for job in finish])
    for job, values in zip(finish, got):
        job.flight = []
        job.take(values)
    return outs


class Pieces:
    def __init__(self, plan):
        self.bufs, self.plan = {}, plan

    def part(self, lanes):
        plan = [p for p in self.plan if p[1] in lanes]
        names = sorted({p[0] for p in plan})
        return [self.bufs[n] for n in names], [(names.index(b), lane - lanes[0], at, col) for b, lane, at, col in plan]


class Grid:
    parts = 8

    @staticmethod
    def gather(shard, pieces):
        own = shard[None]
        for base, lane in ((0, 0), (5, 1)):
            pieces.plan.append((base, lane, (4, 4, 2, 0, 0), 0))
            pieces.plan.append((base + 1, lane, (4, 4, 2, 1, 0), 0))
            pieces.plan.append((base + 2, lane + 2, (4, 4, 2, 0, 0), 0))
            pieces.plan.append((base + 3, lane + 2, (2, 4, 0, 1, 0), 0))
            pieces.plan.append((base + 4, lane + 2, (2, 4, 0, 3, 0), 0))
        (far_z,) = yield [(own, PZ2)]
        pair = jnp.concatenate([own, far_z], 0)
        (near_z,) = yield [(pair, PZ1)]
        line = jnp.concatenate([pair, near_z], 0)
        over_x, over_y, line_far = yield [(line, PX), (line, PY), (line, PC)]
        pieces.bufs.update({0: line, 1: over_y, 2: over_x, 5: line_far})
        diag_x, diag_y, over_y_far, over_x_far = yield [
            (over_y[:2], PX),
            (over_x[2:], PY),
            (over_y, PC),
            (over_x, PC),
        ]
        pieces.bufs.update({3: diag_x, 4: diag_y, 6: over_y_far, 7: over_x_far})
        diag_x_far, diag_y_far = yield [(diag_x, PC), (diag_y, PC)]
        pieces.bufs.update({8: diag_x_far, 9: diag_y_far})

    @staticmethod
    def gather_plane_first(shard, pieces, first_col):
        own = shard[None]
        over_x, over_y = yield [(own, PX), (own, PY)]
        (diag,) = yield [(over_y, PX)]
        plane = jnp.concatenate([own, over_y, over_x, diag], 0)
        (far_z,) = yield [(plane, PZ2)]
        half = jnp.concatenate([plane, far_z], 0)
        (near_z,) = yield [(half, PZ1)]
        half_far, near_z_far = yield [(half, PC), (near_z, PC)]
        for n, (buf, core) in enumerate(((half, 0), (near_z, 0), (half_far, 1), (near_z_far, 1))):
            near = 2 * (n % 2)
            name = 20 + n
            pieces.bufs[name] = buf
            for x in range(2):
                pieces.plan.append((name, 2 * x + core, (4, 1, 4, near, 2), first_col + x))

    @staticmethod
    def slot(block, dp):
        place = block ^ dp
        return (place & 1) * 4 + (place & 2) + (place >> 2)

    @staticmethod
    def scatter_sum(far, near):
        (got,) = yield [(far, PC)]
        out_x, out_y = add_first(near, got)
        from_x, from_y = yield [(out_x, PX), (out_y, PY)]
        out_x, out_y = add_second(near, got, from_x, from_y)
        in_x, in_y = yield [(out_x, PX), (out_y, PY)]
        return near, got, in_x, in_y

    @staticmethod
    def scatter_line(near, got, in_x, in_y):
        out_z, kept = add_third(near, got, in_x, in_y)
        (from_z,) = yield [(out_z, PZ1)]
        out_z, kept = add_fourth(kept, from_z)
        (last,) = yield [(out_z, PZ2)]
        return kept, last

    @staticmethod
    def scatter_z_first(far, near):
        (got,) = yield [(far, PC)]
        out_1, out_0 = add_near_z(near, got)
        (from_1,) = yield [(out_1, PZ1)]
        out_x, out_y = add_corner(near, got, from_1)
        from_x, from_y, from_0 = yield [(out_x, PX), (out_y, PY), (out_0, PZ1)]
        out_x, out_y = add_sides(near, got, from_1, from_0, from_x, from_y)
        in_x, in_y = yield [(out_x, PX), (out_y, PY)]
        out_z, kept = add_own(near, got, from_0, in_x, in_y)
        (last,) = yield [(out_z, PZ2)]
        return kept, last

    @staticmethod
    def gather_lane(vec):
        (other,) = yield [(vec, PX)]
        pair = jnp.stack([vec, other])
        (more,) = yield [(pair, PC)]
        return jnp.stack([pair, more], 1).reshape((4,) + vec.shape)

    @staticmethod
    def sum_max(both, is_top):
        for perm in (PC, PZ1, PZ2, PX, PY):
            (other,) = yield [(both, perm)]
            both = jnp.where(is_top, jnp.maximum(both, other), both + other)
        return both

    @staticmethod
    def me():
        return lax.axis_index("dp"), lax.axis_index("tensor")


class Plain:
    parts = 1

    @staticmethod
    def gather(shard, pieces, first_col=0):
        rows = lax.all_gather(shard, "dp", axis=0, tiled=True)
        full = lax.all_gather(rows, "tensor", axis=0)
        for k in range(full.shape[0]):
            pieces.plan.append((first_col + k, k, None, first_col))
            pieces.bufs[first_col + k] = full[k][None]
        return
        yield

    gather_plane_first = gather

    @staticmethod
    def slot(block, dp):
        return block

    @staticmethod
    def scatter_sum(far, near):
        grads = jnp.stack([near[0], far[0], near[1], far[1]]).astype(f32)
        return (grads.reshape((4, -1, grads.shape[-1])),)
        yield

    @staticmethod
    def scatter_line(grads):
        own = lax.psum_scatter(grads, "tensor", scatter_dimension=0, tiled=False)
        own = lax.psum_scatter(own, "dp", scatter_dimension=0, tiled=True)
        return own, jnp.zeros_like(own)
        yield

    @staticmethod
    def scatter_z_first(far, near):
        grads = yield from Plain.scatter_sum(far, near)
        return (yield from Plain.scatter_line(*grads))

    @staticmethod
    def gather_lane(vec):
        return lax.all_gather(vec, "tensor", axis=0)
        yield

    @staticmethod
    def sum_max(both, is_top):
        return jnp.where(is_top, lax.pmax(both, ALL), lax.psum(both, ALL))
        yield

    @staticmethod
    def me():
        return 0, 0


VM = pl.BlockSpec(memory_space=pltpu.VMEM)
SM = pl.BlockSpec(memory_space=pltpu.SMEM)
VMEM_MIB = 14


def like(shape, dtype=f32):
    return jax.ShapeDtypeStruct(shape, dtype)


def call(kernel, name, specs, outs, scratch=(), flops=0, moved=0):
    return pl.pallas_call(
        kernel,
        name=name,
        out_shape=outs,
        in_specs=specs,
        out_specs=[VM] * len(outs),
        scratch_shapes=list(scratch),
        compiler_params=pltpu.CompilerParams(vmem_limit_bytes=VMEM_MIB * 2**20),
        cost_estimate=pl.CostEstimate(flops=flops, bytes_accessed=moved, transcendentals=0),
    )


def glue(kernel, outs, *ins):
    return call(kernel, kernel.__name__, [VM] * len(ins), outs)(*ins)


def add_first(near, got):
    def first_sums(near, got, out_x, out_y):
        for k in range(2):
            out_x[k] = (near[1, 4 + k].astype(f32) + got[1, 4 + k].astype(f32)).astype(bf16)
            out_y[k] = (near[1, 6 + k].astype(f32) + got[1, 6 + k].astype(f32)).astype(bf16)

    part = like((2,) + near.shape[2:], bf16)
    return glue(first_sums, [part, part], near, got)


def add_second(near, got, from_x, from_y):
    def second_sums(near, got, from_x, from_y, out_x, out_y):
        for k in range(4):
            over_x = near[1, k].astype(f32) + got[1, k].astype(f32)
            over_y = near[0, 4 + k].astype(f32) + got[0, 4 + k].astype(f32)
            if k < 2:
                over_y = over_y + from_x[k].astype(f32)
            else:
                over_x = over_x + from_y[k - 2].astype(f32)
            out_x[k] = over_x.astype(bf16)
            out_y[k] = over_y.astype(bf16)

    part = like((4,) + near.shape[2:], bf16)
    return glue(second_sums, [part, part], near, got, from_x, from_y)


def add_third(near, got, in_x, in_y):
    def third_sums(near, got, in_x, in_y, out, kept):
        for k in range(4):
            total = near[0, k].astype(f32) + got[0, k].astype(f32) + in_x[k].astype(f32) + in_y[k].astype(f32)
            if k < 2:
                kept[k] = total
            else:
                out[k - 2] = total.astype(bf16)

    shape = (2,) + near.shape[2:]
    return glue(third_sums, [like(shape, bf16), like(shape)], near, got, in_x, in_y)


def add_fourth(kept, from_z):
    def fourth_sums(kept, from_z, out, mine):
        mine[...] = kept[0] + from_z[0].astype(f32)
        out[...] = (kept[1] + from_z[1].astype(f32)).astype(bf16)

    shape = kept.shape[1:]
    return glue(fourth_sums, [like(shape, bf16), like(shape)], kept, from_z)


def add_near_z(near, got):
    def near_z_sums(near, got, out_1, out_0):
        for x, out in ((1, out_1), (0, out_0)):
            for y in range(2):
                for k in range(2):
                    at = 4 * y + 2 + k
                    out[2 * y + k] = (near[x, at].astype(f32) + got[x, at].astype(f32)).astype(bf16)

    part = like((4,) + near.shape[2:], bf16)
    return glue(near_z_sums, [part, part], near, got)


def three(near, got, from_z, x, y, k):
    return near[x, 4 * y + k].astype(f32) + got[x, 4 * y + k].astype(f32) + from_z[2 * y + k].astype(f32)


def add_corner(near, got, from_1):
    def corner_sums(near, got, from_1, out_x, out_y):
        out_x[...] = three(near, got, from_1, 1, 1, 0).astype(bf16)
        out_y[...] = three(near, got, from_1, 1, 1, 1).astype(bf16)

    part = like(near.shape[2:], bf16)
    return glue(corner_sums, [part, part], near, got, from_1)


def add_sides(near, got, from_1, from_0, from_x, from_y):
    def side_sums(near, got, from_1, from_0, from_x, from_y, out_x, out_y):
        out_x[0] = three(near, got, from_1, 1, 0, 0).astype(bf16)
        out_x[1] = (three(near, got, from_1, 1, 0, 1) + from_y[...].astype(f32)).astype(bf16)
        out_y[0] = (three(near, got, from_0, 0, 1, 0) + from_x[...].astype(f32)).astype(bf16)
        out_y[1] = three(near, got, from_0, 0, 1, 1).astype(bf16)

    part = like((2,) + near.shape[2:], bf16)
    return glue(side_sums, [part, part], near, got, from_1, from_0, from_x, from_y)


def add_own(near, got, from_0, in_x, in_y):
    def own_sums(near, got, from_0, in_x, in_y, out, kept):
        kept[...] = three(near, got, from_0, 0, 0, 0) + in_x[0].astype(f32) + in_y[0].astype(f32)
        out[...] = (three(near, got, from_0, 0, 0, 1) + in_x[1].astype(f32) + in_y[1].astype(f32)).astype(bf16)

    shape = near.shape[2:]
    return glue(own_sums, [like(shape, bf16), like(shape)], near, got, from_0, in_x, in_y)


def attn_grads(kept, last):
    rows, width = kept.shape
    cols = width // 4

    def attn_sums(kept, last, qkv, out):
        total = kept[...] + last[...].astype(f32)
        for j in range(3):
            qkv[j] = total[:, j * cols : (j + 1) * cols]
        out[...] = total[:, 3 * cols :].T

    return glue(attn_sums, [like((3, rows, cols)), like((cols, rows))], kept, last)


def attn_shard(qkv_weight, out_weight):
    _, rows, cols = qkv_weight.shape

    def attn_weights(qkv, out_weight, out):
        for j in range(3):
            out[:, j * cols : (j + 1) * cols] = qkv[j].astype(bf16)
        out[:, 3 * cols :] = out_weight[...].T.astype(bf16)

    return glue(attn_weights, [like((rows, 4 * cols), bf16)], qkv_weight, out_weight)[0]


def assemble(plan, bufs, dst, dp):
    for buf, lane, places, col in plan:
        src = bufs[buf]
        _, rows, width = src.shape
        x, col = (col & 1, col - (col & 1))
        cols = pl.ds(col, width)
        if places is None:
            dst[lane, :, cols] = src[0]
            continue
        count, a, b, c, skip = places

        def move(i, carry):
            place = a * (i & 1) + b * (i >> 1) + c
            at = pl.multiple_of((dp ^ place) * rows, rows)
            dst[lane, pl.ds(at, rows), cols] = src[i + skip * ((i >> 1) + x)]
            return carry

        lax.fori_loop(0, count, move, 0)


def row(vec):
    return vec[...].reshape(1, -1)


def row_stats(summed):
    centered = summed - jnp.mean(summed, axis=-1, keepdims=True)
    inv = lax.rsqrt(jnp.mean(centered * centered, axis=-1, keepdims=True) + epsilon)
    return centered * inv, inv


def norm_backward(scaled, normed, inv):
    row_mean = jnp.mean(scaled, axis=-1, keepdims=True)
    row_cross = jnp.mean(scaled * normed, axis=-1, keepdims=True)
    return inv * (scaled - row_mean - normed * row_cross)


def col_sum(values):
    return jnp.sum(values, axis=0, keepdims=True)


def top_of(values):
    return jnp.full((1, 128), jnp.max(jnp.abs(values)), f32)


def fill_mask(mask, longs, shorts):
    per_block = LONG_LEN // SHORT_LEN
    block = lax.axis_index("tensor")
    n_long = longs.shape[0]
    is_long = block < n_long
    whole = longs[jnp.minimum(block, n_long - 1)]
    first = jnp.maximum(block - n_long, 0) * per_block
    shift = jnp.where(is_long, LONG_LEN.bit_length() - 1, SHORT_LEN.bit_length() - 1)
    size = jnp.where(is_long, LONG_LEN, SHORT_LEN)
    k_pos = lax.broadcasted_iota(jnp.int32, (LONG_LEN, 1), 0)
    q_pos = lax.broadcasted_iota(jnp.int32, (1, LONG_LEN), 1)
    k_seg = lax.shift_right_logical(k_pos, jnp.full_like(k_pos, shift))
    q_seg = lax.shift_right_logical(q_pos, jnp.full_like(q_pos, shift))
    limit = jnp.zeros_like(k_pos)
    for j in range(per_block):
        limit = jnp.where(k_seg == j, jnp.where(is_long, whole, shorts[first + j]), limit)
    k_seg = jnp.where(k_pos - k_seg * size < limit, k_seg, -1)
    mask[...] = jnp.where(k_seg == q_seg, 0.0, NEG)


def attn_forward(net, plan, nb, dims, lim, longs, shorts, tokens, bias, *rest):
    blocks, cols, width = dims
    bufs, rest = rest[:nb], rest[nb:]
    qkv_out, lse_out, in_t, ctx_low, ctx_slope, top_out, weight, in_low, mask, ctx_t, top_ctx = rest
    heads = cols // HEAD_DIM
    low_q = 3 * cols + HEAD_DIM
    assemble(plan, bufs, weight, net.me()[0])
    inputs = tokens[...].astype(f32)
    in_low[...] = jnp.clip(inputs, -lim[0], lim[0]).astype(bf16)
    in_t[...] = in_low[...].T
    top_out[0:1, :] = top_of(inputs)
    fill_mask(mask, longs, shorts)
    ctx_t[0:HEAD_DIM, :] = jnp.zeros((HEAD_DIM, ctx_t.shape[1]), f32)
    top_ctx[...] = jnp.zeros_like(top_ctx)
    inv_limit = 1.0 / jnp.full((1, 1), lim[1], f32)

    def each(lane, carry):
        qkv = (mm(in_low[...], weight[lane, :, :low_q]) + bias[lane, :, :low_q]).astype(bf16)
        qkv_out[lane] = qkv
        for h in range(heads):
            at = h * HEAD_DIM
            q = qkv[:, at : at + HEAD_DIM]
            k = qkv[:, cols + at : cols + at + HEAD_DIM]
            v = qkv[:, 2 * cols + at : 2 * cols + at + HEAD_DIM]
            scores = mm_nt(k, q) * score_scale + mask[...]
            peak = jnp.max(scores, axis=0, keepdims=True)
            grown = jnp.exp(scores - peak)
            total = jnp.sum(grown, axis=0, keepdims=True)
            lse_out[lane, h : h + 1, :] = peak + jnp.log(total)
            shares = (grown * (1.0 / total)).astype(bf16)
            ctx_t[HEAD_DIM + at : 2 * HEAD_DIM + at, :] = mm_tn(v, shares)
        context = ctx_t[...].T
        bent = jnp.tanh(context * inv_limit)
        ctx_low[lane] = (lim[1] * bent).astype(bf16)
        ctx_slope[lane] = 1.0 - bent * bent
        top_ctx[...] = jnp.maximum(top_ctx[...], jnp.max(jnp.abs(context).reshape(-1, 8, context.shape[1]), axis=0))
        return carry

    lax.fori_loop(0, blocks, each, 0)
    top_out[1:2, :] = top_of(top_ctx[...])


def attn_finish(dims, lim, ctx_low, tokens, out_bias, gain, shift, weight, *outs):
    blocks, cols, width = dims
    normed_out, inv_out, middle_out, mid_slope, mid_low, mid_t, top_out, acc = outs
    at = 3 * cols - HEAD_DIM
    acc[...] = tokens[...].astype(f32) + row(out_bias)

    def each(lane, carry):
        acc[...] += mm_nt(ctx_low[lane], weight[lane, :, at:])
        return carry

    lax.fori_loop(0, blocks, each, 0)
    normed, inv = row_stats(acc[...])
    normed_out[...] = normed
    inv_out[...] = inv
    middle = normed * row(gain) + row(shift)
    middle_out[...] = middle
    bent = jnp.tanh(middle * (1.0 / jnp.full((1, 1), lim[2], f32)))
    low = (lim[2] * bent).astype(bf16)
    mid_low[...] = low
    mid_slope[...] = 1.0 - bent * bent
    mid_t[...] = low.T
    top_out[...] = jnp.broadcast_to(top_of(middle), top_out.shape)


def up_forward(net, plan, nb, first, low_q, lim, mid_low, bias, *rest):
    bufs, rest = rest[:nb], rest[nb:]
    act_out, slope_out, top_out, weight, top_hid = rest
    assemble(plan, bufs, weight, net.me()[0])
    top_hid[...] = jnp.zeros_like(top_hid)
    inv_limit = 1.0 / jnp.full((1, 1), lim[3], f32)

    rows = mid_low.shape[0] // 2

    def each(n, carry):
        lane = n // 2
        part = pl.ds(pl.multiple_of((n % 2) * rows, rows), rows)
        up = mm(mid_low[part, :], weight[lane]) + bias[first + lane, :, low_q:]
        half = 0.5 * (1.0 + lax.erf(up * root_half))
        hidden = up * half
        top_hid[...] = jnp.maximum(top_hid[...], jnp.max(jnp.abs(hidden).reshape(-1, 8, hidden.shape[1]), axis=0))
        bent = jnp.tanh(hidden * inv_limit)
        act_out[lane, part] = (lim[3] * bent).astype(bf16)
        slope_out[lane, part] = (1.0 - bent * bent) * (half + up * jnp.exp(-0.5 * up * up) * density_scale)
        return carry

    lax.fori_loop(0, 2 * weight.shape[0], each, 0)
    top_out[...] = jnp.broadcast_to(top_of(top_hid[...]), top_out.shape)


def down_both(net, plan, nb, act0, act1, slope0, slope1, middle, cotangent, down_bias, gain, shift, *rest):
    bufs, rest = rest[:nb], rest[nb:]
    layer_out, grad_out, ffn_t, sums, grad_up, up_sums, weight, acc, ffn_low = rest
    assemble(plan, bufs, weight, net.me()[0])
    acc[...] = middle[...] + row(down_bias)
    half = act0.shape[0]
    for act, first in ((act0, 0), (act1, half)):

        def each(i, carry):
            acc[...] += mm_nt(act[i], weight[first + i])
            return carry

        lax.fori_loop(0, half, each, 0)
    normed, inv = row_stats(acc[...])
    layer_out[...] = (normed * row(gain) + row(shift)).astype(bf16)
    incoming = cotangent[...].astype(f32)
    grad = norm_backward(incoming * row(gain), normed, inv)
    grad_out[...] = grad
    ffn_low[...] = grad.astype(bf16)
    ffn_t[...] = ffn_low[...].T
    sums[...] = jnp.zeros_like(sums)
    sums[0:1, :] = col_sum(grad)
    sums[1:2, :] = col_sum(incoming * normed)
    sums[2:3, :] = col_sum(incoming)
    lane_me = net.me()[1]
    for slope, first in ((slope0, 0), (slope1, half)):

        def back(i, carry):
            low = (mm(ffn_low[...], weight[first + i]) * slope[i]).astype(bf16)
            grad_up[first + i] = low
            up_sums[(first + i) ^ lane_me] = col_sum(low.astype(f32))
            return carry

        lax.fori_loop(0, half, back, 0)


def weight_grad(net, left_t, *rest):
    *rights, far, near = rest
    rows = left_t.shape[0] // net.parts
    dp = net.me()[0]
    half = far.shape[0]
    for x in range(half):
        for out, lane in ((far, 2 * x + 1), (near, 2 * x)):
            right = rights[lane // rights[0].shape[0]]
            grad = mm(left_t[...], right[lane % right.shape[0]]).astype(bf16)
            for block in range(net.parts):
                out[x, net.slot(block, dp)] = grad[block * rows : (block + 1) * rows]


def mid_backward(grad_up, grad_second, mid_slope, normed, inv, gain, weight0, weight1, grad_out, attn_low, attn_t, sums, acc):
    acc[...] = jnp.zeros_like(acc)
    half = weight0.shape[0]
    for weight, first in ((weight0, 0), (weight1, half)):

        def each(i, carry):
            acc[...] += mm_nt(grad_up[first + i], weight[i])
            return carry

        lax.fori_loop(0, half, each, 0)
    incoming = grad_second[...] + acc[...] * mid_slope[...]
    grad = norm_backward(incoming * row(gain), normed[...], inv[...])
    grad_out[...] = grad
    attn_low[...] = grad.astype(bf16)
    attn_t[...] = attn_low[...].T
    sums[...] = jnp.zeros_like(sums)
    sums[0:1, :] = col_sum(grad)
    sums[1:2, :] = col_sum(incoming * normed[...])
    sums[2:3, :] = col_sum(incoming)


def heads_backward(first, dims, lane_me, qkv, lse, attn_low, weight, ctx_slope, mask, grad_ctx, out, sums):
    blocks, cols, width = dims
    heads = cols // HEAD_DIM

    def each(i, carry):
        lane = first + i
        part = mm(attn_low[...], weight[lane, :, 3 * cols - HEAD_DIM :])
        grad_ctx[...] = (part * ctx_slope[lane]).astype(bf16)
        for h in range(heads):
            at = h * HEAD_DIM
            q = qkv[lane, :, at : at + HEAD_DIM]
            k = qkv[lane, :, cols + at : cols + at + HEAD_DIM]
            v = qkv[lane, :, 2 * cols + at : 2 * cols + at + HEAD_DIM]
            grad = grad_ctx[:, HEAD_DIM + at : 2 * HEAD_DIM + at]
            shares = jnp.exp(mm_nt(k, q) * score_scale + mask[...] - lse[lane, h : h + 1, :])
            grad_shares = mm_nt(v, grad)
            inner = jnp.sum(shares * grad_shares, axis=0, keepdims=True)
            grad_scores = (shares * (grad_shares - inner)).astype(bf16)
            grad_v = mm(shares.astype(bf16), grad)
            grad_k = mm(grad_scores, q) * score_scale
            grad_q = (mm_tn(k, grad_scores) * score_scale).T
            out[i, :, at : at + HEAD_DIM] = grad_q.astype(bf16)
            out[i, :, cols + at : cols + at + HEAD_DIM] = grad_k.astype(bf16)
            out[i, :, 2 * cols + at : 2 * cols + at + HEAD_DIM] = grad_v.astype(bf16)
        out[i, :, 3 * cols :] = jnp.zeros((out.shape[1], HEAD_DIM), bf16)
        sums[lane ^ lane_me] = col_sum(out[i].astype(f32))
        return carry

    lax.fori_loop(0, out.shape[0], each, 0)


def attn_backward(net, first, dims, longs, shorts, qkv, lse, attn_low, weight, ctx_slope, out, sums, mask, grad_ctx):
    fill_mask(mask, longs, shorts)
    sums[...] = jnp.zeros_like(sums)
    heads_backward(first, dims, net.me()[1], qkv, lse, attn_low, weight, ctx_slope, mask, grad_ctx, out, sums)


def attn_backward_last(net, dims, longs, shorts, lim, qkv, lse, attn_low, weight, ctx_slope, *rest):
    blocks, cols, width = dims
    in_t, attn_t, ctx_low, grad_first, tokens, more_out, more, *rest = rest
    up_sums, sums_a, sums_b, tops_a, tops_m, top0, top1, *rest = rest
    far, near, packed, tokens_out, out, sums, mask, grad_ctx, acc = rest
    rows = in_t.shape[0] // net.parts
    half = far.shape[0]
    wide = 3 * cols + HEAD_DIM
    start = 3 * cols - HEAD_DIM
    dp, lane_me = net.me()
    fill_mask(mask, longs, shorts)
    sums[...] = more[...]
    heads_backward(0, dims, lane_me, qkv, lse, attn_low, weight, ctx_slope, mask, grad_ctx, out, sums)
    for x, grads in enumerate((out, more_out)):

        def weights(core, carry):
            left = mm(in_t[...], grads[core])
            right = mm(attn_t[...], ctx_low[2 * x + core])
            mixed = (left[:, start:] + right[:, : wide - start]).astype(bf16)
            left, right = left[:, :start].astype(bf16), right[:, wide - start :].astype(bf16)
            for to, wanted in ((near, 0), (far, 1)):

                @pl.when(core == wanted)
                def _():
                    for block in range(net.parts):
                        rs = slice(block * rows, (block + 1) * rows)
                        place = net.slot(block, dp)
                        to[x, place, :, :start] = left[rs]
                        to[x, place, :, start:wide] = mixed[rs]
                        to[x, place, :, wide:] = right[rs]

            return carry

        lax.fori_loop(0, 2, weights, 0)
    acc[...] = jnp.zeros_like(acc)
    for grads, first in ((out, 0), (more_out, half)):

        def back(i, carry):
            acc[...] += mm_nt(grads[i], weight[first + i, :, :wide])
            return carry

        lax.fori_loop(0, half, back, 0)
    inputs = tokens[...].astype(f32)
    tokens_out[...] = (grad_first[...] + jnp.where(jnp.abs(inputs) <= lim[0], acc[...], 0.0)).astype(bf16)
    packed[...] = jnp.zeros_like(packed)
    for j in range(blocks):
        packed[j : j + 1, :] = up_sums[j]
        packed[blocks + j : blocks + j + 1, : sums.shape[2]] = sums[j]
    packed[2 * blocks : 2 * blocks + 3, :] = sums_a[0:3, :]
    packed[2 * blocks + 3 : 2 * blocks + 6, :] = sums_b[0:3, :]
    tops = (tops_a[0:1, :], tops_a[1:2, :], tops_m[0:1, :], jnp.maximum(top0[0:1, :], top1[0:1, :]))
    for j, top in enumerate(tops):
        packed[2 * blocks + 6 : 2 * blocks + 7, 128 * j : 128 * j + 128] = top


def make_body(net):
    def body(
        tokens,
        cotangent,
        qkv_weight,
        qv_bias,
        out_weight,
        out_bias,
        first_gain,
        first_shift,
        up_weight,
        up_bias,
        down_weight,
        down_bias,
        second_gain,
        second_shift,
        act_ranges,
        long_lengths,
        short_lengths,
    ):
        lane = lax.axis_index("tensor")
        rows, width = tokens.shape
        assert rows == LONG_LEN
        cols = qkv_weight.shape[2]
        up_cols = up_weight.shape[1]
        blocks = lax.axis_size("tensor")
        half = blocks // 2
        dims = (blocks, cols, width)
        wide = 3 * cols + HEAD_DIM
        out_cols = cols + HEAD_DIM
        every = tuple(range(blocks))

        pieces_a, pieces_u, pieces_d = Pieces([]), Pieces([]), Pieces([])
        shard_a = attn_shard(qkv_weight, out_weight)
        shard_a, up_bias, down_weight = tie(shard_a, up_bias, down_weight)
        job_a = Job(net.gather(shard_a, pieces_a))
        bias_row = jnp.concatenate(
            [qv_bias[0], jnp.zeros((cols,), f32), qv_bias[1], jnp.zeros((HEAD_DIM,), f32), up_bias]
        )
        job_b = Job(net.gather_lane(bias_row[None]))
        job_u = Job(net.gather(up_weight.astype(bf16), pieces_u))
        shard_d = down_weight.T.astype(bf16)
        col = up_cols // 2
        job_d = Job(net.gather(shard_d[:, :col], pieces_d))
        job_p = Job(net.gather_plane_first(shard_d[:, col:], pieces_d, col))

        def vmem(*shape, dtype=f32):
            return pltpu.VMEM(shape, dtype)

        unit = 2 * rows * width * width * blocks
        moved = 2 * width * width * blocks

        step((), None, [job_a, job_p, job_b], [job_a, job_p, job_b])
        step((), None, [job_a, job_p, job_b], [job_a, job_p, job_b])
        step((), None, [job_a, job_u, job_d], [job_a, job_u, job_d])
        step((), None, [job_a, job_u], [job_a, job_u])
        step((), None, [job_a, job_u], [job_a])
        biases = job_b.value

        bufs, plan = pieces_a.part(every)
        qkv, lse, in_t, ctx_low, ctx_slope, tops_a, weight_a = step(
            (act_ranges, long_lengths, short_lengths, tokens, biases, *bufs),
            call(
                functools.partial(attn_forward, net, plan, len(bufs), dims),
                "attn_forward",
                [SM] * 3 + [VM] * 2 + [VM] * len(bufs),
                [
                    like((blocks, rows, wide), bf16),
                    like((blocks, 8, rows)),
                    like((width, rows), bf16),
                    like((blocks, rows, out_cols), bf16),
                    like((blocks, rows, out_cols)),
                    like((8, 128)),
                    like((blocks, width, 4 * cols), bf16),
                ],
                [vmem(rows, width, dtype=bf16), vmem(rows, rows), vmem(out_cols, rows), vmem(8, out_cols)],
                4 * unit,
                3 * moved,
            ),
            [job_d, job_p],
            [job_u, job_d, job_p],
        )
        normed, inv, middle, mid_slope, mid_low, mid_t, tops_m = step(
            (act_ranges, ctx_low, tokens, out_bias, first_gain, first_shift, weight_a),
            call(
                functools.partial(attn_finish, dims),
                "attn_finish",
                [SM] + [VM] * 6,
                [
                    like((rows, width)),
                    like((rows, 1)),
                    like((rows, width)),
                    like((rows, width)),
                    like((rows, width), bf16),
                    like((width, rows), bf16),
                    like((8, 128)),
                ],
                [vmem(rows, width)],
                2 * unit,
                2 * moved,
            ),
            [job_u, job_p],
            [job_u],
        )

        def up_part(lanes, start, finish):
            bufs, plan = pieces_u.part(lanes)
            return step(
                (act_ranges, mid_low, biases, *bufs),
                call(
                    functools.partial(up_forward, net, plan, len(bufs), lanes[0], wide),
                    f"up_forward_{lanes[0]}",
                    [SM] + [VM] * 2 + [VM] * len(bufs),
                    [
                        like((half, rows, up_cols), bf16),
                        like((half, rows, up_cols)),
                        like((8, 128)),
                        like((half, width, up_cols), bf16),
                    ],
                    [vmem(8, up_cols)],
                    2 * unit,
                    2 * moved,
                ),
                start,
                finish,
            )

        act0, slope0, top0, weight_u0 = up_part(every[:half], [job_u, job_d], [job_u])
        act1, slope1, top1, weight_u1 = up_part(every[half:], [], [job_d, job_p])
        step((), None, [job_d], [job_d])
        step((), None, [job_d, job_p], [job_d, job_p])
        bufs_d, plan_d = pieces_d.part(every)
        layer_out, grad_second, ffn_t, sums_b, grad_up, up_sums = step(
            (act0, act1, slope0, slope1, middle, cotangent, down_bias, second_gain, second_shift, *bufs_d),
            call(
                functools.partial(down_both, net, plan_d, len(bufs_d)),
                "down_both",
                [VM] * 9 + [VM] * len(bufs_d),
                [
                    like((rows, width), bf16),
                    like((rows, width)),
                    like((width, rows), bf16),
                    like((8, width)),
                    like((blocks, rows, up_cols), bf16),
                    like((blocks, 1, up_cols)),
                ],
                [
                    vmem(blocks, width, up_cols, dtype=bf16),
                    vmem(rows, width),
                    vmem(rows, width, dtype=bf16),
                ],
                2 * unit,
                4 * moved,
            ),
        )

        grad_shape = like((net.parts, width // net.parts, up_cols), bf16)
        both_shape = like((half,) + grad_shape.shape, bf16)

        def grad_of(name, left_t, rights, start=(), finish=()):
            return step(
                (left_t, *rights),
                call(
                    functools.partial(weight_grad, net),
                    name,
                    [VM] * (1 + len(rights)),
                    [both_shape, both_shape],
                    (),
                    unit,
                    moved,
                ),
                start,
                finish,
            )

        sum_d = Job(net.scatter_z_first(*grad_of("down_grad", ffn_t, (act0, act1))))
        sum_u = Job(net.scatter_sum(*grad_of("up_grad", mid_t, (grad_up,), [sum_d], [sum_d])))
        grad_first, attn_low, attn_t, sums_a = step(
            (grad_up, grad_second, mid_slope, normed, inv, first_gain, weight_u0, weight_u1),
            call(
                mid_backward,
                "mid_backward",
                [VM] * 8,
                [like((rows, width)), like((rows, width), bf16), like((width, rows), bf16), like((8, width))],
                [vmem(rows, width)],
                unit + unit // 3,
                3 * moved,
            ),
            [sum_u, sum_d],
            [sum_u],
        )
        grads_1, more = step(
            (long_lengths, short_lengths, qkv, lse, attn_low, weight_a, ctx_slope),
            call(
                functools.partial(attn_backward, net, half, dims),
                "attn_backward",
                [SM] * 2 + [VM] * 5,
                [like((half, rows, wide), bf16), like((blocks, 1, wide))],
                [vmem(rows, rows), vmem(rows, out_cols, dtype=bf16)],
                2 * unit,
                2 * moved,
            ),
            [sum_u],
            [sum_u, sum_d],
        )
        far, near, packed, tokens_grad = step(
            (long_lengths, short_lengths, act_ranges, qkv, lse, attn_low, weight_a, ctx_slope)
            + (in_t, attn_t, ctx_low, grad_first, tokens, grads_1, more)
            + (up_sums, sums_a, sums_b, tops_a, tops_m, top0, top1),
            call(
                functools.partial(attn_backward_last, net, dims),
                "attn_backward_last",
                [SM] * 3 + [VM] * 19,
                [both_shape, both_shape, like((16, width)), like((rows, width), bf16)],
                [
                    vmem(half, rows, wide, dtype=bf16),
                    vmem(blocks, 1, wide),
                    vmem(rows, rows),
                    vmem(rows, out_cols, dtype=bf16),
                    vmem(rows, width),
                ],
                4 * unit,
                2 * moved,
            ),
            [sum_u, sum_d],
            [sum_u, sum_d],
        )
        sum_a = Job(net.scatter_sum(far, near))
        is_top = (jnp.arange(packed.shape[0]) == 2 * blocks + 6)[:, None]
        sum_s = Job(net.sum_max(packed, is_top))
        line_u = Job(net.scatter_line(*sum_u.value))
        step((), None, [sum_a, sum_d, line_u, sum_s], [sum_a, sum_s])
        step((), None, [sum_a], [sum_a, sum_d, line_u])
        step((), None, [sum_a, sum_d, line_u, sum_s], [sum_a, sum_d, line_u, sum_s])
        line_a = Job(net.scatter_line(*sum_a.value))
        step((), None, [line_a, sum_s], [line_a, sum_s])
        step((), None, [line_a, sum_s], [sum_s])
        step((), None, [sum_s], [line_a, sum_s])

        packed = sum_s.value
        down_grad, up_grad = (kept + last.astype(f32) for kept, last in (sum_d.value, line_u.value))
        down_grad = down_grad.T
        qkv_grad, out_grad = attn_grads(*line_a.value)
        own = lax.dynamic_slice_in_dim(packed, blocks + lane, 1)
        shared = packed[2 * blocks : 2 * blocks + 6]
        qv_bias_grad = jnp.concatenate([own[:, :cols], own[:, 2 * cols : 3 * cols]], 0)
        up_bias_grad = lax.dynamic_slice_in_dim(packed, lane, 1)[0]
        new_ranges = ema_decay * act_ranges + (1.0 - ema_decay) * packed[2 * blocks + 6, 0:512:128]
        return (
            layer_out,
            tokens_grad,
            qkv_grad,
            qv_bias_grad,
            out_grad,
            shared[0],
            shared[1],
            shared[2],
            up_grad,
            up_bias_grad,
            down_grad,
            shared[3],
            shared[4],
            shared[5],
            new_ranges,
        )

    return body


def solution(mesh):
    in_specs = (
        P(ALL, None),
        P(ALL, None),
        P(None, "dp", "tensor"),
        P(None, "tensor"),
        P("tensor", "dp"),
        P(),
        P(),
        P(),
        P("dp", "tensor"),
        P("tensor"),
        P("tensor", "dp"),
        P(),
        P(),
        P(),
        P(),
        P("dp"),
        P("dp"),
    )
    out_specs = (
        P(ALL, None),
        P(ALL, None),
        P(None, "dp", "tensor"),
        P(None, "tensor"),
        P("tensor", "dp"),
        P(),
        P(),
        P(),
        P("dp", "tensor"),
        P("tensor"),
        P("tensor", "dp"),
        P(),
        P(),
        P(),
        P(),
    )
    net = Grid() if mesh.shape["dp"] == 8 and mesh.shape["tensor"] == 4 else Plain()
    return jax.shard_map(make_body(net), mesh=mesh, in_specs=in_specs, out_specs=out_specs, check_vma=False)
```

```python
import functools
import itertools

import jax
import jax.numpy as jnp
from jax import lax
from jax.experimental import pallas as pl
from jax.experimental.pallas import tpu as pltpu
from jax.sharding import PartitionSpec as P

HEAD_DIM = 64
LONG_LEN = 512
SHORT_LEN = 128
ALL = ("dp", "tensor")

ema_decay = 0.9
epsilon = 1e-06
root_half = 0.7071067811865476
density_scale = 0.3989422804014327
score_scale = HEAD_DIM ** (-0.5)
NEG = -1000000000.0

f32 = jnp.float32
bf16 = jnp.bfloat16


def mm(left, right):
    return jnp.dot(left, right, preferred_element_type=f32)


def mm_tn(left, right):
    return lax.dot_general(left, right, (((0,), (0,)), ((), ())), preferred_element_type=f32)


def mm_nt(left, right):
    return lax.dot_general(left, right, (((1,), (1,)), ((), ())), preferred_element_type=f32)


def _lin(z, y, x, c):
    return (z * 2 + y) * 4 + x * 2 + c


def _perm(fn):
    out = []
    for z, y, x, c in itertools.product(range(4), range(2), range(2), range(2)):
        out.append((_lin(z, y, x, c), _lin(*fn(z, y, x, c))))
    return out


PC = _perm(lambda z, y, x, c: (z, y, x, 1 - c))
PX = _perm(lambda z, y, x, c: (z, y, 1 - x, c))
PY = _perm(lambda z, y, x, c: (z, 1 - y, x, c))
PZ1 = _perm(lambda z, y, x, c: (z ^ 1, y, x, c))
PZ2 = _perm(lambda z, y, x, c: (z ^ 2, y, x, c))


def tie(*trees):
    leaves, spec = jax.tree.flatten(trees)
    return jax.tree.unflatten(spec, lax.optimization_barrier(leaves))


class Job:
    def __init__(self, stages):
        self.stages, self.value, self.out, self.flight, self.over = stages, None, [], [], False
        self.take(None)

    def take(self, got):
        if not self.over:
            try:
                self.out = self.stages.send(got)
            except StopIteration as stop:
                self.value, self.out, self.over = stop.value, [], True


def step(ins, run=None, start=(), finish=()):
    ins, sends = tie(ins, [[value for value, _ in job.out] for job in start])
    for job, values in zip(start, sends):
        job.flight = [lax.ppermute(v, ALL, perm) for v, (_, perm) in zip(values, job.out)]
    outs = run(*ins) if run else ins
    outs, got = tie(outs, [job.flight for job in finish])
    for job, values in zip(finish, got):
        job.flight = []
        job.take(values)
    return outs


class Pieces:
    def __init__(self, plan):
        self.bufs, self.plan = {}, plan

    def part(self, lanes):
        plan = [p for p in self.plan if p[1] in lanes]
        names = sorted({p[0] for p in plan})
        return [self.bufs[n] for n in names], [(names.index(b), lane - lanes[0], at, col) for b, lane, at, col in plan]


class Grid:
    parts = 8

    @staticmethod
    def gather(shard, pieces):
        own = shard[None]
        for base, lane in ((0, 0), (5, 1)):
            pieces.plan.append((base, lane, (4, 4, 2, 0, 0), 0))
            pieces.plan.append((base + 1, lane, (4, 4, 2, 1, 0), 0))
            pieces.plan.append((base + 2, lane + 2, (4, 4, 2, 0, 0), 0))
            pieces.plan.append((base + 3, lane + 2, (2, 4, 0, 1, 0), 0))
            pieces.plan.append((base + 4, lane + 2, (2, 4, 0, 3, 0), 0))
        (far_z,) = yield [(own, PZ2)]
        pair = jnp.concatenate([own, far_z], 0)
        (near_z,) = yield [(pair, PZ1)]
        line = jnp.concatenate([pair, near_z], 0)
        over_x, over_y, line_far = yield [(line, PX), (line, PY), (line, PC)]
        pieces.bufs.update({0: line, 1: over_y, 2: over_x, 5: line_far})
        diag_x, diag_y, over_y_far, over_x_far = yield [
            (over_y[:2], PX),
            (over_x[2:], PY),
            (over_y, PC),
            (over_x, PC),
        ]
        pieces.bufs.update({3: diag_x, 4: diag_y, 6: over_y_far, 7: over_x_far})
        diag_x_far, diag_y_far = yield [(diag_x, PC), (diag_y, PC)]
        pieces.bufs.update({8: diag_x_far, 9: diag_y_far})

    @staticmethod
    def gather_plane_first(shard, pieces, first_col):
        own = shard[None]
        over_x, over_y = yield [(own, PX), (own, PY)]
        (diag,) = yield [(over_y, PX)]
        plane = jnp.concatenate([own, over_y, over_x, diag], 0)
        (far_z,) = yield [(plane, PZ2)]
        half = jnp.concatenate([plane, far_z], 0)
        (near_z,) = yield [(half, PZ1)]
        half_far, near_z_far = yield [(half, PC), (near_z, PC)]
        for n, (buf, core) in enumerate(((half, 0), (near_z, 0), (half_far, 1), (near_z_far, 1))):
            near = 2 * (n % 2)
            name = 20 + n
            pieces.bufs[name] = buf
            for x in range(2):
                pieces.plan.append((name, 2 * x + core, (4, 1, 4, near, 2), first_col + x))

    @staticmethod
    def slot(block, dp):
        place = block ^ dp
        return (place & 1) * 4 + (place & 2) + (place >> 2)

    @staticmethod
    def scatter_sum(far, near):
        (got,) = yield [(far, PC)]
        out_x, out_y = add_first(near, got)
        from_x, from_y = yield [(out_x, PX), (out_y, PY)]
        out_x, out_y = add_second(near, got, from_x, from_y)
        in_x, in_y = yield [(out_x, PX), (out_y, PY)]
        return near, got, in_x, in_y

    @staticmethod
    def scatter_line(near, got, in_x, in_y):
        out_z, kept = add_third(near, got, in_x, in_y)
        (from_z,) = yield [(out_z, PZ1)]
        out_z, kept = add_fourth(kept, from_z)
        (last,) = yield [(out_z, PZ2)]
        return kept, last

    @staticmethod
    def scatter_z_first(far, near):
        (got,) = yield [(far, PC)]
        out_1, out_0 = add_near_z(near, got)
        (from_1,) = yield [(out_1, PZ1)]
        out_x, out_y = add_corner(near, got, from_1)
        from_x, from_y, from_0 = yield [(out_x, PX), (out_y, PY), (out_0, PZ1)]
        out_x, out_y = add_sides(near, got, from_1, from_0, from_x, from_y)
        in_x, in_y = yield [(out_x, PX), (out_y, PY)]
        out_z, kept = add_own(near, got, from_0, in_x, in_y)
        (last,) = yield [(out_z, PZ2)]
        return kept, last

    @staticmethod
    def gather_lane(vec):
        (other,) = yield [(vec, PX)]
        pair = jnp.stack([vec, other])
        (more,) = yield [(pair, PC)]
        return jnp.stack([pair, more], 1).reshape((4,) + vec.shape)

    @staticmethod
    def sum_max(both, is_top):
        for perm in (PC, PZ1, PZ2, PX, PY):
            (other,) = yield [(both, perm)]
            both = jnp.where(is_top, jnp.maximum(both, other), both + other)
        return both

    @staticmethod
    def me():
        return lax.axis_index("dp"), lax.axis_index("tensor")


class Plain:
    parts = 1

    @staticmethod
    def gather(shard, pieces, first_col=0):
        rows = lax.all_gather(shard, "dp", axis=0, tiled=True)
        full = lax.all_gather(rows, "tensor", axis=0)
        for k in range(full.shape[0]):
            pieces.plan.append((first_col + k, k, None, first_col))
            pieces.bufs[first_col + k] = full[k][None]
        return
        yield

    gather_plane_first = gather

    @staticmethod
    def slot(block, dp):
        return block

    @staticmethod
    def scatter_sum(far, near):
        grads = jnp.stack([near[0], far[0], near[1], far[1]]).astype(f32)
        return (grads.reshape((4, -1, grads.shape[-1])),)
        yield

    @staticmethod
    def scatter_line(grads):
        own = lax.psum_scatter(grads, "tensor", scatter_dimension=0, tiled=False)
        own = lax.psum_scatter(own, "dp", scatter_dimension=0, tiled=True)
        return own, jnp.zeros_like(own)
        yield

    @staticmethod
    def scatter_z_first(far, near):
        grads = yield from Plain.scatter_sum(far, near)
        return (yield from Plain.scatter_line(*grads))

    @staticmethod
    def gather_lane(vec):
        return lax.all_gather(vec, "tensor", axis=0)
        yield

    @staticmethod
    def sum_max(both, is_top):
        return jnp.where(is_top, lax.pmax(both, ALL), lax.psum(both, ALL))
        yield

    @staticmethod
    def me():
        return 0, 0


VM = pl.BlockSpec(memory_space=pltpu.VMEM)
SM = pl.BlockSpec(memory_space=pltpu.SMEM)
VMEM_MIB = 8
ROOMY = ("down_both",)


def like(shape, dtype=f32):
    return jax.ShapeDtypeStruct(shape, dtype)


def call(kernel, name, specs, outs, scratch=(), flops=0, moved=0):
    return pl.pallas_call(
        kernel,
        name=name,
        out_shape=outs,
        in_specs=specs,
        out_specs=[VM] * len(outs),
        scratch_shapes=list(scratch),
        compiler_params=pltpu.CompilerParams(vmem_limit_bytes=(14 if name in ROOMY else VMEM_MIB) * 2**20),
        cost_estimate=pl.CostEstimate(flops=flops, bytes_accessed=moved, transcendentals=0),
    )


def glue(kernel, outs, *ins):
    return call(kernel, kernel.__name__, [VM] * len(ins), outs)(*ins)


def add_first(near, got):
    def first_sums(near, got, out_x, out_y):
        for k in range(2):
            out_x[k] = (near[1, 4 + k].astype(f32) + got[1, 4 + k].astype(f32)).astype(bf16)
            out_y[k] = (near[1, 6 + k].astype(f32) + got[1, 6 + k].astype(f32)).astype(bf16)

    part = like((2,) + near.shape[2:], bf16)
    return glue(first_sums, [part, part], near, got)


def add_second(near, got, from_x, from_y):
    def second_sums(near, got, from_x, from_y, out_x, out_y):
        for k in range(4):
            over_x = near[1, k].astype(f32) + got[1, k].astype(f32)
            over_y = near[0, 4 + k].astype(f32) + got[0, 4 + k].astype(f32)
            if k < 2:
                over_y = over_y + from_x[k].astype(f32)
            else:
                over_x = over_x + from_y[k - 2].astype(f32)
            out_x[k] = over_x.astype(bf16)
            out_y[k] = over_y.astype(bf16)

    part = like((4,) + near.shape[2:], bf16)
    return glue(second_sums, [part, part], near, got, from_x, from_y)


def add_third(near, got, in_x, in_y):
    def third_sums(near, got, in_x, in_y, out, kept):
        for k in range(4):
            total = near[0, k].astype(f32) + got[0, k].astype(f32) + in_x[k].astype(f32) + in_y[k].astype(f32)
            if k < 2:
                kept[k] = total
            else:
                out[k - 2] = total.astype(bf16)

    shape = (2,) + near.shape[2:]
    return glue(third_sums, [like(shape, bf16), like(shape)], near, got, in_x, in_y)


def add_fourth(kept, from_z):
    def fourth_sums(kept, from_z, out, mine):
        mine[...] = kept[0] + from_z[0].astype(f32)
        out[...] = (kept[1] + from_z[1].astype(f32)).astype(bf16)

    shape = kept.shape[1:]
    return glue(fourth_sums, [like(shape, bf16), like(shape)], kept, from_z)


def add_near_z(near, got):
    def near_z_sums(near, got, out_1, out_0):
        for x, out in ((1, out_1), (0, out_0)):
            for y in range(2):
                for k in range(2):
                    at = 4 * y + 2 + k
                    out[2 * y + k] = (near[x, at].astype(f32) + got[x, at].astype(f32)).astype(bf16)

    part = like((4,) + near.shape[2:], bf16)
    return glue(near_z_sums, [part, part], near, got)


def three(near, got, from_z, x, y, k):
    return near[x, 4 * y + k].astype(f32) + got[x, 4 * y + k].astype(f32) + from_z[2 * y + k].astype(f32)


def add_corner(near, got, from_1):
    def corner_sums(near, got, from_1, out_x, out_y):
        out_x[...] = three(near, got, from_1, 1, 1, 0).astype(bf16)
        out_y[...] = three(near, got, from_1, 1, 1, 1).astype(bf16)

    part = like(near.shape[2:], bf16)
    return glue(corner_sums, [part, part], near, got, from_1)


def add_sides(near, got, from_1, from_0, from_x, from_y):
    def side_sums(near, got, from_1, from_0, from_x, from_y, out_x, out_y):
        out_x[0] = three(near, got, from_1, 1, 0, 0).astype(bf16)
        out_x[1] = (three(near, got, from_1, 1, 0, 1) + from_y[...].astype(f32)).astype(bf16)
        out_y[0] = (three(near, got, from_0, 0, 1, 0) + from_x[...].astype(f32)).astype(bf16)
        out_y[1] = three(near, got, from_0, 0, 1, 1).astype(bf16)

    part = like((2,) + near.shape[2:], bf16)
    return glue(side_sums, [part, part], near, got, from_1, from_0, from_x, from_y)


def add_own(near, got, from_0, in_x, in_y):
    def own_sums(near, got, from_0, in_x, in_y, out, kept):
        kept[...] = three(near, got, from_0, 0, 0, 0) + in_x[0].astype(f32) + in_y[0].astype(f32)
        out[...] = (three(near, got, from_0, 0, 0, 1) + in_x[1].astype(f32) + in_y[1].astype(f32)).astype(bf16)

    shape = near.shape[2:]
    return glue(own_sums, [like(shape, bf16), like(shape)], near, got, from_0, in_x, in_y)


def attn_grads(kept, last):
    rows, width = kept.shape
    cols = width // 4

    def attn_sums(kept, last, qkv, out):
        total = kept[...] + last[...].astype(f32)
        for j in range(3):
            qkv[j] = total[:, j * cols : (j + 1) * cols]
        out[...] = total[:, 3 * cols :].T

    return glue(attn_sums, [like((3, rows, cols)), like((cols, rows))], kept, last)


def shards(qkv_weight, out_weight, qv_bias, up_bias, down_weight_t):
    _, rows, cols = qkv_weight.shape
    wide = 3 * cols + HEAD_DIM
    width = down_weight_t.shape[1]

    def first_shards(qkv, out_weight, qv_bias, up_bias, down, attn, down_0, down_1, biases):
        for j in range(3):
            attn[:, j * cols : (j + 1) * cols] = qkv[j].astype(bf16)
        attn[:, 3 * cols :] = out_weight[...].T.astype(bf16)
        down_0[...] = down[:, : width // 2].astype(bf16)
        down_1[...] = down[:, width // 2 :].astype(bf16)
        biases[...] = jnp.zeros_like(biases)
        biases[:, :cols] = qv_bias[0:1, :]
        biases[:, 2 * cols : 3 * cols] = qv_bias[1:2, :]
        biases[:, wide:] = row(up_bias)

    part = like((rows, width // 2), bf16)
    outs = [like((rows, 4 * cols), bf16), part, part, like((1, wide + width))]
    return glue(first_shards, outs, qkv_weight, out_weight, qv_bias, up_bias, down_weight_t)


def assemble(plan, bufs, dst, dp):
    for buf, lane, places, col in plan:
        src = bufs[buf]
        _, rows, width = src.shape
        x, col = (col & 1, col - (col & 1))
        cols = pl.ds(col, width)
        if places is None:
            dst[lane, :, cols] = src[0]
            continue
        count, a, b, c, skip = places

        def move(i, carry):
            place = a * (i & 1) + b * (i >> 1) + c
            at = pl.multiple_of((dp ^ place) * rows, rows)
            dst[lane, pl.ds(at, rows), cols] = src[i + skip * ((i >> 1) + x)]
            return carry

        lax.fori_loop(0, count, move, 0)


def row(vec):
    return vec[...].reshape(1, -1)


def row_stats(summed):
    centered = summed - jnp.mean(summed, axis=-1, keepdims=True)
    inv = lax.rsqrt(jnp.mean(centered * centered, axis=-1, keepdims=True) + epsilon)
    return centered * inv, inv


def norm_backward(scaled, normed, inv):
    row_mean = jnp.mean(scaled, axis=-1, keepdims=True)
    row_cross = jnp.mean(scaled * normed, axis=-1, keepdims=True)
    return inv * (scaled - row_mean - normed * row_cross)


def col_sum(values):
    return jnp.sum(values, axis=0, keepdims=True)


def top_of(values):
    return jnp.full((1, 128), jnp.max(jnp.abs(values)), f32)


def fill_mask(mask, longs, shorts):
    per_block = LONG_LEN // SHORT_LEN
    block = lax.axis_index("tensor")
    n_long = longs.shape[0]
    is_long = block < n_long
    whole = longs[jnp.minimum(block, n_long - 1)]
    first = jnp.maximum(block - n_long, 0) * per_block
    shift = jnp.where(is_long, LONG_LEN.bit_length() - 1, SHORT_LEN.bit_length() - 1)
    size = jnp.where(is_long, LONG_LEN, SHORT_LEN)
    k_pos = lax.broadcasted_iota(jnp.int32, (LONG_LEN, 1), 0)
    q_pos = lax.broadcasted_iota(jnp.int32, (1, LONG_LEN), 1)
    k_seg = lax.shift_right_logical(k_pos, jnp.full_like(k_pos, shift))
    q_seg = lax.shift_right_logical(q_pos, jnp.full_like(q_pos, shift))
    limit = jnp.zeros_like(k_pos)
    for j in range(per_block):
        limit = jnp.where(k_seg == j, jnp.where(is_long, whole, shorts[first + j]), limit)
    k_seg = jnp.where(k_pos - k_seg * size < limit, k_seg, -1)
    mask[...] = jnp.where(k_seg == q_seg, 0.0, NEG)


def attn_forward(net, plan, nb, dims, lim, longs, shorts, tokens, bias, *rest):
    blocks, cols, width = dims
    bufs, rest = rest[:nb], rest[nb:]
    qkv_out, lse_out, in_t, ctx_low, ctx_slope, top_out, weight, in_low, mask, ctx_t, top_ctx = rest
    heads = cols // HEAD_DIM
    low_q = 3 * cols + HEAD_DIM
    assemble(plan, bufs, weight, net.me()[0])
    inputs = tokens[...].astype(f32)
    in_low[...] = jnp.clip(inputs, -lim[0], lim[0]).astype(bf16)
    in_t[...] = in_low[...].T
    top_out[0:1, :] = top_of(inputs)
    fill_mask(mask, longs, shorts)
    ctx_t[0:HEAD_DIM, :] = jnp.zeros((HEAD_DIM, ctx_t.shape[1]), f32)
    top_ctx[...] = jnp.zeros_like(top_ctx)
    inv_limit = 1.0 / jnp.full((1, 1), lim[1], f32)

    def each(lane, carry):
        qkv = (mm(in_low[...], weight[lane, :, :low_q]) + bias[lane, :, :low_q]).astype(bf16)
        qkv_out[lane] = qkv
        for h in range(heads):
            at = h * HEAD_DIM
            q = qkv[:, at : at + HEAD_DIM]
            k = qkv[:, cols + at : cols + at + HEAD_DIM]
            v = qkv[:, 2 * cols + at : 2 * cols + at + HEAD_DIM]
            scores = mm_nt(k, q) * score_scale + mask[...]
            peak = jnp.max(scores, axis=0, keepdims=True)
            grown = jnp.exp(scores - peak)
            total = jnp.sum(grown, axis=0, keepdims=True)
            lse_out[lane, h : h + 1, :] = peak + jnp.log(total)
            shares = (grown * (1.0 / total)).astype(bf16)
            ctx_t[HEAD_DIM + at : 2 * HEAD_DIM + at, :] = mm_tn(v, shares)
        context = ctx_t[...].T
        bent = jnp.tanh(context * inv_limit)
        ctx_low[lane] = (lim[1] * bent).astype(bf16)
        ctx_slope[lane] = 1.0 - bent * bent
        top_ctx[...] = jnp.maximum(top_ctx[...], jnp.max(jnp.abs(context).reshape(-1, 8, context.shape[1]), axis=0))
        return carry

    lax.fori_loop(0, blocks, each, 0)
    top_out[1:2, :] = top_of(top_ctx[...])


def attn_finish(dims, lim, ctx_low, tokens, out_bias, gain, shift, weight, *outs):
    blocks, cols, width = dims
    normed_out, inv_out, middle_out, mid_slope, mid_low, mid_t, top_out, acc = outs
    at = 3 * cols - HEAD_DIM
    acc[...] = tokens[...].astype(f32) + row(out_bias)

    def each(lane, carry):
        acc[...] += mm_nt(ctx_low[lane], weight[lane, :, at:])
        return carry

    lax.fori_loop(0, blocks, each, 0)
    normed, inv = row_stats(acc[...])
    normed_out[...] = normed
    inv_out[...] = inv
    middle = normed * row(gain) + row(shift)
    middle_out[...] = middle
    bent = jnp.tanh(middle * (1.0 / jnp.full((1, 1), lim[2], f32)))
    low = (lim[2] * bent).astype(bf16)
    mid_low[...] = low
    mid_slope[...] = 1.0 - bent * bent
    mid_t[...] = low.T
    top_out[...] = jnp.broadcast_to(top_of(middle), top_out.shape)


def up_forward(net, plan, nb, first, low_q, lim, mid_low, bias, *rest):
    bufs, rest = rest[:nb], rest[nb:]
    act_out, slope_out, top_out, weight, top_hid = rest
    assemble(plan, bufs, weight, net.me()[0])
    top_hid[...] = jnp.zeros_like(top_hid)
    inv_limit = 1.0 / jnp.full((1, 1), lim[3], f32)

    rows = mid_low.shape[0] // 2

    def each(n, carry):
        lane = n // 2
        part = pl.ds(pl.multiple_of((n % 2) * rows, rows), rows)
        up = mm(mid_low[part, :], weight[lane]) + bias[first + lane, :, low_q:]
        half = 0.5 * (1.0 + lax.erf(up * root_half))
        hidden = up * half
        top_hid[...] = jnp.maximum(top_hid[...], jnp.max(jnp.abs(hidden).reshape(-1, 8, hidden.shape[1]), axis=0))
        bent = jnp.tanh(hidden * inv_limit)
        act_out[lane, part] = (lim[3] * bent).astype(bf16)
        slope_out[lane, part] = (1.0 - bent * bent) * (half + up * jnp.exp(-0.5 * up * up) * density_scale)
        return carry

    lax.fori_loop(0, 2 * weight.shape[0], each, 0)
    top_out[...] = jnp.broadcast_to(top_of(top_hid[...]), top_out.shape)


def down_both(net, plan, nb, act0, act1, slope0, slope1, middle, cotangent, down_bias, gain, shift, *rest):
    bufs, rest = rest[:nb], rest[nb:]
    layer_out, grad_out, ffn_t, sums, grad_up, up_sums, weight, acc, ffn_low = rest
    assemble(plan, bufs, weight, net.me()[0])
    acc[...] = middle[...] + row(down_bias)
    half = act0.shape[0]
    for act, first in ((act0, 0), (act1, half)):

        def each(i, carry):
            acc[...] += mm_nt(act[i], weight[first + i])
            return carry

        lax.fori_loop(0, half, each, 0)
    normed, inv = row_stats(acc[...])
    layer_out[...] = (normed * row(gain) + row(shift)).astype(bf16)
    incoming = cotangent[...].astype(f32)
    grad = norm_backward(incoming * row(gain), normed, inv)
    grad_out[...] = grad
    ffn_low[...] = grad.astype(bf16)
    ffn_t[...] = ffn_low[...].T
    sums[...] = jnp.zeros_like(sums)
    sums[0:1, :] = col_sum(grad)
    sums[1:2, :] = col_sum(incoming * normed)
    sums[2:3, :] = col_sum(incoming)
    lane_me = net.me()[1]
    for slope, first in ((slope0, 0), (slope1, half)):

        def back(i, carry):
            low = (mm(ffn_low[...], weight[first + i]) * slope[i]).astype(bf16)
            grad_up[first + i] = low
            up_sums[(first + i) ^ lane_me] = col_sum(low.astype(f32))
            return carry

        lax.fori_loop(0, half, back, 0)


def weight_grad(net, left_t, *rest):
    *rights, far, near = rest
    rows = left_t.shape[0] // net.parts
    dp = net.me()[0]
    half = far.shape[0]
    for x in range(half):
        for out, lane in ((far, 2 * x + 1), (near, 2 * x)):
            right = rights[lane // rights[0].shape[0]]
            grad = mm(left_t[...], right[lane % right.shape[0]]).astype(bf16)
            for block in range(net.parts):
                out[x, net.slot(block, dp)] = grad[block * rows : (block + 1) * rows]


def mid_backward(grad_up, grad_second, mid_slope, normed, inv, gain, weight0, weight1, grad_out, attn_low, attn_t, sums, acc):
    acc[...] = jnp.zeros_like(acc)
    half = weight0.shape[0]
    for weight, first in ((weight0, 0), (weight1, half)):

        def each(i, carry):
            acc[...] += mm_nt(grad_up[first + i], weight[i])
            return carry

        lax.fori_loop(0, half, each, 0)
    incoming = grad_second[...] + acc[...] * mid_slope[...]
    grad = norm_backward(incoming * row(gain), normed[...], inv[...])
    grad_out[...] = grad
    attn_low[...] = grad.astype(bf16)
    attn_t[...] = attn_low[...].T
    sums[...] = jnp.zeros_like(sums)
    sums[0:1, :] = col_sum(grad)
    sums[1:2, :] = col_sum(incoming * normed[...])
    sums[2:3, :] = col_sum(incoming)


def heads_backward(first, dims, lane_me, qkv, lse, attn_low, weight, ctx_slope, mask, grad_ctx, out, sums):
    blocks, cols, width = dims
    heads = cols // HEAD_DIM

    def each(i, carry):
        lane = first + i
        part = mm(attn_low[...], weight[lane, :, 3 * cols - HEAD_DIM :])
        grad_ctx[...] = (part * ctx_slope[lane]).astype(bf16)
        for h in range(heads):
            at = h * HEAD_DIM
            q = qkv[lane, :, at : at + HEAD_DIM]
            k = qkv[lane, :, cols + at : cols + at + HEAD_DIM]
            v = qkv[lane, :, 2 * cols + at : 2 * cols + at + HEAD_DIM]
            grad = grad_ctx[:, HEAD_DIM + at : 2 * HEAD_DIM + at]
            shares = jnp.exp(mm_nt(k, q) * score_scale + mask[...] - lse[lane, h : h + 1, :])
            grad_shares = mm_nt(v, grad)
            inner = jnp.sum(shares * grad_shares, axis=0, keepdims=True)
            grad_scores = (shares * (grad_shares - inner)).astype(bf16)
            grad_v = mm(shares.astype(bf16), grad)
            grad_k = mm(grad_scores, q) * score_scale
            grad_q = (mm_tn(k, grad_scores) * score_scale).T
            out[i, :, at : at + HEAD_DIM] = grad_q.astype(bf16)
            out[i, :, cols + at : cols + at + HEAD_DIM] = grad_k.astype(bf16)
            out[i, :, 2 * cols + at : 2 * cols + at + HEAD_DIM] = grad_v.astype(bf16)
        out[i, :, 3 * cols :] = jnp.zeros((out.shape[1], HEAD_DIM), bf16)
        sums[lane ^ lane_me] = col_sum(out[i].astype(f32))
        return carry

    lax.fori_loop(0, out.shape[0], each, 0)


def attn_backward(net, first, dims, longs, shorts, qkv, lse, attn_low, weight, ctx_slope, out, sums, mask, grad_ctx):
    fill_mask(mask, longs, shorts)
    sums[...] = jnp.zeros_like(sums)
    heads_backward(first, dims, net.me()[1], qkv, lse, attn_low, weight, ctx_slope, mask, grad_ctx, out, sums)


def attn_backward_last(net, dims, longs, shorts, qkv, lse, attn_low, weight, ctx_slope, *rest):
    blocks, cols, width = dims
    in_t, attn_t, ctx_low, more_out, more, *rest = rest
    up_sums, sums_a, sums_b, tops_a, tops_m, top0, top1, *rest = rest
    out, far, near, packed, sums, mask, grad_ctx = rest
    rows = in_t.shape[0] // net.parts
    wide = 3 * cols + HEAD_DIM
    start = 3 * cols - HEAD_DIM
    dp, lane_me = net.me()
    fill_mask(mask, longs, shorts)
    sums[...] = more[...]
    heads_backward(0, dims, lane_me, qkv, lse, attn_low, weight, ctx_slope, mask, grad_ctx, out, sums)
    for x, grads in enumerate((out, more_out)):

        def weights(core, carry):
            left = mm(in_t[...], grads[core])
            right = mm(attn_t[...], ctx_low[2 * x + core])
            mixed = (left[:, start:] + right[:, : wide - start]).astype(bf16)
            left, right = left[:, :start].astype(bf16), right[:, wide - start :].astype(bf16)
            for to, wanted in ((near, 0), (far, 1)):

                @pl.when(core == wanted)
                def _():
                    for block in range(net.parts):
                        rs = slice(block * rows, (block + 1) * rows)
                        place = net.slot(block, dp)
                        to[x, place, :, :start] = left[rs]
                        to[x, place, :, start:wide] = mixed[rs]
                        to[x, place, :, wide:] = right[rs]

            return carry

        lax.fori_loop(0, 2, weights, 0)
    packed[...] = jnp.zeros_like(packed)
    for j in range(blocks):
        packed[j : j + 1, :] = up_sums[j]
        packed[blocks + j : blocks + j + 1, : sums.shape[2]] = sums[j]
    packed[2 * blocks : 2 * blocks + 3, :] = sums_a[0:3, :]
    packed[2 * blocks + 3 : 2 * blocks + 6, :] = sums_b[0:3, :]
    tops = (tops_a[0:1, :], tops_a[1:2, :], tops_m[0:1, :], jnp.maximum(top0[0:1, :], top1[0:1, :]))
    for j, top in enumerate(tops):
        packed[2 * blocks + 6 : 2 * blocks + 7, 128 * j : 128 * j + 128] = top


def token_backward(dims, lim, grads_0, grads_1, grad_first, tokens, weight, out, acc):
    blocks, cols, width = dims
    acc[...] = jnp.zeros_like(acc)
    half = grads_0.shape[0]
    for grads, first in ((grads_0, 0), (grads_1, half)):

        def back(i, carry):
            acc[...] += mm_nt(grads[i], weight[first + i, :, : 3 * cols + HEAD_DIM])
            return carry

        lax.fori_loop(0, half, back, 0)
    inputs = tokens[...].astype(f32)
    out[...] = (grad_first[...] + jnp.where(jnp.abs(inputs) <= lim[0], acc[...], 0.0)).astype(bf16)


def make_body(net):
    def body(
        tokens,
        cotangent,
        qkv_weight,
        qv_bias,
        out_weight,
        out_bias,
        first_gain,
        first_shift,
        up_weight,
        up_bias,
        down_weight,
        down_bias,
        second_gain,
        second_shift,
        act_ranges,
        long_lengths,
        short_lengths,
    ):
        lane = lax.axis_index("tensor")
        rows, width = tokens.shape
        assert rows == LONG_LEN
        cols = qkv_weight.shape[2]
        up_cols = up_weight.shape[1]
        blocks = lax.axis_size("tensor")
        half = blocks // 2
        dims = (blocks, cols, width)
        wide = 3 * cols + HEAD_DIM
        out_cols = cols + HEAD_DIM
        every = tuple(range(blocks))

        pieces_a, pieces_u, pieces_d = Pieces([]), Pieces([]), Pieces([])
        shard_a, shard_d, shard_p, bias_row = shards(qkv_weight, out_weight, qv_bias, up_bias, down_weight.T)
        job_a = Job(net.gather(shard_a, pieces_a))
        job_b = Job(net.gather_lane(bias_row))
        job_u = Job(net.gather(up_weight.astype(bf16), pieces_u))
        job_d = Job(net.gather(shard_d, pieces_d))
        job_p = Job(net.gather_plane_first(shard_p, pieces_d, up_cols // 2))

        def vmem(*shape, dtype=f32):
            return pltpu.VMEM(shape, dtype)

        unit = 2 * rows * width * width * blocks
        moved = 2 * width * width * blocks

        step((), None, [job_a, job_p, job_b], [job_a, job_p, job_b])
        step((), None, [job_a, job_p, job_b, job_d], [job_a, job_p, job_b])
        step((), None, [job_a, job_u], [job_a, job_u, job_d])
        step((), None, [job_a, job_u], [job_a, job_u])
        step((), None, [job_a, job_u], [job_a])
        biases = job_b.value

        bufs, plan = pieces_a.part(every)
        qkv, lse, in_t, ctx_low, ctx_slope, tops_a, weight_a = step(
            (act_ranges, long_lengths, short_lengths, tokens, biases, *bufs),
            call(
                functools.partial(attn_forward, net, plan, len(bufs), dims),
                "attn_forward",
                [SM] * 3 + [VM] * 2 + [VM] * len(bufs),
                [
                    like((blocks, rows, wide), bf16),
                    like((blocks, 8, rows)),
                    like((width, rows), bf16),
                    like((blocks, rows, out_cols), bf16),
                    like((blocks, rows, out_cols)),
                    like((8, 128)),
                    like((blocks, width, 4 * cols), bf16),
                ],
                [vmem(rows, width, dtype=bf16), vmem(rows, rows), vmem(out_cols, rows), vmem(8, out_cols)],
                4 * unit,
                3 * moved,
            ),
            [job_d, job_p],
            [job_u, job_d, job_p],
        )
        normed, inv, middle, mid_slope, mid_low, mid_t, tops_m = step(
            (act_ranges, ctx_low, tokens, out_bias, first_gain, first_shift, weight_a),
            call(
                functools.partial(attn_finish, dims),
                "attn_finish",
                [SM] + [VM] * 6,
                [
                    like((rows, width)),
                    like((rows, 1)),
                    like((rows, width)),
                    like((rows, width)),
                    like((rows, width), bf16),
                    like((width, rows), bf16),
                    like((8, 128)),
                ],
                [vmem(rows, width)],
                2 * unit,
                2 * moved,
            ),
            [job_u, job_p],
            [job_u],
        )

        def up_part(lanes, start, finish):
            bufs, plan = pieces_u.part(lanes)
            return step(
                (act_ranges, mid_low, biases, *bufs),
                call(
                    functools.partial(up_forward, net, plan, len(bufs), lanes[0], wide),
                    f"up_forward_{lanes[0]}",
                    [SM] + [VM] * 2 + [VM] * len(bufs),
                    [
                        like((half, rows, up_cols), bf16),
                        like((half, rows, up_cols)),
                        like((8, 128)),
                        like((half, width, up_cols), bf16),
                    ],
                    [vmem(8, up_cols)],
                    2 * unit,
                    2 * moved,
                ),
                start,
                finish,
            )

        act0, slope0, top0, weight_u0 = up_part(every[:half], [job_u, job_d], [job_u])
        act1, slope1, top1, weight_u1 = up_part(every[half:], [], [job_d, job_p])
        step((), None, [job_d], [job_d])
        step((), None, [job_d, job_p], [job_d, job_p])
        bufs_d, plan_d = pieces_d.part(every)
        layer_out, grad_second, ffn_t, sums_b, grad_up, up_sums = step(
            (act0, act1, slope0, slope1, middle, cotangent, down_bias, second_gain, second_shift, *bufs_d),
            call(
                functools.partial(down_both, net, plan_d, len(bufs_d)),
                "down_both",
                [VM] * 9 + [VM] * len(bufs_d),
                [
                    like((rows, width), bf16),
                    like((rows, width)),
                    like((width, rows), bf16),
                    like((8, width)),
                    like((blocks, rows, up_cols), bf16),
                    like((blocks, 1, up_cols)),
                ],
                [
                    vmem(blocks, width, up_cols, dtype=bf16),
                    vmem(rows, width),
                    vmem(rows, width, dtype=bf16),
                ],
                2 * unit,
                4 * moved,
            ),
        )

        grad_shape = like((net.parts, width // net.parts, up_cols), bf16)
        both_shape = like((half,) + grad_shape.shape, bf16)

        def grad_of(name, left_t, rights, start=(), finish=()):
            return step(
                (left_t, *rights),
                call(
                    functools.partial(weight_grad, net),
                    name,
                    [VM] * (1 + len(rights)),
                    [both_shape, both_shape],
                    (),
                    unit,
                    moved,
                ),
                start,
                finish,
            )

        sum_d = Job(net.scatter_z_first(*grad_of("down_grad", ffn_t, (act0, act1))))
        sum_u = Job(net.scatter_sum(*grad_of("up_grad", mid_t, (grad_up,), [sum_d], [sum_d])))
        grad_first, attn_low, attn_t, sums_a = step(
            (grad_up, grad_second, mid_slope, normed, inv, first_gain, weight_u0, weight_u1),
            call(
                mid_backward,
                "mid_backward",
                [VM] * 8,
                [like((rows, width)), like((rows, width), bf16), like((width, rows), bf16), like((8, width))],
                [vmem(rows, width)],
                unit + unit // 3,
                3 * moved,
            ),
            [sum_u, sum_d],
            [sum_u],
        )
        grads_1, more = step(
            (long_lengths, short_lengths, qkv, lse, attn_low, weight_a, ctx_slope),
            call(
                functools.partial(attn_backward, net, half, dims),
                "attn_backward",
                [SM] * 2 + [VM] * 5,
                [like((half, rows, wide), bf16), like((blocks, 1, wide))],
                [vmem(rows, rows), vmem(rows, out_cols, dtype=bf16)],
                2 * unit,
                2 * moved,
            ),
            [sum_u],
            [sum_u, sum_d],
        )
        grads_0, far, near, packed = step(
            (long_lengths, short_lengths, qkv, lse, attn_low, weight_a, ctx_slope)
            + (in_t, attn_t, ctx_low, grads_1, more)
            + (up_sums, sums_a, sums_b, tops_a, tops_m, top0, top1),
            call(
                functools.partial(attn_backward_last, net, dims),
                "attn_backward_last",
                [SM] * 2 + [VM] * 17,
                [like((half, rows, wide), bf16), both_shape, both_shape, like((16, width))],
                [vmem(blocks, 1, wide), vmem(rows, rows), vmem(rows, out_cols, dtype=bf16)],
                4 * unit,
                2 * moved,
            ),
            [sum_u, sum_d],
            [sum_u, sum_d],
        )
        sum_a = Job(net.scatter_sum(far, near))
        is_top = (jnp.arange(packed.shape[0]) == 2 * blocks + 6)[:, None]
        sum_s = Job(net.sum_max(packed, is_top))
        line_u = Job(net.scatter_line(*sum_u.value))
        tokens_grad = step(
            (act_ranges, grads_0, grads_1, grad_first, tokens, weight_a),
            call(
                functools.partial(token_backward, dims),
                "token_backward",
                [SM] + [VM] * 5,
                [like((rows, width), bf16)],
                [vmem(rows, width)],
                unit,
                2 * moved,
            ),
            [sum_a, sum_d, line_u, sum_s],
            [sum_a, sum_d, line_u, sum_s],
        )[0]
        step((), None, [sum_a, sum_d], [sum_a, sum_d])
        step((), None, [sum_a, line_u, sum_s], [sum_a, line_u, sum_s])
        line_a = Job(net.scatter_line(*sum_a.value))
        step((), None, [line_a, sum_s], [line_a, sum_s])
        step((), None, [line_a, sum_s], [sum_s])
        step((), None, [sum_s], [line_a, sum_s])

        packed = sum_s.value
        down_grad, up_grad = (kept + last.astype(f32) for kept, last in (sum_d.value, line_u.value))
        down_grad = down_grad.T
        qkv_grad, out_grad = attn_grads(*line_a.value)
        own = lax.dynamic_slice_in_dim(packed, blocks + lane, 1)
        shared = packed[2 * blocks : 2 * blocks + 6]
        qv_bias_grad = jnp.concatenate([own[:, :cols], own[:, 2 * cols : 3 * cols]], 0)
        up_bias_grad = lax.dynamic_slice_in_dim(packed, lane, 1)[0]
        new_ranges = ema_decay * act_ranges + (1.0 - ema_decay) * packed[2 * blocks + 6, 0:512:128]
        return (
            layer_out,
            tokens_grad,
            qkv_grad,
            qv_bias_grad,
            out_grad,
            shared[0],
            shared[1],
            shared[2],
            up_grad,
            up_bias_grad,
            down_grad,
            shared[3],
            shared[4],
            shared[5],
            new_ranges,
        )

    return body


def solution(mesh):
    in_specs = (
        P(ALL, None),
        P(ALL, None),
        P(None, "dp", "tensor"),
        P(None, "tensor"),
        P("tensor", "dp"),
        P(),
        P(),
        P(),
        P("dp", "tensor"),
        P("tensor"),
        P("tensor", "dp"),
        P(),
        P(),
        P(),
        P(),
        P("dp"),
        P("dp"),
    )
    out_specs = (
        P(ALL, None),
        P(ALL, None),
        P(None, "dp", "tensor"),
        P(None, "tensor"),
        P("tensor", "dp"),
        P(),
        P(),
        P(),
        P("dp", "tensor"),
        P("tensor"),
        P("tensor", "dp"),
        P(),
        P(),
        P(),
        P(),
    )
    net = Grid() if mesh.shape["dp"] == 8 and mesh.shape["tensor"] == 4 else Plain()
    return jax.shard_map(make_body(net), mesh=mesh, in_specs=in_specs, out_specs=out_specs, check_vma=False)
```

```python
import functools
import itertools

import jax
import jax.numpy as jnp
from jax import lax
from jax.experimental import pallas as pl
from jax.experimental.pallas import tpu as pltpu
from jax.sharding import PartitionSpec as P

HEAD_DIM = 64
LONG_LEN = 512
SHORT_LEN = 128
ALL = ("dp", "tensor")

ema_decay = 0.9
epsilon = 1e-06
root_half = 0.7071067811865476
density_scale = 0.3989422804014327
score_scale = HEAD_DIM ** (-0.5)
NEG = -1000000000.0

f32 = jnp.float32
bf16 = jnp.bfloat16


def mm(left, right):
    return jnp.dot(left, right, preferred_element_type=f32)


def mm_tn(left, right):
    return lax.dot_general(left, right, (((0,), (0,)), ((), ())), preferred_element_type=f32)


def mm_nt(left, right):
    return lax.dot_general(left, right, (((1,), (1,)), ((), ())), preferred_element_type=f32)


def _lin(z, y, x, c):
    return (z * 2 + y) * 4 + x * 2 + c


def _perm(fn):
    out = []
    for z, y, x, c in itertools.product(range(4), range(2), range(2), range(2)):
        out.append((_lin(z, y, x, c), _lin(*fn(z, y, x, c))))
    return out


PC = _perm(lambda z, y, x, c: (z, y, x, 1 - c))
PX = _perm(lambda z, y, x, c: (z, y, 1 - x, c))
PY = _perm(lambda z, y, x, c: (z, 1 - y, x, c))
PZ1 = _perm(lambda z, y, x, c: (z ^ 1, y, x, c))
PZ2 = _perm(lambda z, y, x, c: (z ^ 2, y, x, c))


def tie(*trees):
    leaves, spec = jax.tree.flatten(trees)
    return jax.tree.unflatten(spec, lax.optimization_barrier(leaves))


class Job:
    def __init__(self, stages):
        self.stages, self.value, self.out, self.flight, self.over = stages, None, [], [], False
        self.take(None)

    def take(self, got):
        if not self.over:
            try:
                self.out = self.stages.send(got)
            except StopIteration as stop:
                self.value, self.out, self.over = stop.value, [], True


def step(ins, run=None, start=(), finish=()):
    ins, sends = tie(ins, [[value for value, _ in job.out] for job in start])
    for job, values in zip(start, sends):
        job.flight = [lax.ppermute(v, ALL, perm) for v, (_, perm) in zip(values, job.out)]
    outs = run(*ins) if run else ins
    outs, got = tie(outs, [job.flight for job in finish])
    for job, values in zip(finish, got):
        job.flight = []
        job.take(values)
    return outs


class Pieces:
    def __init__(self, plan):
        self.bufs, self.plan = {}, plan

    def part(self, lanes):
        plan = [p for p in self.plan if p[1] in lanes]
        names = sorted({p[0] for p in plan})
        return [self.bufs[n] for n in names], [(names.index(b), lane - lanes[0], at, col) for b, lane, at, col in plan]


class Grid:
    parts = 8

    @staticmethod
    def gather(shard, pieces):
        own = shard[None]
        for base, lane in ((0, 0), (5, 1)):
            pieces.plan.append((base, lane, (4, 4, 2, 0, 0), 0))
            pieces.plan.append((base + 1, lane, (4, 4, 2, 1, 0), 0))
            pieces.plan.append((base + 2, lane + 2, (4, 4, 2, 0, 0), 0))
            pieces.plan.append((base + 3, lane + 2, (2, 4, 0, 1, 0), 0))
            pieces.plan.append((base + 4, lane + 2, (2, 4, 0, 3, 0), 0))
        (far_z,) = yield [(own, PZ2)]
        pair = jnp.concatenate([own, far_z], 0)
        (near_z,) = yield [(pair, PZ1)]
        line = jnp.concatenate([pair, near_z], 0)
        over_x, over_y, line_far = yield [(line, PX), (line, PY), (line, PC)]
        pieces.bufs.update({0: line, 1: over_y, 2: over_x, 5: line_far})
        diag_x, diag_y, over_y_far, over_x_far = yield [
            (over_y[:2], PX),
            (over_x[2:], PY),
            (over_y, PC),
            (over_x, PC),
        ]
        pieces.bufs.update({3: diag_x, 4: diag_y, 6: over_y_far, 7: over_x_far})
        diag_x_far, diag_y_far = yield [(diag_x, PC), (diag_y, PC)]
        pieces.bufs.update({8: diag_x_far, 9: diag_y_far})

    @staticmethod
    def gather_plane_first(shard, pieces, first_col):
        own = shard[None]
        over_x, over_y = yield [(own, PX), (own, PY)]
        (diag,) = yield [(over_y, PX)]
        plane = jnp.concatenate([own, over_y, over_x, diag], 0)
        (far_z,) = yield [(plane, PZ2)]
        half = jnp.concatenate([plane, far_z], 0)
        (near_z,) = yield [(half, PZ1)]
        half_far, near_z_far = yield [(half, PC), (near_z, PC)]
        for n, (buf, core) in enumerate(((half, 0), (near_z, 0), (half_far, 1), (near_z_far, 1))):
            near = 2 * (n % 2)
            name = 20 + n
            pieces.bufs[name] = buf
            for x in range(2):
                pieces.plan.append((name, 2 * x + core, (4, 1, 4, near, 2), first_col + x))

    @staticmethod
    def slot(block, dp):
        place = block ^ dp
        return (place & 1) * 4 + (place & 2) + (place >> 2)

    @staticmethod
    def scatter_sum(far, near):
        (got,) = yield [(far, PC)]
        out_x, out_y = add_first(near, got)
        from_x, from_y = yield [(out_x, PX), (out_y, PY)]
        out_x, out_y = add_second(near, got, from_x, from_y)
        in_x, in_y = yield [(out_x, PX), (out_y, PY)]
        return near, got, in_x, in_y

    @staticmethod
    def scatter_line(near, got, in_x, in_y):
        out_z, kept = add_third(near, got, in_x, in_y)
        (from_z,) = yield [(out_z, PZ1)]
        out_z, kept = add_fourth(kept, from_z)
        (last,) = yield [(out_z, PZ2)]
        return kept, last

    @staticmethod
    def scatter_z_first(far, near):
        (got,) = yield [(far, PC)]
        out_1, out_0 = add_near_z(near, got)
        (from_1,) = yield [(out_1, PZ1)]
        out_x, out_y = add_corner(near, got, from_1)
        from_x, from_y, from_0 = yield [(out_x, PX), (out_y, PY), (out_0, PZ1)]
        out_x, out_y = add_sides(near, got, from_1, from_0, from_x, from_y)
        in_x, in_y = yield [(out_x, PX), (out_y, PY)]
        out_z, kept = add_own(near, got, from_0, in_x, in_y)
        (last,) = yield [(out_z, PZ2)]
        return kept, last

    @staticmethod
    def gather_lane(vec):
        (other,) = yield [(vec, PX)]
        pair = jnp.stack([vec, other])
        (more,) = yield [(pair, PC)]
        return jnp.stack([pair, more], 1).reshape((4,) + vec.shape)

    @staticmethod
    def sum_max(both, is_top):
        for perm in (PC, PZ1, PZ2, PX, PY):
            (other,) = yield [(both, perm)]
            both = jnp.where(is_top, jnp.maximum(both, other), both + other)
        return both

    @staticmethod
    def me():
        return lax.axis_index("dp"), lax.axis_index("tensor")


class Plain:
    parts = 1

    @staticmethod
    def gather(shard, pieces, first_col=0):
        rows = lax.all_gather(shard, "dp", axis=0, tiled=True)
        full = lax.all_gather(rows, "tensor", axis=0)
        for k in range(full.shape[0]):
            pieces.plan.append((first_col + k, k, None, first_col))
            pieces.bufs[first_col + k] = full[k][None]
        return
        yield

    gather_plane_first = gather

    @staticmethod
    def slot(block, dp):
        return block

    @staticmethod
    def scatter_sum(far, near):
        grads = jnp.stack([near[0], far[0], near[1], far[1]]).astype(f32)
        return (grads.reshape((4, -1, grads.shape[-1])),)
        yield

    @staticmethod
    def scatter_line(grads):
        own = lax.psum_scatter(grads, "tensor", scatter_dimension=0, tiled=False)
        own = lax.psum_scatter(own, "dp", scatter_dimension=0, tiled=True)
        return own, jnp.zeros_like(own)
        yield

    @staticmethod
    def scatter_z_first(far, near):
        grads = yield from Plain.scatter_sum(far, near)
        return (yield from Plain.scatter_line(*grads))

    @staticmethod
    def gather_lane(vec):
        return lax.all_gather(vec, "tensor", axis=0)
        yield

    @staticmethod
    def sum_max(both, is_top):
        return jnp.where(is_top, lax.pmax(both, ALL), lax.psum(both, ALL))
        yield

    @staticmethod
    def me():
        return 0, 0


VM = pl.BlockSpec(memory_space=pltpu.VMEM)
SM = pl.BlockSpec(memory_space=pltpu.SMEM)
VMEM_MIB = 8
ROOMY = ("down_both",)


def like(shape, dtype=f32):
    return jax.ShapeDtypeStruct(shape, dtype)


def call(kernel, name, specs, outs, scratch=(), flops=0, moved=0):
    return pl.pallas_call(
        kernel,
        name=name,
        out_shape=outs,
        in_specs=specs,
        out_specs=[VM] * len(outs),
        scratch_shapes=list(scratch),
        compiler_params=pltpu.CompilerParams(vmem_limit_bytes=(14 if name in ROOMY else VMEM_MIB) * 2**20),
        cost_estimate=pl.CostEstimate(flops=flops, bytes_accessed=moved, transcendentals=0),
    )


def glue(kernel, outs, *ins):
    return call(kernel, kernel.__name__, [VM] * len(ins), outs)(*ins)


def add_first(near, got):
    def first_sums(near, got, out_x, out_y):
        for k in range(2):
            out_x[k] = (near[1, 4 + k].astype(f32) + got[1, 4 + k].astype(f32)).astype(bf16)
            out_y[k] = (near[1, 6 + k].astype(f32) + got[1, 6 + k].astype(f32)).astype(bf16)

    part = like((2,) + near.shape[2:], bf16)
    return glue(first_sums, [part, part], near, got)


def add_second(near, got, from_x, from_y):
    def second_sums(near, got, from_x, from_y, out_x, out_y):
        for k in range(4):
            over_x = near[1, k].astype(f32) + got[1, k].astype(f32)
            over_y = near[0, 4 + k].astype(f32) + got[0, 4 + k].astype(f32)
            if k < 2:
                over_y = over_y + from_x[k].astype(f32)
            else:
                over_x = over_x + from_y[k - 2].astype(f32)
            out_x[k] = over_x.astype(bf16)
            out_y[k] = over_y.astype(bf16)

    part = like((4,) + near.shape[2:], bf16)
    return glue(second_sums, [part, part], near, got, from_x, from_y)


def add_third(near, got, in_x, in_y):
    def third_sums(near, got, in_x, in_y, out, kept):
        for k in range(4):
            total = near[0, k].astype(f32) + got[0, k].astype(f32) + in_x[k].astype(f32) + in_y[k].astype(f32)
            if k < 2:
                kept[k] = total
            else:
                out[k - 2] = total.astype(bf16)

    shape = (2,) + near.shape[2:]
    return glue(third_sums, [like(shape, bf16), like(shape)], near, got, in_x, in_y)


def add_fourth(kept, from_z):
    def fourth_sums(kept, from_z, out, mine):
        mine[...] = kept[0] + from_z[0].astype(f32)
        out[...] = (kept[1] + from_z[1].astype(f32)).astype(bf16)

    shape = kept.shape[1:]
    return glue(fourth_sums, [like(shape, bf16), like(shape)], kept, from_z)


def add_near_z(near, got):
    def near_z_sums(near, got, out_1, out_0):
        for x, out in ((1, out_1), (0, out_0)):
            for y in range(2):
                for k in range(2):
                    at = 4 * y + 2 + k
                    out[2 * y + k] = (near[x, at].astype(f32) + got[x, at].astype(f32)).astype(bf16)

    part = like((4,) + near.shape[2:], bf16)
    return glue(near_z_sums, [part, part], near, got)


def three(near, got, from_z, x, y, k):
    return near[x, 4 * y + k].astype(f32) + got[x, 4 * y + k].astype(f32) + from_z[2 * y + k].astype(f32)


def add_corner(near, got, from_1):
    def corner_sums(near, got, from_1, out_x, out_y):
        out_x[...] = three(near, got, from_1, 1, 1, 0).astype(bf16)
        out_y[...] = three(near, got, from_1, 1, 1, 1).astype(bf16)

    part = like(near.shape[2:], bf16)
    return glue(corner_sums, [part, part], near, got, from_1)


def add_sides(near, got, from_1, from_0, from_x, from_y):
    def side_sums(near, got, from_1, from_0, from_x, from_y, out_x, out_y):
        out_x[0] = three(near, got, from_1, 1, 0, 0).astype(bf16)
        out_x[1] = (three(near, got, from_1, 1, 0, 1) + from_y[...].astype(f32)).astype(bf16)
        out_y[0] = (three(near, got, from_0, 0, 1, 0) + from_x[...].astype(f32)).astype(bf16)
        out_y[1] = three(near, got, from_0, 0, 1, 1).astype(bf16)

    part = like((2,) + near.shape[2:], bf16)
    return glue(side_sums, [part, part], near, got, from_1, from_0, from_x, from_y)


def add_own(near, got, from_0, in_x, in_y):
    def own_sums(near, got, from_0, in_x, in_y, out, kept):
        kept[...] = three(near, got, from_0, 0, 0, 0) + in_x[0].astype(f32) + in_y[0].astype(f32)
        out[...] = (three(near, got, from_0, 0, 0, 1) + in_x[1].astype(f32) + in_y[1].astype(f32)).astype(bf16)

    shape = near.shape[2:]
    return glue(own_sums, [like(shape, bf16), like(shape)], near, got, from_0, in_x, in_y)


def attn_grads(kept, last):
    rows, width = kept.shape
    cols = width // 4

    def attn_sums(kept, last, qkv, out):
        total = kept[...] + last[...].astype(f32)
        for j in range(3):
            qkv[j] = total[:, j * cols : (j + 1) * cols]
        out[...] = total[:, 3 * cols :].T

    return glue(attn_sums, [like((3, rows, cols)), like((cols, rows))], kept, last)


def shards(qkv_weight, out_weight, qv_bias, up_bias, down_weight_t):
    _, rows, cols = qkv_weight.shape
    wide = 3 * cols + HEAD_DIM
    width = down_weight_t.shape[1]

    def first_shards(qkv, out_weight, qv_bias, up_bias, down, attn, down_0, down_1, biases):
        for j in range(3):
            attn[:, j * cols : (j + 1) * cols] = qkv[j].astype(bf16)
        attn[:, 3 * cols :] = out_weight[...].T.astype(bf16)
        down_0[...] = down[:, : width // 2].astype(bf16)
        down_1[...] = down[:, width // 2 :].astype(bf16)
        biases[...] = jnp.zeros_like(biases)
        biases[:, :cols] = qv_bias[0:1, :]
        biases[:, 2 * cols : 3 * cols] = qv_bias[1:2, :]
        biases[:, wide:] = row(up_bias)

    part = like((rows, width // 2), bf16)
    outs = [like((rows, 4 * cols), bf16), part, part, like((1, wide + width))]
    return glue(first_shards, outs, qkv_weight, out_weight, qv_bias, up_bias, down_weight_t)


def assemble(plan, bufs, dst, dp):
    for buf, lane, places, col in plan:
        src = bufs[buf]
        _, rows, width = src.shape
        x, col = (col & 1, col - (col & 1))
        cols = pl.ds(col, width)
        if places is None:
            dst[lane, :, cols] = src[0]
            continue
        count, a, b, c, skip = places

        def move(i, carry):
            place = a * (i & 1) + b * (i >> 1) + c
            at = pl.multiple_of((dp ^ place) * rows, rows)
            dst[lane, pl.ds(at, rows), cols] = src[i + skip * ((i >> 1) + x)]
            return carry

        lax.fori_loop(0, count, move, 0)


def row(vec):
    return vec[...].reshape(1, -1)


def row_stats(summed):
    centered = summed - jnp.mean(summed, axis=-1, keepdims=True)
    inv = lax.rsqrt(jnp.mean(centered * centered, axis=-1, keepdims=True) + epsilon)
    return centered * inv, inv


def norm_backward(scaled, normed, inv):
    row_mean = jnp.mean(scaled, axis=-1, keepdims=True)
    row_cross = jnp.mean(scaled * normed, axis=-1, keepdims=True)
    return inv * (scaled - row_mean - normed * row_cross)


def col_sum(values):
    return jnp.sum(values, axis=0, keepdims=True)


def top_of(values):
    return jnp.full((1, 128), jnp.max(jnp.abs(values)), f32)


def fill_mask(mask, longs, shorts):
    per_block = LONG_LEN // SHORT_LEN
    block = lax.axis_index("tensor")
    n_long = longs.shape[0]
    is_long = block < n_long
    whole = longs[jnp.minimum(block, n_long - 1)]
    first = jnp.maximum(block - n_long, 0) * per_block
    shift = jnp.where(is_long, LONG_LEN.bit_length() - 1, SHORT_LEN.bit_length() - 1)
    size = jnp.where(is_long, LONG_LEN, SHORT_LEN)
    k_pos = lax.broadcasted_iota(jnp.int32, (LONG_LEN, 1), 0)
    q_pos = lax.broadcasted_iota(jnp.int32, (1, LONG_LEN), 1)
    k_seg = lax.shift_right_logical(k_pos, jnp.full_like(k_pos, shift))
    q_seg = lax.shift_right_logical(q_pos, jnp.full_like(q_pos, shift))
    limit = jnp.zeros_like(k_pos)
    for j in range(per_block):
        limit = jnp.where(k_seg == j, jnp.where(is_long, whole, shorts[first + j]), limit)
    k_seg = jnp.where(k_pos - k_seg * size < limit, k_seg, -1)
    mask[...] = jnp.where(k_seg == q_seg, 0.0, NEG)


def attn_forward(net, plan, nb, dims, lim, longs, shorts, tokens, bias, *rest):
    blocks, cols, width = dims
    bufs, rest = rest[:nb], rest[nb:]
    qkv_out, lse_out, in_t, ctx_low, ctx_slope, top_out, weight, in_low, mask, ctx_t, top_ctx = rest
    heads = cols // HEAD_DIM
    low_q = 3 * cols + HEAD_DIM
    assemble(plan, bufs, weight, net.me()[0])
    inputs = tokens[...].astype(f32)
    in_low[...] = jnp.clip(inputs, -lim[0], lim[0]).astype(bf16)
    in_t[...] = in_low[...].T
    top_out[0:1, :] = top_of(inputs)
    fill_mask(mask, longs, shorts)
    ctx_t[0:HEAD_DIM, :] = jnp.zeros((HEAD_DIM, ctx_t.shape[1]), f32)
    top_ctx[...] = jnp.zeros_like(top_ctx)
    inv_limit = 1.0 / jnp.full((1, 1), lim[1], f32)

    def each(lane, carry):
        qkv = (mm(in_low[...], weight[lane, :, :low_q]) + bias[lane, :, :low_q]).astype(bf16)
        qkv_out[lane] = qkv
        for h in range(heads):
            at = h * HEAD_DIM
            q = qkv[:, at : at + HEAD_DIM]
            k = qkv[:, cols + at : cols + at + HEAD_DIM]
            v = qkv[:, 2 * cols + at : 2 * cols + at + HEAD_DIM]
            scores = mm_nt(k, q) * score_scale + mask[...]
            peak = jnp.max(scores, axis=0, keepdims=True)
            grown = jnp.exp(scores - peak)
            total = jnp.sum(grown, axis=0, keepdims=True)
            lse_out[lane, h : h + 1, :] = peak + jnp.log(total)
            shares = (grown * (1.0 / total)).astype(bf16)
            ctx_t[HEAD_DIM + at : 2 * HEAD_DIM + at, :] = mm_tn(v, shares)
        context = ctx_t[...].T
        bent = jnp.tanh(context * inv_limit)
        ctx_low[lane] = (lim[1] * bent).astype(bf16)
        ctx_slope[lane] = 1.0 - bent * bent
        top_ctx[...] = jnp.maximum(top_ctx[...], jnp.max(jnp.abs(context).reshape(-1, 8, context.shape[1]), axis=0))
        return carry

    lax.fori_loop(0, blocks, each, 0)
    top_out[1:2, :] = top_of(top_ctx[...])


def attn_finish(dims, lim, ctx_low, tokens, out_bias, gain, shift, weight, *outs):
    blocks, cols, width = dims
    normed_out, inv_out, middle_out, mid_slope, mid_low, mid_t, top_out, acc = outs
    at = 3 * cols - HEAD_DIM
    acc[...] = tokens[...].astype(f32) + row(out_bias)

    def each(lane, carry):
        acc[...] += mm_nt(ctx_low[lane], weight[lane, :, at:])
        return carry

    lax.fori_loop(0, blocks, each, 0)
    normed, inv = row_stats(acc[...])
    normed_out[...] = normed
    inv_out[...] = inv
    middle = normed * row(gain) + row(shift)
    middle_out[...] = middle
    bent = jnp.tanh(middle * (1.0 / jnp.full((1, 1), lim[2], f32)))
    low = (lim[2] * bent).astype(bf16)
    mid_low[...] = low
    mid_slope[...] = 1.0 - bent * bent
    mid_t[...] = low.T
    top_out[...] = jnp.broadcast_to(top_of(middle), top_out.shape)


def up_forward(net, plan, nb, first, low_q, lim, mid_low, bias, *rest):
    bufs, rest = rest[:nb], rest[nb:]
    act_out, slope_out, top_out, weight, top_hid = rest
    assemble(plan, bufs, weight, net.me()[0])
    top_hid[...] = jnp.zeros_like(top_hid)
    inv_limit = 1.0 / jnp.full((1, 1), lim[3], f32)

    rows = mid_low.shape[0] // 2

    def each(n, carry):
        lane = n // 2
        part = pl.ds(pl.multiple_of((n % 2) * rows, rows), rows)
        up = mm(mid_low[part, :], weight[lane]) + bias[first + lane, :, low_q:]
        half = 0.5 * (1.0 + lax.erf(up * root_half))
        hidden = up * half
        top_hid[...] = jnp.maximum(top_hid[...], jnp.max(jnp.abs(hidden).reshape(-1, 8, hidden.shape[1]), axis=0))
        bent = jnp.tanh(hidden * inv_limit)
        act_out[lane, part] = (lim[3] * bent).astype(bf16)
        slope_out[lane, part] = (1.0 - bent * bent) * (half + up * jnp.exp(-0.5 * up * up) * density_scale)
        return carry

    lax.fori_loop(0, 2 * weight.shape[0], each, 0)
    top_out[...] = jnp.broadcast_to(top_of(top_hid[...]), top_out.shape)


def down_both(net, plan, nb, act0, act1, slope0, slope1, middle, cotangent, down_bias, gain, shift, *rest):
    bufs, rest = rest[:nb], rest[nb:]
    layer_out, grad_out, ffn_t, sums, grad_up, up_sums, weight, acc, ffn_low = rest
    assemble(plan, bufs, weight, net.me()[0])
    acc[...] = middle[...] + row(down_bias)
    half = act0.shape[0]
    for act, first in ((act0, 0), (act1, half)):

        def each(i, carry):
            acc[...] += mm_nt(act[i], weight[first + i])
            return carry

        lax.fori_loop(0, half, each, 0)
    normed, inv = row_stats(acc[...])
    layer_out[...] = (normed * row(gain) + row(shift)).astype(bf16)
    incoming = cotangent[...].astype(f32)
    grad = norm_backward(incoming * row(gain), normed, inv)
    grad_out[...] = grad
    ffn_low[...] = grad.astype(bf16)
    ffn_t[...] = ffn_low[...].T
    sums[...] = jnp.zeros_like(sums)
    sums[0:1, :] = col_sum(grad)
    sums[1:2, :] = col_sum(incoming * normed)
    sums[2:3, :] = col_sum(incoming)
    lane_me = net.me()[1]
    for slope, first in ((slope0, 0), (slope1, half)):

        def back(i, carry):
            low = (mm(ffn_low[...], weight[first + i]) * slope[i]).astype(bf16)
            grad_up[first + i] = low
            up_sums[(first + i) ^ lane_me] = col_sum(low.astype(f32))
            return carry

        lax.fori_loop(0, half, back, 0)


def weight_grad(net, left_t, *rest):
    *rights, far, near = rest
    rows = left_t.shape[0] // net.parts
    dp = net.me()[0]
    half = far.shape[0]
    for x in range(half):
        for out, lane in ((far, 2 * x + 1), (near, 2 * x)):
            right = rights[lane // rights[0].shape[0]]
            grad = mm(left_t[...], right[lane % right.shape[0]]).astype(bf16)
            for block in range(net.parts):
                out[x, net.slot(block, dp)] = grad[block * rows : (block + 1) * rows]


def mid_backward(grad_up, grad_second, mid_slope, normed, inv, gain, weight0, weight1, grad_out, attn_low, attn_t, sums, acc):
    acc[...] = jnp.zeros_like(acc)
    half = weight0.shape[0]
    for weight, first in ((weight0, 0), (weight1, half)):

        def each(i, carry):
            acc[...] += mm_nt(grad_up[first + i], weight[i])
            return carry

        lax.fori_loop(0, half, each, 0)
    incoming = grad_second[...] + acc[...] * mid_slope[...]
    grad = norm_backward(incoming * row(gain), normed[...], inv[...])
    grad_out[...] = grad
    attn_low[...] = grad.astype(bf16)
    attn_t[...] = attn_low[...].T
    sums[...] = jnp.zeros_like(sums)
    sums[0:1, :] = col_sum(grad)
    sums[1:2, :] = col_sum(incoming * normed[...])
    sums[2:3, :] = col_sum(incoming)


def heads_backward(first, dims, lane_me, qkv, lse, attn_low, weight, ctx_slope, mask, grad_ctx, out, sums):
    blocks, cols, width = dims
    heads = cols // HEAD_DIM

    def each(i, carry):
        lane = first + i
        part = mm(attn_low[...], weight[lane, :, 3 * cols - HEAD_DIM :])
        grad_ctx[...] = (part * ctx_slope[lane]).astype(bf16)
        for h in range(heads):
            at = h * HEAD_DIM
            q = qkv[lane, :, at : at + HEAD_DIM]
            k = qkv[lane, :, cols + at : cols + at + HEAD_DIM]
            v = qkv[lane, :, 2 * cols + at : 2 * cols + at + HEAD_DIM]
            grad = grad_ctx[:, HEAD_DIM + at : 2 * HEAD_DIM + at]
            shares = jnp.exp(mm_nt(k, q) * score_scale + mask[...] - lse[lane, h : h + 1, :])
            grad_shares = mm_nt(v, grad)
            inner = jnp.sum(shares * grad_shares, axis=0, keepdims=True)
            grad_scores = (shares * (grad_shares - inner)).astype(bf16)
            grad_v = mm(shares.astype(bf16), grad)
            grad_k = mm(grad_scores, q) * score_scale
            grad_q = (mm_tn(k, grad_scores) * score_scale).T
            out[i, :, at : at + HEAD_DIM] = grad_q.astype(bf16)
            out[i, :, cols + at : cols + at + HEAD_DIM] = grad_k.astype(bf16)
            out[i, :, 2 * cols + at : 2 * cols + at + HEAD_DIM] = grad_v.astype(bf16)
        out[i, :, 3 * cols :] = jnp.zeros((out.shape[1], HEAD_DIM), bf16)
        sums[lane ^ lane_me] = col_sum(out[i].astype(f32))
        return carry

    lax.fori_loop(0, out.shape[0], each, 0)


def attn_backward(net, first, dims, longs, shorts, qkv, lse, attn_low, weight, ctx_slope, out, sums, mask, grad_ctx):
    fill_mask(mask, longs, shorts)
    sums[...] = jnp.zeros_like(sums)
    heads_backward(first, dims, net.me()[1], qkv, lse, attn_low, weight, ctx_slope, mask, grad_ctx, out, sums)


def attn_backward_last(net, dims, longs, shorts, qkv, lse, attn_low, weight, ctx_slope, *rest):
    blocks, cols, width = dims
    in_t, attn_t, ctx_low, more_out, more, *rest = rest
    up_sums, sums_a, sums_b, tops_a, tops_m, top0, top1, *rest = rest
    out, far, near, packed, sums, mask, grad_ctx = rest
    rows = in_t.shape[0] // net.parts
    wide = 3 * cols + HEAD_DIM
    start = 3 * cols - HEAD_DIM
    dp, lane_me = net.me()
    fill_mask(mask, longs, shorts)
    sums[...] = more[...]
    heads_backward(0, dims, lane_me, qkv, lse, attn_low, weight, ctx_slope, mask, grad_ctx, out, sums)
    for x, grads in enumerate((out, more_out)):

        def weights(core, carry):
            left = mm(in_t[...], grads[core])
            right = mm(attn_t[...], ctx_low[2 * x + core])
            mixed = (left[:, start:] + right[:, : wide - start]).astype(bf16)
            left, right = left[:, :start].astype(bf16), right[:, wide - start :].astype(bf16)
            for to, wanted in ((near, 0), (far, 1)):

                @pl.when(core == wanted)
                def _():
                    for block in range(net.parts):
                        rs = slice(block * rows, (block + 1) * rows)
                        place = net.slot(block, dp)
                        to[x, place, :, :start] = left[rs]
                        to[x, place, :, start:wide] = mixed[rs]
                        to[x, place, :, wide:] = right[rs]

            return carry

        lax.fori_loop(0, 2, weights, 0)
    packed[...] = jnp.zeros_like(packed)
    for j in range(blocks):
        packed[j : j + 1, :] = up_sums[j]
        packed[blocks + j : blocks + j + 1, : sums.shape[2]] = sums[j]
    packed[2 * blocks : 2 * blocks + 3, :] = sums_a[0:3, :]
    packed[2 * blocks + 3 : 2 * blocks + 6, :] = sums_b[0:3, :]
    tops = (tops_a[0:1, :], tops_a[1:2, :], tops_m[0:1, :], jnp.maximum(top0[0:1, :], top1[0:1, :]))
    for j, top in enumerate(tops):
        packed[2 * blocks + 6 : 2 * blocks + 7, 128 * j : 128 * j + 128] = top


def token_backward(dims, lim, grads_0, grads_1, grad_first, tokens, weight, out, acc):
    blocks, cols, width = dims
    acc[...] = jnp.zeros_like(acc)
    half = grads_0.shape[0]
    for grads, first in ((grads_0, 0), (grads_1, half)):

        def back(i, carry):
            acc[...] += mm_nt(grads[i], weight[first + i, :, : 3 * cols + HEAD_DIM])
            return carry

        lax.fori_loop(0, half, back, 0)
    inputs = tokens[...].astype(f32)
    out[...] = (grad_first[...] + jnp.where(jnp.abs(inputs) <= lim[0], acc[...], 0.0)).astype(bf16)


def make_body(net):
    def body(
        tokens,
        cotangent,
        qkv_weight,
        qv_bias,
        out_weight,
        out_bias,
        first_gain,
        first_shift,
        up_weight,
        up_bias,
        down_weight,
        down_bias,
        second_gain,
        second_shift,
        act_ranges,
        long_lengths,
        short_lengths,
    ):
        lane = lax.axis_index("tensor")
        rows, width = tokens.shape
        assert rows == LONG_LEN
        cols = qkv_weight.shape[2]
        up_cols = up_weight.shape[1]
        blocks = lax.axis_size("tensor")
        half = blocks // 2
        dims = (blocks, cols, width)
        wide = 3 * cols + HEAD_DIM
        out_cols = cols + HEAD_DIM
        every = tuple(range(blocks))

        pieces_a, pieces_u, pieces_d = Pieces([]), Pieces([]), Pieces([])
        shard_a, shard_d, shard_p, bias_row = shards(qkv_weight, out_weight, qv_bias, up_bias, down_weight.T)
        job_a = Job(net.gather(shard_a, pieces_a))
        job_b = Job(net.gather_lane(bias_row))
        job_u = Job(net.gather(up_weight.astype(bf16), pieces_u))
        job_d = Job(net.gather(shard_d, pieces_d))
        job_p = Job(net.gather_plane_first(shard_p, pieces_d, up_cols // 2))

        def vmem(*shape, dtype=f32):
            return pltpu.VMEM(shape, dtype)

        unit = 2 * rows * width * width * blocks
        moved = 2 * width * width * blocks

        step((), None, [job_a, job_p, job_b], [job_a, job_p, job_b])
        step((), None, [job_a, job_p, job_b, job_d], [job_a, job_p, job_b])
        step((), None, [job_a, job_u], [job_a, job_u, job_d])
        step((), None, [job_a, job_u], [job_a, job_u])
        step((), None, [job_a, job_u], [job_a])
        biases = job_b.value

        bufs, plan = pieces_a.part(every)
        qkv, lse, in_t, ctx_low, ctx_slope, tops_a, weight_a = step(
            (act_ranges, long_lengths, short_lengths, tokens, biases, *bufs),
            call(
                functools.partial(attn_forward, net, plan, len(bufs), dims),
                "attn_forward",
                [SM] * 3 + [VM] * 2 + [VM] * len(bufs),
                [
                    like((blocks, rows, wide), bf16),
                    like((blocks, 8, rows)),
                    like((width, rows), bf16),
                    like((blocks, rows, out_cols), bf16),
                    like((blocks, rows, out_cols)),
                    like((8, 128)),
                    like((blocks, width, 4 * cols), bf16),
                ],
                [vmem(rows, width, dtype=bf16), vmem(rows, rows), vmem(out_cols, rows), vmem(8, out_cols)],
                4 * unit,
                3 * moved,
            ),
            [job_d, job_p],
            [job_u, job_d, job_p],
        )
        normed, inv, middle, mid_slope, mid_low, mid_t, tops_m = step(
            (act_ranges, ctx_low, tokens, out_bias, first_gain, first_shift, weight_a),
            call(
                functools.partial(attn_finish, dims),
                "attn_finish",
                [SM] + [VM] * 6,
                [
                    like((rows, width)),
                    like((rows, 1)),
                    like((rows, width)),
                    like((rows, width)),
                    like((rows, width), bf16),
                    like((width, rows), bf16),
                    like((8, 128)),
                ],
                [vmem(rows, width)],
                2 * unit,
                2 * moved,
            ),
            [job_u, job_p],
            [job_u],
        )

        def up_part(lanes, start, finish):
            bufs, plan = pieces_u.part(lanes)
            return step(
                (act_ranges, mid_low, biases, *bufs),
                call(
                    functools.partial(up_forward, net, plan, len(bufs), lanes[0], wide),
                    f"up_forward_{lanes[0]}",
                    [SM] + [VM] * 2 + [VM] * len(bufs),
                    [
                        like((half, rows, up_cols), bf16),
                        like((half, rows, up_cols)),
                        like((8, 128)),
                        like((half, width, up_cols), bf16),
                    ],
                    [vmem(8, up_cols)],
                    2 * unit,
                    2 * moved,
                ),
                start,
                finish,
            )

        act0, slope0, top0, weight_u0 = up_part(every[:half], [job_u, job_d], [job_u])
        act1, slope1, top1, weight_u1 = up_part(every[half:], [], [job_d, job_p])
        step((), None, [job_d], [job_d])
        step((), None, [job_d, job_p], [job_d, job_p])
        bufs_d, plan_d = pieces_d.part(every)
        layer_out, grad_second, ffn_t, sums_b, grad_up, up_sums = step(
            (act0, act1, slope0, slope1, middle, cotangent, down_bias, second_gain, second_shift, *bufs_d),
            call(
                functools.partial(down_both, net, plan_d, len(bufs_d)),
                "down_both",
                [VM] * 9 + [VM] * len(bufs_d),
                [
                    like((rows, width), bf16),
                    like((rows, width)),
                    like((width, rows), bf16),
                    like((8, width)),
                    like((blocks, rows, up_cols), bf16),
                    like((blocks, 1, up_cols)),
                ],
                [
                    vmem(blocks, width, up_cols, dtype=bf16),
                    vmem(rows, width),
                    vmem(rows, width, dtype=bf16),
                ],
                2 * unit,
                4 * moved,
            ),
        )

        grad_shape = like((net.parts, width // net.parts, up_cols), bf16)
        both_shape = like((half,) + grad_shape.shape, bf16)

        def grad_of(name, left_t, rights, start=(), finish=()):
            return step(
                (left_t, *rights),
                call(
                    functools.partial(weight_grad, net),
                    name,
                    [VM] * (1 + len(rights)),
                    [both_shape, both_shape],
                    (),
                    unit,
                    moved,
                ),
                start,
                finish,
            )

        sum_d = Job(net.scatter_z_first(*grad_of("down_grad", ffn_t, (act0, act1))))
        sum_u = Job(net.scatter_sum(*grad_of("up_grad", mid_t, (grad_up,), [sum_d], [sum_d])))
        grad_first, attn_low, attn_t, sums_a = step(
            (grad_up, grad_second, mid_slope, normed, inv, first_gain, weight_u0, weight_u1),
            call(
                mid_backward,
                "mid_backward",
                [VM] * 8,
                [like((rows, width)), like((rows, width), bf16), like((width, rows), bf16), like((8, width))],
                [vmem(rows, width)],
                unit + unit // 3,
                3 * moved,
            ),
            [sum_u, sum_d],
            [sum_u],
        )
        grads_1, more = step(
            (long_lengths, short_lengths, qkv, lse, attn_low, weight_a, ctx_slope),
            call(
                functools.partial(attn_backward, net, half, dims),
                "attn_backward",
                [SM] * 2 + [VM] * 5,
                [like((half, rows, wide), bf16), like((blocks, 1, wide))],
                [vmem(rows, rows), vmem(rows, out_cols, dtype=bf16)],
                2 * unit,
                2 * moved,
            ),
            [sum_u],
            [sum_u, sum_d],
        )
        grads_0, far, near, packed = step(
            (long_lengths, short_lengths, qkv, lse, attn_low, weight_a, ctx_slope)
            + (in_t, attn_t, ctx_low, grads_1, more)
            + (up_sums, sums_a, sums_b, tops_a, tops_m, top0, top1),
            call(
                functools.partial(attn_backward_last, net, dims),
                "attn_backward_last",
                [SM] * 2 + [VM] * 17,
                [like((half, rows, wide), bf16), both_shape, both_shape, like((16, width))],
                [vmem(blocks, 1, wide), vmem(rows, rows), vmem(rows, out_cols, dtype=bf16)],
                4 * unit,
                2 * moved,
            ),
            [sum_u, sum_d],
            [sum_u, sum_d],
        )
        sum_a = Job(net.scatter_sum(far, near))
        is_top = (jnp.arange(packed.shape[0]) == 2 * blocks + 6)[:, None]
        sum_s = Job(net.sum_max(packed, is_top))
        line_u = Job(net.scatter_line(*sum_u.value))
        tokens_grad = step(
            (act_ranges, grads_0, grads_1, grad_first, tokens, weight_a),
            call(
                functools.partial(token_backward, dims),
                "token_backward",
                [SM] + [VM] * 5,
                [like((rows, width), bf16)],
                [vmem(rows, width)],
                unit,
                2 * moved,
            ),
            [sum_a, sum_d, line_u, sum_s],
            [sum_a, sum_d, line_u, sum_s],
        )[0]
        step((), None, [sum_a, sum_d, sum_s], [sum_a, sum_s])
        step((), None, [sum_a, line_u, sum_s], [sum_a, sum_d, line_u, sum_s])
        line_a = Job(net.scatter_line(*sum_a.value))
        step((), None, [line_a, sum_s], [sum_s])
        step((), None, [sum_s], [line_a, sum_s])

        def finish(packed, down, up, ranges):
            own = lax.dynamic_slice_in_dim(packed, blocks + lane, 1)
            shared = packed[2 * blocks : 2 * blocks + 6]
            return (
                down[0] + down[1].astype(f32),
                up[0] + up[1].astype(f32),
                jnp.concatenate([own[:, :cols], own[:, 2 * cols : 3 * cols]], 0),
                lax.dynamic_slice_in_dim(packed, lane, 1)[0],
                [shared[n] for n in range(6)],
                ema_decay * ranges + (1.0 - ema_decay) * packed[2 * blocks + 6, 0:512:128],
            )

        down_grad, up_grad, qv_bias_grad, up_bias_grad, shared, new_ranges = step(
            (sum_s.value, sum_d.value, line_u.value, act_ranges), finish, [line_a], [line_a]
        )
        down_grad = down_grad.T
        qkv_grad, out_grad = attn_grads(*line_a.value)
        return (
            layer_out,
            tokens_grad,
            qkv_grad,
            qv_bias_grad,
            out_grad,
            shared[0],
            shared[1],
            shared[2],
            up_grad,
            up_bias_grad,
            down_grad,
            shared[3],
            shared[4],
            shared[5],
            new_ranges,
        )

    return body


def solution(mesh):
    in_specs = (
        P(ALL, None),
        P(ALL, None),
        P(None, "dp", "tensor"),
        P(None, "tensor"),
        P("tensor", "dp"),
        P(),
        P(),
        P(),
        P("dp", "tensor"),
        P("tensor"),
        P("tensor", "dp"),
        P(),
        P(),
        P(),
        P(),
        P("dp"),
        P("dp"),
    )
    out_specs = (
        P(ALL, None),
        P(ALL, None),
        P(None, "dp", "tensor"),
        P(None, "tensor"),
        P("tensor", "dp"),
        P(),
        P(),
        P(),
        P("dp", "tensor"),
        P("tensor"),
        P("tensor", "dp"),
        P(),
        P(),
        P(),
        P(),
    )
    net = Grid() if mesh.shape["dp"] == 8 and mesh.shape["tensor"] == 4 else Plain()
    return jax.shard_map(make_body(net), mesh=mesh, in_specs=in_specs, out_specs=out_specs, check_vma=False)
```

```python
import functools
import itertools

import jax
import jax.numpy as jnp
from jax import lax
from jax.experimental import pallas as pl
from jax.experimental.pallas import tpu as pltpu
from jax.sharding import PartitionSpec as P

HEAD_DIM = 64
LONG_LEN = 512
SHORT_LEN = 128
ALL = ("dp", "tensor")

ema_decay = 0.9
epsilon = 1e-06
root_half = 0.7071067811865476
density_scale = 0.3989422804014327
score_scale = HEAD_DIM ** (-0.5)
NEG = -1000000000.0

f32 = jnp.float32
bf16 = jnp.bfloat16


def mm(left, right):
    return jnp.dot(left, right, preferred_element_type=f32)


def mm_tn(left, right):
    return lax.dot_general(left, right, (((0,), (0,)), ((), ())), preferred_element_type=f32)


def mm_nt(left, right):
    return lax.dot_general(left, right, (((1,), (1,)), ((), ())), preferred_element_type=f32)


def _lin(z, y, x, c):
    return (z * 2 + y) * 4 + x * 2 + c


def _perm(fn):
    out = []
    for z, y, x, c in itertools.product(range(4), range(2), range(2), range(2)):
        out.append((_lin(z, y, x, c), _lin(*fn(z, y, x, c))))
    return out


PC = _perm(lambda z, y, x, c: (z, y, x, 1 - c))
PX = _perm(lambda z, y, x, c: (z, y, 1 - x, c))
PY = _perm(lambda z, y, x, c: (z, 1 - y, x, c))
PZ1 = _perm(lambda z, y, x, c: (z ^ 1, y, x, c))
PZ2 = _perm(lambda z, y, x, c: (z ^ 2, y, x, c))


def tie(*trees):
    leaves, spec = jax.tree.flatten(trees)
    return jax.tree.unflatten(spec, lax.optimization_barrier(leaves))


class Job:
    def __init__(self, stages):
        self.stages, self.value, self.out, self.flight, self.over = stages, None, [], [], False
        self.take(None)

    def take(self, got):
        if not self.over:
            try:
                self.out = self.stages.send(got)
            except StopIteration as stop:
                self.value, self.out, self.over = stop.value, [], True


def step(ins, run=None, start=(), finish=()):
    ins, sends = tie(ins, [[value for value, _ in job.out] for job in start])
    for job, values in zip(start, sends):
        job.flight = [lax.ppermute(v, ALL, perm) for v, (_, perm) in zip(values, job.out)]
    outs = run(*ins) if run else ins
    outs, got = tie(outs, [job.flight for job in finish])
    for job, values in zip(finish, got):
        job.flight = []
        job.take(values)
    return outs


class Pieces:
    def __init__(self, plan):
        self.bufs, self.plan = {}, plan

    def part(self, lanes):
        plan = [p for p in self.plan if p[1] in lanes]
        names = sorted({p[0] for p in plan})
        return [self.bufs[n] for n in names], [(names.index(b), lane - lanes[0], at, col) for b, lane, at, col in plan]


class Grid:
    parts = 8

    @staticmethod
    def gather(shard, pieces):
        own = shard[None]
        for base, lane in ((0, 0), (5, 1)):
            pieces.plan.append((base, lane, (4, 4, 2, 0, 0), 0))
            pieces.plan.append((base + 1, lane, (4, 4, 2, 1, 0), 0))
            pieces.plan.append((base + 2, lane + 2, (4, 4, 2, 0, 0), 0))
            pieces.plan.append((base + 3, lane + 2, (2, 4, 0, 1, 0), 0))
            pieces.plan.append((base + 4, lane + 2, (2, 4, 0, 3, 0), 0))
        (far_z,) = yield [(own, PZ2)]
        pair = jnp.concatenate([own, far_z], 0)
        (near_z,) = yield [(pair, PZ1)]
        line = jnp.concatenate([pair, near_z], 0)
        over_x, over_y, line_far = yield [(line, PX), (line, PY), (line, PC)]
        pieces.bufs.update({0: line, 1: over_y, 2: over_x, 5: line_far})
        diag_x, diag_y, over_y_far, over_x_far = yield [
            (over_y[:2], PX),
            (over_x[2:], PY),
            (over_y, PC),
            (over_x, PC),
        ]
        pieces.bufs.update({3: diag_x, 4: diag_y, 6: over_y_far, 7: over_x_far})
        diag_x_far, diag_y_far = yield [(diag_x, PC), (diag_y, PC)]
        pieces.bufs.update({8: diag_x_far, 9: diag_y_far})

    @staticmethod
    def gather_plane_first(shard, pieces, first_col):
        own = shard[None]
        over_x, over_y = yield [(own, PX), (own, PY)]
        (diag,) = yield [(over_y, PX)]
        plane = jnp.concatenate([own, over_y, over_x, diag], 0)
        (far_z,) = yield [(plane, PZ2)]
        half = jnp.concatenate([plane, far_z], 0)
        (near_z,) = yield [(half, PZ1)]
        half_far, near_z_far = yield [(half, PC), (near_z, PC)]
        for n, (buf, core) in enumerate(((half, 0), (near_z, 0), (half_far, 1), (near_z_far, 1))):
            near = 2 * (n % 2)
            name = 20 + n
            pieces.bufs[name] = buf
            for x in range(2):
                pieces.plan.append((name, 2 * x + core, (4, 1, 4, near, 2), first_col + x))

    @staticmethod
    def slot(block, dp):
        place = block ^ dp
        return (place & 1) * 4 + (place & 2) + (place >> 2)

    @staticmethod
    def scatter_sum(far, near):
        (got,) = yield [(far, PC)]
        out_x, out_y = add_first(near, got)
        from_x, from_y = yield [(out_x, PX), (out_y, PY)]
        out_x, out_y = add_second(near, got, near, got, from_x, from_y)
        in_x, in_y = yield [(out_x, PX), (out_y, PY)]
        return near, got, in_x, in_y

    @staticmethod
    def scatter_halves(far_1, near_1, late):
        (got_1,) = yield [(far_1, PC)]
        out_x, out_y = add_first(near_1, got_1)
        from_x, from_y, got = yield [(out_x, PX), (out_y, PY), (late["far"], PC)]
        near = late["near"]
        out_x, out_y = add_second(near_1, got_1, near, got, from_x, from_y)
        in_x, in_y = yield [(out_x, PX), (out_y, PY)]
        return near, got, in_x, in_y

    @staticmethod
    def scatter_line(near, got, in_x, in_y):
        out_z, kept = add_third(near, got, in_x, in_y)
        (from_z,) = yield [(out_z, PZ1)]
        out_z, kept = add_fourth(kept, from_z)
        (last,) = yield [(out_z, PZ2)]
        return kept, last

    @staticmethod
    def scatter_z_first(far, near):
        (got,) = yield [(far, PC)]
        out_1, out_0 = add_near_z(near, got)
        (from_1,) = yield [(out_1, PZ1)]
        out_x, out_y = add_corner(near, got, from_1)
        from_x, from_y, from_0 = yield [(out_x, PX), (out_y, PY), (out_0, PZ1)]
        out_x, out_y = add_sides(near, got, from_1, from_0, from_x, from_y)
        in_x, in_y = yield [(out_x, PX), (out_y, PY)]
        out_z, kept = add_own(near, got, from_0, in_x, in_y)
        (last,) = yield [(out_z, PZ2)]
        return kept, last

    @staticmethod
    def gather_lane(vec):
        (other,) = yield [(vec, PX)]
        pair = jnp.stack([vec, other])
        (more,) = yield [(pair, PC)]
        return jnp.stack([pair, more], 1).reshape((4,) + vec.shape)

    @staticmethod
    def sum_max(both, is_top):
        for perm in (PC, PZ1, PZ2, PX, PY):
            (other,) = yield [(both, perm)]
            both = jnp.where(is_top, jnp.maximum(both, other), both + other)
        return both

    @staticmethod
    def me():
        return lax.axis_index("dp"), lax.axis_index("tensor")


class Plain:
    parts = 1

    @staticmethod
    def gather(shard, pieces, first_col=0):
        rows = lax.all_gather(shard, "dp", axis=0, tiled=True)
        full = lax.all_gather(rows, "tensor", axis=0)
        for k in range(full.shape[0]):
            pieces.plan.append((first_col + k, k, None, first_col))
            pieces.bufs[first_col + k] = full[k][None]
        return
        yield

    gather_plane_first = gather

    @staticmethod
    def slot(block, dp):
        return block

    @staticmethod
    def scatter_sum(far, near):
        grads = jnp.stack([near[0], far[0], near[1], far[1]]).astype(f32)
        return (grads.reshape((4, -1, grads.shape[-1])),)
        yield

    @staticmethod
    def scatter_halves(far_1, near_1, late):
        while not late:
            yield []
        far = jnp.concatenate([late["far"], far_1], 0)
        return (yield from Plain.scatter_sum(far, jnp.concatenate([late["near"], near_1], 0)))

    @staticmethod
    def scatter_line(grads):
        own = lax.psum_scatter(grads, "tensor", scatter_dimension=0, tiled=False)
        own = lax.psum_scatter(own, "dp", scatter_dimension=0, tiled=True)
        return own, jnp.zeros_like(own)
        yield

    @staticmethod
    def scatter_z_first(far, near):
        grads = yield from Plain.scatter_sum(far, near)
        return (yield from Plain.scatter_line(*grads))

    @staticmethod
    def gather_lane(vec):
        return lax.all_gather(vec, "tensor", axis=0)
        yield

    @staticmethod
    def sum_max(both, is_top):
        return jnp.where(is_top, lax.pmax(both, ALL), lax.psum(both, ALL))
        yield

    @staticmethod
    def me():
        return 0, 0


VM = pl.BlockSpec(memory_space=pltpu.VMEM)
SM = pl.BlockSpec(memory_space=pltpu.SMEM)
VMEM_MIB = 8
ROOMY = ("down_both",)


def like(shape, dtype=f32):
    return jax.ShapeDtypeStruct(shape, dtype)


def call(kernel, name, specs, outs, scratch=(), flops=0, moved=0):
    return pl.pallas_call(
        kernel,
        name=name,
        out_shape=outs,
        in_specs=specs,
        out_specs=[VM] * len(outs),
        scratch_shapes=list(scratch),
        compiler_params=pltpu.CompilerParams(vmem_limit_bytes=(14 if name in ROOMY else VMEM_MIB) * 2**20),
        cost_estimate=pl.CostEstimate(flops=flops, bytes_accessed=moved, transcendentals=0),
    )


def glue(kernel, outs, *ins):
    return call(kernel, kernel.__name__, [VM] * len(ins), outs)(*ins)


def add_first(near, got):
    top = near.shape[0] - 1

    def first_sums(near, got, out_x, out_y):
        for k in range(2):
            out_x[k] = (near[top, 4 + k].astype(f32) + got[top, 4 + k].astype(f32)).astype(bf16)
            out_y[k] = (near[top, 6 + k].astype(f32) + got[top, 6 + k].astype(f32)).astype(bf16)

    part = like((2,) + near.shape[2:], bf16)
    return glue(first_sums, [part, part], near, got)


def add_second(near_1, got_1, near, got, from_x, from_y):
    top = near_1.shape[0] - 1

    def second_sums(near_1, got_1, near, got, from_x, from_y, out_x, out_y):
        for k in range(4):
            over_x = near_1[top, k].astype(f32) + got_1[top, k].astype(f32)
            over_y = near[0, 4 + k].astype(f32) + got[0, 4 + k].astype(f32)
            if k < 2:
                over_y = over_y + from_x[k].astype(f32)
            else:
                over_x = over_x + from_y[k - 2].astype(f32)
            out_x[k] = over_x.astype(bf16)
            out_y[k] = over_y.astype(bf16)

    part = like((4,) + near.shape[2:], bf16)
    return glue(second_sums, [part, part], near_1, got_1, near, got, from_x, from_y)


def add_third(near, got, in_x, in_y):
    def third_sums(near, got, in_x, in_y, out, kept):
        for k in range(4):
            total = near[0, k].astype(f32) + got[0, k].astype(f32) + in_x[k].astype(f32) + in_y[k].astype(f32)
            if k < 2:
                kept[k] = total
            else:
                out[k - 2] = total.astype(bf16)

    shape = (2,) + near.shape[2:]
    return glue(third_sums, [like(shape, bf16), like(shape)], near, got, in_x, in_y)


def add_fourth(kept, from_z):
    def fourth_sums(kept, from_z, out, mine):
        mine[...] = kept[0] + from_z[0].astype(f32)
        out[...] = (kept[1] + from_z[1].astype(f32)).astype(bf16)

    shape = kept.shape[1:]
    return glue(fourth_sums, [like(shape, bf16), like(shape)], kept, from_z)


def add_near_z(near, got):
    def near_z_sums(near, got, out_1, out_0):
        for x, out in ((1, out_1), (0, out_0)):
            for y in range(2):
                for k in range(2):
                    at = 4 * y + 2 + k
                    out[2 * y + k] = (near[x, at].astype(f32) + got[x, at].astype(f32)).astype(bf16)

    part = like((4,) + near.shape[2:], bf16)
    return glue(near_z_sums, [part, part], near, got)


def three(near, got, from_z, x, y, k):
    return near[x, 4 * y + k].astype(f32) + got[x, 4 * y + k].astype(f32) + from_z[2 * y + k].astype(f32)


def add_corner(near, got, from_1):
    def corner_sums(near, got, from_1, out_x, out_y):
        out_x[...] = three(near, got, from_1, 1, 1, 0).astype(bf16)
        out_y[...] = three(near, got, from_1, 1, 1, 1).astype(bf16)

    part = like(near.shape[2:], bf16)
    return glue(corner_sums, [part, part], near, got, from_1)


def add_sides(near, got, from_1, from_0, from_x, from_y):
    def side_sums(near, got, from_1, from_0, from_x, from_y, out_x, out_y):
        out_x[0] = three(near, got, from_1, 1, 0, 0).astype(bf16)
        out_x[1] = (three(near, got, from_1, 1, 0, 1) + from_y[...].astype(f32)).astype(bf16)
        out_y[0] = (three(near, got, from_0, 0, 1, 0) + from_x[...].astype(f32)).astype(bf16)
        out_y[1] = three(near, got, from_0, 0, 1, 1).astype(bf16)

    part = like((2,) + near.shape[2:], bf16)
    return glue(side_sums, [part, part], near, got, from_1, from_0, from_x, from_y)


def add_own(near, got, from_0, in_x, in_y):
    def own_sums(near, got, from_0, in_x, in_y, out, kept):
        kept[...] = three(near, got, from_0, 0, 0, 0) + in_x[0].astype(f32) + in_y[0].astype(f32)
        out[...] = (three(near, got, from_0, 0, 0, 1) + in_x[1].astype(f32) + in_y[1].astype(f32)).astype(bf16)

    shape = near.shape[2:]
    return glue(own_sums, [like(shape, bf16), like(shape)], near, got, from_0, in_x, in_y)


def attn_grads(kept, last):
    rows, width = kept.shape
    cols = width // 4

    def attn_sums(kept, last, qkv, out):
        total = kept[...] + last[...].astype(f32)
        for j in range(3):
            qkv[j] = total[:, j * cols : (j + 1) * cols]
        out[...] = total[:, 3 * cols :].T

    return glue(attn_sums, [like((3, rows, cols)), like((cols, rows))], kept, last)


def shards(qkv_weight, out_weight, qv_bias, up_bias, down_weight_t):
    _, rows, cols = qkv_weight.shape
    wide = 3 * cols + HEAD_DIM
    width = down_weight_t.shape[1]

    def first_shards(qkv, out_weight, qv_bias, up_bias, down, attn, down_0, down_1, biases):
        for j in range(3):
            attn[:, j * cols : (j + 1) * cols] = qkv[j].astype(bf16)
        attn[:, 3 * cols :] = out_weight[...].T.astype(bf16)
        down_0[...] = down[:, : width // 2].astype(bf16)
        down_1[...] = down[:, width // 2 :].astype(bf16)
        biases[...] = jnp.zeros_like(biases)
        biases[:, :cols] = qv_bias[0:1, :]
        biases[:, 2 * cols : 3 * cols] = qv_bias[1:2, :]
        biases[:, wide:] = row(up_bias)

    part = like((rows, width // 2), bf16)
    outs = [like((rows, 4 * cols), bf16), part, part, like((1, wide + width))]
    return glue(first_shards, outs, qkv_weight, out_weight, qv_bias, up_bias, down_weight_t)


def assemble(plan, bufs, dst, dp):
    for buf, lane, places, col in plan:
        src = bufs[buf]
        _, rows, width = src.shape
        x, col = (col & 1, col - (col & 1))
        cols = pl.ds(col, width)
        if places is None:
            dst[lane, :, cols] = src[0]
            continue
        count, a, b, c, skip = places

        def move(i, carry):
            place = a * (i & 1) + b * (i >> 1) + c
            at = pl.multiple_of((dp ^ place) * rows, rows)
            dst[lane, pl.ds(at, rows), cols] = src[i + skip * ((i >> 1) + x)]
            return carry

        lax.fori_loop(0, count, move, 0)


def row(vec):
    return vec[...].reshape(1, -1)


def row_stats(summed):
    centered = summed - jnp.mean(summed, axis=-1, keepdims=True)
    inv = lax.rsqrt(jnp.mean(centered * centered, axis=-1, keepdims=True) + epsilon)
    return centered * inv, inv


def norm_backward(scaled, normed, inv):
    row_mean = jnp.mean(scaled, axis=-1, keepdims=True)
    row_cross = jnp.mean(scaled * normed, axis=-1, keepdims=True)
    return inv * (scaled - row_mean - normed * row_cross)


def col_sum(values):
    return jnp.sum(values, axis=0, keepdims=True)


def top_of(values):
    return jnp.full((1, 128), jnp.max(jnp.abs(values)), f32)


def fill_mask(mask, longs, shorts):
    per_block = LONG_LEN // SHORT_LEN
    block = lax.axis_index("tensor")
    n_long = longs.shape[0]
    is_long = block < n_long
    whole = longs[jnp.minimum(block, n_long - 1)]
    first = jnp.maximum(block - n_long, 0) * per_block
    shift = jnp.where(is_long, LONG_LEN.bit_length() - 1, SHORT_LEN.bit_length() - 1)
    size = jnp.where(is_long, LONG_LEN, SHORT_LEN)
    k_pos = lax.broadcasted_iota(jnp.int32, (LONG_LEN, 1), 0)
    q_pos = lax.broadcasted_iota(jnp.int32, (1, LONG_LEN), 1)
    k_seg = lax.shift_right_logical(k_pos, jnp.full_like(k_pos, shift))
    q_seg = lax.shift_right_logical(q_pos, jnp.full_like(q_pos, shift))
    limit = jnp.zeros_like(k_pos)
    for j in range(per_block):
        limit = jnp.where(k_seg == j, jnp.where(is_long, whole, shorts[first + j]), limit)
    k_seg = jnp.where(k_pos - k_seg * size < limit, k_seg, -1)
    mask[...] = jnp.where(k_seg == q_seg, 0.0, NEG)


def attn_forward(net, plan, nb, dims, lim, longs, shorts, tokens, bias, *rest):
    blocks, cols, width = dims
    bufs, rest = rest[:nb], rest[nb:]
    qkv_out, lse_out, in_t, ctx_low, ctx_slope, top_out, weight, in_low, mask, ctx_t, top_ctx = rest
    heads = cols // HEAD_DIM
    low_q = 3 * cols + HEAD_DIM
    assemble(plan, bufs, weight, net.me()[0])
    inputs = tokens[...].astype(f32)
    in_low[...] = jnp.clip(inputs, -lim[0], lim[0]).astype(bf16)
    in_t[...] = in_low[...].T
    top_out[0:1, :] = top_of(inputs)
    fill_mask(mask, longs, shorts)
    ctx_t[0:HEAD_DIM, :] = jnp.zeros((HEAD_DIM, ctx_t.shape[1]), f32)
    top_ctx[...] = jnp.zeros_like(top_ctx)
    inv_limit = 1.0 / jnp.full((1, 1), lim[1], f32)

    def each(lane, carry):
        qkv = (mm(in_low[...], weight[lane, :, :low_q]) + bias[lane, :, :low_q]).astype(bf16)
        qkv_out[lane] = qkv
        for h in range(heads):
            at = h * HEAD_DIM
            q = qkv[:, at : at + HEAD_DIM]
            k = qkv[:, cols + at : cols + at + HEAD_DIM]
            v = qkv[:, 2 * cols + at : 2 * cols + at + HEAD_DIM]
            scores = mm_nt(k, q) * score_scale + mask[...]
            peak = jnp.max(scores, axis=0, keepdims=True)
            grown = jnp.exp(scores - peak)
            total = jnp.sum(grown, axis=0, keepdims=True)
            lse_out[lane, h : h + 1, :] = peak + jnp.log(total)
            shares = (grown * (1.0 / total)).astype(bf16)
            ctx_t[HEAD_DIM + at : 2 * HEAD_DIM + at, :] = mm_tn(v, shares)
        context = ctx_t[...].T
        bent = jnp.tanh(context * inv_limit)
        ctx_low[lane] = (lim[1] * bent).astype(bf16)
        ctx_slope[lane] = 1.0 - bent * bent
        top_ctx[...] = jnp.maximum(top_ctx[...], jnp.max(jnp.abs(context).reshape(-1, 8, context.shape[1]), axis=0))
        return carry

    lax.fori_loop(0, blocks, each, 0)
    top_out[1:2, :] = top_of(top_ctx[...])


def attn_finish(dims, lim, ctx_low, tokens, out_bias, gain, shift, weight, *outs):
    blocks, cols, width = dims
    normed_out, inv_out, middle_out, mid_slope, mid_low, mid_t, top_out, acc = outs
    at = 3 * cols - HEAD_DIM
    acc[...] = tokens[...].astype(f32) + row(out_bias)

    def each(lane, carry):
        acc[...] += mm_nt(ctx_low[lane], weight[lane, :, at:])
        return carry

    lax.fori_loop(0, blocks, each, 0)
    normed, inv = row_stats(acc[...])
    normed_out[...] = normed
    inv_out[...] = inv
    middle = normed * row(gain) + row(shift)
    middle_out[...] = middle
    bent = jnp.tanh(middle * (1.0 / jnp.full((1, 1), lim[2], f32)))
    low = (lim[2] * bent).astype(bf16)
    mid_low[...] = low
    mid_slope[...] = 1.0 - bent * bent
    mid_t[...] = low.T
    top_out[...] = jnp.broadcast_to(top_of(middle), top_out.shape)


def up_forward(net, plan, nb, first, low_q, lim, mid_low, bias, *rest):
    bufs, rest = rest[:nb], rest[nb:]
    act_out, slope_out, top_out, weight, top_hid = rest
    assemble(plan, bufs, weight, net.me()[0])
    top_hid[...] = jnp.zeros_like(top_hid)
    inv_limit = 1.0 / jnp.full((1, 1), lim[3], f32)

    rows = mid_low.shape[0] // 2

    def each(n, carry):
        lane = n // 2
        part = pl.ds(pl.multiple_of((n % 2) * rows, rows), rows)
        up = mm(mid_low[part, :], weight[lane]) + bias[first + lane, :, low_q:]
        half = 0.5 * (1.0 + lax.erf(up * root_half))
        hidden = up * half
        top_hid[...] = jnp.maximum(top_hid[...], jnp.max(jnp.abs(hidden).reshape(-1, 8, hidden.shape[1]), axis=0))
        bent = jnp.tanh(hidden * inv_limit)
        act_out[lane, part] = (lim[3] * bent).astype(bf16)
        slope_out[lane, part] = (1.0 - bent * bent) * (half + up * jnp.exp(-0.5 * up * up) * density_scale)
        return carry

    lax.fori_loop(0, 2 * weight.shape[0], each, 0)
    top_out[...] = jnp.broadcast_to(top_of(top_hid[...]), top_out.shape)


def down_both(net, plan, nb, act0, act1, slope0, slope1, middle, cotangent, down_bias, gain, shift, *rest):
    bufs, rest = rest[:nb], rest[nb:]
    layer_out, grad_out, ffn_t, sums, grad_up, up_sums, weight, acc, ffn_low = rest
    assemble(plan, bufs, weight, net.me()[0])
    acc[...] = middle[...] + row(down_bias)
    half = act0.shape[0]
    for act, first in ((act0, 0), (act1, half)):

        def each(i, carry):
            acc[...] += mm_nt(act[i], weight[first + i])
            return carry

        lax.fori_loop(0, half, each, 0)
    normed, inv = row_stats(acc[...])
    layer_out[...] = (normed * row(gain) + row(shift)).astype(bf16)
    incoming = cotangent[...].astype(f32)
    grad = norm_backward(incoming * row(gain), normed, inv)
    grad_out[...] = grad
    ffn_low[...] = grad.astype(bf16)
    ffn_t[...] = ffn_low[...].T
    sums[...] = jnp.zeros_like(sums)
    sums[0:1, :] = col_sum(grad)
    sums[1:2, :] = col_sum(incoming * normed)
    sums[2:3, :] = col_sum(incoming)
    lane_me = net.me()[1]
    for slope, first in ((slope0, 0), (slope1, half)):

        def back(i, carry):
            low = (mm(ffn_low[...], weight[first + i]) * slope[i]).astype(bf16)
            grad_up[first + i] = low
            up_sums[(first + i) ^ lane_me] = col_sum(low.astype(f32))
            return carry

        lax.fori_loop(0, half, back, 0)


def weight_grad(net, left_t, *rest):
    *rights, far, near = rest
    rows = left_t.shape[0] // net.parts
    dp = net.me()[0]
    half = far.shape[0]
    for x in range(half):
        for out, lane in ((far, 2 * x + 1), (near, 2 * x)):
            right = rights[lane // rights[0].shape[0]]
            grad = mm(left_t[...], right[lane % right.shape[0]]).astype(bf16)
            for block in range(net.parts):
                out[x, net.slot(block, dp)] = grad[block * rows : (block + 1) * rows]


def mid_backward(grad_up, grad_second, mid_slope, normed, inv, gain, weight0, weight1, grad_out, attn_low, attn_t, sums, acc):
    acc[...] = jnp.zeros_like(acc)
    half = weight0.shape[0]
    for weight, first in ((weight0, 0), (weight1, half)):

        def each(i, carry):
            acc[...] += mm_nt(grad_up[first + i], weight[i])
            return carry

        lax.fori_loop(0, half, each, 0)
    incoming = grad_second[...] + acc[...] * mid_slope[...]
    grad = norm_backward(incoming * row(gain), normed[...], inv[...])
    grad_out[...] = grad
    attn_low[...] = grad.astype(bf16)
    attn_t[...] = attn_low[...].T
    sums[...] = jnp.zeros_like(sums)
    sums[0:1, :] = col_sum(grad)
    sums[1:2, :] = col_sum(incoming * normed[...])
    sums[2:3, :] = col_sum(incoming)


def heads_backward(first, dims, lane_me, qkv, lse, attn_low, weight, ctx_slope, mask, grad_ctx, out, sums):
    blocks, cols, width = dims
    heads = cols // HEAD_DIM

    def each(i, carry):
        lane = first + i
        part = mm(attn_low[...], weight[lane, :, 3 * cols - HEAD_DIM :])
        grad_ctx[...] = (part * ctx_slope[lane]).astype(bf16)
        for h in range(heads):
            at = h * HEAD_DIM
            q = qkv[lane, :, at : at + HEAD_DIM]
            k = qkv[lane, :, cols + at : cols + at + HEAD_DIM]
            v = qkv[lane, :, 2 * cols + at : 2 * cols + at + HEAD_DIM]
            grad = grad_ctx[:, HEAD_DIM + at : 2 * HEAD_DIM + at]
            shares = jnp.exp(mm_nt(k, q) * score_scale + mask[...] - lse[lane, h : h + 1, :])
            grad_shares = mm_nt(v, grad)
            inner = jnp.sum(shares * grad_shares, axis=0, keepdims=True)
            grad_scores = (shares * (grad_shares - inner)).astype(bf16)
            grad_v = mm(shares.astype(bf16), grad)
            grad_k = mm(grad_scores, q) * score_scale
            grad_q = (mm_tn(k, grad_scores) * score_scale).T
            out[i, :, at : at + HEAD_DIM] = grad_q.astype(bf16)
            out[i, :, cols + at : cols + at + HEAD_DIM] = grad_k.astype(bf16)
            out[i, :, 2 * cols + at : 2 * cols + at + HEAD_DIM] = grad_v.astype(bf16)
        out[i, :, 3 * cols :] = jnp.zeros((out.shape[1], HEAD_DIM), bf16)
        sums[lane ^ lane_me] = col_sum(out[i].astype(f32))
        return carry

    lax.fori_loop(0, out.shape[0], each, 0)


def in_weight_grads(net, first, dims, in_t, attn_t, ctx_low, grads, far, near):
    blocks, cols, width = dims
    rows = in_t.shape[0] // net.parts
    wide = 3 * cols + HEAD_DIM
    start = 3 * cols - HEAD_DIM
    dp = net.me()[0]

    def weights(core, carry):
        left = mm(in_t[...], grads[core])
        right = mm(attn_t[...], ctx_low[first + core])
        mixed = (left[:, start:] + right[:, : wide - start]).astype(bf16)
        left, right = left[:, :start].astype(bf16), right[:, wide - start :].astype(bf16)
        for to, wanted in ((near, 0), (far, 1)):

            @pl.when(core == wanted)
            def _():
                for block in range(net.parts):
                    rs = slice(block * rows, (block + 1) * rows)
                    place = net.slot(block, dp)
                    to[0, place, :, :start] = left[rs]
                    to[0, place, :, start:wide] = mixed[rs]
                    to[0, place, :, wide:] = right[rs]

        return carry

    lax.fori_loop(0, 2, weights, 0)


def attn_backward(net, first, dims, longs, shorts, qkv, lse, attn_low, weight, ctx_slope, in_t, attn_t, ctx_low, *rest):
    out, far, near, sums, mask, grad_ctx = rest
    fill_mask(mask, longs, shorts)
    sums[...] = jnp.zeros_like(sums)
    heads_backward(first, dims, net.me()[1], qkv, lse, attn_low, weight, ctx_slope, mask, grad_ctx, out, sums)
    in_weight_grads(net, first, dims, in_t, attn_t, ctx_low, out, far, near)


def attn_backward_last(net, dims, longs, shorts, qkv, lse, attn_low, weight, ctx_slope, in_t, attn_t, ctx_low, *rest):
    blocks, cols, width = dims
    more, up_sums, sums_a, sums_b, tops_a, tops_m, top0, top1, out, far, near, packed, sums, mask, grad_ctx = rest
    fill_mask(mask, longs, shorts)
    sums[...] = more[...]
    heads_backward(0, dims, net.me()[1], qkv, lse, attn_low, weight, ctx_slope, mask, grad_ctx, out, sums)
    in_weight_grads(net, 0, dims, in_t, attn_t, ctx_low, out, far, near)
    packed[...] = jnp.zeros_like(packed)
    for j in range(blocks):
        packed[j : j + 1, :] = up_sums[j]
        packed[blocks + j : blocks + j + 1, : sums.shape[2]] = sums[j]
    packed[2 * blocks : 2 * blocks + 3, :] = sums_a[0:3, :]
    packed[2 * blocks + 3 : 2 * blocks + 6, :] = sums_b[0:3, :]
    tops = (tops_a[0:1, :], tops_a[1:2, :], tops_m[0:1, :], jnp.maximum(top0[0:1, :], top1[0:1, :]))
    for j, top in enumerate(tops):
        packed[2 * blocks + 6 : 2 * blocks + 7, 128 * j : 128 * j + 128] = top


def token_backward(dims, lim, grads_0, grads_1, grad_first, tokens, weight, out, acc):
    blocks, cols, width = dims
    acc[...] = jnp.zeros_like(acc)
    half = grads_0.shape[0]
    for grads, first in ((grads_0, 0), (grads_1, half)):

        def back(i, carry):
            acc[...] += mm_nt(grads[i], weight[first + i, :, : 3 * cols + HEAD_DIM])
            return carry

        lax.fori_loop(0, half, back, 0)
    inputs = tokens[...].astype(f32)
    out[...] = (grad_first[...] + jnp.where(jnp.abs(inputs) <= lim[0], acc[...], 0.0)).astype(bf16)


def make_body(net):
    def body(
        tokens,
        cotangent,
        qkv_weight,
        qv_bias,
        out_weight,
        out_bias,
        first_gain,
        first_shift,
        up_weight,
        up_bias,
        down_weight,
        down_bias,
        second_gain,
        second_shift,
        act_ranges,
        long_lengths,
        short_lengths,
    ):
        lane = lax.axis_index("tensor")
        rows, width = tokens.shape
        assert rows == LONG_LEN
        cols = qkv_weight.shape[2]
        up_cols = up_weight.shape[1]
        blocks = lax.axis_size("tensor")
        half = blocks // 2
        dims = (blocks, cols, width)
        wide = 3 * cols + HEAD_DIM
        out_cols = cols + HEAD_DIM
        every = tuple(range(blocks))

        pieces_a, pieces_u, pieces_d = Pieces([]), Pieces([]), Pieces([])
        shard_a, shard_d, shard_p, bias_row = shards(qkv_weight, out_weight, qv_bias, up_bias, down_weight.T)
        job_a = Job(net.gather(shard_a, pieces_a))
        job_b = Job(net.gather_lane(bias_row))
        job_u = Job(net.gather(up_weight.astype(bf16), pieces_u))
        job_d = Job(net.gather(shard_d, pieces_d))
        job_p = Job(net.gather_plane_first(shard_p, pieces_d, up_cols // 2))

        def vmem(*shape, dtype=f32):
            return pltpu.VMEM(shape, dtype)

        unit = 2 * rows * width * width * blocks
        moved = 2 * width * width * blocks

        step((), None, [job_a, job_p, job_b], [job_a, job_p, job_b])
        step((), None, [job_a, job_p, job_b, job_d], [job_a, job_p, job_b])
        step((), None, [job_a, job_u], [job_a, job_u, job_d])
        step((), None, [job_a, job_u], [job_a, job_u])
        step((), None, [job_a, job_u], [job_a])
        biases = job_b.value

        bufs, plan = pieces_a.part(every)
        qkv, lse, in_t, ctx_low, ctx_slope, tops_a, weight_a = step(
            (act_ranges, long_lengths, short_lengths, tokens, biases, *bufs),
            call(
                functools.partial(attn_forward, net, plan, len(bufs), dims),
                "attn_forward",
                [SM] * 3 + [VM] * 2 + [VM] * len(bufs),
                [
                    like((blocks, rows, wide), bf16),
                    like((blocks, 8, rows)),
                    like((width, rows), bf16),
                    like((blocks, rows, out_cols), bf16),
                    like((blocks, rows, out_cols)),
                    like((8, 128)),
                    like((blocks, width, 4 * cols), bf16),
                ],
                [vmem(rows, width, dtype=bf16), vmem(rows, rows), vmem(out_cols, rows), vmem(8, out_cols)],
                4 * unit,
                3 * moved,
            ),
            [job_d, job_p],
            [job_u, job_d, job_p],
        )
        normed, inv, middle, mid_slope, mid_low, mid_t, tops_m = step(
            (act_ranges, ctx_low, tokens, out_bias, first_gain, first_shift, weight_a),
            call(
                functools.partial(attn_finish, dims),
                "attn_finish",
                [SM] + [VM] * 6,
                [
                    like((rows, width)),
                    like((rows, 1)),
                    like((rows, width)),
                    like((rows, width)),
                    like((rows, width), bf16),
                    like((width, rows), bf16),
                    like((8, 128)),
                ],
                [vmem(rows, width)],
                2 * unit,
                2 * moved,
            ),
            [job_u, job_p],
            [job_u],
        )

        def up_part(lanes, start, finish):
            bufs, plan = pieces_u.part(lanes)
            return step(
                (act_ranges, mid_low, biases, *bufs),
                call(
                    functools.partial(up_forward, net, plan, len(bufs), lanes[0], wide),
                    f"up_forward_{lanes[0]}",
                    [SM] + [VM] * 2 + [VM] * len(bufs),
                    [
                        like((half, rows, up_cols), bf16),
                        like((half, rows, up_cols)),
                        like((8, 128)),
                        like((half, width, up_cols), bf16),
                    ],
                    [vmem(8, up_cols)],
                    2 * unit,
                    2 * moved,
                ),
                start,
                finish,
            )

        act0, slope0, top0, weight_u0 = up_part(every[:half], [job_u, job_d], [job_u])
        act1, slope1, top1, weight_u1 = up_part(every[half:], [], [job_d, job_p])
        step((), None, [job_d], [job_d])
        step((), None, [job_d, job_p], [job_d, job_p])
        bufs_d, plan_d = pieces_d.part(every)
        layer_out, grad_second, ffn_t, sums_b, grad_up, up_sums = step(
            (act0, act1, slope0, slope1, middle, cotangent, down_bias, second_gain, second_shift, *bufs_d),
            call(
                functools.partial(down_both, net, plan_d, len(bufs_d)),
                "down_both",
                [VM] * 9 + [VM] * len(bufs_d),
                [
                    like((rows, width), bf16),
                    like((rows, width)),
                    like((width, rows), bf16),
                    like((8, width)),
                    like((blocks, rows, up_cols), bf16),
                    like((blocks, 1, up_cols)),
                ],
                [
                    vmem(blocks, width, up_cols, dtype=bf16),
                    vmem(rows, width),
                    vmem(rows, width, dtype=bf16),
                ],
                2 * unit,
                4 * moved,
            ),
        )

        grad_shape = like((net.parts, width // net.parts, up_cols), bf16)
        both_shape = like((half,) + grad_shape.shape, bf16)

        def grad_of(name, left_t, rights, start=(), finish=()):
            return step(
                (left_t, *rights),
                call(
                    functools.partial(weight_grad, net),
                    name,
                    [VM] * (1 + len(rights)),
                    [both_shape, both_shape],
                    (),
                    unit,
                    moved,
                ),
                start,
                finish,
            )

        sum_d = Job(net.scatter_z_first(*grad_of("down_grad", ffn_t, (act0, act1))))
        sum_u = Job(net.scatter_sum(*grad_of("up_grad", mid_t, (grad_up,), [sum_d], [sum_d])))
        grad_first, attn_low, attn_t, sums_a = step(
            (grad_up, grad_second, mid_slope, normed, inv, first_gain, weight_u0, weight_u1),
            call(
                mid_backward,
                "mid_backward",
                [VM] * 8,
                [like((rows, width)), like((rows, width), bf16), like((width, rows), bf16), like((8, width))],
                [vmem(rows, width)],
                unit + unit // 3,
                3 * moved,
            ),
            [sum_u, sum_d],
            [sum_u],
        )
        half_shape = like((1,) + grad_shape.shape, bf16)
        grads_1, far, near, more = step(
            (long_lengths, short_lengths, qkv, lse, attn_low, weight_a, ctx_slope, in_t, attn_t, ctx_low),
            call(
                functools.partial(attn_backward, net, half, dims),
                "attn_backward",
                [SM] * 2 + [VM] * 8,
                [like((half, rows, wide), bf16), half_shape, half_shape, like((blocks, 1, wide))],
                [vmem(rows, rows), vmem(rows, out_cols, dtype=bf16)],
                2 * unit,
                2 * moved,
            ),
            [sum_u],
            [sum_u, sum_d],
        )
        late = {}
        sum_a = Job(net.scatter_halves(far, near, late))
        grads_0, far, near, packed = step(
            (long_lengths, short_lengths, qkv, lse, attn_low, weight_a, ctx_slope, in_t, attn_t, ctx_low)
            + (more, up_sums, sums_a, sums_b, tops_a, tops_m, top0, top1),
            call(
                functools.partial(attn_backward_last, net, dims),
                "attn_backward_last",
                [SM] * 2 + [VM] * 16,
                [like((half, rows, wide), bf16), half_shape, half_shape, like((16, width))],
                [vmem(blocks, 1, wide), vmem(rows, rows), vmem(rows, out_cols, dtype=bf16)],
                4 * unit,
                2 * moved,
            ),
            [sum_u, sum_a, sum_d],
            [sum_u, sum_d],
        )
        late.update(far=far, near=near)
        step((), None, [], [sum_a])
        is_top = (jnp.arange(packed.shape[0]) == 2 * blocks + 6)[:, None]
        sum_s = Job(net.sum_max(packed, is_top))
        line_u = Job(net.scatter_line(*sum_u.value))
        tokens_grad = step(
            (act_ranges, grads_0, grads_1, grad_first, tokens, weight_a),
            call(
                functools.partial(token_backward, dims),
                "token_backward",
                [SM] + [VM] * 5,
                [like((rows, width), bf16)],
                [vmem(rows, width)],
                unit,
                2 * moved,
            ),
            [sum_a, sum_d],
            [sum_a, sum_d],
        )[0]
        step((), None, [sum_a, line_u, sum_d, sum_s], [line_u, sum_d, sum_s])
        step((), None, [line_u, sum_s], [sum_a, line_u, sum_s])
        line_a = Job(net.scatter_line(*sum_a.value))
        step((), None, [line_a, sum_s], [line_a, sum_s])

        def finish(down, up):
            return down[0] + down[1].astype(f32), up[0] + up[1].astype(f32)

        down_grad, up_grad = step((sum_d.value, line_u.value), finish, [line_a, sum_s], [sum_s])
        step((), None, [sum_s], [line_a, sum_s])
        packed = sum_s.value
        own = lax.dynamic_slice_in_dim(packed, blocks + lane, 1)
        shared = packed[2 * blocks : 2 * blocks + 6]
        qv_bias_grad = jnp.concatenate([own[:, :cols], own[:, 2 * cols : 3 * cols]], 0)
        up_bias_grad = lax.dynamic_slice_in_dim(packed, lane, 1)[0]
        new_ranges = ema_decay * act_ranges + (1.0 - ema_decay) * packed[2 * blocks + 6, 0:512:128]
        down_grad = down_grad.T
        qkv_grad, out_grad = attn_grads(*line_a.value)
        return (
            layer_out,
            tokens_grad,
            qkv_grad,
            qv_bias_grad,
            out_grad,
            shared[0],
            shared[1],
            shared[2],
            up_grad,
            up_bias_grad,
            down_grad,
            shared[3],
            shared[4],
            shared[5],
            new_ranges,
        )

    return body


def solution(mesh):
    in_specs = (
        P(ALL, None),
        P(ALL, None),
        P(None, "dp", "tensor"),
        P(None, "tensor"),
        P("tensor", "dp"),
        P(),
        P(),
        P(),
        P("dp", "tensor"),
        P("tensor"),
        P("tensor", "dp"),
        P(),
        P(),
        P(),
        P(),
        P("dp"),
        P("dp"),
    )
    out_specs = (
        P(ALL, None),
        P(ALL, None),
        P(None, "dp", "tensor"),
        P(None, "tensor"),
        P("tensor", "dp"),
        P(),
        P(),
        P(),
        P("dp", "tensor"),
        P("tensor"),
        P("tensor", "dp"),
        P(),
        P(),
        P(),
        P(),
    )
    net = Grid() if mesh.shape["dp"] == 8 and mesh.shape["tensor"] == 4 else Plain()
    return jax.shard_map(make_body(net), mesh=mesh, in_specs=in_specs, out_specs=out_specs, check_vma=False)
```

```python
import functools
import itertools

import jax
import jax.numpy as jnp
from jax import lax
from jax.experimental import pallas as pl
from jax.experimental.pallas import tpu as pltpu
from jax.sharding import PartitionSpec as P

HEAD_DIM = 64
LONG_LEN = 512
SHORT_LEN = 128
ALL = ("dp", "tensor")

ema_decay = 0.9
epsilon = 1e-06
root_half = 0.7071067811865476
density_scale = 0.3989422804014327
score_scale = HEAD_DIM ** (-0.5)
NEG = -1000000000.0

f32 = jnp.float32
bf16 = jnp.bfloat16


def mm(left, right):
    return jnp.dot(left, right, preferred_element_type=f32)


def mm_tn(left, right):
    return lax.dot_general(left, right, (((0,), (0,)), ((), ())), preferred_element_type=f32)


def mm_nt(left, right):
    return lax.dot_general(left, right, (((1,), (1,)), ((), ())), preferred_element_type=f32)


def _lin(z, y, x, c):
    return (z * 2 + y) * 4 + x * 2 + c


def _perm(fn):
    out = []
    for z, y, x, c in itertools.product(range(4), range(2), range(2), range(2)):
        out.append((_lin(z, y, x, c), _lin(*fn(z, y, x, c))))
    return out


PC = _perm(lambda z, y, x, c: (z, y, x, 1 - c))
PX = _perm(lambda z, y, x, c: (z, y, 1 - x, c))
PY = _perm(lambda z, y, x, c: (z, 1 - y, x, c))
PZ1 = _perm(lambda z, y, x, c: (z ^ 1, y, x, c))
PZ2 = _perm(lambda z, y, x, c: (z ^ 2, y, x, c))


def tie(*trees):
    leaves, spec = jax.tree.flatten(trees)
    return jax.tree.unflatten(spec, lax.optimization_barrier(leaves))


class Job:
    def __init__(self, stages):
        self.stages, self.value, self.out, self.flight, self.over = stages, None, [], [], False
        self.take(None)

    def take(self, got):
        if not self.over:
            try:
                self.out = self.stages.send(got)
            except StopIteration as stop:
                self.value, self.out, self.over = stop.value, [], True


def step(ins, run=None, start=(), finish=()):
    ins, sends = tie(ins, [[value for value, _ in job.out] for job in start])
    for job, values in zip(start, sends):
        job.flight = [lax.ppermute(v, ALL, perm) for v, (_, perm) in zip(values, job.out)]
    outs = run(*ins) if run else ins
    outs, got = tie(outs, [job.flight for job in finish])
    for job, values in zip(finish, got):
        job.flight = []
        job.take(values)
    return outs


class Pieces:
    def __init__(self, plan):
        self.bufs, self.plan = {}, plan

    def part(self, lanes):
        plan = [p for p in self.plan if p[1] in lanes]
        names = sorted({p[0] for p in plan})
        return [self.bufs[n] for n in names], [(names.index(b), lane - lanes[0], at, col) for b, lane, at, col in plan]


class Grid:
    parts = 8

    @staticmethod
    def gather(shard, pieces):
        own = shard[None]
        for base, lane in ((0, 0), (5, 1)):
            pieces.plan.append((base, lane, (4, 4, 2, 0, 0), 0))
            pieces.plan.append((base + 1, lane, (4, 4, 2, 1, 0), 0))
            pieces.plan.append((base + 2, lane + 2, (4, 4, 2, 0, 0), 0))
            pieces.plan.append((base + 3, lane + 2, (2, 4, 0, 1, 0), 0))
            pieces.plan.append((base + 4, lane + 2, (2, 4, 0, 3, 0), 0))
        (far_z,) = yield [(own, PZ2)]
        pair = jnp.concatenate([own, far_z], 0)
        (near_z,) = yield [(pair, PZ1)]
        line = jnp.concatenate([pair, near_z], 0)
        over_x, over_y, line_far = yield [(line, PX), (line, PY), (line, PC)]
        pieces.bufs.update({0: line, 1: over_y, 2: over_x, 5: line_far})
        diag_x, diag_y, over_y_far, over_x_far = yield [
            (over_y[:2], PX),
            (over_x[2:], PY),
            (over_y, PC),
            (over_x, PC),
        ]
        pieces.bufs.update({3: diag_x, 4: diag_y, 6: over_y_far, 7: over_x_far})
        diag_x_far, diag_y_far = yield [(diag_x, PC), (diag_y, PC)]
        pieces.bufs.update({8: diag_x_far, 9: diag_y_far})

    @staticmethod
    def gather_plane_first(shard, pieces, first_col):
        own = shard[None]
        over_x, over_y = yield [(own, PX), (own, PY)]
        (diag,) = yield [(over_y, PX)]
        plane = jnp.concatenate([own, over_y, over_x, diag], 0)
        (far_z,) = yield [(plane, PZ2)]
        half = jnp.concatenate([plane, far_z], 0)
        (near_z,) = yield [(half, PZ1)]
        half_far, near_z_far = yield [(half, PC), (near_z, PC)]
        for n, (buf, core) in enumerate(((half, 0), (near_z, 0), (half_far, 1), (near_z_far, 1))):
            near = 2 * (n % 2)
            name = 20 + n
            pieces.bufs[name] = buf
            for x in range(2):
                pieces.plan.append((name, 2 * x + core, (4, 1, 4, near, 2), first_col + x))

    @staticmethod
    def slot(block, dp):
        place = block ^ dp
        return (place & 1) * 4 + (place & 2) + (place >> 2)

    @staticmethod
    def scatter_sum(far, near):
        (got,) = yield [(far, PC)]
        out_x, out_y = add_first(near, got)
        from_x, from_y = yield [(out_x, PX), (out_y, PY)]
        out_x, out_y = add_second(near, got, from_x, from_y)
        in_x, in_y = yield [(out_x, PX), (out_y, PY)]
        return near, got, in_x, in_y

    @staticmethod
    def scatter_line(near, got, in_x, in_y):
        out_z, kept = add_third(near, got, in_x, in_y)
        (from_z,) = yield [(out_z, PZ1)]
        out_z, kept = add_fourth(kept, from_z)
        (last,) = yield [(out_z, PZ2)]
        return kept, last

    @staticmethod
    def scatter_z_first(far, near):
        (got,) = yield [(far, PC)]
        out_1, out_0 = add_near_z(near, got)
        (from_1,) = yield [(out_1, PZ1)]
        out_x, out_y = add_corner(near, got, from_1)
        from_x, from_y, from_0 = yield [(out_x, PX), (out_y, PY), (out_0, PZ1)]
        out_x, out_y = add_sides(near, got, from_1, from_0, from_x, from_y)
        in_x, in_y = yield [(out_x, PX), (out_y, PY)]
        out_z, kept = add_own(near, got, from_0, in_x, in_y)
        (last,) = yield [(out_z, PZ2)]
        return kept, last

    @staticmethod
    def gather_lane(vec):
        (other,) = yield [(vec, PX)]
        pair = jnp.stack([vec, other])
        (more,) = yield [(pair, PC)]
        return jnp.stack([pair, more], 1).reshape((4,) + vec.shape)

    @staticmethod
    def sum_max(both, is_top):
        for perm in (PC, PZ1, PZ2, PX, PY):
            (other,) = yield [(both, perm)]
            both = jnp.where(is_top, jnp.maximum(both, other), both + other)
        return both

    @staticmethod
    def me():
        return lax.axis_index("dp"), lax.axis_index("tensor")


class Plain:
    parts = 1

    @staticmethod
    def gather(shard, pieces, first_col=0):
        rows = lax.all_gather(shard, "dp", axis=0, tiled=True)
        full = lax.all_gather(rows, "tensor", axis=0)
        for k in range(full.shape[0]):
            pieces.plan.append((first_col + k, k, None, first_col))
            pieces.bufs[first_col + k] = full[k][None]
        return
        yield

    gather_plane_first = gather

    @staticmethod
    def slot(block, dp):
        return block

    @staticmethod
    def scatter_sum(far, near):
        grads = jnp.stack([near[0], far[0], near[1], far[1]]).astype(f32)
        return (grads.reshape((4, -1, grads.shape[-1])),)
        yield

    @staticmethod
    def scatter_line(grads):
        own = lax.psum_scatter(grads, "tensor", scatter_dimension=0, tiled=False)
        own = lax.psum_scatter(own, "dp", scatter_dimension=0, tiled=True)
        return own, jnp.zeros_like(own)
        yield

    @staticmethod
    def scatter_z_first(far, near):
        grads = yield from Plain.scatter_sum(far, near)
        return (yield from Plain.scatter_line(*grads))

    @staticmethod
    def gather_lane(vec):
        return lax.all_gather(vec, "tensor", axis=0)
        yield

    @staticmethod
    def sum_max(both, is_top):
        return jnp.where(is_top, lax.pmax(both, ALL), lax.psum(both, ALL))
        yield

    @staticmethod
    def me():
        return 0, 0


VM = pl.BlockSpec(memory_space=pltpu.VMEM)
SM = pl.BlockSpec(memory_space=pltpu.SMEM)
VMEM_MIB = {"down_both": 14, "first_shards": 60}


def like(shape, dtype=f32):
    return jax.ShapeDtypeStruct(shape, dtype)


def call(kernel, name, specs, outs, scratch=(), flops=0, moved=0):
    return pl.pallas_call(
        kernel,
        name=name,
        out_shape=outs,
        in_specs=specs,
        out_specs=[VM] * len(outs),
        scratch_shapes=list(scratch),
        compiler_params=pltpu.CompilerParams(vmem_limit_bytes=VMEM_MIB.get(name, 8) * 2**20),
        cost_estimate=pl.CostEstimate(flops=flops, bytes_accessed=moved, transcendentals=0),
    )


def glue(kernel, outs, *ins):
    return call(kernel, kernel.__name__, [VM] * len(ins), outs)(*ins)


def add_first(near, got):
    def first_sums(near, got, out_x, out_y):
        for k in range(2):
            out_x[k] = (near[1, 4 + k].astype(f32) + got[1, 4 + k].astype(f32)).astype(bf16)
            out_y[k] = (near[1, 6 + k].astype(f32) + got[1, 6 + k].astype(f32)).astype(bf16)

    part = like((2,) + near.shape[2:], bf16)
    return glue(first_sums, [part, part], near, got)


def add_second(near, got, from_x, from_y):
    def second_sums(near, got, from_x, from_y, out_x, out_y):
        for k in range(4):
            over_x = near[1, k].astype(f32) + got[1, k].astype(f32)
            over_y = near[0, 4 + k].astype(f32) + got[0, 4 + k].astype(f32)
            if k < 2:
                over_y = over_y + from_x[k].astype(f32)
            else:
                over_x = over_x + from_y[k - 2].astype(f32)
            out_x[k] = over_x.astype(bf16)
            out_y[k] = over_y.astype(bf16)

    part = like((4,) + near.shape[2:], bf16)
    return glue(second_sums, [part, part], near, got, from_x, from_y)


def add_third(near, got, in_x, in_y):
    def third_sums(near, got, in_x, in_y, out, kept):
        for k in range(4):
            total = near[0, k].astype(f32) + got[0, k].astype(f32) + in_x[k].astype(f32) + in_y[k].astype(f32)
            if k < 2:
                kept[k] = total
            else:
                out[k - 2] = total.astype(bf16)

    shape = (2,) + near.shape[2:]
    return glue(third_sums, [like(shape, bf16), like(shape)], near, got, in_x, in_y)


def add_fourth(kept, from_z):
    def fourth_sums(kept, from_z, out, mine):
        mine[...] = kept[0] + from_z[0].astype(f32)
        out[...] = (kept[1] + from_z[1].astype(f32)).astype(bf16)

    shape = kept.shape[1:]
    return glue(fourth_sums, [like(shape, bf16), like(shape)], kept, from_z)


def add_near_z(near, got):
    def near_z_sums(near, got, out_1, out_0):
        for x, out in ((1, out_1), (0, out_0)):
            for y in range(2):
                for k in range(2):
                    at = 4 * y + 2 + k
                    out[2 * y + k] = (near[x, at].astype(f32) + got[x, at].astype(f32)).astype(bf16)

    part = like((4,) + near.shape[2:], bf16)
    return glue(near_z_sums, [part, part], near, got)


def three(near, got, from_z, x, y, k):
    return near[x, 4 * y + k].astype(f32) + got[x, 4 * y + k].astype(f32) + from_z[2 * y + k].astype(f32)


def add_corner(near, got, from_1):
    def corner_sums(near, got, from_1, out_x, out_y):
        out_x[...] = three(near, got, from_1, 1, 1, 0).astype(bf16)
        out_y[...] = three(near, got, from_1, 1, 1, 1).astype(bf16)

    part = like(near.shape[2:], bf16)
    return glue(corner_sums, [part, part], near, got, from_1)


def add_sides(near, got, from_1, from_0, from_x, from_y):
    def side_sums(near, got, from_1, from_0, from_x, from_y, out_x, out_y):
        out_x[0] = three(near, got, from_1, 1, 0, 0).astype(bf16)
        out_x[1] = (three(near, got, from_1, 1, 0, 1) + from_y[...].astype(f32)).astype(bf16)
        out_y[0] = (three(near, got, from_0, 0, 1, 0) + from_x[...].astype(f32)).astype(bf16)
        out_y[1] = three(near, got, from_0, 0, 1, 1).astype(bf16)

    part = like((2,) + near.shape[2:], bf16)
    return glue(side_sums, [part, part], near, got, from_1, from_0, from_x, from_y)


def add_own(near, got, from_0, in_x, in_y):
    def own_sums(near, got, from_0, in_x, in_y, out, kept):
        kept[...] = three(near, got, from_0, 0, 0, 0) + in_x[0].astype(f32) + in_y[0].astype(f32)
        out[...] = (three(near, got, from_0, 0, 0, 1) + in_x[1].astype(f32) + in_y[1].astype(f32)).astype(bf16)

    shape = near.shape[2:]
    return glue(own_sums, [like(shape, bf16), like(shape)], near, got, from_0, in_x, in_y)


def attn_grads(kept, last):
    rows, width = kept.shape
    cols = width // 4

    def attn_sums(kept, last, qkv, out):
        total = kept[...] + last[...].astype(f32)
        for j in range(3):
            qkv[j] = total[:, j * cols : (j + 1) * cols]
        out[...] = total[:, 3 * cols :].T

    return glue(attn_sums, [like((3, rows, cols)), like((cols, rows))], kept, last)


def shards(qkv_weight, out_weight, qv_bias, up_bias, down_weight_t):
    _, rows, cols = qkv_weight.shape
    wide = 3 * cols + HEAD_DIM
    width = down_weight_t.shape[1]

    def first_shards(*refs):
        sources, (attn, down_0, down_1, biases), locals_, sems = refs[:5], refs[5:9], refs[9:14], refs[14]
        copies = [pltpu.make_async_copy(src, dst, sems.at[n]) for n, (src, dst) in enumerate(zip(sources, locals_))]
        for copy in copies:
            copy.start()
        for copy in copies:
            copy.wait()
        qkv, out_weight, qv_bias, up_bias, down = locals_
        for j in range(3):
            attn[:, j * cols : (j + 1) * cols] = qkv[j].astype(bf16)
        attn[:, 3 * cols :] = out_weight[...].T.astype(bf16)
        down_0[...] = down[:, : width // 2].astype(bf16)
        down_1[...] = down[:, width // 2 :].astype(bf16)
        biases[...] = jnp.zeros_like(biases)
        biases[:, :cols] = qv_bias[0:1, :]
        biases[:, 2 * cols : 3 * cols] = qv_bias[1:2, :]
        biases[:, wide:] = row(up_bias)

    part = like((rows, width // 2), bf16)
    outs = [like((rows, 4 * cols), bf16), part, part, like((1, wide + width))]
    ins = (qkv_weight, out_weight, qv_bias, up_bias, down_weight_t)
    scratch = [pltpu.VMEM(value.shape, f32) for value in ins] + [pltpu.SemaphoreType.DMA((len(ins),))]
    return call(first_shards, "first_shards", [pl.BlockSpec(memory_space=pltpu.HBM)] * len(ins), outs, scratch)(*ins)


def assemble(plan, bufs, dst, dp):
    for buf, lane, places, col in plan:
        src = bufs[buf]
        _, rows, width = src.shape
        x, col = (col & 1, col - (col & 1))
        cols = pl.ds(col, width)
        if places is None:
            dst[lane, :, cols] = src[0]
            continue
        count, a, b, c, skip = places

        def move(i, carry):
            place = a * (i & 1) + b * (i >> 1) + c
            at = pl.multiple_of((dp ^ place) * rows, rows)
            dst[lane, pl.ds(at, rows), cols] = src[i + skip * ((i >> 1) + x)]
            return carry

        lax.fori_loop(0, count, move, 0)


def row(vec):
    return vec[...].reshape(1, -1)


def row_stats(summed):
    centered = summed - jnp.mean(summed, axis=-1, keepdims=True)
    inv = lax.rsqrt(jnp.mean(centered * centered, axis=-1, keepdims=True) + epsilon)
    return centered * inv, inv


def norm_backward(scaled, normed, inv):
    row_mean = jnp.mean(scaled, axis=-1, keepdims=True)
    row_cross = jnp.mean(scaled * normed, axis=-1, keepdims=True)
    return inv * (scaled - row_mean - normed * row_cross)


def col_sum(values):
    return jnp.sum(values, axis=0, keepdims=True)


def top_of(values):
    return jnp.full((1, 128), jnp.max(jnp.abs(values)), f32)


def fill_mask(mask, longs, shorts):
    per_block = LONG_LEN // SHORT_LEN
    block = lax.axis_index("tensor")
    n_long = longs.shape[0]
    is_long = block < n_long
    whole = longs[jnp.minimum(block, n_long - 1)]
    first = jnp.maximum(block - n_long, 0) * per_block
    shift = jnp.where(is_long, LONG_LEN.bit_length() - 1, SHORT_LEN.bit_length() - 1)
    size = jnp.where(is_long, LONG_LEN, SHORT_LEN)
    k_pos = lax.broadcasted_iota(jnp.int32, (LONG_LEN, 1), 0)
    q_pos = lax.broadcasted_iota(jnp.int32, (1, LONG_LEN), 1)
    k_seg = lax.shift_right_logical(k_pos, jnp.full_like(k_pos, shift))
    q_seg = lax.shift_right_logical(q_pos, jnp.full_like(q_pos, shift))
    limit = jnp.zeros_like(k_pos)
    for j in range(per_block):
        limit = jnp.where(k_seg == j, jnp.where(is_long, whole, shorts[first + j]), limit)
    k_seg = jnp.where(k_pos - k_seg * size < limit, k_seg, -1)
    mask[...] = jnp.where(k_seg == q_seg, 0.0, NEG)


def attn_forward(net, plan, nb, dims, lim, longs, shorts, tokens, bias, *rest):
    blocks, cols, width = dims
    bufs, rest = rest[:nb], rest[nb:]
    qkv_out, lse_out, in_t, ctx_low, ctx_slope, top_out, weight, in_low, mask, ctx_t, top_ctx = rest
    heads = cols // HEAD_DIM
    low_q = 3 * cols + HEAD_DIM
    assemble(plan, bufs, weight, net.me()[0])
    inputs = tokens[...].astype(f32)
    in_low[...] = jnp.clip(inputs, -lim[0], lim[0]).astype(bf16)
    in_t[...] = in_low[...].T
    top_out[0:1, :] = top_of(inputs)
    fill_mask(mask, longs, shorts)
    ctx_t[0:HEAD_DIM, :] = jnp.zeros((HEAD_DIM, ctx_t.shape[1]), f32)
    top_ctx[...] = jnp.zeros_like(top_ctx)
    inv_limit = 1.0 / jnp.full((1, 1), lim[1], f32)

    def each(lane, carry):
        qkv = (mm(in_low[...], weight[lane, :, :low_q]) + bias[lane, :, :low_q]).astype(bf16)
        qkv_out[lane] = qkv
        for h in range(heads):
            at = h * HEAD_DIM
            q = qkv[:, at : at + HEAD_DIM]
            k = qkv[:, cols + at : cols + at + HEAD_DIM]
            v = qkv[:, 2 * cols + at : 2 * cols + at + HEAD_DIM]
            scores = mm_nt(k, q) * score_scale + mask[...]
            peak = jnp.max(scores, axis=0, keepdims=True)
            grown = jnp.exp(scores - peak)
            total = jnp.sum(grown, axis=0, keepdims=True)
            lse_out[lane, h : h + 1, :] = peak + jnp.log(total)
            shares = (grown * (1.0 / total)).astype(bf16)
            ctx_t[HEAD_DIM + at : 2 * HEAD_DIM + at, :] = mm_tn(v, shares)
        context = ctx_t[...].T
        bent = jnp.tanh(context * inv_limit)
        ctx_low[lane] = (lim[1] * bent).astype(bf16)
        ctx_slope[lane] = 1.0 - bent * bent
        top_ctx[...] = jnp.maximum(top_ctx[...], jnp.max(jnp.abs(context).reshape(-1, 8, context.shape[1]), axis=0))
        return carry

    lax.fori_loop(0, blocks, each, 0)
    top_out[1:2, :] = top_of(top_ctx[...])


def attn_finish(dims, lim, ctx_low, tokens, out_bias, gain, shift, weight, *outs):
    blocks, cols, width = dims
    normed_out, inv_out, middle_out, mid_slope, mid_low, mid_t, top_out, acc = outs
    at = 3 * cols - HEAD_DIM
    acc[...] = tokens[...].astype(f32) + row(out_bias)

    def each(lane, carry):
        acc[...] += mm_nt(ctx_low[lane], weight[lane, :, at:])
        return carry

    lax.fori_loop(0, blocks, each, 0)
    normed, inv = row_stats(acc[...])
    normed_out[...] = normed
    inv_out[...] = inv
    middle = normed * row(gain) + row(shift)
    middle_out[...] = middle
    bent = jnp.tanh(middle * (1.0 / jnp.full((1, 1), lim[2], f32)))
    low = (lim[2] * bent).astype(bf16)
    mid_low[...] = low
    mid_slope[...] = 1.0 - bent * bent
    mid_t[...] = low.T
    top_out[...] = jnp.broadcast_to(top_of(middle), top_out.shape)


def up_forward(net, plan, nb, first, low_q, lim, mid_low, bias, *rest):
    bufs, rest = rest[:nb], rest[nb:]
    act_out, slope_out, top_out, weight, top_hid = rest
    assemble(plan, bufs, weight, net.me()[0])
    top_hid[...] = jnp.zeros_like(top_hid)
    inv_limit = 1.0 / jnp.full((1, 1), lim[3], f32)

    rows = mid_low.shape[0] // 2

    def each(n, carry):
        lane = n // 2
        part = pl.ds(pl.multiple_of((n % 2) * rows, rows), rows)
        up = mm(mid_low[part, :], weight[lane]) + bias[first + lane, :, low_q:]
        half = 0.5 * (1.0 + lax.erf(up * root_half))
        hidden = up * half
        top_hid[...] = jnp.maximum(top_hid[...], jnp.max(jnp.abs(hidden).reshape(-1, 8, hidden.shape[1]), axis=0))
        bent = jnp.tanh(hidden * inv_limit)
        act_out[lane, part] = (lim[3] * bent).astype(bf16)
        slope_out[lane, part] = (1.0 - bent * bent) * (half + up * jnp.exp(-0.5 * up * up) * density_scale)
        return carry

    lax.fori_loop(0, 2 * weight.shape[0], each, 0)
    top_out[...] = jnp.broadcast_to(top_of(top_hid[...]), top_out.shape)


def down_both(net, plan, nb, act0, act1, slope0, slope1, middle, cotangent, down_bias, gain, shift, *rest):
    bufs, rest = rest[:nb], rest[nb:]
    layer_out, grad_out, ffn_t, sums, grad_up, up_sums, weight, acc, ffn_low = rest
    assemble(plan, bufs, weight, net.me()[0])
    acc[...] = middle[...] + row(down_bias)
    half = act0.shape[0]
    for act, first in ((act0, 0), (act1, half)):

        def each(i, carry):
            acc[...] += mm_nt(act[i], weight[first + i])
            return carry

        lax.fori_loop(0, half, each, 0)
    normed, inv = row_stats(acc[...])
    layer_out[...] = (normed * row(gain) + row(shift)).astype(bf16)
    incoming = cotangent[...].astype(f32)
    grad = norm_backward(incoming * row(gain), normed, inv)
    grad_out[...] = grad
    ffn_low[...] = grad.astype(bf16)
    ffn_t[...] = ffn_low[...].T
    sums[...] = jnp.zeros_like(sums)
    sums[0:1, :] = col_sum(grad)
    sums[1:2, :] = col_sum(incoming * normed)
    sums[2:3, :] = col_sum(incoming)
    lane_me = net.me()[1]
    for slope, first in ((slope0, 0), (slope1, half)):

        def back(i, carry):
            low = (mm(ffn_low[...], weight[first + i]) * slope[i]).astype(bf16)
            grad_up[first + i] = low
            up_sums[(first + i) ^ lane_me] = col_sum(low.astype(f32))
            return carry

        lax.fori_loop(0, half, back, 0)


def weight_grad(net, left_t, *rest):
    *rights, far, near = rest
    rows = left_t.shape[0] // net.parts
    dp = net.me()[0]
    half = far.shape[0]
    for x in range(half):
        for out, lane in ((far, 2 * x + 1), (near, 2 * x)):
            right = rights[lane // rights[0].shape[0]]
            grad = mm(left_t[...], right[lane % right.shape[0]]).astype(bf16)
            for block in range(net.parts):
                out[x, net.slot(block, dp)] = grad[block * rows : (block + 1) * rows]


def mid_backward(grad_up, grad_second, mid_slope, normed, inv, gain, weight0, weight1, grad_out, attn_low, attn_t, sums, acc):
    acc[...] = jnp.zeros_like(acc)
    half = weight0.shape[0]
    for weight, first in ((weight0, 0), (weight1, half)):

        def each(i, carry):
            acc[...] += mm_nt(grad_up[first + i], weight[i])
            return carry

        lax.fori_loop(0, half, each, 0)
    incoming = grad_second[...] + acc[...] * mid_slope[...]
    grad = norm_backward(incoming * row(gain), normed[...], inv[...])
    grad_out[...] = grad
    attn_low[...] = grad.astype(bf16)
    attn_t[...] = attn_low[...].T
    sums[...] = jnp.zeros_like(sums)
    sums[0:1, :] = col_sum(grad)
    sums[1:2, :] = col_sum(incoming * normed[...])
    sums[2:3, :] = col_sum(incoming)


def heads_backward(first, dims, lane_me, qkv, lse, attn_low, weight, ctx_slope, mask, grad_ctx, out, sums):
    blocks, cols, width = dims
    heads = cols // HEAD_DIM

    def each(i, carry):
        lane = first + i
        part = mm(attn_low[...], weight[lane, :, 3 * cols - HEAD_DIM :])
        grad_ctx[...] = (part * ctx_slope[lane]).astype(bf16)
        for h in range(heads):
            at = h * HEAD_DIM
            q = qkv[lane, :, at : at + HEAD_DIM]
            k = qkv[lane, :, cols + at : cols + at + HEAD_DIM]
            v = qkv[lane, :, 2 * cols + at : 2 * cols + at + HEAD_DIM]
            grad = grad_ctx[:, HEAD_DIM + at : 2 * HEAD_DIM + at]
            shares = jnp.exp(mm_nt(k, q) * score_scale + mask[...] - lse[lane, h : h + 1, :])
            grad_shares = mm_nt(v, grad)
            inner = jnp.sum(shares * grad_shares, axis=0, keepdims=True)
            grad_scores = (shares * (grad_shares - inner)).astype(bf16)
            grad_v = mm(shares.astype(bf16), grad)
            grad_k = mm(grad_scores, q) * score_scale
            grad_q = (mm_tn(k, grad_scores) * score_scale).T
            out[i, :, at : at + HEAD_DIM] = grad_q.astype(bf16)
            out[i, :, cols + at : cols + at + HEAD_DIM] = grad_k.astype(bf16)
            out[i, :, 2 * cols + at : 2 * cols + at + HEAD_DIM] = grad_v.astype(bf16)
        out[i, :, 3 * cols :] = jnp.zeros((out.shape[1], HEAD_DIM), bf16)
        sums[lane ^ lane_me] = col_sum(out[i].astype(f32))
        return carry

    lax.fori_loop(0, out.shape[0], each, 0)


def attn_backward(net, first, dims, longs, shorts, qkv, lse, attn_low, weight, ctx_slope, out, sums, mask, grad_ctx):
    fill_mask(mask, longs, shorts)
    sums[...] = jnp.zeros_like(sums)
    heads_backward(first, dims, net.me()[1], qkv, lse, attn_low, weight, ctx_slope, mask, grad_ctx, out, sums)


def attn_backward_last(net, dims, longs, shorts, qkv, lse, attn_low, weight, ctx_slope, *rest):
    blocks, cols, width = dims
    in_t, attn_t, ctx_low, more_out, more, *rest = rest
    up_sums, sums_a, sums_b, tops_a, tops_m, top0, top1, *rest = rest
    out, far, near, packed, sums, mask, grad_ctx = rest
    rows = in_t.shape[0] // net.parts
    wide = 3 * cols + HEAD_DIM
    start = 3 * cols - HEAD_DIM
    dp, lane_me = net.me()
    fill_mask(mask, longs, shorts)
    sums[...] = more[...]
    heads_backward(0, dims, lane_me, qkv, lse, attn_low, weight, ctx_slope, mask, grad_ctx, out, sums)
    for x, grads in enumerate((out, more_out)):

        def weights(core, carry):
            left = mm(in_t[...], grads[core])
            right = mm(attn_t[...], ctx_low[2 * x + core])
            mixed = (left[:, start:] + right[:, : wide - start]).astype(bf16)
            left, right = left[:, :start].astype(bf16), right[:, wide - start :].astype(bf16)
            for to, wanted in ((near, 0), (far, 1)):

                @pl.when(core == wanted)
                def _():
                    for block in range(net.parts):
                        rs = slice(block * rows, (block + 1) * rows)
                        place = net.slot(block, dp)
                        to[x, place, :, :start] = left[rs]
                        to[x, place, :, start:wide] = mixed[rs]
                        to[x, place, :, wide:] = right[rs]

            return carry

        lax.fori_loop(0, 2, weights, 0)
    packed[...] = jnp.zeros_like(packed)
    for j in range(blocks):
        packed[j : j + 1, :] = up_sums[j]
        packed[blocks + j : blocks + j + 1, : sums.shape[2]] = sums[j]
    packed[2 * blocks : 2 * blocks + 3, :] = sums_a[0:3, :]
    packed[2 * blocks + 3 : 2 * blocks + 6, :] = sums_b[0:3, :]
    tops = (tops_a[0:1, :], tops_a[1:2, :], tops_m[0:1, :], jnp.maximum(top0[0:1, :], top1[0:1, :]))
    for j, top in enumerate(tops):
        packed[2 * blocks + 6 : 2 * blocks + 7, 128 * j : 128 * j + 128] = top


def token_backward(dims, lim, grads_0, grads_1, grad_first, tokens, weight, out, acc):
    blocks, cols, width = dims
    acc[...] = jnp.zeros_like(acc)
    half = grads_0.shape[0]
    for grads, first in ((grads_0, 0), (grads_1, half)):

        def back(i, carry):
            acc[...] += mm_nt(grads[i], weight[first + i, :, : 3 * cols + HEAD_DIM])
            return carry

        lax.fori_loop(0, half, back, 0)
    inputs = tokens[...].astype(f32)
    out[...] = (grad_first[...] + jnp.where(jnp.abs(inputs) <= lim[0], acc[...], 0.0)).astype(bf16)


def make_body(net):
    def body(
        tokens,
        cotangent,
        qkv_weight,
        qv_bias,
        out_weight,
        out_bias,
        first_gain,
        first_shift,
        up_weight,
        up_bias,
        down_weight,
        down_bias,
        second_gain,
        second_shift,
        act_ranges,
        long_lengths,
        short_lengths,
    ):
        lane = lax.axis_index("tensor")
        rows, width = tokens.shape
        assert rows == LONG_LEN
        cols = qkv_weight.shape[2]
        up_cols = up_weight.shape[1]
        blocks = lax.axis_size("tensor")
        half = blocks // 2
        dims = (blocks, cols, width)
        wide = 3 * cols + HEAD_DIM
        out_cols = cols + HEAD_DIM
        every = tuple(range(blocks))

        pieces_a, pieces_u, pieces_d = Pieces([]), Pieces([]), Pieces([])
        shard_a, shard_d, shard_p, bias_row = shards(qkv_weight, out_weight, qv_bias, up_bias, down_weight.T)
        job_a = Job(net.gather(shard_a, pieces_a))
        job_b = Job(net.gather_lane(bias_row))
        job_u = Job(net.gather(up_weight.astype(bf16), pieces_u))
        job_d = Job(net.gather(shard_d, pieces_d))
        job_p = Job(net.gather_plane_first(shard_p, pieces_d, up_cols // 2))

        def vmem(*shape, dtype=f32):
            return pltpu.VMEM(shape, dtype)

        unit = 2 * rows * width * width * blocks
        moved = 2 * width * width * blocks

        step((), None, [job_a, job_p, job_b], [job_a, job_p, job_b])
        step((), None, [job_a, job_p, job_b, job_d], [job_a, job_p, job_b])
        step((), None, [job_a, job_u], [job_a, job_u, job_d])
        step((), None, [job_a, job_u], [job_a, job_u])
        step((), None, [job_a, job_u], [job_a])
        biases = job_b.value

        bufs, plan = pieces_a.part(every)
        qkv, lse, in_t, ctx_low, ctx_slope, tops_a, weight_a = step(
            (act_ranges, long_lengths, short_lengths, tokens, biases, *bufs),
            call(
                functools.partial(attn_forward, net, plan, len(bufs), dims),
                "attn_forward",
                [SM] * 3 + [VM] * 2 + [VM] * len(bufs),
                [
                    like((blocks, rows, wide), bf16),
                    like((blocks, 8, rows)),
                    like((width, rows), bf16),
                    like((blocks, rows, out_cols), bf16),
                    like((blocks, rows, out_cols)),
                    like((8, 128)),
                    like((blocks, width, 4 * cols), bf16),
                ],
                [vmem(rows, width, dtype=bf16), vmem(rows, rows), vmem(out_cols, rows), vmem(8, out_cols)],
                4 * unit,
                3 * moved,
            ),
            [job_d, job_p],
            [job_u, job_d, job_p],
        )
        normed, inv, middle, mid_slope, mid_low, mid_t, tops_m = step(
            (act_ranges, ctx_low, tokens, out_bias, first_gain, first_shift, weight_a),
            call(
                functools.partial(attn_finish, dims),
                "attn_finish",
                [SM] + [VM] * 6,
                [
                    like((rows, width)),
                    like((rows, 1)),
                    like((rows, width)),
                    like((rows, width)),
                    like((rows, width), bf16),
                    like((width, rows), bf16),
                    like((8, 128)),
                ],
                [vmem(rows, width)],
                2 * unit,
                2 * moved,
            ),
            [job_u, job_p],
            [job_u],
        )

        def up_part(lanes, start, finish):
            bufs, plan = pieces_u.part(lanes)
            return step(
                (act_ranges, mid_low, biases, *bufs),
                call(
                    functools.partial(up_forward, net, plan, len(bufs), lanes[0], wide),
                    f"up_forward_{lanes[0]}",
                    [SM] + [VM] * 2 + [VM] * len(bufs),
                    [
                        like((half, rows, up_cols), bf16),
                        like((half, rows, up_cols)),
                        like((8, 128)),
                        like((half, width, up_cols), bf16),
                    ],
                    [vmem(8, up_cols)],
                    2 * unit,
                    2 * moved,
                ),
                start,
                finish,
            )

        act0, slope0, top0, weight_u0 = up_part(every[:half], [job_u, job_d], [job_u])
        act1, slope1, top1, weight_u1 = up_part(every[half:], [], [job_d, job_p])
        step((), None, [job_d], [job_d])
        step((), None, [job_d, job_p], [job_d, job_p])
        bufs_d, plan_d = pieces_d.part(every)
        layer_out, grad_second, ffn_t, sums_b, grad_up, up_sums = step(
            (act0, act1, slope0, slope1, middle, cotangent, down_bias, second_gain, second_shift, *bufs_d),
            call(
                functools.partial(down_both, net, plan_d, len(bufs_d)),
                "down_both",
                [VM] * 9 + [VM] * len(bufs_d),
                [
                    like((rows, width), bf16),
                    like((rows, width)),
                    like((width, rows), bf16),
                    like((8, width)),
                    like((blocks, rows, up_cols), bf16),
                    like((blocks, 1, up_cols)),
                ],
                [
                    vmem(blocks, width, up_cols, dtype=bf16),
                    vmem(rows, width),
                    vmem(rows, width, dtype=bf16),
                ],
                2 * unit,
                4 * moved,
            ),
        )

        grad_shape = like((net.parts, width // net.parts, up_cols), bf16)
        both_shape = like((half,) + grad_shape.shape, bf16)

        def grad_of(name, left_t, rights, start=(), finish=()):
            return step(
                (left_t, *rights),
                call(
                    functools.partial(weight_grad, net),
                    name,
                    [VM] * (1 + len(rights)),
                    [both_shape, both_shape],
                    (),
                    unit,
                    moved,
                ),
                start,
                finish,
            )

        sum_d = Job(net.scatter_z_first(*grad_of("down_grad", ffn_t, (act0, act1))))
        sum_u = Job(net.scatter_sum(*grad_of("up_grad", mid_t, (grad_up,), [sum_d], [sum_d])))
        grad_first, attn_low, attn_t, sums_a = step(
            (grad_up, grad_second, mid_slope, normed, inv, first_gain, weight_u0, weight_u1),
            call(
                mid_backward,
                "mid_backward",
                [VM] * 8,
                [like((rows, width)), like((rows, width), bf16), like((width, rows), bf16), like((8, width))],
                [vmem(rows, width)],
                unit + unit // 3,
                3 * moved,
            ),
            [sum_u, sum_d],
            [sum_u],
        )
        grads_1, more = step(
            (long_lengths, short_lengths, qkv, lse, attn_low, weight_a, ctx_slope),
            call(
                functools.partial(attn_backward, net, half, dims),
                "attn_backward",
                [SM] * 2 + [VM] * 5,
                [like((half, rows, wide), bf16), like((blocks, 1, wide))],
                [vmem(rows, rows), vmem(rows, out_cols, dtype=bf16)],
                2 * unit,
                2 * moved,
            ),
            [sum_u],
            [sum_u, sum_d],
        )
        grads_0, far, near, packed = step(
            (long_lengths, short_lengths, qkv, lse, attn_low, weight_a, ctx_slope)
            + (in_t, attn_t, ctx_low, grads_1, more)
            + (up_sums, sums_a, sums_b, tops_a, tops_m, top0, top1),
            call(
                functools.partial(attn_backward_last, net, dims),
                "attn_backward_last",
                [SM] * 2 + [VM] * 17,
                [like((half, rows, wide), bf16), both_shape, both_shape, like((16, width))],
                [vmem(blocks, 1, wide), vmem(rows, rows), vmem(rows, out_cols, dtype=bf16)],
                4 * unit,
                2 * moved,
            ),
            [sum_u, sum_d],
            [sum_u, sum_d],
        )
        sum_a = Job(net.scatter_sum(far, near))
        is_top = (jnp.arange(packed.shape[0]) == 2 * blocks + 6)[:, None]
        sum_s = Job(net.sum_max(packed, is_top))
        line_u = Job(net.scatter_line(*sum_u.value))
        tokens_grad = step(
            (act_ranges, grads_0, grads_1, grad_first, tokens, weight_a),
            call(
                functools.partial(token_backward, dims),
                "token_backward",
                [SM] + [VM] * 5,
                [like((rows, width), bf16)],
                [vmem(rows, width)],
                unit,
                2 * moved,
            ),
            [sum_a, sum_d, line_u, sum_s],
            [sum_a, sum_d, line_u, sum_s],
        )[0]
        step((), None, [sum_a, sum_d], [sum_a, sum_d])
        step((), None, [sum_a, line_u, sum_s], [sum_a, line_u, sum_s])
        line_a = Job(net.scatter_line(*sum_a.value))
        step((), None, [line_a, sum_s], [line_a, sum_s])

        def finish(down, up):
            return down[0] + down[1].astype(f32), up[0] + up[1].astype(f32)

        down_grad, up_grad = step((sum_d.value, line_u.value), finish, [line_a, sum_s], [sum_s])
        step((), None, [sum_s], [line_a, sum_s])

        packed = sum_s.value
        down_grad = down_grad.T
        qkv_grad, out_grad = attn_grads(*line_a.value)
        own = lax.dynamic_slice_in_dim(packed, blocks + lane, 1)
        shared = packed[2 * blocks : 2 * blocks + 6]
        qv_bias_grad = jnp.concatenate([own[:, :cols], own[:, 2 * cols : 3 * cols]], 0)
        up_bias_grad = lax.dynamic_slice_in_dim(packed, lane, 1)[0]
        new_ranges = ema_decay * act_ranges + (1.0 - ema_decay) * packed[2 * blocks + 6, 0:512:128]
        return (
            layer_out,
            tokens_grad,
            qkv_grad,
            qv_bias_grad,
            out_grad,
            shared[0],
            shared[1],
            shared[2],
            up_grad,
            up_bias_grad,
            down_grad,
            shared[3],
            shared[4],
            shared[5],
            new_ranges,
        )

    return body


def solution(mesh):
    in_specs = (
        P(ALL, None),
        P(ALL, None),
        P(None, "dp", "tensor"),
        P(None, "tensor"),
        P("tensor", "dp"),
        P(),
        P(),
        P(),
        P("dp", "tensor"),
        P("tensor"),
        P("tensor", "dp"),
        P(),
        P(),
        P(),
        P(),
        P("dp"),
        P("dp"),
    )
    out_specs = (
        P(ALL, None),
        P(ALL, None),
        P(None, "dp", "tensor"),
        P(None, "tensor"),
        P("tensor", "dp"),
        P(),
        P(),
        P(),
        P("dp", "tensor"),
        P("tensor"),
        P("tensor", "dp"),
        P(),
        P(),
        P(),
        P(),
    )
    net = Grid() if mesh.shape["dp"] == 8 and mesh.shape["tensor"] == 4 else Plain()
    return jax.shard_map(make_body(net), mesh=mesh, in_specs=in_specs, out_specs=out_specs, check_vma=False)
```

```python
import functools
import itertools

import jax
import jax.numpy as jnp
from jax import lax
from jax.experimental import pallas as pl
from jax.experimental.pallas import tpu as pltpu
from jax.sharding import PartitionSpec as P

HEAD_DIM = 64
LONG_LEN = 512
SHORT_LEN = 128
ALL = ("dp", "tensor")

ema_decay = 0.9
epsilon = 1e-06
root_half = 0.7071067811865476
density_scale = 0.3989422804014327
score_scale = HEAD_DIM ** (-0.5)
NEG = -1000000000.0

f32 = jnp.float32
bf16 = jnp.bfloat16


def mm(left, right):
    return jnp.dot(left, right, preferred_element_type=f32)


def mm_tn(left, right):
    return lax.dot_general(left, right, (((0,), (0,)), ((), ())), preferred_element_type=f32)


def mm_nt(left, right):
    return lax.dot_general(left, right, (((1,), (1,)), ((), ())), preferred_element_type=f32)


def _lin(z, y, x, c):
    return (z * 2 + y) * 4 + x * 2 + c


def _perm(fn):
    out = []
    for z, y, x, c in itertools.product(range(4), range(2), range(2), range(2)):
        out.append((_lin(z, y, x, c), _lin(*fn(z, y, x, c))))
    return out


PC = _perm(lambda z, y, x, c: (z, y, x, 1 - c))
PX = _perm(lambda z, y, x, c: (z, y, 1 - x, c))
PY = _perm(lambda z, y, x, c: (z, 1 - y, x, c))
PZ1 = _perm(lambda z, y, x, c: (z ^ 1, y, x, c))
PZ2 = _perm(lambda z, y, x, c: (z ^ 2, y, x, c))


def tie(*trees):
    leaves, spec = jax.tree.flatten(trees)
    return jax.tree.unflatten(spec, lax.optimization_barrier(leaves))


class Job:
    def __init__(self, stages):
        self.stages, self.value, self.out, self.flight, self.over = stages, None, [], [], False
        self.take(None)

    def take(self, got):
        if not self.over:
            try:
                self.out = self.stages.send(got)
            except StopIteration as stop:
                self.value, self.out, self.over = stop.value, [], True


def step(ins, run=None, start=(), finish=()):
    ins, sends = tie(ins, [[value for value, _ in job.out] for job in start])
    for job, values in zip(start, sends):
        job.flight = [lax.ppermute(v, ALL, perm) for v, (_, perm) in zip(values, job.out)]
    outs = run(*ins) if run else ins
    outs, got = tie(outs, [job.flight for job in finish])
    for job, values in zip(finish, got):
        job.flight = []
        job.take(values)
    return outs


class Pieces:
    def __init__(self, plan):
        self.bufs, self.plan = {}, plan

    def part(self, lanes):
        plan = [p for p in self.plan if p[1] in lanes]
        names = sorted({p[0] for p in plan})
        return [self.bufs[n] for n in names], [(names.index(b), lane - lanes[0], at, col) for b, lane, at, col in plan]


class Grid:
    parts = 8

    @staticmethod
    def gather(shard, pieces):
        own = shard[None]
        for base, lane in ((0, 0), (5, 1)):
            pieces.plan.append((base, lane, (4, 4, 2, 0, 0), 0))
            pieces.plan.append((base + 1, lane, (4, 4, 2, 1, 0), 0))
            pieces.plan.append((base + 2, lane + 2, (4, 4, 2, 0, 0), 0))
            pieces.plan.append((base + 3, lane + 2, (2, 4, 0, 1, 0), 0))
            pieces.plan.append((base + 4, lane + 2, (2, 4, 0, 3, 0), 0))
        (far_z,) = yield [(own, PZ2)]
        pair = jnp.concatenate([own, far_z], 0)
        (near_z,) = yield [(pair, PZ1)]
        line = jnp.concatenate([pair, near_z], 0)
        over_x, over_y, line_far = yield [(line, PX), (line, PY), (line, PC)]
        pieces.bufs.update({0: line, 1: over_y, 2: over_x, 5: line_far})
        diag_x, diag_y, over_y_far, over_x_far = yield [
            (over_y[:2], PX),
            (over_x[2:], PY),
            (over_y, PC),
            (over_x, PC),
        ]
        pieces.bufs.update({3: diag_x, 4: diag_y, 6: over_y_far, 7: over_x_far})
        diag_x_far, diag_y_far = yield [(diag_x, PC), (diag_y, PC)]
        pieces.bufs.update({8: diag_x_far, 9: diag_y_far})

    @staticmethod
    def gather_plane_first(shard, pieces, first_col):
        own = shard[None]
        over_x, over_y = yield [(own, PX), (own, PY)]
        (diag,) = yield [(over_y, PX)]
        plane = jnp.concatenate([own, over_y, over_x, diag], 0)
        (far_z,) = yield [(plane, PZ2)]
        half = jnp.concatenate([plane, far_z], 0)
        (near_z,) = yield [(half, PZ1)]
        half_far, near_z_far = yield [(half, PC), (near_z, PC)]
        for n, (buf, core) in enumerate(((half, 0), (near_z, 0), (half_far, 1), (near_z_far, 1))):
            near = 2 * (n % 2)
            name = 20 + n
            pieces.bufs[name] = buf
            for x in range(2):
                pieces.plan.append((name, 2 * x + core, (4, 1, 4, near, 2), first_col + x))

    @staticmethod
    def slot(block, dp):
        place = block ^ dp
        return (place & 1) * 4 + (place & 2) + (place >> 2)

    @staticmethod
    def scatter_sum(far, near):
        (got,) = yield [(far, PC)]
        out_x, out_y = add_first(near, got)
        from_x, from_y = yield [(out_x, PX), (out_y, PY)]
        out_x, out_y = add_second(near, got, from_x, from_y)
        in_x, in_y = yield [(out_x, PX), (out_y, PY)]
        return near, got, in_x, in_y

    @staticmethod
    def scatter_line(near, got, in_x, in_y):
        out_z, kept = add_third(near, got, in_x, in_y)
        (from_z,) = yield [(out_z, PZ1)]
        out_z, kept = add_fourth(kept, from_z)
        (last,) = yield [(out_z, PZ2)]
        return kept, last

    @staticmethod
    def scatter_z_first(far, near):
        (got,) = yield [(far, PC)]
        out_1, out_0 = add_near_z(near, got)
        (from_1,) = yield [(out_1, PZ1)]
        out_x, out_y = add_corner(near, got, from_1)
        from_x, from_y, from_0 = yield [(out_x, PX), (out_y, PY), (out_0, PZ1)]
        out_x, out_y = add_sides(near, got, from_1, from_0, from_x, from_y)
        in_x, in_y = yield [(out_x, PX), (out_y, PY)]
        out_z, kept = add_own(near, got, from_0, in_x, in_y)
        (last,) = yield [(out_z, PZ2)]
        return kept, last

    @staticmethod
    def gather_lane(vec):
        (other,) = yield [(vec, PX)]
        pair = jnp.stack([vec, other])
        (more,) = yield [(pair, PC)]
        return jnp.stack([pair, more], 1).reshape((4,) + vec.shape)

    @staticmethod
    def sum_max(both, is_top):
        for perm in (PC, PZ1, PZ2, PX, PY):
            (other,) = yield [(both, perm)]
            both = jnp.where(is_top, jnp.maximum(both, other), both + other)
        return both

    @staticmethod
    def me():
        return lax.axis_index("dp"), lax.axis_index("tensor")


class Plain:
    parts = 1

    @staticmethod
    def gather(shard, pieces, first_col=0):
        rows = lax.all_gather(shard, "dp", axis=0, tiled=True)
        full = lax.all_gather(rows, "tensor", axis=0)
        for k in range(full.shape[0]):
            pieces.plan.append((first_col + k, k, None, first_col))
            pieces.bufs[first_col + k] = full[k][None]
        return
        yield

    gather_plane_first = gather

    @staticmethod
    def slot(block, dp):
        return block

    @staticmethod
    def scatter_sum(far, near):
        grads = jnp.stack([near[0], far[0], near[1], far[1]]).astype(f32)
        return (grads.reshape((4, -1, grads.shape[-1])),)
        yield

    @staticmethod
    def scatter_line(grads):
        own = lax.psum_scatter(grads, "tensor", scatter_dimension=0, tiled=False)
        own = lax.psum_scatter(own, "dp", scatter_dimension=0, tiled=True)
        return own, jnp.zeros_like(own)
        yield

    @staticmethod
    def scatter_z_first(far, near):
        grads = yield from Plain.scatter_sum(far, near)
        return (yield from Plain.scatter_line(*grads))

    @staticmethod
    def gather_lane(vec):
        return lax.all_gather(vec, "tensor", axis=0)
        yield

    @staticmethod
    def sum_max(both, is_top):
        return jnp.where(is_top, lax.pmax(both, ALL), lax.psum(both, ALL))
        yield

    @staticmethod
    def me():
        return 0, 0


VM = pl.BlockSpec(memory_space=pltpu.VMEM)
SM = pl.BlockSpec(memory_space=pltpu.SMEM)
VMEM_MIB = 8
ROOMY = ("down_both",)


def like(shape, dtype=f32):
    return jax.ShapeDtypeStruct(shape, dtype)


def call(kernel, name, specs, outs, scratch=(), flops=0, moved=0):
    return pl.pallas_call(
        kernel,
        name=name,
        out_shape=outs,
        in_specs=specs,
        out_specs=[VM] * len(outs),
        scratch_shapes=list(scratch),
        compiler_params=pltpu.CompilerParams(vmem_limit_bytes=(14 if name in ROOMY else VMEM_MIB) * 2**20),
        cost_estimate=pl.CostEstimate(flops=flops, bytes_accessed=moved, transcendentals=0),
    )


def glue(kernel, outs, *ins):
    return call(kernel, kernel.__name__, [VM] * len(ins), outs)(*ins)


def add_first(near, got):
    def first_sums(near, got, out_x, out_y):
        for k in range(2):
            out_x[k] = (near[1, 4 + k].astype(f32) + got[1, 4 + k].astype(f32)).astype(bf16)
            out_y[k] = (near[1, 6 + k].astype(f32) + got[1, 6 + k].astype(f32)).astype(bf16)

    part = like((2,) + near.shape[2:], bf16)
    return glue(first_sums, [part, part], near, got)


def add_second(near, got, from_x, from_y):
    def second_sums(near, got, from_x, from_y, out_x, out_y):
        for k in range(4):
            over_x = near[1, k].astype(f32) + got[1, k].astype(f32)
            over_y = near[0, 4 + k].astype(f32) + got[0, 4 + k].astype(f32)
            if k < 2:
                over_y = over_y + from_x[k].astype(f32)
            else:
                over_x = over_x + from_y[k - 2].astype(f32)
            out_x[k] = over_x.astype(bf16)
            out_y[k] = over_y.astype(bf16)

    part = like((4,) + near.shape[2:], bf16)
    return glue(second_sums, [part, part], near, got, from_x, from_y)


def add_third(near, got, in_x, in_y):
    def third_sums(near, got, in_x, in_y, out, kept):
        for k in range(4):
            total = near[0, k].astype(f32) + got[0, k].astype(f32) + in_x[k].astype(f32) + in_y[k].astype(f32)
            if k < 2:
                kept[k] = total
            else:
                out[k - 2] = total.astype(bf16)

    shape = (2,) + near.shape[2:]
    return glue(third_sums, [like(shape, bf16), like(shape)], near, got, in_x, in_y)


def add_fourth(kept, from_z):
    def fourth_sums(kept, from_z, out, mine):
        mine[...] = kept[0] + from_z[0].astype(f32)
        out[...] = (kept[1] + from_z[1].astype(f32)).astype(bf16)

    shape = kept.shape[1:]
    return glue(fourth_sums, [like(shape, bf16), like(shape)], kept, from_z)


def add_near_z(near, got):
    def near_z_sums(near, got, out_1, out_0):
        for x, out in ((1, out_1), (0, out_0)):
            for y in range(2):
                for k in range(2):
                    at = 4 * y + 2 + k
                    out[2 * y + k] = (near[x, at].astype(f32) + got[x, at].astype(f32)).astype(bf16)

    part = like((4,) + near.shape[2:], bf16)
    return glue(near_z_sums, [part, part], near, got)


def three(near, got, from_z, x, y, k):
    return near[x, 4 * y + k].astype(f32) + got[x, 4 * y + k].astype(f32) + from_z[2 * y + k].astype(f32)


def add_corner(near, got, from_1):
    def corner_sums(near, got, from_1, out_x, out_y):
        out_x[...] = three(near, got, from_1, 1, 1, 0).astype(bf16)
        out_y[...] = three(near, got, from_1, 1, 1, 1).astype(bf16)

    part = like(near.shape[2:], bf16)
    return glue(corner_sums, [part, part], near, got, from_1)


def add_sides(near, got, from_1, from_0, from_x, from_y):
    def side_sums(near, got, from_1, from_0, from_x, from_y, out_x, out_y):
        out_x[0] = three(near, got, from_1, 1, 0, 0).astype(bf16)
        out_x[1] = (three(near, got, from_1, 1, 0, 1) + from_y[...].astype(f32)).astype(bf16)
        out_y[0] = (three(near, got, from_0, 0, 1, 0) + from_x[...].astype(f32)).astype(bf16)
        out_y[1] = three(near, got, from_0, 0, 1, 1).astype(bf16)

    part = like((2,) + near.shape[2:], bf16)
    return glue(side_sums, [part, part], near, got, from_1, from_0, from_x, from_y)


def add_own(near, got, from_0, in_x, in_y):
    def own_sums(near, got, from_0, in_x, in_y, out, kept):
        kept[...] = three(near, got, from_0, 0, 0, 0) + in_x[0].astype(f32) + in_y[0].astype(f32)
        out[...] = (three(near, got, from_0, 0, 0, 1) + in_x[1].astype(f32) + in_y[1].astype(f32)).astype(bf16)

    shape = near.shape[2:]
    return glue(own_sums, [like(shape, bf16), like(shape)], near, got, from_0, in_x, in_y)


def attn_grads(kept, last):
    rows, width = kept.shape
    cols = width // 4

    def attn_sums(kept, last, qkv, out):
        total = kept[...] + last[...].astype(f32)
        for j in range(3):
            qkv[j] = total[:, j * cols : (j + 1) * cols]
        out[...] = total[:, 3 * cols :].T

    return glue(attn_sums, [like((3, rows, cols)), like((cols, rows))], kept, last)


def shards(qkv_weight, out_weight, qv_bias, up_bias, down_weight_t):
    _, rows, cols = qkv_weight.shape
    wide = 3 * cols + HEAD_DIM
    width = down_weight_t.shape[1]

    def first_shards(qkv, out_weight, qv_bias, up_bias, down, attn, down_0, down_1, biases):
        for j in range(3):
            attn[:, j * cols : (j + 1) * cols] = qkv[j].astype(bf16)
        attn[:, 3 * cols :] = out_weight[...].T.astype(bf16)
        down_0[...] = down[:, : width // 2].astype(bf16)
        down_1[...] = down[:, width // 2 :].astype(bf16)
        biases[...] = jnp.zeros_like(biases)
        biases[:, :cols] = qv_bias[0:1, :]
        biases[:, 2 * cols : 3 * cols] = qv_bias[1:2, :]
        biases[:, wide:] = row(up_bias)

    part = like((rows, width // 2), bf16)
    outs = [like((rows, 4 * cols), bf16), part, part, like((1, wide + width))]
    return glue(first_shards, outs, qkv_weight, out_weight, qv_bias, up_bias, down_weight_t)


def assemble(plan, bufs, dst, dp):
    for buf, lane, places, col in plan:
        src = bufs[buf]
        _, rows, width = src.shape
        x, col = (col & 1, col - (col & 1))
        cols = pl.ds(col, width)
        if places is None:
            dst[lane, :, cols] = src[0]
            continue
        count, a, b, c, skip = places

        def move(i, carry):
            place = a * (i & 1) + b * (i >> 1) + c
            at = pl.multiple_of((dp ^ place) * rows, rows)
            dst[lane, pl.ds(at, rows), cols] = src[i + skip * ((i >> 1) + x)]
            return carry

        lax.fori_loop(0, count, move, 0)


def row(vec):
    return vec[...].reshape(1, -1)


def row_stats(summed):
    centered = summed - jnp.mean(summed, axis=-1, keepdims=True)
    inv = lax.rsqrt(jnp.mean(centered * centered, axis=-1, keepdims=True) + epsilon)
    return centered * inv, inv


def norm_backward(scaled, normed, inv):
    row_mean = jnp.mean(scaled, axis=-1, keepdims=True)
    row_cross = jnp.mean(scaled * normed, axis=-1, keepdims=True)
    return inv * (scaled - row_mean - normed * row_cross)


def col_sum(values):
    return jnp.sum(values, axis=0, keepdims=True)


def top_of(values):
    return jnp.full((1, 128), jnp.max(jnp.abs(values)), f32)


def fill_mask(mask, longs, shorts):
    per_block = LONG_LEN // SHORT_LEN
    block = lax.axis_index("tensor")
    n_long = longs.shape[0]
    is_long = block < n_long
    whole = longs[jnp.minimum(block, n_long - 1)]
    first = jnp.maximum(block - n_long, 0) * per_block
    shift = jnp.where(is_long, LONG_LEN.bit_length() - 1, SHORT_LEN.bit_length() - 1)
    size = jnp.where(is_long, LONG_LEN, SHORT_LEN)
    k_pos = lax.broadcasted_iota(jnp.int32, (LONG_LEN, 1), 0)
    q_pos = lax.broadcasted_iota(jnp.int32, (1, LONG_LEN), 1)
    k_seg = lax.shift_right_logical(k_pos, jnp.full_like(k_pos, shift))
    q_seg = lax.shift_right_logical(q_pos, jnp.full_like(q_pos, shift))
    limit = jnp.zeros_like(k_pos)
    for j in range(per_block):
        limit = jnp.where(k_seg == j, jnp.where(is_long, whole, shorts[first + j]), limit)
    k_seg = jnp.where(k_pos - k_seg * size < limit, k_seg, -1)
    mask[...] = jnp.where(k_seg == q_seg, 0.0, NEG)


def attn_forward(net, plan, nb, dims, lim, longs, shorts, tokens, bias, *rest):
    blocks, cols, width = dims
    bufs, rest = rest[:nb], rest[nb:]
    qkv_out, lse_out, in_t, ctx_low, ctx_slope, top_out, weight, in_low, mask, ctx_t, top_ctx = rest
    heads = cols // HEAD_DIM
    low_q = 3 * cols + HEAD_DIM
    assemble(plan, bufs, weight, net.me()[0])
    inputs = tokens[...].astype(f32)
    in_low[...] = jnp.clip(inputs, -lim[0], lim[0]).astype(bf16)
    in_t[...] = in_low[...].T
    top_out[0:1, :] = top_of(inputs)
    fill_mask(mask, longs, shorts)
    ctx_t[0:HEAD_DIM, :] = jnp.zeros((HEAD_DIM, ctx_t.shape[1]), f32)
    top_ctx[...] = jnp.zeros_like(top_ctx)
    inv_limit = 1.0 / jnp.full((1, 1), lim[1], f32)

    def each(lane, carry):
        qkv = (mm(in_low[...], weight[lane, :, :low_q]) + bias[lane, :, :low_q]).astype(bf16)
        qkv_out[lane] = qkv
        for h in range(heads):
            at = h * HEAD_DIM
            q = qkv[:, at : at + HEAD_DIM]
            k = qkv[:, cols + at : cols + at + HEAD_DIM]
            v = qkv[:, 2 * cols + at : 2 * cols + at + HEAD_DIM]
            scores = mm_nt(k, q) * score_scale + mask[...]
            peak = jnp.max(scores, axis=0, keepdims=True)
            grown = jnp.exp(scores - peak)
            total = jnp.sum(grown, axis=0, keepdims=True)
            lse_out[lane, h : h + 1, :] = peak + jnp.log(total)
            shares = (grown * (1.0 / total)).astype(bf16)
            ctx_t[HEAD_DIM + at : 2 * HEAD_DIM + at, :] = mm_tn(v, shares)
        context = ctx_t[...].T
        bent = jnp.tanh(context * inv_limit)
        ctx_low[lane] = (lim[1] * bent).astype(bf16)
        ctx_slope[lane] = 1.0 - bent * bent
        top_ctx[...] = jnp.maximum(top_ctx[...], jnp.max(jnp.abs(context).reshape(-1, 8, context.shape[1]), axis=0))
        return carry

    lax.fori_loop(0, blocks, each, 0)
    top_out[1:2, :] = top_of(top_ctx[...])


def attn_finish(dims, lim, ctx_low, tokens, out_bias, gain, shift, weight, *outs):
    blocks, cols, width = dims
    normed_out, inv_out, middle_out, mid_slope, mid_low, mid_t, top_out, acc = outs
    at = 3 * cols - HEAD_DIM
    acc[...] = tokens[...].astype(f32) + row(out_bias)

    def each(lane, carry):
        acc[...] += mm_nt(ctx_low[lane], weight[lane, :, at:])
        return carry

    lax.fori_loop(0, blocks, each, 0)
    normed, inv = row_stats(acc[...])
    normed_out[...] = normed
    inv_out[...] = inv
    middle = normed * row(gain) + row(shift)
    middle_out[...] = middle
    bent = jnp.tanh(middle * (1.0 / jnp.full((1, 1), lim[2], f32)))
    low = (lim[2] * bent).astype(bf16)
    mid_low[...] = low
    mid_slope[...] = 1.0 - bent * bent
    mid_t[...] = low.T
    top_out[...] = jnp.broadcast_to(top_of(middle), top_out.shape)


def up_forward(net, plan, nb, first, low_q, lim, mid_low, bias, *rest):
    bufs, rest = rest[:nb], rest[nb:]
    act_out, slope_out, top_out, weight, top_hid = rest
    assemble(plan, bufs, weight, net.me()[0])
    top_hid[...] = jnp.zeros_like(top_hid)
    inv_limit = 1.0 / jnp.full((1, 1), lim[3], f32)

    rows = mid_low.shape[0] // 2

    def each(n, carry):
        lane = n // 2
        part = pl.ds(pl.multiple_of((n % 2) * rows, rows), rows)
        up = mm(mid_low[part, :], weight[lane]) + bias[first + lane, :, low_q:]
        half = 0.5 * (1.0 + lax.erf(up * root_half))
        hidden = up * half
        top_hid[...] = jnp.maximum(top_hid[...], jnp.max(jnp.abs(hidden).reshape(-1, 8, hidden.shape[1]), axis=0))
        bent = jnp.tanh(hidden * inv_limit)
        act_out[lane, part] = (lim[3] * bent).astype(bf16)
        slope_out[lane, part] = (1.0 - bent * bent) * (half + up * jnp.exp(-0.5 * up * up) * density_scale)
        return carry

    lax.fori_loop(0, 2 * weight.shape[0], each, 0)
    top_out[...] = jnp.broadcast_to(top_of(top_hid[...]), top_out.shape)


def down_both(net, plan, nb, act0, act1, slope0, slope1, middle, cotangent, down_bias, gain, shift, *rest):
    bufs, rest = rest[:nb], rest[nb:]
    layer_out, grad_out, ffn_t, sums, grad_up, up_sums, weight, acc, ffn_low = rest
    assemble(plan, bufs, weight, net.me()[0])
    acc[...] = middle[...] + row(down_bias)
    half = act0.shape[0]
    for act, first in ((act0, 0), (act1, half)):

        def each(i, carry):
            acc[...] += mm_nt(act[i], weight[first + i])
            return carry

        lax.fori_loop(0, half, each, 0)
    normed, inv = row_stats(acc[...])
    layer_out[...] = (normed * row(gain) + row(shift)).astype(bf16)
    incoming = cotangent[...].astype(f32)
    grad = norm_backward(incoming * row(gain), normed, inv)
    grad_out[...] = grad
    ffn_low[...] = grad.astype(bf16)
    ffn_t[...] = ffn_low[...].T
    sums[...] = jnp.zeros_like(sums)
    sums[0:1, :] = col_sum(grad)
    sums[1:2, :] = col_sum(incoming * normed)
    sums[2:3, :] = col_sum(incoming)
    lane_me = net.me()[1]
    for slope, first in ((slope0, 0), (slope1, half)):

        def back(i, carry):
            low = (mm(ffn_low[...], weight[first + i]) * slope[i]).astype(bf16)
            grad_up[first + i] = low
            up_sums[(first + i) ^ lane_me] = col_sum(low.astype(f32))
            return carry

        lax.fori_loop(0, half, back, 0)


def weight_grad(net, left_t, *rest):
    *rights, far, near = rest
    rows = left_t.shape[0] // net.parts
    dp = net.me()[0]
    half = far.shape[0]
    for x in range(half):
        for out, lane in ((far, 2 * x + 1), (near, 2 * x)):
            right = rights[lane // rights[0].shape[0]]
            grad = mm(left_t[...], right[lane % right.shape[0]]).astype(bf16)
            for block in range(net.parts):
                out[x, net.slot(block, dp)] = grad[block * rows : (block + 1) * rows]


def mid_backward(grad_up, grad_second, mid_slope, normed, inv, gain, weight0, weight1, grad_out, attn_low, attn_t, sums, acc):
    acc[...] = jnp.zeros_like(acc)
    half = weight0.shape[0]
    for weight, first in ((weight0, 0), (weight1, half)):

        def each(i, carry):
            acc[...] += mm_nt(grad_up[first + i], weight[i])
            return carry

        lax.fori_loop(0, half, each, 0)
    incoming = grad_second[...] + acc[...] * mid_slope[...]
    grad = norm_backward(incoming * row(gain), normed[...], inv[...])
    grad_out[...] = grad
    attn_low[...] = grad.astype(bf16)
    attn_t[...] = attn_low[...].T
    sums[...] = jnp.zeros_like(sums)
    sums[0:1, :] = col_sum(grad)
    sums[1:2, :] = col_sum(incoming * normed[...])
    sums[2:3, :] = col_sum(incoming)


def heads_backward(first, dims, lane_me, qkv, lse, attn_low, weight, ctx_slope, mask, grad_ctx, out, sums):
    blocks, cols, width = dims
    heads = cols // HEAD_DIM

    def each(i, carry):
        lane = first + i
        part = mm(attn_low[...], weight[lane, :, 3 * cols - HEAD_DIM :])
        grad_ctx[...] = (part * ctx_slope[lane]).astype(bf16)
        for h in range(heads):
            at = h * HEAD_DIM
            q = qkv[lane, :, at : at + HEAD_DIM]
            k = qkv[lane, :, cols + at : cols + at + HEAD_DIM]
            v = qkv[lane, :, 2 * cols + at : 2 * cols + at + HEAD_DIM]
            grad = grad_ctx[:, HEAD_DIM + at : 2 * HEAD_DIM + at]
            shares = jnp.exp(mm_nt(k, q) * score_scale + mask[...] - lse[lane, h : h + 1, :])
            grad_shares = mm_nt(v, grad)
            inner = jnp.sum(shares * grad_shares, axis=0, keepdims=True)
            grad_scores = (shares * (grad_shares - inner)).astype(bf16)
            grad_v = mm(shares.astype(bf16), grad)
            grad_k = mm(grad_scores, q) * score_scale
            grad_q = (mm_tn(k, grad_scores) * score_scale).T
            out[i, :, at : at + HEAD_DIM] = grad_q.astype(bf16)
            out[i, :, cols + at : cols + at + HEAD_DIM] = grad_k.astype(bf16)
            out[i, :, 2 * cols + at : 2 * cols + at + HEAD_DIM] = grad_v.astype(bf16)
        out[i, :, 3 * cols :] = jnp.zeros((out.shape[1], HEAD_DIM), bf16)
        sums[lane ^ lane_me] = col_sum(out[i].astype(f32))
        return carry

    lax.fori_loop(0, out.shape[0], each, 0)


def attn_backward(net, first, dims, longs, shorts, qkv, lse, attn_low, weight, ctx_slope, out, sums, mask, grad_ctx):
    fill_mask(mask, longs, shorts)
    sums[...] = jnp.zeros_like(sums)
    heads_backward(first, dims, net.me()[1], qkv, lse, attn_low, weight, ctx_slope, mask, grad_ctx, out, sums)


def attn_backward_last(net, dims, longs, shorts, qkv, lse, attn_low, weight, ctx_slope, *rest):
    blocks, cols, width = dims
    in_t, attn_t, ctx_low, more_out, more, *rest = rest
    up_sums, sums_a, sums_b, tops_a, tops_m, top0, top1, *rest = rest
    out, far, near, packed, sums, mask, grad_ctx = rest
    rows = in_t.shape[0] // net.parts
    wide = 3 * cols + HEAD_DIM
    start = 3 * cols - HEAD_DIM
    dp, lane_me = net.me()
    fill_mask(mask, longs, shorts)
    sums[...] = more[...]
    heads_backward(0, dims, lane_me, qkv, lse, attn_low, weight, ctx_slope, mask, grad_ctx, out, sums)
    for x, grads in enumerate((out, more_out)):

        def weights(core, carry):
            left = mm(in_t[...], grads[core])
            right = mm(attn_t[...], ctx_low[2 * x + core])
            mixed = (left[:, start:] + right[:, : wide - start]).astype(bf16)
            left, right = left[:, :start].astype(bf16), right[:, wide - start :].astype(bf16)
            for to, wanted in ((near, 0), (far, 1)):

                @pl.when(core == wanted)
                def _():
                    for block in range(net.parts):
                        rs = slice(block * rows, (block + 1) * rows)
                        place = net.slot(block, dp)
                        to[x, place, :, :start] = left[rs]
                        to[x, place, :, start:wide] = mixed[rs]
                        to[x, place, :, wide:] = right[rs]

            return carry

        lax.fori_loop(0, 2, weights, 0)
    packed[...] = jnp.zeros_like(packed)
    for j in range(blocks):
        packed[j : j + 1, :] = up_sums[j]
        packed[blocks + j : blocks + j + 1, : sums.shape[2]] = sums[j]
    packed[2 * blocks : 2 * blocks + 3, :] = sums_a[0:3, :]
    packed[2 * blocks + 3 : 2 * blocks + 6, :] = sums_b[0:3, :]
    tops = (tops_a[0:1, :], tops_a[1:2, :], tops_m[0:1, :], jnp.maximum(top0[0:1, :], top1[0:1, :]))
    for j, top in enumerate(tops):
        packed[2 * blocks + 6 : 2 * blocks + 7, 128 * j : 128 * j + 128] = top


def token_backward(dims, lim, grads_0, grads_1, grad_first, tokens, weight, out, acc):
    blocks, cols, width = dims
    acc[...] = jnp.zeros_like(acc)
    half = grads_0.shape[0]
    for grads, first in ((grads_0, 0), (grads_1, half)):

        def back(i, carry):
            acc[...] += mm_nt(grads[i], weight[first + i, :, : 3 * cols + HEAD_DIM])
            return carry

        lax.fori_loop(0, half, back, 0)
    inputs = tokens[...].astype(f32)
    out[...] = (grad_first[...] + jnp.where(jnp.abs(inputs) <= lim[0], acc[...], 0.0)).astype(bf16)


def make_body(net):
    def body(
        tokens,
        cotangent,
        qkv_weight,
        qv_bias,
        out_weight,
        out_bias,
        first_gain,
        first_shift,
        up_weight,
        up_bias,
        down_weight,
        down_bias,
        second_gain,
        second_shift,
        act_ranges,
        long_lengths,
        short_lengths,
    ):
        lane = lax.axis_index("tensor")
        rows, width = tokens.shape
        assert rows == LONG_LEN
        cols = qkv_weight.shape[2]
        up_cols = up_weight.shape[1]
        blocks = lax.axis_size("tensor")
        half = blocks // 2
        dims = (blocks, cols, width)
        wide = 3 * cols + HEAD_DIM
        out_cols = cols + HEAD_DIM
        every = tuple(range(blocks))

        pieces_a, pieces_u, pieces_d = Pieces([]), Pieces([]), Pieces([])
        shard_a, shard_d, shard_p, bias_row = shards(qkv_weight, out_weight, qv_bias, up_bias, down_weight.T)
        job_a = Job(net.gather(shard_a, pieces_a))
        job_b = Job(net.gather_lane(bias_row))
        job_u = Job(net.gather(up_weight.astype(bf16), pieces_u))
        job_d = Job(net.gather(shard_d, pieces_d))
        job_p = Job(net.gather_plane_first(shard_p, pieces_d, up_cols // 2))

        def vmem(*shape, dtype=f32):
            return pltpu.VMEM(shape, dtype)

        unit = 2 * rows * width * width * blocks
        moved = 2 * width * width * blocks

        step((), None, [job_a, job_p, job_b], [job_a, job_p, job_b])
        step((), None, [job_a, job_p, job_b, job_d], [job_a, job_p, job_b])
        step((), None, [job_a, job_u], [job_a, job_u, job_d])
        step((), None, [job_a, job_u], [job_a, job_u])
        step((), None, [job_a, job_u], [job_a])
        biases = job_b.value

        bufs, plan = pieces_a.part(every)
        qkv, lse, in_t, ctx_low, ctx_slope, tops_a, weight_a = step(
            (act_ranges, long_lengths, short_lengths, tokens, biases, *bufs),
            call(
                functools.partial(attn_forward, net, plan, len(bufs), dims),
                "attn_forward",
                [SM] * 3 + [VM] * 2 + [VM] * len(bufs),
                [
                    like((blocks, rows, wide), bf16),
                    like((blocks, 8, rows)),
                    like((width, rows), bf16),
                    like((blocks, rows, out_cols), bf16),
                    like((blocks, rows, out_cols)),
                    like((8, 128)),
                    like((blocks, width, 4 * cols), bf16),
                ],
                [vmem(rows, width, dtype=bf16), vmem(rows, rows), vmem(out_cols, rows), vmem(8, out_cols)],
                4 * unit,
                3 * moved,
            ),
            [job_d, job_p],
            [job_u, job_d, job_p],
        )
        normed, inv, middle, mid_slope, mid_low, mid_t, tops_m = step(
            (act_ranges, ctx_low, tokens, out_bias, first_gain, first_shift, weight_a),
            call(
                functools.partial(attn_finish, dims),
                "attn_finish",
                [SM] + [VM] * 6,
                [
                    like((rows, width)),
                    like((rows, 1)),
                    like((rows, width)),
                    like((rows, width)),
                    like((rows, width), bf16),
                    like((width, rows), bf16),
                    like((8, 128)),
                ],
                [vmem(rows, width)],
                2 * unit,
                2 * moved,
            ),
            [job_u, job_p],
            [job_u],
        )

        def up_part(lanes, start, finish):
            bufs, plan = pieces_u.part(lanes)
            return step(
                (act_ranges, mid_low, biases, *bufs),
                call(
                    functools.partial(up_forward, net, plan, len(bufs), lanes[0], wide),
                    f"up_forward_{lanes[0]}",
                    [SM] + [VM] * 2 + [VM] * len(bufs),
                    [
                        like((half, rows, up_cols), bf16),
                        like((half, rows, up_cols)),
                        like((8, 128)),
                        like((half, width, up_cols), bf16),
                    ],
                    [vmem(8, up_cols)],
                    2 * unit,
                    2 * moved,
                ),
                start,
                finish,
            )

        act0, slope0, top0, weight_u0 = up_part(every[:half], [job_u, job_d], [job_u])
        act1, slope1, top1, weight_u1 = up_part(every[half:], [], [job_d, job_p])
        step((), None, [job_d], [job_d])
        step((), None, [job_d, job_p], [job_d, job_p])
        bufs_d, plan_d = pieces_d.part(every)
        layer_out, grad_second, ffn_t, sums_b, grad_up, up_sums = step(
            (act0, act1, slope0, slope1, middle, cotangent, down_bias, second_gain, second_shift, *bufs_d),
            call(
                functools.partial(down_both, net, plan_d, len(bufs_d)),
                "down_both",
                [VM] * 9 + [VM] * len(bufs_d),
                [
                    like((rows, width), bf16),
                    like((rows, width)),
                    like((width, rows), bf16),
                    like((8, width)),
                    like((blocks, rows, up_cols), bf16),
                    like((blocks, 1, up_cols)),
                ],
                [
                    vmem(blocks, width, up_cols, dtype=bf16),
                    vmem(rows, width),
                    vmem(rows, width, dtype=bf16),
                ],
                2 * unit,
                4 * moved,
            ),
        )

        grad_shape = like((net.parts, width // net.parts, up_cols), bf16)
        both_shape = like((half,) + grad_shape.shape, bf16)

        def grad_of(name, left_t, rights, start=(), finish=()):
            return step(
                (left_t, *rights),
                call(
                    functools.partial(weight_grad, net),
                    name,
                    [VM] * (1 + len(rights)),
                    [both_shape, both_shape],
                    (),
                    unit,
                    moved,
                ),
                start,
                finish,
            )

        sum_d = Job(net.scatter_z_first(*grad_of("down_grad", ffn_t, (act0, act1))))
        sum_u = Job(net.scatter_sum(*grad_of("up_grad", mid_t, (grad_up,), [sum_d], [sum_d])))
        grad_first, attn_low, attn_t, sums_a = step(
            (grad_up, grad_second, mid_slope, normed, inv, first_gain, weight_u0, weight_u1),
            call(
                mid_backward,
                "mid_backward",
                [VM] * 8,
                [like((rows, width)), like((rows, width), bf16), like((width, rows), bf16), like((8, width))],
                [vmem(rows, width)],
                unit + unit // 3,
                3 * moved,
            ),
            [sum_u, sum_d],
            [sum_u],
        )
        grads_1, more = step(
            (long_lengths, short_lengths, qkv, lse, attn_low, weight_a, ctx_slope),
            call(
                functools.partial(attn_backward, net, half, dims),
                "attn_backward",
                [SM] * 2 + [VM] * 5,
                [like((half, rows, wide), bf16), like((blocks, 1, wide))],
                [vmem(rows, rows), vmem(rows, out_cols, dtype=bf16)],
                2 * unit,
                2 * moved,
            ),
            [sum_u],
            [sum_u, sum_d],
        )
        grads_0, far, near, packed = step(
            (long_lengths, short_lengths, qkv, lse, attn_low, weight_a, ctx_slope)
            + (in_t, attn_t, ctx_low, grads_1, more)
            + (up_sums, sums_a, sums_b, tops_a, tops_m, top0, top1),
            call(
                functools.partial(attn_backward_last, net, dims),
                "attn_backward_last",
                [SM] * 2 + [VM] * 17,
                [like((half, rows, wide), bf16), both_shape, both_shape, like((16, width))],
                [vmem(blocks, 1, wide), vmem(rows, rows), vmem(rows, out_cols, dtype=bf16)],
                4 * unit,
                2 * moved,
            ),
            [sum_u, sum_d],
            [sum_u, sum_d],
        )
        sum_a = Job(net.scatter_sum(far, near))
        is_top = (jnp.arange(packed.shape[0]) == 2 * blocks + 6)[:, None]
        sum_s = Job(net.sum_max(packed, is_top))
        line_u = Job(net.scatter_line(*sum_u.value))
        tokens_grad = step(
            (act_ranges, grads_0, grads_1, grad_first, tokens, weight_a),
            call(
                functools.partial(token_backward, dims),
                "token_backward",
                [SM] + [VM] * 5,
                [like((rows, width), bf16)],
                [vmem(rows, width)],
                unit,
                2 * moved,
            ),
            [sum_a, sum_d, line_u, sum_s],
            [sum_a, sum_d, line_u, sum_s],
        )[0]
        step((), None, [sum_a, sum_d], [sum_a])
        step((), None, [sum_a, line_u, sum_s], [sum_a, sum_d, line_u, sum_s])
        line_a = Job(net.scatter_line(*sum_a.value))
        step((), None, [line_a, sum_s], [line_a, sum_s])
        step((), None, [line_a, sum_s], [sum_s])
        step((), None, [sum_s], [line_a, sum_s])

        packed = sum_s.value
        down_grad, up_grad = (kept + last.astype(f32) for kept, last in (sum_d.value, line_u.value))
        down_grad = down_grad.T
        qkv_grad, out_grad = attn_grads(*line_a.value)
        own = lax.dynamic_slice_in_dim(packed, blocks + lane, 1)
        shared = packed[2 * blocks : 2 * blocks + 6]
        qv_bias_grad = jnp.concatenate([own[:, :cols], own[:, 2 * cols : 3 * cols]], 0)
        up_bias_grad = lax.dynamic_slice_in_dim(packed, lane, 1)[0]
        new_ranges = ema_decay * act_ranges + (1.0 - ema_decay) * packed[2 * blocks + 6, 0:512:128]
        return (
            layer_out,
            tokens_grad,
            qkv_grad,
            qv_bias_grad,
            out_grad,
            shared[0],
            shared[1],
            shared[2],
            up_grad,
            up_bias_grad,
            down_grad,
            shared[3],
            shared[4],
            shared[5],
            new_ranges,
        )

    return body


def solution(mesh):
    in_specs = (
        P(ALL, None),
        P(ALL, None),
        P(None, "dp", "tensor"),
        P(None, "tensor"),
        P("tensor", "dp"),
        P(),
        P(),
        P(),
        P("dp", "tensor"),
        P("tensor"),
        P("tensor", "dp"),
        P(),
        P(),
        P(),
        P(),
        P("dp"),
        P("dp"),
    )
    out_specs = (
        P(ALL, None),
        P(ALL, None),
        P(None, "dp", "tensor"),
        P(None, "tensor"),
        P("tensor", "dp"),
        P(),
        P(),
        P(),
        P("dp", "tensor"),
        P("tensor"),
        P("tensor", "dp"),
        P(),
        P(),
        P(),
        P(),
    )
    net = Grid() if mesh.shape["dp"] == 8 and mesh.shape["tensor"] == 4 else Plain()
    return jax.shard_map(make_body(net), mesh=mesh, in_specs=in_specs, out_specs=out_specs, check_vma=False)
```
